32 devices in a mesh: dp: 16 (over z, x, core), tensor: 2 (over y).
Axes of the slice: x: 2, y: 2, z: 4, core: 2. Of those that a mesh axis runs over, the one named last changes fastest.
Arguments:
- tokens: bfloat16 [32768, 1024], P(('dp', 'tensor')), may hold values from -6 to 6
- alpha_logit: float32 [1024, 16], P('tensor'), may hold values from -6 to 0
- delta_logit: float32 [1024, 16], P('tensor'), may hold values from -3 to 3
- ema_beta: float32 [1024, 16], P('tensor'), may hold values from -1.73 to 1.73
- ema_eta: float32 [1024, 16], P('tensor'), may hold values from -0.43 to 0.43
- ema_omega: float32 [1024], P('tensor'), may hold values from -1.73 to 1.73
- w_z: bfloat16 [1024, 128], replicated, may hold values from -0.1875 to 0.1875
- qk_gain: float32 [2, 128], replicated, may hold values from -2.6 to 2.6
- qk_bias: float32 [2, 128], replicated, may hold values from -0.87 to 0.87
- w_v: bfloat16 [1024, 2048], P(None, 'tensor'), may hold values from -0.1875 to 0.1875
- w_gamma: bfloat16 [1024, 2048], P(None, 'tensor'), may hold values from -0.1875 to 0.1875
- u_h: bfloat16 [2048, 1024], P('tensor'), may hold values from -0.75 to 0.75
- w_h: bfloat16 [1024, 1024], P('tensor'), may hold values from -0.1875 to 0.1875
- w_phi: bfloat16 [1024, 1024], P('tensor'), may hold values from -0.1875 to 0.1875
- w_up: bfloat16 [1024, 4096], P(None, 'tensor'), may hold values from -0.1875 to 0.1875
- w_down: bfloat16 [4096, 1024], P('tensor'), may hold values from -0.09375 to 0.09375
- cotangent: bfloat16 [32768, 1024], P(('dp', 'tensor')), may hold values from -6 to 6
Outputs:
- output: bfloat16 [32768, 1024], P(('dp', 'tensor'))
- input_grad: float32 [32768, 1024], P(('dp', 'tensor'))
- alpha_grad: float32 [1024, 16], P('tensor')
- delta_grad: float32 [1024, 16], P('tensor')
- beta_grad: float32 [1024, 16], P('tensor')
- eta_grad: float32 [1024, 16], P('tensor')
- omega_grad: float32 [1024], P('tensor')
- z_grad: float32 [1024, 128], P('dp')
- gain_grad: float32 [2, 128], replicated
- bias_grad: float32 [2, 128], replicated
- value_grad: float32 [1024, 2048], P('dp', 'tensor')
- gamma_grad: float32 [1024, 2048], P('dp', 'tensor')
- uh_grad: float32 [2048, 1024], P('tensor', 'dp')
- wh_grad: float32 [1024, 1024], P('tensor', 'dp')
- phi_grad: float32 [1024, 1024], P('tensor', 'dp')
- up_grad: float32 [1024, 4096], P('dp', 'tensor')
- down_grad: float32 [4096, 1024], P('tensor', 'dp')
The draws below stay inside these ranges and needn't reach their ends.
All inputs are finite; a program needn't handle non-finite values.
Results may differ from the reference program's by a relative error of at most 0.023.
Values may be sent and summed in bfloat16 or wider, within the bound.
No kernel may reach another device: no remote copies, remote signals or barrier semaphores. Data moves between devices by JAX's collectives and lax.ppermute only.
A program may use at most 320 MiB of HBM per device.

```python
import jax
import jax.numpy as jnp
from jax import lax

D = 1024
Z = 128
V = 2048
H = 16
F = 4096
LEN = 1024
SEQS = 2
TOKENS = 32768
VB = 1024
N_DP = 16
N_TENSOR = 2


def spiked(array, stream_key, source, target, shards_of, factor):
    owner, partner = [(jnp.arange(array.shape[dim]) // (array.shape[dim] // shards_of)).reshape([-1 if axis == dim else 1 for axis in range(array.ndim)]) for dim in (source, target)]
    chosen = jax.random.permutation(stream_key, shards_of)[partner]
    strong = (owner == chosen) | (owner == (partner + shards_of // 2) % shards_of)
    return jnp.where(strong, factor * array, array)


def levels(rng, extent, cuts, low, largest):
    loudness, own = 1.0, jax.random.fold_in(rng, 6)
    for dim, blocks in cuts:
        heights = jnp.exp(jax.random.uniform(jax.random.fold_in(own, dim), (blocks,), jnp.float32, low / len(cuts), largest / len(cuts)))
        loudness = loudness * jnp.repeat(heights, extent[dim] // blocks).reshape([-1 if axis == dim else 1 for axis in range(len(extent))])
    return loudness


def normal_values(own_key, extent, spread, limit, cuts=(), kind=jnp.bfloat16):
    array = jax.random.normal(own_key, extent, jnp.float32) * spread
    if len(cuts) > 0:
        array = levels(own_key, extent, cuts, -0.22, 0.18) * array
    return jnp.clip(array, min=-limit, max=limit).astype(kind)


def bell_draw_with(key, dims, width, most, shards, heavy, kind=jnp.bfloat16):
    drawn = width * jax.random.normal(key, dims, jnp.float32)
    if shards:
        drawn = drawn * levels(key, dims, shards, -0.22, 0.18)
    return jnp.clip(spiked(drawn, jax.random.fold_in(key, 3), *heavy), -most, most).astype(kind)


def setup_inputs(seed: int = 0) -> dict:
    splits = jax.random.split(jax.random.key(seed), 18)
    tokens = bell_draw_with(splits[0], (TOKENS, D), 1.0, 6.0, ((0, 32),), (0, 1, 32, 2.75))
    alpha_logit = jnp.clip(-6.0 + 6.0 * jax.random.uniform(splits[1], (D, H), jnp.float32) ** levels(splits[1], (D, H), ((0, 2),), -0.2, 0.2), -6.0, 0.0)
    delta_logit = jnp.clip(jax.random.uniform(splits[2], (D, H), jnp.float32, -3.0, 3.0) * levels(splits[2], (D, H), ((0, 2),), -0.4, 0.0), -3.0, 3.0)
    ema_beta = jnp.clip(jax.random.uniform(splits[3], (D, H), jnp.float32, -1.73, 1.73) * levels(splits[3], (D, H), ((0, 2),), -0.4, 0.0), -1.73, 1.73)
    ema_eta = jnp.clip(jax.random.uniform(splits[4], (D, H), jnp.float32, -0.43, 0.43) * levels(splits[4], (D, H), ((0, 2),), -0.4, 0.0), -0.43, 0.43)
    ema_omega = jnp.clip(jax.random.uniform(splits[5], (D,), jnp.float32, -1.73, 1.73) * levels(splits[5], (D,), ((0, 2),), -0.4, 0.0), -1.73, 1.73)
    w_z = normal_values(splits[6], (D, Z), D ** -0.5, 0.1875)
    qk_gain = jnp.clip(jax.random.uniform(splits[7], (2, Z), jnp.float32, -2.6, 2.6), -2.6, 2.6)
    qk_bias = jnp.clip(jax.random.uniform(splits[8], (2, Z), jnp.float32, -0.87, 0.87), -0.87, 0.87)
    w_v = normal_values(splits[9], (D, V), D ** -0.5, 0.1875, ((1, 2),))
    w_gamma = normal_values(splits[10], (D, V), D ** -0.5, 0.1875, ((1, 2),))
    u_h = normal_values(splits[11], (V, D), (V // 32) ** -0.5, 0.75, ((0, 2),))
    w_h = normal_values(splits[12], (D, D), D ** -0.5, 0.1875, ((0, 2),))
    w_phi = normal_values(splits[13], (D, D), D ** -0.5, 0.1875, ((0, 2),))
    w_up = normal_values(splits[14], (D, F), D ** -0.5, 0.1875, ((1, 2),))
    w_down = normal_values(splits[15], (F, D), F ** -0.5, 0.09375, ((0, 2),))
    cotangent = bell_draw_with(splits[16], (TOKENS, D), 1.0, 6.0, ((0, 32),), (0, 1, 32, 2.75))
    return dict(tokens=tokens, alpha_logit=alpha_logit, delta_logit=delta_logit, ema_beta=ema_beta, ema_eta=ema_eta, ema_omega=ema_omega, w_z=w_z, qk_gain=qk_gain, qk_bias=qk_bias, w_v=w_v, w_gamma=w_gamma, u_h=u_h, w_h=w_h, w_phi=w_phi, w_up=w_up, w_down=w_down, cotangent=cotangent)


norm_eps = 1e-06
masked_value = -1e+30

@jax.custom_vjp
def low(v):
    return lax.optimization_barrier(v.astype(jnp.bfloat16)).astype(jnp.float32)

@jax.custom_vjp
def low_back(v):
    return v

def low_keep(v):
    return (low(v), None)

def low_pass(kept, grad):
    return (grad,)

def back_keep(v):
    return (v, None)

def back_low(kept, grad):
    return (low(grad),)
low.defvjp(low_keep, low_pass)
low_back.defvjp(back_keep, back_low)

def matmul_hi(left, right):
    return jnp.dot(left, right, precision=lax.Precision.HIGHEST)

def rms_rows(values_in):
    return values_in * lax.rsqrt(lax.optimization_barrier(jnp.mean(values_in * values_in, axis=-1, keepdims=True)) + norm_eps)

def ema_kernel(alpha_logit, delta_logit, ema_beta, ema_eta):
    alpha_rate = jax.nn.sigmoid(alpha_logit)
    decay_rate = 1.0 - alpha_rate * jax.nn.sigmoid(delta_logit)
    lags = jnp.arange(LEN, dtype=jnp.float32)
    powers = jnp.exp(lags[:, None, None] * jnp.log(decay_rate)[None])
    return lax.optimization_barrier(jnp.sum(powers * (alpha_rate * ema_beta * ema_eta)[None], axis=-1))

def ema_mix(signal, kernel):
    spectrum = jnp.fft.rfft(signal, n=2 * LEN, axis=0) * jnp.fft.rfft(kernel, n=2 * LEN, axis=0)
    return jnp.fft.irfft(spectrum, n=2 * LEN, axis=0)[:LEN]

def attention(query, key_rows, value_rows):
    seq_count = query.shape[0] // LEN
    scale = Z ** (-0.5)
    position = jnp.arange(LEN)
    visible = position[None, :] <= position[:, None]

    def one_seq(triple):
        q_seq, k_seq, v_seq = triple
        raw_scores = matmul_hi(q_seq, k_seq.T) * scale
        pieces = []
        for part_id in range(N_TENSOR):
            scores = jnp.where(visible, low_back(raw_scores), masked_value)
            probs = low(jax.nn.softmax(scores, axis=-1))
            pieces.append(matmul_hi(probs, v_seq[:, part_id * VB:(part_id + 1) * VB]))
        return jnp.concatenate(pieces, axis=-1)
    stacked = (query.reshape(seq_count, LEN, Z), key_rows.reshape(seq_count, LEN, Z), value_rows.reshape(seq_count, LEN, V))
    return lax.map(jax.checkpoint(one_seq), stacked).reshape(-1, V)

def forward(x_rows, alpha_logit, delta_logit, ema_beta, ema_eta, ema_omega, w_z, qk_gain, qk_bias, w_v, w_gamma, u_h, w_h, w_phi, w_up, w_down):
    seq_count = x_rows.shape[0] // LEN
    normed = low(rms_rows(x_rows))
    kernel = ema_kernel(alpha_logit, delta_logit, ema_beta, ema_eta)
    signal = normed.reshape(seq_count, LEN, D)
    ema_pre = jax.vmap(lambda one_signal: ema_mix(one_signal, kernel))(signal).reshape(-1, D) + ema_omega * normed
    ema_out = low(jax.nn.silu(ema_pre))
    z_pre = low_back(matmul_hi(ema_out, w_z))
    z_act = jax.nn.silu(z_pre)
    query = low(z_act * qk_gain[0] + qk_bias[0])
    key_rows = low(z_act * qk_gain[1] + qk_bias[1])
    values = low(jax.nn.silu(low_back(matmul_hi(normed, w_v))))
    gamma = jax.nn.silu(low_back(matmul_hi(ema_out, w_gamma)))
    attended = low_back(attention(query, key_rows, values))
    gated = low(gamma * attended)
    h_pre = low_back(matmul_hi(gated, u_h) + matmul_hi(ema_out, w_h))
    f_pre = low_back(matmul_hi(ema_out, w_phi))
    update = jax.nn.sigmoid(f_pre)
    mixed = update * jax.nn.silu(h_pre) + (1.0 - update) * x_rows
    lowered = low(rms_rows(mixed))
    up_pre = low_back(matmul_hi(lowered, w_up))
    hidden = low(jax.nn.silu(up_pre))
    return mixed + matmul_hi(hidden, w_down)

def reference(tokens, alpha_logit, delta_logit, ema_beta, ema_eta, ema_omega, w_z, qk_gain, qk_bias, w_v, w_gamma, u_h, w_h, w_phi, w_up, w_down, cotangent):
    weights = tuple((array_in.astype(jnp.float32) for array_in in (alpha_logit, delta_logit, ema_beta, ema_eta, ema_omega, w_z, qk_gain, qk_bias, w_v, w_gamma, u_h, w_h, w_phi, w_up, w_down)))
    group_rows = SEQS * LEN
    inputs = tokens.astype(jnp.float32).reshape(N_DP, group_rows, D)
    grads_in = cotangent.astype(jnp.float32).reshape(N_DP, group_rows, D)

    def one_group(totals, group_pair):
        x_group, g_group = group_pair
        result, pull = jax.vjp(forward, x_group, *weights)
        grads = pull(g_group)
        totals = tuple((total_val + grad_val for total_val, grad_val in zip(totals, grads[1:])))
        return (totals, (result, grads[0]))
    start_totals = tuple((jnp.zeros(array_in.shape, jnp.float32) for array_in in weights))
    totals, (results, d_inputs) = lax.scan(one_group, start_totals, (inputs, grads_in))
    return (results.reshape(TOKENS, D).astype(jnp.bfloat16), d_inputs.reshape(TOKENS, D), totals[0], totals[1], totals[2], totals[3], totals[4], totals[5], totals[6], totals[7], totals[8], totals[9], totals[10], totals[11], totals[12], totals[13], totals[14])
```

```python
import math

import jax
import jax.numpy as jnp
from jax import lax
from jax.experimental import pallas as pl
from jax.experimental.pallas import tpu as pltpu
from jax.sharding import PartitionSpec as P

H = 16
LEN = 1024
ATT_BLOCK = 512
EMA_BLOCK = 128


norm_eps = 1e-06
masked_value = -1e30


def rms_rows(values_in):
    return values_in * lax.rsqrt(jnp.mean(values_in * values_in, axis=-1, keepdims=True) + norm_eps)


def matmul(left, right):
    return jnp.dot(left, right, preferred_element_type=jnp.float32)


def row_inner(left, right):
    return lax.dot_general(
        left, right, (((0,), (0,)), ((), ())), preferred_element_type=jnp.float32
    )


def col_inner(left, right):
    return lax.dot_general(
        left, right, (((1,), (1,)), ((), ())), preferred_element_type=jnp.float32
    )


def silu_slope(pre_act):
    logistic = jax.nn.sigmoid(pre_act)
    return logistic * (1.0 + pre_act * (1.0 - logistic))


def gate_apply(h_pre, f_pre, x_rows):
    update = jax.nn.sigmoid(f_pre)
    return update * jax.nn.silu(h_pre) + (1.0 - update) * x_rows


def ema_apply(signal, ema_params):
    alpha_logit, delta_logit, ema_beta, ema_eta, ema_omega = ema_params
    alpha_rate = jax.nn.sigmoid(alpha_logit)
    decay_rate = 1.0 - alpha_rate * jax.nn.sigmoid(delta_logit)
    feed_rate = alpha_rate * ema_beta
    log_decay = jnp.log(decay_rate)
    total_rows, chan_count = signal.shape
    seq_count = total_rows // LEN
    block_count = LEN // EMA_BLOCK
    blocks = signal.reshape(seq_count, block_count, EMA_BLOCK, chan_count)
    steps_in = jnp.arange(EMA_BLOCK, dtype=jnp.float32)
    lag_power = jnp.exp(steps_in[:, None, None] * log_decay[None])
    kernel = jnp.sum(lag_power * (feed_rate * ema_eta)[None], axis=-1)
    offsets = steps_in[:, None] - steps_in[None, :]
    lag_index = jnp.clip(offsets, 0, EMA_BLOCK - 1).astype(jnp.int32)
    toeplitz = jnp.where((offsets >= 0)[:, :, None], kernel[lag_index], 0.0)
    local_part = jnp.einsum("ijc,snjc->snic", toeplitz, blocks)
    tail_power = lag_power[::-1] * feed_rate[None]
    block_state = jnp.einsum("jch,snjc->snch", tail_power, blocks)
    full_decay = jnp.exp(EMA_BLOCK * log_decay)

    def carry_step(state_in, incoming):
        return (full_decay * state_in + incoming, state_in)

    zero_state = jnp.zeros((seq_count, chan_count, H), jnp.float32)
    _, start_state = lax.scan(carry_step, zero_state, jnp.moveaxis(block_state, 1, 0))
    start_state = jnp.moveaxis(start_state, 0, 1)
    head_power = lag_power * decay_rate[None] * ema_eta[None]
    carried = jnp.einsum("ich,snch->snic", head_power, start_state)
    ema_pre = (local_part + carried).reshape(total_rows, chan_count) + ema_omega * signal
    return jax.nn.silu(ema_pre)


def masked_scores(q_rows, k_rows, first_row):
    raw_scores = col_inner(q_rows, k_rows) * q_rows.shape[1] ** (-0.5)
    row_pos = first_row + jnp.arange(q_rows.shape[0])[:, None]
    col_pos = jnp.arange(k_rows.shape[0])[None, :]
    return jnp.where(col_pos <= row_pos, raw_scores, masked_value)


def attend_forward(query_low, key_low, value_low):
    total_rows, value_width = value_low.shape
    seq_count = total_rows // LEN
    per_seq = LEN // ATT_BLOCK

    def attend_one_block(flat_index):
        seq_id = flat_index // per_seq
        blk_id = flat_index % per_seq
        seq_start = seq_id * LEN
        q_rows = lax.dynamic_slice_in_dim(query_low, seq_start + blk_id * ATT_BLOCK, ATT_BLOCK, 0)
        k_rows = lax.dynamic_slice_in_dim(key_low, seq_start, LEN, 0)
        v_rows = lax.dynamic_slice_in_dim(value_low, seq_start, LEN, 0)
        scores = masked_scores(q_rows, k_rows, blk_id * ATT_BLOCK)
        top_score = jnp.max(scores, axis=-1, keepdims=True)
        weights = jnp.exp(scores - top_score)
        total_weight = jnp.sum(weights, axis=-1, keepdims=True)
        probs = (weights / total_weight).astype(jnp.bfloat16)
        return (matmul(probs, v_rows), top_score[:, 0] + jnp.log(total_weight[:, 0]))

    outs, lse_all = lax.map(attend_one_block, jnp.arange(seq_count * per_seq))
    return (outs.reshape(total_rows, value_width), lse_all.reshape(total_rows))


def attend_backward(query_low, key_low, value_low, lse_rows, d_att):
    total_rows, value_width = value_low.shape
    head_width = query_low.shape[1]
    seq_count = total_rows // LEN
    per_seq = LEN // ATT_BLOCK
    scale = head_width ** (-0.5)

    def one_seq(seq_id):
        seq_start = seq_id * LEN
        k_rows = lax.dynamic_slice_in_dim(key_low, seq_start, LEN, 0)
        v_rows = lax.dynamic_slice_in_dim(value_low, seq_start, LEN, 0)

        def one_one_block(carry_in, blk_id):
            d_keys, d_vals = carry_in
            row_start = seq_start + blk_id * ATT_BLOCK
            q_rows = lax.dynamic_slice_in_dim(query_low, row_start, ATT_BLOCK, 0)
            g_rows = lax.dynamic_slice_in_dim(d_att, row_start, ATT_BLOCK, 0)
            lse_part = lax.dynamic_slice_in_dim(lse_rows, row_start, ATT_BLOCK, 0)
            probs = jnp.exp(masked_scores(q_rows, k_rows, blk_id * ATT_BLOCK) - lse_part[:, None])
            d_probs = col_inner(g_rows, v_rows)
            d_scores = (
                probs * (d_probs - jnp.sum(probs * d_probs, axis=-1, keepdims=True))
            ).astype(jnp.bfloat16)
            d_rows = matmul(d_scores, k_rows) * scale
            d_keys = d_keys + row_inner(d_scores, q_rows) * scale
            d_vals = d_vals + row_inner(probs.astype(jnp.bfloat16), g_rows)
            return ((d_keys, d_vals), d_rows)

        start_carry = (
            jnp.zeros((LEN, head_width), jnp.float32),
            jnp.zeros((LEN, value_width), jnp.float32),
        )
        (d_keys, d_vals), d_rows = lax.scan(one_one_block, start_carry, jnp.arange(per_seq))
        return (d_rows.reshape(LEN, head_width), d_keys, d_vals)

    d_query, d_key, d_value = lax.map(one_seq, jnp.arange(seq_count))
    return (
        d_query.reshape(total_rows, head_width),
        d_key.reshape(total_rows, head_width),
        d_value.reshape(total_rows, value_width),
    )


def shards(
    tokens,
    alpha_logit,
    delta_logit,
    ema_beta,
    ema_eta,
    ema_omega,
    w_z,
    qk_gain,
    qk_bias,
    w_v,
    w_gamma,
    u_h,
    w_h,
    w_phi,
    w_up,
    w_down,
    cotangent,
):
    tensor_pos = lax.axis_index("tensor")
    feature_count = tokens.shape[1]
    chan_count = ema_omega.shape[0]
    chan_start = tensor_pos * chan_count
    x_rows = tokens.astype(jnp.float32)
    normed_rows, norm_pull = jax.vjp(rms_rows, x_rows)
    normed, cot_full = (
        lax.all_gather(normed_rows.astype(jnp.bfloat16), "tensor", axis=0, tiled=True),
        lax.all_gather(cotangent, "tensor", axis=0, tiled=True),
    )
    signal = lax.dynamic_slice_in_dim(normed, chan_start, chan_count, 1).astype(jnp.float32)
    ema_params = (alpha_logit, delta_logit, ema_beta, ema_eta, ema_omega)
    ema_val, ema_pull = jax.vjp(ema_apply, signal, ema_params)
    ema_low = ema_val.astype(jnp.bfloat16)
    ema_full = lax.all_gather(ema_low, "tensor", axis=1, tiled=True)
    z_pre = matmul(ema_full, w_z)
    z_act = jax.nn.silu(z_pre)
    query_low = (z_act * qk_gain[0] + qk_bias[0]).astype(jnp.bfloat16)
    key_low = (z_act * qk_gain[1] + qk_bias[1]).astype(jnp.bfloat16)
    values_pre = matmul(normed, w_v)
    value_low = jax.nn.silu(values_pre).astype(jnp.bfloat16)
    gamma_pre = matmul(ema_full, w_gamma)
    gamma_act = jax.nn.silu(gamma_pre)
    attended, lse_rows = attend_forward(query_low, key_low, value_low)
    gated_low = (gamma_act * attended).astype(jnp.bfloat16)
    both_pre = lax.psum_scatter(
        jnp.concatenate(
            [matmul(gated_low, u_h) + matmul(ema_low, w_h), matmul(ema_low, w_phi)], axis=1
        ),
        "tensor",
        scatter_dimension=0,
        tiled=True,
    )
    h_pre = both_pre[:, :feature_count]
    f_pre = both_pre[:, feature_count:]
    mixed, gate_pull = jax.vjp(gate_apply, h_pre, f_pre, x_rows)
    normed_two, norm_two_pull = jax.vjp(rms_rows, mixed)
    lowered = lax.all_gather(normed_two.astype(jnp.bfloat16), "tensor", axis=0, tiled=True)
    up_pre = matmul(lowered, w_up)
    hidden = jax.nn.silu(up_pre).astype(jnp.bfloat16)
    down_rows = lax.psum_scatter(
        matmul(hidden, w_down).astype(jnp.bfloat16), "tensor", scatter_dimension=0, tiled=True
    ).astype(jnp.float32)
    output = (mixed + down_rows).astype(jnp.bfloat16)
    cot_rows = cotangent.astype(jnp.float32)
    d_hidden = col_inner(cot_full, w_down)
    d_up = (d_hidden * silu_slope(up_pre)).astype(jnp.bfloat16)
    down_grad = row_inner(hidden, cot_full)
    up_grad = row_inner(lowered, d_up)
    d_lowered = lax.psum_scatter(col_inner(d_up, w_up), "tensor", scatter_dimension=0, tiled=True)
    d_mixed = cot_rows + norm_two_pull(d_lowered)[0]
    d_hpre, d_fpre, d_direct = gate_pull(d_mixed)
    h_full_grad, f_full_grad = (
        lax.all_gather(d_hpre.astype(jnp.bfloat16), "tensor", axis=0, tiled=True),
        lax.all_gather(d_fpre.astype(jnp.bfloat16), "tensor", axis=0, tiled=True),
    )
    uh_grad = row_inner(gated_low, h_full_grad)
    wh_grad = row_inner(ema_low, h_full_grad)
    phi_grad = row_inner(ema_low, f_full_grad)
    d_gated = col_inner(h_full_grad, u_h)
    d_att = (d_gated * gamma_act).astype(jnp.bfloat16)
    d_gamma = (d_gated * attended * silu_slope(gamma_pre)).astype(jnp.bfloat16)
    d_query, d_key, d_value = attend_backward(query_low, key_low, value_low, lse_rows, d_att)
    d_query, d_key = lax.psum((d_query, d_key), "tensor")
    d_z = (silu_slope(z_pre) * (d_query * qk_gain[0] + d_key * qk_gain[1])).astype(jnp.bfloat16)
    gain_grad = jnp.stack([jnp.sum(d_query * z_act, axis=0), jnp.sum(d_key * z_act, axis=0)])
    bias_grad = jnp.stack([jnp.sum(d_query, axis=0), jnp.sum(d_key, axis=0)])
    z_grad = row_inner(ema_full, d_z)
    gamma_grad = row_inner(ema_full, d_gamma)
    d_value_pre = (d_value * silu_slope(values_pre)).astype(jnp.bfloat16)
    value_grad = row_inner(normed, d_value_pre)
    d_chan = lax.psum_scatter(
        col_inner(d_gamma, w_gamma).astype(jnp.bfloat16), "tensor", scatter_dimension=1, tiled=True
    ).astype(jnp.float32)
    z_rows = lax.dynamic_slice_in_dim(w_z, chan_start, chan_count, 0)
    d_chan = (
        d_chan
        + col_inner(d_z, z_rows)
        + col_inner(h_full_grad, w_h)
        + col_inner(f_full_grad, w_phi)
    )
    d_signal, d_params = ema_pull(d_chan)
    d_norm_part = col_inner(d_value_pre, w_v)
    own_cols = lax.dynamic_slice_in_dim(d_norm_part, chan_start, chan_count, 1)
    d_norm_part = lax.dynamic_update_slice_in_dim(d_norm_part, own_cols + d_signal, chan_start, 1)
    d_normed = lax.psum_scatter(
        d_norm_part.astype(jnp.bfloat16), "tensor", scatter_dimension=0, tiled=True
    ).astype(jnp.float32)
    input_grad = d_direct + norm_pull(d_normed)[0]
    weight_totals = (
        lax.psum_scatter(z_grad.astype(jnp.bfloat16), "dp", scatter_dimension=0, tiled=True).astype(
            jnp.float32
        ),
        lax.psum_scatter(
            value_grad.astype(jnp.bfloat16), "dp", scatter_dimension=0, tiled=True
        ).astype(jnp.float32),
        lax.psum_scatter(
            gamma_grad.astype(jnp.bfloat16), "dp", scatter_dimension=0, tiled=True
        ).astype(jnp.float32),
        lax.psum_scatter(
            uh_grad.astype(jnp.bfloat16), "dp", scatter_dimension=1, tiled=True
        ).astype(jnp.float32),
        lax.psum_scatter(
            wh_grad.astype(jnp.bfloat16), "dp", scatter_dimension=1, tiled=True
        ).astype(jnp.float32),
        lax.psum_scatter(
            phi_grad.astype(jnp.bfloat16), "dp", scatter_dimension=1, tiled=True
        ).astype(jnp.float32),
        lax.psum_scatter(
            up_grad.astype(jnp.bfloat16), "dp", scatter_dimension=0, tiled=True
        ).astype(jnp.float32),
        lax.psum_scatter(
            down_grad.astype(jnp.bfloat16), "dp", scatter_dimension=1, tiled=True
        ).astype(jnp.float32),
    )
    param_totals = lax.psum(
        (d_params[0], d_params[1], d_params[2], d_params[3], d_params[4], gain_grad, bias_grad),
        "dp",
    )
    return (
        output,
        input_grad,
        param_totals[0],
        param_totals[1],
        param_totals[2],
        param_totals[3],
        param_totals[4],
        weight_totals[0],
        param_totals[5],
        param_totals[6],
        weight_totals[1],
        weight_totals[2],
        weight_totals[3],
        weight_totals[4],
        weight_totals[5],
        weight_totals[6],
        weight_totals[7],
    )


CP = pltpu.CompilerParams(vmem_limit_bytes=56 * 1024 * 1024)
BF = jnp.bfloat16
F32 = jnp.float32
ROWS = 256


def sds(shape, dtype=BF):
    return jax.ShapeDtypeStruct(shape, dtype)


def whole(shape):
    return pl.BlockSpec(shape, lambda i, s: (0,) * len(shape), pipeline_mode=pl.Buffered(1))


def rows_of(cols, rows=ROWS):
    return pl.BlockSpec((rows, cols), lambda i, s: (i, 0))


def cols_of(rows, cols):
    return pl.BlockSpec((rows, cols), lambda i, s: (0, i))


def run(body, grid, scal, ins, in_specs, out_shape, out_specs, scratch=(), flops=0, name=None):
    moved = sum(a.size * a.dtype.itemsize for a in ins)
    moved += sum(math.prod(o.shape) * jnp.dtype(o.dtype).itemsize for o in out_shape)
    return pl.pallas_call(
        body,
        out_shape=out_shape,
        grid_spec=pltpu.PrefetchScalarGridSpec(
            num_scalar_prefetch=1,
            grid=grid,
            in_specs=in_specs,
            out_specs=out_specs,
            scratch_shapes=list(scratch),
        ),
        compiler_params=CP,
        cost_estimate=pl.CostEstimate(flops=int(flops), bytes_accessed=int(moved), transcendentals=0),
        name=name,
    )(scal, *ins)


def sig(u):
    return 1.0 / (1.0 + jnp.exp(-u))


def silu_pair(u):
    s = sig(u)
    return u * s, s * (1.0 + u * (1.0 - s))


def place(scr, s, pieces, base=0):
    rows = pieces[0].shape[0]
    for p in range(4):
        scr[pl.ds(pl.multiple_of(base + s[p] * rows, rows), rows), :] = pieces[p][...]


def piece_block(rows, cols, row_block):
    return pl.BlockSpec((rows, cols), lambda i, s: (row_block, i))


def piece_whole(rows, cols, row_block):
    return pl.BlockSpec((rows, cols), lambda i, s: (row_block, 0), pipeline_mode=pl.Buffered(1))


def k_value_own(scal, tokens, w_own):
    n, d = tokens.shape
    cols = w_own.shape[1]
    tn = 512

    def body(s, x_ref, w_ref, n_ref, v_ref, sl_ref):
        @pl.when(pl.program_id(0) == 0)
        def _():
            x = x_ref[...].astype(F32)
            n_ref[...] = (x * lax.rsqrt(jnp.mean(x * x, axis=-1, keepdims=True) + norm_eps)).astype(BF)

        act, slope = silu_pair(matmul(n_ref[...], w_ref[...]))
        v_ref[...] = act.astype(BF)
        sl_ref[...] = slope.astype(BF)

    return run(
        body, (cols // tn,), scal, [tokens, w_own],
        [whole((n, d)), cols_of(d, tn)],
        [sds((n, d)), sds((n, cols)), sds((n, cols))],
        [pl.BlockSpec((n, d), lambda i, s: (0, 0)), cols_of(n, tn), cols_of(n, tn)],
        flops=2 * n * d * cols, name="value_own",
    )


def k_act_own(scal, x, w_own, tn):
    n, d = x.shape
    cols = w_own.shape[1]

    def body(s, x_ref, w_ref, v_ref, sl_ref):
        act, slope = silu_pair(matmul(x_ref[...], w_ref[...]))
        v_ref[...] = act.astype(BF)
        sl_ref[...] = slope.astype(BF)

    return run(
        body, (cols // tn,), scal, [x, w_own],
        [whole((n, d)), cols_of(d, tn)],
        [sds((n, cols)), sds((n, cols))],
        [cols_of(n, tn), cols_of(n, tn)],
        flops=2 * n * d * cols, name="act_own",
    )


def k_act_other(scal, x, pieces, rows, row_block, tn):
    n, d = x.shape
    cols = pieces[0].shape[1]

    def body(s, x_ref, p0, p1, p2, p3, v_ref, sl_ref, w_scr):
        place(w_scr, s, (p0, p1, p2, p3))
        act, slope = silu_pair(matmul(x_ref[...], w_scr[...]))
        v_ref[...] = act.astype(BF)
        sl_ref[...] = slope.astype(BF)

    return run(
        body, (cols // tn,), scal, [x, *pieces],
        [whole((n, d))] + [piece_block(rows, tn, row_block)] * 4,
        [sds((n, cols)), sds((n, cols))],
        [cols_of(n, tn), cols_of(n, tn)],
        [pltpu.VMEM((d, tn), BF)],
        flops=2 * n * d * cols, name="act_other",
    )


def k_query_key(scal, ema_low, w_z, qk_gain, qk_bias):
    n, d = ema_low.shape
    zw = w_z.shape[1]

    def body(s, e_ref, w_ref, g_ref, b_ref, z_ref, q_ref, k_ref):
        z_pre = matmul(e_ref[...], w_ref[...])
        z_ref[...] = z_pre
        act = z_pre * sig(z_pre)
        q_ref[...] = (act * g_ref[0:1, :] + b_ref[0:1, :]).astype(BF)
        k_ref[...] = (act * g_ref[1:2, :] + b_ref[1:2, :]).astype(BF)

    return run(
        body, (2,), scal, [ema_low, w_z, qk_gain, qk_bias],
        [rows_of(d, n // 2), whole((d, zw)), whole((2, zw)), whole((2, zw))],
        [sds((n, zw), F32), sds((n, zw)), sds((n, zw))],
        [rows_of(zw, n // 2)] * 3,
        flops=2 * n * d * zw, name="query_key",
    )


def k_ema_forward(scal, normed, decay, coef, omega):
    n, d = normed.shape
    groups = d // 128
    tb = 128

    def body(s, x_ref, dec_ref, cf_ref, om_ref, e_ref, sl_ref, st, xs, ys):
        @pl.when(pl.program_id(0) == 0)
        def _():
            st[...] = jnp.zeros_like(st)

        for g in range(groups):
            xs[pl.ds(g, tb, stride=groups), :] = x_ref[:, g * 128 : (g + 1) * 128].astype(F32)
        dec = [dec_ref[k * groups : (k + 1) * groups, :] for k in range(H)]
        cf = [cf_ref[k * groups : (k + 1) * groups, :] for k in range(H)]
        om = om_ref[...]

        def steps(b, carry):
            states = list(carry)
            for u in range(8):
                row = pl.multiple_of((b * 8 + u) * groups, groups)
                xt = xs[pl.ds(row, groups), :]
                parts = [om * xt, None, None, None]
                for k in range(H):
                    states[k] = dec[k] * states[k] + xt
                    term = cf[k] * states[k]
                    parts[k % 4] = term if parts[k % 4] is None else parts[k % 4] + term
                ys[pl.ds(row, groups), :] = (parts[0] + parts[1]) + (parts[2] + parts[3])
            return tuple(states)

        start = tuple(st[k * groups : (k + 1) * groups, :] for k in range(H))
        end = lax.fori_loop(0, tb // 8, steps, start)
        for k in range(H):
            st[k * groups : (k + 1) * groups, :] = end[k]
        for g in range(groups):
            act, slope = silu_pair(ys[pl.ds(g, tb, stride=groups), :])
            e_ref[:, g * 128 : (g + 1) * 128] = act.astype(BF)
            sl_ref[:, g * 128 : (g + 1) * 128] = slope.astype(BF)

    return run(
        body, (n // tb,), scal, [normed, decay, coef, omega],
        [rows_of(d, tb), whole((H * groups, 128)), whole((H * groups, 128)), whole((groups, 128))],
        [sds((n, d)), sds((n, d))],
        [rows_of(d, tb)] * 2,
        [pltpu.VMEM((H * groups, 128), F32), pltpu.VMEM((tb * groups, 128), F32), pltpu.VMEM((tb * groups, 128), F32)],
        flops=20e9, name="ema_forward",
    )


def k_ema_backward(scal, normed, d_e, decay, coef, omega):
    n, d = normed.shape
    groups = d // 128
    tb = 128
    nb = n // tb
    half = H // 2
    gh = groups * half

    def body(s, x_ref, g_ref, dec_ref, cf_ref, om_ref, o_ref, a_ref, b_ref, w_ref, back, deriv, xs, gs, ys):
        @pl.when(pl.program_id(0) == 0)
        def _():
            back[...] = jnp.zeros_like(back)
            deriv[...] = jnp.zeros_like(deriv)
            a_ref[...] = jnp.zeros_like(a_ref)
            b_ref[...] = jnp.zeros_like(b_ref)
            w_ref[...] = jnp.zeros_like(w_ref)

        for g in range(groups):
            xs[pl.ds(g, tb, stride=groups), :] = x_ref[:, g * 128 : (g + 1) * 128].astype(F32)
            gs[pl.ds(g, tb, stride=groups), :] = g_ref[:, g * 128 : (g + 1) * 128]

        for part in range(2):
            first = part * gh
            at = [slice(first + k * groups, first + (k + 1) * groups) for k in range(half)]
            dec = [dec_ref[a, :] for a in at]

            def steps(b, carry, part=part, at=at, dec=dec):
                bk, dv, aa, bb, ww = (list(c) for c in carry)
                for u in range(4):
                    row = pl.multiple_of((tb - 1 - (b * 4 + u)) * groups, groups)
                    xt = xs[pl.ds(row, groups), :]
                    gt = gs[pl.ds(row, groups), :]
                    if part == 0:
                        outs = [om_ref[...] * gt, None]
                        ww[0] = ww[0] + xt * gt
                    else:
                        outs = [ys[pl.ds(row, groups), :], None]
                    for k in range(half):
                        dv[k] = dec[k] * dv[k] + bk[k]
                        bk[k] = dec[k] * bk[k] + gt
                        term = cf_ref[at[k], :] * bk[k]
                        outs[k % 2] = term if outs[k % 2] is None else outs[k % 2] + term
                        aa[k] = aa[k] + xt * bk[k]
                        bb[k] = bb[k] + xt * dv[k]
                    ys[pl.ds(row, groups), :] = outs[0] + outs[1]
                return tuple(bk), tuple(dv), tuple(aa), tuple(bb), tuple(ww)

            start = (
                tuple(back[a, :] for a in at),
                tuple(deriv[a, :] for a in at),
                tuple(a_ref[a, :] for a in at),
                tuple(b_ref[a, :] for a in at),
                (w_ref[...],),
            )
            bk, dv, aa, bb, ww = lax.fori_loop(0, tb // 4, steps, start)
            for k in range(half):
                back[at[k], :] = bk[k]
                deriv[at[k], :] = dv[k]
                a_ref[at[k], :] = aa[k]
                b_ref[at[k], :] = bb[k]
            w_ref[...] = ww[0]
        for g in range(groups):
            o_ref[:, g * 128 : (g + 1) * 128] = ys[pl.ds(g, tb, stride=groups), :]

    back_rows = pl.BlockSpec((tb, d), lambda i, s: (nb - 1 - i, 0))
    par = (H * groups, 128)
    const = pl.BlockSpec(par, lambda i, s: (0, 0))
    return run(
        body, (nb,), scal, [normed, d_e, decay, coef, omega],
        [back_rows, back_rows, whole(par), whole(par), whole((groups, 128))],
        [sds((n, d), F32), sds(par, F32), sds(par, F32), sds((groups, 128), F32)],
        [back_rows, const, const, pl.BlockSpec((groups, 128), lambda i, s: (0, 0))],
        [pltpu.VMEM(par, F32), pltpu.VMEM(par, F32)] + [pltpu.VMEM((tb * groups, 128), F32)] * 3,
        flops=40e9, name="ema_backward",
    )


def k_attend(scal, q, k, v_own, v_oth, g_own, g_oth, gs_own, gs_oth):
    n, zw = q.shape
    half = v_own.shape[1]
    blocks = n // ROWS
    scale = zw ** (-0.5)

    def body(s, q_ref, k_ref, vo, vt, go, gt, so, st, gated_o, gated_t, mo, mt, p_ref):
        for i in range(blocks):

            @pl.when(pl.program_id(0) == i)
            def _(i=i):
                seen = (i + 1) * ROWS
                sc = col_inner(q_ref[...], k_ref[0:seen, :]) * scale
                row = i * ROWS + lax.broadcasted_iota(jnp.int32, (ROWS, seen), 0)
                col = lax.broadcasted_iota(jnp.int32, (ROWS, seen), 1)
                sc = jnp.where(col <= row, sc, masked_value)
                e = jnp.exp(sc - jnp.max(sc, axis=-1, keepdims=True))
                p = (e * (1.0 / jnp.sum(e, axis=-1, keepdims=True))).astype(BF)
                p_ref[:, 0:seen] = p
                for v_ref, g_ref, sl_ref, gated, m in ((vo, go, so, gated_o, mo), (vt, gt, st, gated_t, mt)):
                    att = matmul(p, v_ref[0:seen, :])
                    gated[...] = (g_ref[...].astype(F32) * att).astype(BF)
                    m[...] = (sl_ref[...].astype(F32) * att).astype(BF)

    return run(
        body, (blocks,), scal, [q, k, v_own, v_oth, g_own, g_oth, gs_own, gs_oth],
        [rows_of(zw), whole((n, zw)), whole((n, half)), whole((n, half))] + [rows_of(half)] * 4,
        [sds((n, half))] * 4 + [sds((n, n))],
        [rows_of(half)] * 4 + [rows_of(n)],
        flops=n * n * (zw + 2 * half) * 1.25, name="attend",
    )


def k_gate(scal, gated_own, gated_oth, ema_low, tokens, u_own, h_own, f_own, packs, rows):
    n, d = tokens.shape
    half = u_own.shape[0]
    ch = h_own.shape[0]
    ru, rh = rows

    def body(s, go, gt, e_ref, x_ref, uo, ho, fo, u0, u1, u2, u3, h0, h1, h2, h3, f0, f1, f2, f3,
             mix_ref, low_ref, a_ref, b_ref, up_ref, u_scr, h_scr, f_scr):
        @pl.when(pl.program_id(0) == 0)
        def _():
            place(u_scr, s, (u0, u1, u2, u3))
            own = pl.multiple_of(s[6] * ch, ch)
            oth = s[7] * ch
            h_scr[pl.ds(own, ch), :] = ho[...]
            f_scr[pl.ds(own, ch), :] = fo[...]
            place(h_scr, s, (h0, h1, h2, h3), oth)
            place(f_scr, s, (f0, f1, f2, f3), oth)

        h_pre = matmul(go[...], uo[...]) + matmul(gt[...], u_scr[...]) + matmul(e_ref[...], h_scr[...])
        f_pre = matmul(e_ref[...], f_scr[...])
        x = x_ref[...].astype(F32)
        act, slope = silu_pair(h_pre)
        update = sig(f_pre)
        mixed = update * act + (1.0 - update) * x
        mix_ref[...] = mixed
        low_ref[...] = (mixed * lax.rsqrt(jnp.mean(mixed * mixed, axis=-1, keepdims=True) + norm_eps)).astype(BF)
        a_ref[...] = (update * slope).astype(BF)
        b_ref[...] = ((act - x) * update * (1.0 - update)).astype(BF)
        up_ref[...] = (1.0 - update).astype(BF)

    ins = [gated_own, gated_oth, ema_low, tokens, u_own, h_own, f_own, *packs, *packs, *packs]
    specs = [rows_of(half), rows_of(half), rows_of(d), rows_of(d), whole((half, d)), whole((ch, d)), whole((ch, d))]
    specs += [piece_whole(ru, d, 0)] * 4 + [piece_whole(rh, d, ru // rh)] * 4 + [piece_whole(rh, d, ru // rh + 1)] * 4
    return run(
        body, (n // ROWS,), scal, ins, specs,
        [sds((n, d), F32), sds((n, d)), sds((n, d)), sds((n, d)), sds((n, d))],
        [rows_of(d)] * 5,
        [pltpu.VMEM((half, d), BF), pltpu.VMEM((2 * ch, d), BF), pltpu.VMEM((2 * ch, d), BF)],
        flops=2 * n * d * (2 * half + 4 * ch), name="gate",
    )


def k_down_own(scal, hid, us, w_own, cot):
    n, cols = hid.shape
    d = w_own.shape[1]
    tn = 512

    def body(s, h_ref, us_ref, w_ref, c_ref, acc_ref, du_ref):
        part = matmul(h_ref[...], w_ref[...])

        @pl.when(pl.program_id(0) == 0)
        def _():
            acc_ref[...] = part

        @pl.when(pl.program_id(0) > 0)
        def _():
            acc_ref[...] += part

        du_ref[...] = (col_inner(c_ref[...], w_ref[...]) * us_ref[...].astype(F32)).astype(BF)

    return run(
        body, (cols // tn,), scal, [hid, us, w_own, cot],
        [cols_of(n, tn), cols_of(n, tn), rows_of(d, tn), whole((n, d))],
        [sds((n, d), F32), sds((n, cols))],
        [pl.BlockSpec((n, d), lambda i, s: (0, 0)), cols_of(n, tn)],
        flops=4 * n * d * cols, name="down_own",
    )


def k_down_other(scal, hid, us, packs, cot, acc, mixed):
    n, cols = hid.shape
    rp, d = packs[0].shape

    def body(s, h_ref, us_ref, w0, w1, w2, w3, c_ref, in_ref, m_ref, out_ref, du_ref, acc_ref):
        for p, w_ref in enumerate((w0, w1, w2, w3)):

            @pl.when(pl.program_id(0) == p)
            def _(p=p, w_ref=w_ref):
                part = matmul(h_ref[...], w_ref[...])
                if p == 0:
                    acc_ref[...] = part + in_ref[...]
                elif p < 3:
                    acc_ref[...] += part
                else:
                    out_ref[...] = (m_ref[...] + (acc_ref[...] + part)).astype(BF)
                du_ref[...] = (col_inner(c_ref[...], w_ref[...]) * us_ref[...].astype(F32)).astype(BF)

    at = pl.BlockSpec((n, rp), lambda i, s: (0, s[i]))
    return run(
        body, (4,), scal, [hid, us, *packs, cot, acc, mixed],
        [at, at] + [whole((rp, d))] * 4 + [whole((n, d))] * 3,
        [sds((n, d)), sds((n, cols))],
        [pl.BlockSpec((n, d), lambda i, s: (0, 0)), at],
        [pltpu.VMEM((n, d), F32)],
        flops=4 * n * d * cols, name="down_other",
    )


def k_lowered_back(scal, du_own, du_oth, w_own, packs, cot, mixed, a, b, keep):
    n, cols = du_own.shape
    d = w_own.shape[0]
    rp = packs[0].shape[0]

    def body(s, do, dt, wo, w0, w1, w2, w3, c_ref, m_ref, a_ref, b_ref, k_ref, dh_ref, df_ref, dir_ref, w_scr):
        @pl.when(pl.program_id(0) == 0)
        def _():
            place(w_scr, s, (w0, w1, w2, w3))

        dl = col_inner(do[...], wo[...]) + col_inner(dt[...], w_scr[...])
        m = m_ref[...]
        r = lax.rsqrt(jnp.mean(m * m, axis=-1, keepdims=True) + norm_eps)
        n2 = m * r
        dm = c_ref[...].astype(F32) + r * (dl - n2 * jnp.mean(dl * n2, axis=-1, keepdims=True))
        dh_ref[...] = (dm * a_ref[...].astype(F32)).astype(BF)
        df_ref[...] = (dm * b_ref[...].astype(F32)).astype(BF)
        dir_ref[...] = (dm * k_ref[...].astype(F32)).astype(BF)

    return run(
        body, (n // ROWS,), scal, [du_own, du_oth, w_own, *packs, cot, mixed, a, b, keep],
        [rows_of(cols), rows_of(cols), whole((d, cols))] + [whole((rp, cols))] * 4 + [rows_of(d)] * 5,
        [sds((n, d))] * 3,
        [rows_of(d)] * 3,
        [pltpu.VMEM((d, cols), BF)],
        flops=4 * n * d * cols, name="lowered_back",
    )


def k_gated_back(scal, dh, u_own, packs, rp, g_own, g_oth, m_own, m_oth):
    n, d = dh.shape
    half = u_own.shape[0]
    own_steps = half // rp

    def body(s, dh_ref, uo, u0, u1, u2, u3, go, gt, mo, mt, ao, at, co, ct):
        for i in range(own_steps + 4):

            @pl.when(pl.program_id(0) == i)
            def _(i=i):
                if i < own_steps:
                    w, g_ref, m_ref, a_ref, c_ref = uo[i * rp : (i + 1) * rp, :], go, mo, ao, co
                else:
                    w, g_ref, m_ref, a_ref, c_ref = (u0, u1, u2, u3)[i - own_steps][...], gt, mt, at, ct
                dg = col_inner(dh_ref[...], w)
                a_ref[...] = (dg * g_ref[...].astype(F32)).astype(BF)
                c_ref[...] = (dg * m_ref[...].astype(F32)).astype(BF)

    first = pl.BlockSpec((n, rp), lambda i, s: (0, jnp.minimum(i, own_steps - 1)))
    second = pl.BlockSpec((n, rp), lambda i, s: (0, s[jnp.maximum(i - own_steps, 0)]))
    return run(
        body, (own_steps + 4,), scal, [dh, u_own, *packs, g_own, g_oth, m_own, m_oth],
        [whole((n, d)), whole((half, d))] + [piece_whole(rp, d, 0)] * 4 + [first, second, first, second],
        [sds((n, half))] * 4,
        [first, second, first, second],
        flops=4 * n * d * half, name="gated_back",
    )


def k_value_back(scal, p, da_own, da_oth, vs_own, vs_oth):
    n = p.shape[0]
    half = da_own.shape[1]
    blocks = n // ROWS

    def body(s, p_ref, ao, at, so, st, oo, ot):
        for j in range(blocks):

            @pl.when(pl.program_id(0) == j)
            def _(j=j):
                pj = p_ref[j * ROWS :, :]
                oo[...] = (row_inner(pj, ao[j * ROWS :, :]) * so[...].astype(F32)).astype(BF)
                ot[...] = (row_inner(pj, at[j * ROWS :, :]) * st[...].astype(F32)).astype(BF)

    return run(
        body, (blocks,), scal, [p, da_own, da_oth, vs_own, vs_oth],
        [cols_of(n, ROWS), whole((n, half)), whole((n, half)), rows_of(half), rows_of(half)],
        [sds((n, half))] * 2,
        [rows_of(half)] * 2,
        flops=n * n * 2 * half * 1.25, name="value_back",
    )


def k_score_back(scal, p, da_own, da_oth, v_own, v_oth, q, k, z_pre, gain):
    n, zw = q.shape
    half = da_own.shape[1]
    blocks = n // ROWS
    scale = zw ** (-0.5)

    def body(s, p_ref, ao, at, vo, vt, q_ref, k_ref, z_ref, g_ref, dz_ref, st_ref, ds, dq):
        for i in range(blocks):

            @pl.when(pl.program_id(0) == i)
            def _(i=i):
                seen = (i + 1) * ROWS
                pr = p_ref[:, 0:seen].astype(F32)
                dp = col_inner(ao[...], vo[0:seen, :]) + col_inner(at[...], vt[0:seen, :])
                d = (pr * (dp - jnp.sum(pr * dp, axis=-1, keepdims=True))).astype(BF)
                ds[i * ROWS : (i + 1) * ROWS, 0:seen] = d
                dq[i * ROWS : (i + 1) * ROWS, :] = matmul(d, k_ref[0:seen, :]) * scale
                if i == blocks - 1:
                    sums = [jnp.zeros((1, zw), F32)] * 4
                    for j in range(blocks):
                        at_j = slice(j * ROWS, (j + 1) * ROWS)
                        dk = row_inner(ds[j * ROWS :, at_j], q_ref[j * ROWS :, :]) * scale
                        dqj = dq[at_j, :]
                        act, slope = silu_pair(z_ref[at_j, :])
                        dz_ref[at_j, :] = (slope * (dqj * g_ref[0:1, :] + dk * g_ref[1:2, :])).astype(BF)
                        for n_, v in enumerate((dqj * act, dk * act, dqj, dk)):
                            sums[n_] = sums[n_] + jnp.sum(v, axis=0, keepdims=True)
                    for n_ in range(4):
                        st_ref[n_ : n_ + 1, :] = sums[n_]
                    st_ref[4:8, :] = jnp.zeros((4, zw), F32)

    return run(
        body, (blocks,), scal, [p, da_own, da_oth, v_own, v_oth, q, k, z_pre, gain],
        [rows_of(n), rows_of(half), rows_of(half), whole((n, half)), whole((n, half)), whole((n, zw)),
         whole((n, zw)), whole((n, zw)), whole((2, zw))],
        [sds((n, zw)), sds((8, zw), F32)],
        [pl.BlockSpec((n, zw), lambda i, s: (0, 0)), pl.BlockSpec((8, zw), lambda i, s: (0, 0))],
        [pltpu.VMEM((n, n), BF), pltpu.VMEM((n, zw), F32)],
        flops=n * n * 2 * half * 1.25, name="score_back",
    )


def k_ema_out_back(scal, dg_own, dg_oth, dz, dh, df, slope, wg_own, w_z, h_own, f_own, packs_g, rg, packs_h, rows):
    n, d = dh.shape
    half = dg_own.shape[1]
    ch = h_own.shape[0]
    zw = w_z.shape[1]
    ru, rh = rows

    def body(s, go, gt, dz_ref, dh_ref, df_ref, sl_ref, wo, wz, ho, fo, g0, g1, g2, g3, h0, h1, h2, h3,
             f0, f1, f2, f3, o_ref, w_scr, h_scr, f_scr):
        @pl.when(pl.program_id(0) == 0)
        def _():
            place(w_scr, s, (g0, g1, g2, g3))
            own = pl.multiple_of(s[6] * ch, ch)
            oth = s[7] * ch
            h_scr[pl.ds(own, ch), :] = ho[...]
            f_scr[pl.ds(own, ch), :] = fo[...]
            place(h_scr, s, (h0, h1, h2, h3), oth)
            place(f_scr, s, (f0, f1, f2, f3), oth)

        total = col_inner(go[...], wo[...]) + col_inner(gt[...], w_scr[...]) + col_inner(dz_ref[...], wz[...])
        total = total + col_inner(dh_ref[...], h_scr[...]) + col_inner(df_ref[...], f_scr[...])
        o_ref[...] = total * sl_ref[...].astype(F32)

    ins = [dg_own, dg_oth, dz, dh, df, slope, wg_own, w_z, h_own, f_own, *packs_g, *packs_h, *packs_h]
    specs = [rows_of(half), rows_of(half), rows_of(zw), rows_of(d), rows_of(d), rows_of(d)]
    specs += [whole((d, half)), whole((d, zw)), whole((ch, d)), whole((ch, d))]
    specs += [piece_whole(rg, half, 1)] * 4
    specs += [piece_whole(rh, d, ru // rh)] * 4 + [piece_whole(rh, d, ru // rh + 1)] * 4
    return run(
        body, (n // ROWS,), scal, ins, specs,
        [sds((n, d), F32)], [rows_of(d)],
        [pltpu.VMEM((d, half), BF), pltpu.VMEM((2 * ch, d), BF), pltpu.VMEM((2 * ch, d), BF)],
        flops=2 * n * d * (2 * half + 4 * ch + zw), name="ema_out_back",
    )[0]


def k_input_back(scal, dv_own, dv_oth, w_own, packs, rp, d_sig, tokens, direct):
    n, d = tokens.shape
    half = dv_own.shape[1]

    def body(s, vo, vt, wo, w0, w1, w2, w3, sg, x_ref, dir_ref, o_ref, w_scr):
        @pl.when(pl.program_id(0) == 0)
        def _():
            place(w_scr, s, (w0, w1, w2, w3))

        dn = col_inner(vo[...], wo[...]) + col_inner(vt[...], w_scr[...]) + sg[...]
        x = x_ref[...].astype(F32)
        r = lax.rsqrt(jnp.mean(x * x, axis=-1, keepdims=True) + norm_eps)
        n1 = x * r
        o_ref[...] = dir_ref[...].astype(F32) + r * (dn - n1 * jnp.mean(dn * n1, axis=-1, keepdims=True))

    return run(
        body, (n // ROWS,), scal, [dv_own, dv_oth, w_own, *packs, d_sig, tokens, direct],
        [rows_of(half), rows_of(half), whole((d, half))] + [piece_whole(rp, half, 0)] * 4 + [rows_of(d)] * 3,
        [sds((n, d), F32)], [rows_of(d)],
        [pltpu.VMEM((d, half), BF)],
        flops=4 * n * d * half, name="input_back",
    )[0]


def k_weight(scal, left, right, at, cols, tn, adds=(), name="weight"):
    n, d = left.shape
    steps = cols // tn

    def body(s, l_ref, r_ref, *refs):
        total = row_inner(l_ref[...], r_ref[...])
        for ref in refs[:-1]:
            total = total + ref[...].astype(F32)
        refs[-1][...] = total.astype(BF)

    ins = [left, right] + [a for a, _ in adds]
    specs = [whole((n, d)), pl.BlockSpec((n, tn), lambda i, s: (0, at(s) * steps + i))]
    specs += [pl.BlockSpec((d, tn), lambda i, s, o=o: (0, o * steps + i)) for _, o in adds]
    return run(
        body, (steps,), scal, ins, specs, [sds((d, cols))], [cols_of(d, tn)],
        flops=2 * n * d * cols, name=name,
    )[0]


def swap(values, axis, bit, size):
    return lax.ppermute(values, axis, [(i, i ^ bit) for i in range(size)])


def pick(values, index, axis):
    return lax.dynamic_index_in_dim(values, index, axis, keepdims=False)


def one_sequence(
    tokens, alpha_logit, delta_logit, ema_beta, ema_eta, ema_omega, w_z, qk_gain, qk_bias,
    w_v, w_gamma, u_h, w_h, w_phi, w_up, w_down, cotangent,
):
    n, d = tokens.shape
    dp_size = lax.axis_size("dp")
    me = lax.axis_index("dp").astype(jnp.int32)
    t = lax.axis_index("tensor").astype(jnp.int32)
    core = me % 2
    x_pos = (me // 2) % 2
    z_pos = me // 4
    k0 = me % 4
    scal = jnp.stack([k0, k0 ^ 2, k0 ^ 1, k0 ^ 3, core, 1 - core, t, 1 - t])

    def my_rows(w):
        rows = w.shape[0] // 4
        return lax.dynamic_slice_in_dim(w, k0 * rows, rows, 0)

    def fetch(values):
        by_y = swap(values, "tensor", 1, 2)
        by_x = swap(by_y, "dp", 2, dp_size)
        return by_y, by_x, swap(by_y, "dp", 1, dp_size), swap(by_x, "dp", 1, dp_size)

    own_params = jnp.concatenate(
        [a.T for a in (alpha_logit, delta_logit, ema_beta, ema_eta)] + [ema_omega[None]], axis=0
    )
    oth_params = swap(own_params, "tensor", 1, 2)
    pv = fetch(jnp.concatenate([my_rows(w_v), my_rows(w_gamma)], axis=0))
    ph = fetch(jnp.concatenate([my_rows(u_h), my_rows(w_h), my_rows(w_phi)], axis=0))
    pu = fetch(my_rows(w_up))
    pd = fetch(my_rows(w_down))
    rv = w_v.shape[0] // 4
    rh = (u_h.shape[0] // 4, w_h.shape[0] // 4)

    params = jnp.where(
        t == 0,
        jnp.concatenate([own_params, oth_params], axis=1),
        jnp.concatenate([oth_params, own_params], axis=1),
    )
    al, de, be, et = (params[i * H : (i + 1) * H] for i in range(4))
    alpha_rate = jax.nn.sigmoid(al)
    decay = (1.0 - alpha_rate * jax.nn.sigmoid(de)).reshape(-1, 128)
    coef = (alpha_rate * be * et).reshape(-1, 128)
    omega = params[4 * H].reshape(-1, 128)

    normed, v_own, vs_own = k_value_own(scal, tokens, w_v)
    ema_low, e_slope = k_ema_forward(scal, normed, decay, coef, omega)
    z_pre, query, key = k_query_key(scal, ema_low, w_z, qk_gain, qk_bias)
    g_own, gs_own = k_act_own(scal, ema_low, w_gamma, 512)
    v_oth, vs_oth = k_act_other(scal, normed, pv, rv, 0, 512)
    g_oth, gs_oth = k_act_other(scal, ema_low, pv, rv, 1, 512)
    gated_own, gated_oth, m_own, m_oth, probs = k_attend(
        scal, query, key, v_own, v_oth, g_own, g_oth, gs_own, gs_oth
    )
    mixed, lowered, fac_h, fac_f, keep = k_gate(
        scal, gated_own, gated_oth, ema_low, tokens, u_h, w_h, w_phi, ph, rh
    )
    hid_own, us_own = k_act_own(scal, lowered, w_up, 1024)
    hid_oth, us_oth = k_act_other(scal, lowered, pu, pu[0].shape[0], 0, 1024)
    acc, du_own = k_down_own(scal, hid_own, us_own, w_down, cotangent)
    output, du_oth = k_down_other(scal, hid_oth, us_oth, pd, cotangent, acc, mixed)
    dh, df, direct = k_lowered_back(
        scal, du_own, du_oth, w_up, pu, cotangent, mixed, fac_h, fac_f, keep
    )
    da_own, da_oth, dg_own, dg_oth = k_gated_back(
        scal, dh, u_h, ph, rh[0], g_own, g_oth, m_own, m_oth
    )
    dv_own, dv_oth = k_value_back(scal, probs, da_own, da_oth, vs_own, vs_oth)
    dz, stats = k_score_back(scal, probs, da_own, da_oth, v_own, v_oth, query, key, z_pre, qk_gain)
    d_e = k_ema_out_back(
        scal, dg_own, dg_oth, dz, dh, df, e_slope, w_gamma, w_z, w_h, w_phi, pv, rv, ph, rh
    )
    d_sig, sum_a, sum_b, sum_w = k_ema_backward(scal, normed, d_e, decay, coef, omega)
    input_grad = k_input_back(scal, dv_own, dv_oth, w_v, pv, rv, d_sig, tokens, direct)

    def theirs(s):
        return s[5]

    def mine(s):
        return s[4]

    def chip_sum(left, own, oth, tn):
        quarter = own.shape[1] // 2
        tn = min(tn, quarter)
        sent = [k_weight(scal, left, r, theirs, quarter, tn) for r in (own, oth)]
        got = [swap(v, "dp", 1, dp_size) for v in sent]
        return (
            k_weight(scal, left, own, mine, quarter, tn, [(got[0], 0)]),
            k_weight(scal, left, oth, mine, quarter, tn, [(got[1], 0)]),
        )

    def chip_sum_ema(left):
        quarter = d // 4
        ats = [
            (lambda s: s[6] * 2 + s[5], lambda s: s[6] * 2 + s[4]),
            (lambda s: s[7] * 2 + s[5], lambda s: s[7] * 2 + s[4]),
        ]
        res = []
        for send_at, keep_at in ats:
            got = swap(k_weight(scal, left, ema_low, send_at, quarter, quarter), "dp", 1, dp_size)
            res.append(k_weight(scal, left, ema_low, keep_at, quarter, quarter, [(got, 0)]))
        return tuple(res)

    def over_rows(total):
        c = total.shape[1]
        by_x = total.reshape(4, 2, d // 8, c)
        got = swap(pick(by_x, 1 - x_pos, 1), "dp", 2, dp_size)
        total = (pick(by_x, x_pos, 1).astype(F32) + got.astype(F32)).astype(BF)
        by_z = total.reshape(2, 2, d // 8, c)
        got = swap(pick(by_z, 1 - z_pos % 2, 1), "dp", 4, dp_size)
        total = (pick(by_z, z_pos % 2, 1).astype(F32) + got.astype(F32)).astype(BF)
        got = swap(pick(total, 1 - z_pos // 2, 0), "dp", 8, dp_size)
        return pick(total, z_pos // 2, 0).astype(F32) + got.astype(F32)

    def finish(total):
        c = total.shape[1]
        by_core = total.reshape(2, d // 16, c)
        got = swap(pick(by_core, 1 - core, 0).astype(BF), "dp", 1, dp_size).astype(F32)
        kept = pick(by_core, core, 0)
        return jnp.where(
            core == 0,
            jnp.concatenate([kept, got], axis=1),
            jnp.concatenate([got, kept], axis=1),
        )

    def over_y(pair):
        own, oth = pair
        got = swap(oth, "tensor", 1, 2)
        return (own.astype(F32) + got.astype(F32)).astype(BF)

    down_t = finish(over_rows(over_y(chip_sum(cotangent, hid_own, hid_oth, 1024))))
    up = finish(over_rows(over_y(chip_sum(lowered, du_own, du_oth, 1024))))
    uh_t = finish(over_rows(over_y(chip_sum(dh, gated_own, gated_oth, 512))))
    wh_t = finish(over_rows(over_y(chip_sum_ema(dh))))
    phi_t = finish(over_rows(over_y(chip_sum_ema(df))))
    gamma = finish(over_rows(over_y(chip_sum(ema_low, dg_own, dg_oth, 512))))
    value = finish(over_rows(over_y(chip_sum(normed, dv_own, dv_oth, 512))))
    z_own = k_weight(scal, ema_low, dz, lambda s: 0, dz.shape[1], dz.shape[1])
    z_sum = (z_own.astype(F32) + swap(z_own, "dp", 1, dp_size).astype(F32)).astype(BF)
    z_sum = (z_sum.astype(F32) + swap(z_sum, "tensor", 1, 2).astype(F32)).astype(BF)
    z_grad = pick(over_rows(z_sum).reshape(2, d // 16, -1), core, 0)

    sums = lax.psum(jnp.concatenate([sum_a, sum_b, sum_w, stats], axis=0), ("dp", "tensor"))
    gh = sum_a.shape[0]

    def own_half(v):
        return lax.dynamic_slice_in_dim(v, t * (d // 2), d // 2, 1).T

    tot_a = own_half(sums[:gh].reshape(H, d))
    tot_b = own_half(sums[gh : 2 * gh].reshape(H, d))
    omega_grad = lax.dynamic_slice_in_dim(sums[2 * gh : 2 * gh + d // 128].reshape(d), t * (d // 2), d // 2, 0)
    zsum = sums[2 * gh + d // 128 :]
    rate = jax.nn.sigmoid(alpha_logit)
    damp = jax.nn.sigmoid(delta_logit)
    feed = rate * ema_beta
    feed_grad = ema_eta * tot_a
    decay_grad = feed * ema_eta * tot_b
    alpha_grad = (feed_grad * ema_beta - decay_grad * damp) * rate * (1.0 - rate)
    delta_grad = -decay_grad * rate * damp * (1.0 - damp)
    return (
        output, input_grad, alpha_grad, delta_grad, feed_grad * rate, feed * tot_a, omega_grad,
        z_grad, zsum[0:2], zsum[2:4], value, gamma, uh_t.T, wh_t.T, phi_t.T, up, down_t.T,
    )


def solution(mesh):
    placed = (
        P(("dp", "tensor"), None),
        P("tensor", None),
        P("tensor", None),
        P("tensor", None),
        P("tensor", None),
        P("tensor"),
        P(),
        P(),
        P(),
        P(None, "tensor"),
        P(None, "tensor"),
        P("tensor", None),
        P("tensor", None),
        P("tensor", None),
        P(None, "tensor"),
        P("tensor", None),
        P(("dp", "tensor"), None),
    )

    def per_device(tokens, *rest):
        whole_sequence = tokens.shape[0] == LEN and dict(mesh.shape) == {"dp": 16, "tensor": 2}
        return (one_sequence if whole_sequence else shards)(tokens, *rest)

    return jax.shard_map(
        per_device,
        mesh=mesh,
        in_specs=placed,
        out_specs=(
            P(("dp", "tensor"), None),
            P(("dp", "tensor"), None),
            P("tensor", None),
            P("tensor", None),
            P("tensor", None),
            P("tensor", None),
            P("tensor"),
            P("dp", None),
            P(),
            P(),
            P("dp", "tensor"),
            P("dp", "tensor"),
            P("tensor", "dp"),
            P("tensor", "dp"),
            P("tensor", "dp"),
            P("dp", "tensor"),
            P("tensor", "dp"),
        ),
        check_vma=False,
    )
```

```python
import math

import jax
import jax.numpy as jnp
from jax import lax
from jax.experimental import pallas as pl
from jax.experimental.pallas import tpu as pltpu
from jax.sharding import PartitionSpec as P

H = 16
LEN = 1024
ATT_BLOCK = 512
EMA_BLOCK = 128


norm_eps = 1e-06
masked_value = -1e30


def rms_rows(values_in):
    return values_in * lax.rsqrt(jnp.mean(values_in * values_in, axis=-1, keepdims=True) + norm_eps)


def matmul(left, right):
    return jnp.dot(left, right, preferred_element_type=jnp.float32)


def row_inner(left, right):
    return lax.dot_general(
        left, right, (((0,), (0,)), ((), ())), preferred_element_type=jnp.float32
    )


def col_inner(left, right):
    return lax.dot_general(
        left, right, (((1,), (1,)), ((), ())), preferred_element_type=jnp.float32
    )


def silu_slope(pre_act):
    logistic = jax.nn.sigmoid(pre_act)
    return logistic * (1.0 + pre_act * (1.0 - logistic))


def gate_apply(h_pre, f_pre, x_rows):
    update = jax.nn.sigmoid(f_pre)
    return update * jax.nn.silu(h_pre) + (1.0 - update) * x_rows


def ema_apply(signal, ema_params):
    alpha_logit, delta_logit, ema_beta, ema_eta, ema_omega = ema_params
    alpha_rate = jax.nn.sigmoid(alpha_logit)
    decay_rate = 1.0 - alpha_rate * jax.nn.sigmoid(delta_logit)
    feed_rate = alpha_rate * ema_beta
    log_decay = jnp.log(decay_rate)
    total_rows, chan_count = signal.shape
    seq_count = total_rows // LEN
    block_count = LEN // EMA_BLOCK
    blocks = signal.reshape(seq_count, block_count, EMA_BLOCK, chan_count)
    steps_in = jnp.arange(EMA_BLOCK, dtype=jnp.float32)
    lag_power = jnp.exp(steps_in[:, None, None] * log_decay[None])
    kernel = jnp.sum(lag_power * (feed_rate * ema_eta)[None], axis=-1)
    offsets = steps_in[:, None] - steps_in[None, :]
    lag_index = jnp.clip(offsets, 0, EMA_BLOCK - 1).astype(jnp.int32)
    toeplitz = jnp.where((offsets >= 0)[:, :, None], kernel[lag_index], 0.0)
    local_part = jnp.einsum("ijc,snjc->snic", toeplitz, blocks)
    tail_power = lag_power[::-1] * feed_rate[None]
    block_state = jnp.einsum("jch,snjc->snch", tail_power, blocks)
    full_decay = jnp.exp(EMA_BLOCK * log_decay)

    def carry_step(state_in, incoming):
        return (full_decay * state_in + incoming, state_in)

    zero_state = jnp.zeros((seq_count, chan_count, H), jnp.float32)
    _, start_state = lax.scan(carry_step, zero_state, jnp.moveaxis(block_state, 1, 0))
    start_state = jnp.moveaxis(start_state, 0, 1)
    head_power = lag_power * decay_rate[None] * ema_eta[None]
    carried = jnp.einsum("ich,snch->snic", head_power, start_state)
    ema_pre = (local_part + carried).reshape(total_rows, chan_count) + ema_omega * signal
    return jax.nn.silu(ema_pre)


def masked_scores(q_rows, k_rows, first_row):
    raw_scores = col_inner(q_rows, k_rows) * q_rows.shape[1] ** (-0.5)
    row_pos = first_row + jnp.arange(q_rows.shape[0])[:, None]
    col_pos = jnp.arange(k_rows.shape[0])[None, :]
    return jnp.where(col_pos <= row_pos, raw_scores, masked_value)


def attend_forward(query_low, key_low, value_low):
    total_rows, value_width = value_low.shape
    seq_count = total_rows // LEN
    per_seq = LEN // ATT_BLOCK

    def attend_one_block(flat_index):
        seq_id = flat_index // per_seq
        blk_id = flat_index % per_seq
        seq_start = seq_id * LEN
        q_rows = lax.dynamic_slice_in_dim(query_low, seq_start + blk_id * ATT_BLOCK, ATT_BLOCK, 0)
        k_rows = lax.dynamic_slice_in_dim(key_low, seq_start, LEN, 0)
        v_rows = lax.dynamic_slice_in_dim(value_low, seq_start, LEN, 0)
        scores = masked_scores(q_rows, k_rows, blk_id * ATT_BLOCK)
        top_score = jnp.max(scores, axis=-1, keepdims=True)
        weights = jnp.exp(scores - top_score)
        total_weight = jnp.sum(weights, axis=-1, keepdims=True)
        probs = (weights / total_weight).astype(jnp.bfloat16)
        return (matmul(probs, v_rows), top_score[:, 0] + jnp.log(total_weight[:, 0]))

    outs, lse_all = lax.map(attend_one_block, jnp.arange(seq_count * per_seq))
    return (outs.reshape(total_rows, value_width), lse_all.reshape(total_rows))


def attend_backward(query_low, key_low, value_low, lse_rows, d_att):
    total_rows, value_width = value_low.shape
    head_width = query_low.shape[1]
    seq_count = total_rows // LEN
    per_seq = LEN // ATT_BLOCK
    scale = head_width ** (-0.5)

    def one_seq(seq_id):
        seq_start = seq_id * LEN
        k_rows = lax.dynamic_slice_in_dim(key_low, seq_start, LEN, 0)
        v_rows = lax.dynamic_slice_in_dim(value_low, seq_start, LEN, 0)

        def one_one_block(carry_in, blk_id):
            d_keys, d_vals = carry_in
            row_start = seq_start + blk_id * ATT_BLOCK
            q_rows = lax.dynamic_slice_in_dim(query_low, row_start, ATT_BLOCK, 0)
            g_rows = lax.dynamic_slice_in_dim(d_att, row_start, ATT_BLOCK, 0)
            lse_part = lax.dynamic_slice_in_dim(lse_rows, row_start, ATT_BLOCK, 0)
            probs = jnp.exp(masked_scores(q_rows, k_rows, blk_id * ATT_BLOCK) - lse_part[:, None])
            d_probs = col_inner(g_rows, v_rows)
            d_scores = (
                probs * (d_probs - jnp.sum(probs * d_probs, axis=-1, keepdims=True))
            ).astype(jnp.bfloat16)
            d_rows = matmul(d_scores, k_rows) * scale
            d_keys = d_keys + row_inner(d_scores, q_rows) * scale
            d_vals = d_vals + row_inner(probs.astype(jnp.bfloat16), g_rows)
            return ((d_keys, d_vals), d_rows)

        start_carry = (
            jnp.zeros((LEN, head_width), jnp.float32),
            jnp.zeros((LEN, value_width), jnp.float32),
        )
        (d_keys, d_vals), d_rows = lax.scan(one_one_block, start_carry, jnp.arange(per_seq))
        return (d_rows.reshape(LEN, head_width), d_keys, d_vals)

    d_query, d_key, d_value = lax.map(one_seq, jnp.arange(seq_count))
    return (
        d_query.reshape(total_rows, head_width),
        d_key.reshape(total_rows, head_width),
        d_value.reshape(total_rows, value_width),
    )


def shards(
    tokens,
    alpha_logit,
    delta_logit,
    ema_beta,
    ema_eta,
    ema_omega,
    w_z,
    qk_gain,
    qk_bias,
    w_v,
    w_gamma,
    u_h,
    w_h,
    w_phi,
    w_up,
    w_down,
    cotangent,
):
    tensor_pos = lax.axis_index("tensor")
    feature_count = tokens.shape[1]
    chan_count = ema_omega.shape[0]
    chan_start = tensor_pos * chan_count
    x_rows = tokens.astype(jnp.float32)
    normed_rows, norm_pull = jax.vjp(rms_rows, x_rows)
    normed, cot_full = (
        lax.all_gather(normed_rows.astype(jnp.bfloat16), "tensor", axis=0, tiled=True),
        lax.all_gather(cotangent, "tensor", axis=0, tiled=True),
    )
    signal = lax.dynamic_slice_in_dim(normed, chan_start, chan_count, 1).astype(jnp.float32)
    ema_params = (alpha_logit, delta_logit, ema_beta, ema_eta, ema_omega)
    ema_val, ema_pull = jax.vjp(ema_apply, signal, ema_params)
    ema_low = ema_val.astype(jnp.bfloat16)
    ema_full = lax.all_gather(ema_low, "tensor", axis=1, tiled=True)
    z_pre = matmul(ema_full, w_z)
    z_act = jax.nn.silu(z_pre)
    query_low = (z_act * qk_gain[0] + qk_bias[0]).astype(jnp.bfloat16)
    key_low = (z_act * qk_gain[1] + qk_bias[1]).astype(jnp.bfloat16)
    values_pre = matmul(normed, w_v)
    value_low = jax.nn.silu(values_pre).astype(jnp.bfloat16)
    gamma_pre = matmul(ema_full, w_gamma)
    gamma_act = jax.nn.silu(gamma_pre)
    attended, lse_rows = attend_forward(query_low, key_low, value_low)
    gated_low = (gamma_act * attended).astype(jnp.bfloat16)
    both_pre = lax.psum_scatter(
        jnp.concatenate(
            [matmul(gated_low, u_h) + matmul(ema_low, w_h), matmul(ema_low, w_phi)], axis=1
        ),
        "tensor",
        scatter_dimension=0,
        tiled=True,
    )
    h_pre = both_pre[:, :feature_count]
    f_pre = both_pre[:, feature_count:]
    mixed, gate_pull = jax.vjp(gate_apply, h_pre, f_pre, x_rows)
    normed_two, norm_two_pull = jax.vjp(rms_rows, mixed)
    lowered = lax.all_gather(normed_two.astype(jnp.bfloat16), "tensor", axis=0, tiled=True)
    up_pre = matmul(lowered, w_up)
    hidden = jax.nn.silu(up_pre).astype(jnp.bfloat16)
    down_rows = lax.psum_scatter(
        matmul(hidden, w_down).astype(jnp.bfloat16), "tensor", scatter_dimension=0, tiled=True
    ).astype(jnp.float32)
    output = (mixed + down_rows).astype(jnp.bfloat16)
    cot_rows = cotangent.astype(jnp.float32)
    d_hidden = col_inner(cot_full, w_down)
    d_up = (d_hidden * silu_slope(up_pre)).astype(jnp.bfloat16)
    down_grad = row_inner(hidden, cot_full)
    up_grad = row_inner(lowered, d_up)
    d_lowered = lax.psum_scatter(col_inner(d_up, w_up), "tensor", scatter_dimension=0, tiled=True)
    d_mixed = cot_rows + norm_two_pull(d_lowered)[0]
    d_hpre, d_fpre, d_direct = gate_pull(d_mixed)
    h_full_grad, f_full_grad = (
        lax.all_gather(d_hpre.astype(jnp.bfloat16), "tensor", axis=0, tiled=True),
        lax.all_gather(d_fpre.astype(jnp.bfloat16), "tensor", axis=0, tiled=True),
    )
    uh_grad = row_inner(gated_low, h_full_grad)
    wh_grad = row_inner(ema_low, h_full_grad)
    phi_grad = row_inner(ema_low, f_full_grad)
    d_gated = col_inner(h_full_grad, u_h)
    d_att = (d_gated * gamma_act).astype(jnp.bfloat16)
    d_gamma = (d_gated * attended * silu_slope(gamma_pre)).astype(jnp.bfloat16)
    d_query, d_key, d_value = attend_backward(query_low, key_low, value_low, lse_rows, d_att)
    d_query, d_key = lax.psum((d_query, d_key), "tensor")
    d_z = (silu_slope(z_pre) * (d_query * qk_gain[0] + d_key * qk_gain[1])).astype(jnp.bfloat16)
    gain_grad = jnp.stack([jnp.sum(d_query * z_act, axis=0), jnp.sum(d_key * z_act, axis=0)])
    bias_grad = jnp.stack([jnp.sum(d_query, axis=0), jnp.sum(d_key, axis=0)])
    z_grad = row_inner(ema_full, d_z)
    gamma_grad = row_inner(ema_full, d_gamma)
    d_value_pre = (d_value * silu_slope(values_pre)).astype(jnp.bfloat16)
    value_grad = row_inner(normed, d_value_pre)
    d_chan = lax.psum_scatter(
        col_inner(d_gamma, w_gamma).astype(jnp.bfloat16), "tensor", scatter_dimension=1, tiled=True
    ).astype(jnp.float32)
    z_rows = lax.dynamic_slice_in_dim(w_z, chan_start, chan_count, 0)
    d_chan = (
        d_chan
        + col_inner(d_z, z_rows)
        + col_inner(h_full_grad, w_h)
        + col_inner(f_full_grad, w_phi)
    )
    d_signal, d_params = ema_pull(d_chan)
    d_norm_part = col_inner(d_value_pre, w_v)
    own_cols = lax.dynamic_slice_in_dim(d_norm_part, chan_start, chan_count, 1)
    d_norm_part = lax.dynamic_update_slice_in_dim(d_norm_part, own_cols + d_signal, chan_start, 1)
    d_normed = lax.psum_scatter(
        d_norm_part.astype(jnp.bfloat16), "tensor", scatter_dimension=0, tiled=True
    ).astype(jnp.float32)
    input_grad = d_direct + norm_pull(d_normed)[0]
    weight_totals = (
        lax.psum_scatter(z_grad.astype(jnp.bfloat16), "dp", scatter_dimension=0, tiled=True).astype(
            jnp.float32
        ),
        lax.psum_scatter(
            value_grad.astype(jnp.bfloat16), "dp", scatter_dimension=0, tiled=True
        ).astype(jnp.float32),
        lax.psum_scatter(
            gamma_grad.astype(jnp.bfloat16), "dp", scatter_dimension=0, tiled=True
        ).astype(jnp.float32),
        lax.psum_scatter(
            uh_grad.astype(jnp.bfloat16), "dp", scatter_dimension=1, tiled=True
        ).astype(jnp.float32),
        lax.psum_scatter(
            wh_grad.astype(jnp.bfloat16), "dp", scatter_dimension=1, tiled=True
        ).astype(jnp.float32),
        lax.psum_scatter(
            phi_grad.astype(jnp.bfloat16), "dp", scatter_dimension=1, tiled=True
        ).astype(jnp.float32),
        lax.psum_scatter(
            up_grad.astype(jnp.bfloat16), "dp", scatter_dimension=0, tiled=True
        ).astype(jnp.float32),
        lax.psum_scatter(
            down_grad.astype(jnp.bfloat16), "dp", scatter_dimension=1, tiled=True
        ).astype(jnp.float32),
    )
    param_totals = lax.psum(
        (d_params[0], d_params[1], d_params[2], d_params[3], d_params[4], gain_grad, bias_grad),
        "dp",
    )
    return (
        output,
        input_grad,
        param_totals[0],
        param_totals[1],
        param_totals[2],
        param_totals[3],
        param_totals[4],
        weight_totals[0],
        param_totals[5],
        param_totals[6],
        weight_totals[1],
        weight_totals[2],
        weight_totals[3],
        weight_totals[4],
        weight_totals[5],
        weight_totals[6],
        weight_totals[7],
    )


CP = pltpu.CompilerParams(vmem_limit_bytes=56 * 1024 * 1024)
BF = jnp.bfloat16
F32 = jnp.float32
ROWS = 256


def sds(shape, dtype=BF):
    return jax.ShapeDtypeStruct(shape, dtype)


def whole(shape):
    return pl.BlockSpec(shape, lambda i, s: (0,) * len(shape), pipeline_mode=pl.Buffered(1))


def rows_of(cols, rows=ROWS):
    return pl.BlockSpec((rows, cols), lambda i, s: (i, 0))


def cols_of(rows, cols):
    return pl.BlockSpec((rows, cols), lambda i, s: (0, i))


def run(body, grid, scal, ins, in_specs, out_shape, out_specs, scratch=(), flops=0, name=None):
    moved = sum(a.size * a.dtype.itemsize for a in ins)
    moved += sum(math.prod(o.shape) * jnp.dtype(o.dtype).itemsize for o in out_shape)
    return pl.pallas_call(
        body,
        out_shape=out_shape,
        grid_spec=pltpu.PrefetchScalarGridSpec(
            num_scalar_prefetch=1,
            grid=grid,
            in_specs=in_specs,
            out_specs=out_specs,
            scratch_shapes=list(scratch),
        ),
        compiler_params=CP,
        cost_estimate=pl.CostEstimate(flops=int(flops), bytes_accessed=int(moved), transcendentals=0),
        name=name,
    )(scal, *ins)


def sig(u):
    return 1.0 / (1.0 + jnp.exp(-u))


def silu_pair(u):
    s = sig(u)
    return u * s, s * (1.0 + u * (1.0 - s))


def place(scr, s, pieces, base=0):
    rows = pieces[0].shape[0]
    for p in range(4):
        scr[pl.ds(pl.multiple_of(base + s[p] * rows, rows), rows), :] = pieces[p][...]


def piece_block(rows, cols, row_block):
    return pl.BlockSpec((rows, cols), lambda i, s: (row_block, i))


def piece_whole(rows, cols, row_block):
    return pl.BlockSpec((rows, cols), lambda i, s: (row_block, 0), pipeline_mode=pl.Buffered(1))


def k_value_own(scal, tokens, w_own):
    n, d = tokens.shape
    cols = w_own.shape[1]
    tn = 512

    def body(s, x_ref, w_ref, n_ref, v_ref, sl_ref):
        @pl.when(pl.program_id(0) == 0)
        def _():
            x = x_ref[...].astype(F32)
            n_ref[...] = (x * lax.rsqrt(jnp.mean(x * x, axis=-1, keepdims=True) + norm_eps)).astype(BF)

        act, slope = silu_pair(matmul(n_ref[...], w_ref[...]))
        v_ref[...] = act.astype(BF)
        sl_ref[...] = slope.astype(BF)

    return run(
        body, (cols // tn,), scal, [tokens, w_own],
        [whole((n, d)), cols_of(d, tn)],
        [sds((n, d)), sds((n, cols)), sds((n, cols))],
        [pl.BlockSpec((n, d), lambda i, s: (0, 0)), cols_of(n, tn), cols_of(n, tn)],
        flops=2 * n * d * cols, name="value_own",
    )


def k_act_own(scal, x, w_own, tn):
    n, d = x.shape
    cols = w_own.shape[1]

    def body(s, x_ref, w_ref, v_ref, sl_ref):
        act, slope = silu_pair(matmul(x_ref[...], w_ref[...]))
        v_ref[...] = act.astype(BF)
        sl_ref[...] = slope.astype(BF)

    return run(
        body, (cols // tn,), scal, [x, w_own],
        [whole((n, d)), cols_of(d, tn)],
        [sds((n, cols)), sds((n, cols))],
        [cols_of(n, tn), cols_of(n, tn)],
        flops=2 * n * d * cols, name="act_own",
    )


def k_act_other(scal, x, pieces, rows, row_block, tn):
    n, d = x.shape
    cols = pieces[0].shape[1]

    def body(s, x_ref, p0, p1, p2, p3, v_ref, sl_ref, w_scr):
        place(w_scr, s, (p0, p1, p2, p3))
        act, slope = silu_pair(matmul(x_ref[...], w_scr[...]))
        v_ref[...] = act.astype(BF)
        sl_ref[...] = slope.astype(BF)

    return run(
        body, (cols // tn,), scal, [x, *pieces],
        [whole((n, d))] + [piece_block(rows, tn, row_block)] * 4,
        [sds((n, cols)), sds((n, cols))],
        [cols_of(n, tn), cols_of(n, tn)],
        [pltpu.VMEM((d, tn), BF)],
        flops=2 * n * d * cols, name="act_other",
    )


def k_query_key(scal, ema_low, w_z, qk_gain, qk_bias):
    n, d = ema_low.shape
    zw = w_z.shape[1]

    def body(s, e_ref, w_ref, g_ref, b_ref, z_ref, q_ref, k_ref):
        z_pre = matmul(e_ref[...], w_ref[...])
        z_ref[...] = z_pre
        act = z_pre * sig(z_pre)
        q_ref[...] = (act * g_ref[0:1, :] + b_ref[0:1, :]).astype(BF)
        k_ref[...] = (act * g_ref[1:2, :] + b_ref[1:2, :]).astype(BF)

    return run(
        body, (2,), scal, [ema_low, w_z, qk_gain, qk_bias],
        [rows_of(d, n // 2), whole((d, zw)), whole((2, zw)), whole((2, zw))],
        [sds((n, zw), F32), sds((n, zw)), sds((n, zw))],
        [rows_of(zw, n // 2)] * 3,
        flops=2 * n * d * zw, name="query_key",
    )


def k_ema_forward(scal, normed, decay, coef, omega):
    n, d = normed.shape
    groups = d // 128
    tb = 128

    def body(s, x_ref, dec_ref, cf_ref, om_ref, e_ref, sl_ref, st, xs, ys):
        @pl.when(pl.program_id(0) == 0)
        def _():
            st[...] = jnp.zeros_like(st)

        for g in range(groups):
            xs[pl.ds(g, tb, stride=groups), :] = x_ref[:, g * 128 : (g + 1) * 128].astype(F32)
        dec = [dec_ref[k * groups : (k + 1) * groups, :] for k in range(H)]
        cf = [cf_ref[k * groups : (k + 1) * groups, :] for k in range(H)]
        om = om_ref[...]

        def steps(b, carry):
            states = list(carry)
            for u in range(8):
                row = pl.multiple_of((b * 8 + u) * groups, groups)
                xt = xs[pl.ds(row, groups), :]
                parts = [om * xt, None, None, None]
                for k in range(H):
                    states[k] = dec[k] * states[k] + xt
                    term = cf[k] * states[k]
                    parts[k % 4] = term if parts[k % 4] is None else parts[k % 4] + term
                ys[pl.ds(row, groups), :] = (parts[0] + parts[1]) + (parts[2] + parts[3])
            return tuple(states)

        start = tuple(st[k * groups : (k + 1) * groups, :] for k in range(H))
        end = lax.fori_loop(0, tb // 8, steps, start)
        for k in range(H):
            st[k * groups : (k + 1) * groups, :] = end[k]
        for g in range(groups):
            act, slope = silu_pair(ys[pl.ds(g, tb, stride=groups), :])
            e_ref[:, g * 128 : (g + 1) * 128] = act.astype(BF)
            sl_ref[:, g * 128 : (g + 1) * 128] = slope.astype(BF)

    return run(
        body, (n // tb,), scal, [normed, decay, coef, omega],
        [rows_of(d, tb), whole((H * groups, 128)), whole((H * groups, 128)), whole((groups, 128))],
        [sds((n, d)), sds((n, d))],
        [rows_of(d, tb)] * 2,
        [pltpu.VMEM((H * groups, 128), F32), pltpu.VMEM((tb * groups, 128), F32), pltpu.VMEM((tb * groups, 128), F32)],
        flops=20e9, name="ema_forward",
    )


def k_ema_backward(scal, normed, de_part, dz, slope, w_z, decay, coef, omega):
    n, d = normed.shape
    groups = d // 128
    tb = 128
    nb = n // tb
    half = H // 2
    gh = groups * half

    zw = dz.shape[1]

    def body(s, x_ref, de_ref, z_ref, sl_ref, wz_ref, dec_ref, cf_ref, om_ref, o_ref, a_ref, b_ref, w_ref, back, deriv, xs, gs, ys):
        @pl.when(pl.program_id(0) == 0)
        def _():
            back[...] = jnp.zeros_like(back)
            deriv[...] = jnp.zeros_like(deriv)
            a_ref[...] = jnp.zeros_like(a_ref)
            b_ref[...] = jnp.zeros_like(b_ref)
            w_ref[...] = jnp.zeros_like(w_ref)

        d_e = (de_ref[...] + col_inner(z_ref[...], wz_ref[...])) * sl_ref[...].astype(F32)
        for g in range(groups):
            xs[pl.ds(g, tb, stride=groups), :] = x_ref[:, g * 128 : (g + 1) * 128].astype(F32)
            gs[pl.ds(g, tb, stride=groups), :] = d_e[:, g * 128 : (g + 1) * 128]

        for part in range(2):
            first = part * gh
            at = [slice(first + k * groups, first + (k + 1) * groups) for k in range(half)]
            dec = [dec_ref[a, :] for a in at]

            def steps(b, carry, part=part, at=at, dec=dec):
                bk, dv, aa, bb, ww = (list(c) for c in carry)
                for u in range(4):
                    row = pl.multiple_of((tb - 1 - (b * 4 + u)) * groups, groups)
                    xt = xs[pl.ds(row, groups), :]
                    gt = gs[pl.ds(row, groups), :]
                    if part == 0:
                        outs = [om_ref[...] * gt, None]
                        ww[0] = ww[0] + xt * gt
                    else:
                        outs = [ys[pl.ds(row, groups), :], None]
                    for k in range(half):
                        dv[k] = dec[k] * dv[k] + bk[k]
                        bk[k] = dec[k] * bk[k] + gt
                        term = cf_ref[at[k], :] * bk[k]
                        outs[k % 2] = term if outs[k % 2] is None else outs[k % 2] + term
                        aa[k] = aa[k] + xt * bk[k]
                        bb[k] = bb[k] + xt * dv[k]
                    ys[pl.ds(row, groups), :] = outs[0] + outs[1]
                return tuple(bk), tuple(dv), tuple(aa), tuple(bb), tuple(ww)

            start = (
                tuple(back[a, :] for a in at),
                tuple(deriv[a, :] for a in at),
                tuple(a_ref[a, :] for a in at),
                tuple(b_ref[a, :] for a in at),
                (w_ref[...],),
            )
            bk, dv, aa, bb, ww = lax.fori_loop(0, tb // 4, steps, start)
            for k in range(half):
                back[at[k], :] = bk[k]
                deriv[at[k], :] = dv[k]
                a_ref[at[k], :] = aa[k]
                b_ref[at[k], :] = bb[k]
            w_ref[...] = ww[0]
        for g in range(groups):
            o_ref[:, g * 128 : (g + 1) * 128] = ys[pl.ds(g, tb, stride=groups), :]

    back_rows = pl.BlockSpec((tb, d), lambda i, s: (nb - 1 - i, 0))
    par = (H * groups, 128)
    const = pl.BlockSpec(par, lambda i, s: (0, 0))
    return run(
        body, (nb,), scal, [normed, de_part, dz, slope, w_z, decay, coef, omega],
        [back_rows, back_rows, pl.BlockSpec((tb, zw), lambda i, s: (nb - 1 - i, 0)), back_rows, whole((d, zw)), whole(par), whole(par), whole((groups, 128))],
        [sds((n, d), F32), sds(par, F32), sds(par, F32), sds((groups, 128), F32)],
        [back_rows, const, const, pl.BlockSpec((groups, 128), lambda i, s: (0, 0))],
        [pltpu.VMEM(par, F32), pltpu.VMEM(par, F32)] + [pltpu.VMEM((tb * groups, 128), F32)] * 3,
        flops=40e9, name="ema_backward",
    )


def k_attend(scal, q, k, v_own, v_oth, g_own, g_oth, gs_own, gs_oth):
    n, zw = q.shape
    half = v_own.shape[1]
    blocks = n // ROWS
    scale = zw ** (-0.5)

    def body(s, q_ref, k_ref, vo, vt, go, gt, so, st, gated_o, gated_t, mo, mt, p_ref):
        for i in range(blocks):

            @pl.when(pl.program_id(0) == i)
            def _(i=i):
                seen = (i + 1) * ROWS
                sc = col_inner(q_ref[...], k_ref[0:seen, :]) * scale
                row = i * ROWS + lax.broadcasted_iota(jnp.int32, (ROWS, seen), 0)
                col = lax.broadcasted_iota(jnp.int32, (ROWS, seen), 1)
                sc = jnp.where(col <= row, sc, masked_value)
                e = jnp.exp(sc - jnp.max(sc, axis=-1, keepdims=True))
                p = (e * (1.0 / jnp.sum(e, axis=-1, keepdims=True))).astype(BF)
                p_ref[:, 0:seen] = p
                for v_ref, g_ref, sl_ref, gated, m in ((vo, go, so, gated_o, mo), (vt, gt, st, gated_t, mt)):
                    att = matmul(p, v_ref[0:seen, :])
                    gated[...] = (g_ref[...].astype(F32) * att).astype(BF)
                    m[...] = (sl_ref[...].astype(F32) * att).astype(BF)

    return run(
        body, (blocks,), scal, [q, k, v_own, v_oth, g_own, g_oth, gs_own, gs_oth],
        [rows_of(zw), whole((n, zw)), whole((n, half)), whole((n, half))] + [rows_of(half)] * 4,
        [sds((n, half))] * 4 + [sds((n, n))],
        [rows_of(half)] * 4 + [rows_of(n)],
        flops=n * n * (zw + 2 * half) * 1.25, name="attend",
    )


def k_gate(scal, gated_own, gated_oth, ema_low, tokens, u_own, h_own, f_own, packs, rows):
    n, d = tokens.shape
    half = u_own.shape[0]
    ch = h_own.shape[0]
    ru, rh = rows

    def body(s, go, gt, e_ref, x_ref, uo, ho, fo, u0, u1, u2, u3, h0, h1, h2, h3, f0, f1, f2, f3,
             mix_ref, low_ref, a_ref, b_ref, up_ref, u_scr, h_scr, f_scr):
        @pl.when(pl.program_id(0) == 0)
        def _():
            place(u_scr, s, (u0, u1, u2, u3))
            own = pl.multiple_of(s[6] * ch, ch)
            oth = s[7] * ch
            h_scr[pl.ds(own, ch), :] = ho[...]
            f_scr[pl.ds(own, ch), :] = fo[...]
            place(h_scr, s, (h0, h1, h2, h3), oth)
            place(f_scr, s, (f0, f1, f2, f3), oth)

        h_pre = matmul(go[...], uo[...]) + matmul(gt[...], u_scr[...]) + matmul(e_ref[...], h_scr[...])
        f_pre = matmul(e_ref[...], f_scr[...])
        x = x_ref[...].astype(F32)
        act, slope = silu_pair(h_pre)
        update = sig(f_pre)
        mixed = update * act + (1.0 - update) * x
        mix_ref[...] = mixed
        low_ref[...] = (mixed * lax.rsqrt(jnp.mean(mixed * mixed, axis=-1, keepdims=True) + norm_eps)).astype(BF)
        a_ref[...] = (update * slope).astype(BF)
        b_ref[...] = ((act - x) * update * (1.0 - update)).astype(BF)
        up_ref[...] = (1.0 - update).astype(BF)

    ins = [gated_own, gated_oth, ema_low, tokens, u_own, h_own, f_own, *packs, *packs, *packs]
    specs = [rows_of(half), rows_of(half), rows_of(d), rows_of(d), whole((half, d)), whole((ch, d)), whole((ch, d))]
    specs += [piece_whole(ru, d, 0)] * 4 + [piece_whole(rh, d, ru // rh)] * 4 + [piece_whole(rh, d, ru // rh + 1)] * 4
    return run(
        body, (n // ROWS,), scal, ins, specs,
        [sds((n, d), F32), sds((n, d)), sds((n, d)), sds((n, d)), sds((n, d))],
        [rows_of(d)] * 5,
        [pltpu.VMEM((half, d), BF), pltpu.VMEM((2 * ch, d), BF), pltpu.VMEM((2 * ch, d), BF)],
        flops=2 * n * d * (2 * half + 4 * ch), name="gate",
    )


def k_ffn(scal, lowered, cot, up, down, acc, grad, pieces):
    n, d = lowered.shape
    cols = up[0].shape[1]
    tn = cols // 4
    last = grad is not None
    first_in = [acc, grad] if last else [acc]

    def body(s, low_ref, c_ref, *refs):
        step = pl.program_id(0)
        nu = 4 if pieces else 1
        ups, downs, refs = refs[:nu], refs[nu : 2 * nu], refs[2 * nu :]
        ins, refs = refs[: len(first_in)], refs[len(first_in) :]
        if last:
            out_ref, gl_ref, sent_ref, kept_ref, acc_ref, u_scr = refs
        else:
            acc_ref, gl_ref, sent_ref, kept_ref, u_scr = refs

        @pl.when(step == 0)
        def _():
            acc_ref[...] = ins[0][...]
            gl_ref[...] = ins[1][...] if last else jnp.zeros_like(gl_ref)

        if pieces:
            place(u_scr, s, ups)
            wu = u_scr
        else:
            wu = ups[0]

        def work(wd, grads):
            act, slope = silu_pair(matmul(low_ref[...], wu[...]))
            hid = act.astype(BF)
            acc_ref[...] += matmul(hid, wd[...])
            du = (col_inner(c_ref[...], wd[...]) * slope).astype(BF)
            gl_ref[...] += col_inner(du, wu[...])
            grads[0] = row_inner(c_ref[...], hid).astype(BF)
            grads[1] = row_inner(low_ref[...], du).astype(BF)

        if pieces:
            for i, p in enumerate((2, 3, 0, 1)):

                @pl.when(step == i)
                def _(i=i, p=p):
                    work(downs[p], sent_ref if i < 2 else kept_ref)
        else:

            @pl.when(step < 2)
            def _():
                work(downs[0], sent_ref)

            @pl.when(step >= 2)
            def _():
                work(downs[0], kept_ref)

        if last:

            @pl.when(step == 3)
            def _():
                out_ref[...] = acc_ref[...].astype(BF)

    if pieces:
        specs = [pl.BlockSpec((d // 4, tn), lambda i, s: (0, s[(i + 2) % 4]))] * 4 + [whole((tn, d))] * 4
    else:
        specs = [
            pl.BlockSpec((d, tn), lambda i, s: (0, s[(i + 2) % 4])),
            pl.BlockSpec((tn, d), lambda i, s: (s[(i + 2) % 4], 0)),
        ]
    still = pl.BlockSpec((n, d), lambda i, s: (0, 0))
    pair = (2, d, tn)
    sent = pl.BlockSpec(pair, lambda i, s: (0, 0, s[2 + jnp.minimum(i, 1)] % 2))
    kept = pl.BlockSpec(pair, lambda i, s: (0, 0, s[jnp.maximum(i - 2, 0)] % 2))
    return run(
        body, (4,), scal, [lowered, cot, *up, *down, *first_in],
        [whole((n, d)), whole((n, d))] + specs + [whole((n, d))] * len(first_in),
        [sds((n, d), BF if last else F32), sds((n, d), F32), sds((2, d, cols // 2)), sds((2, d, cols // 2))],
        [still, still, sent, kept],
        ([pltpu.VMEM((n, d), F32)] if last else []) + [pltpu.VMEM((d, tn), BF)],
        flops=12 * n * d * cols, name="ffn_other" if last else "ffn_own",
    )


def k_mid_back(scal, dl, cot, mixed, fac_h, fac_f, keep, g_own, g_oth, m_own, m_oth,
               u_own, wg_own, h_own, f_own, packs_g, packs_h, rows):
    n, d = cot.shape
    half = u_own.shape[0]
    ch = h_own.shape[0]
    ru, rh = rows
    rg = packs_g[0].shape[0]

    def body(s, dl_ref, c_ref, x_ref, a_ref, b_ref, k_ref, go, gt, mo, mt, uo, wo, ho, fo,
             w0, w1, w2, w3, u0, u1, u2, u3, h0, h1, h2, h3, f0, f1, f2, f3,
             dh_ref, df_ref, dir_ref, ao, at, do, dt, de_ref, u_scr, w_scr, h_scr, f_scr):
        @pl.when(pl.program_id(0) == 0)
        def _():
            place(u_scr, s, (u0, u1, u2, u3))
            place(w_scr, s, (w0, w1, w2, w3))
            own = pl.multiple_of(s[6] * ch, ch)
            oth = s[7] * ch
            h_scr[pl.ds(own, ch), :] = ho[...]
            f_scr[pl.ds(own, ch), :] = fo[...]
            place(h_scr, s, (h0, h1, h2, h3), oth)
            place(f_scr, s, (f0, f1, f2, f3), oth)

        dl = dl_ref[...]
        m = x_ref[...]
        r = lax.rsqrt(jnp.mean(m * m, axis=-1, keepdims=True) + norm_eps)
        n2 = m * r
        dm = c_ref[...].astype(F32) + r * (dl - n2 * jnp.mean(dl * n2, axis=-1, keepdims=True))
        dh = (dm * a_ref[...].astype(F32)).astype(BF)
        df = (dm * b_ref[...].astype(F32)).astype(BF)
        dh_ref[...] = dh
        df_ref[...] = df
        dir_ref[...] = (dm * k_ref[...].astype(F32)).astype(BF)
        de = col_inner(dh, h_scr[...]) + col_inner(df, f_scr[...])
        for u, w, g_ref, m_ref, a_out, d_out in ((uo, wo, go, mo, ao, do), (u_scr, w_scr, gt, mt, at, dt)):
            dg = col_inner(dh, u[...])
            a_out[...] = (dg * g_ref[...].astype(F32)).astype(BF)
            low = (dg * m_ref[...].astype(F32)).astype(BF)
            d_out[...] = low
            de = de + col_inner(low, w[...])
        de_ref[...] = de

    ins = [dl, cot, mixed, fac_h, fac_f, keep, g_own, g_oth, m_own, m_oth, u_own, wg_own, h_own, f_own]
    ins += [*packs_g, *packs_h, *packs_h, *packs_h]
    specs = [rows_of(d)] * 6 + [rows_of(half)] * 4
    specs += [whole((half, d)), whole((d, half)), whole((ch, d)), whole((ch, d))]
    specs += [piece_whole(rg, half, 0)] * 4 + [piece_whole(ru, d, 0)] * 4
    specs += [piece_whole(rh, d, ru // rh)] * 4 + [piece_whole(rh, d, ru // rh + 1)] * 4
    return run(
        body, (n // ROWS,), scal, ins, specs,
        [sds((n, d))] * 3 + [sds((n, half))] * 4 + [sds((n, d), F32)],
        [rows_of(d)] * 3 + [rows_of(half)] * 4 + [rows_of(d)],
        [pltpu.VMEM((half, d), BF), pltpu.VMEM((d, half), BF), pltpu.VMEM((2 * ch, d), BF), pltpu.VMEM((2 * ch, d), BF)],
        flops=2 * n * d * (4 * half + 4 * ch), name="mid_back",
    )


def k_value_back(scal, p, da_own, da_oth, vs_own, vs_oth):
    n = p.shape[0]
    half = da_own.shape[1]
    blocks = n // ROWS

    def body(s, p_ref, ao, at, so, st, oo, ot):
        for j in range(blocks):

            @pl.when(pl.program_id(0) == j)
            def _(j=j):
                pj = p_ref[j * ROWS :, :]
                oo[...] = (row_inner(pj, ao[j * ROWS :, :]) * so[...].astype(F32)).astype(BF)
                ot[...] = (row_inner(pj, at[j * ROWS :, :]) * st[...].astype(F32)).astype(BF)

    return run(
        body, (blocks,), scal, [p, da_own, da_oth, vs_own, vs_oth],
        [cols_of(n, ROWS), whole((n, half)), whole((n, half)), rows_of(half), rows_of(half)],
        [sds((n, half))] * 2,
        [rows_of(half)] * 2,
        flops=n * n * 2 * half * 1.25, name="value_back",
    )


def k_score_back(scal, p, da_own, da_oth, v_own, v_oth, q, k, z_pre, gain):
    n, zw = q.shape
    half = da_own.shape[1]
    blocks = n // ROWS
    scale = zw ** (-0.5)

    def body(s, p_ref, ao, at, vo, vt, q_ref, k_ref, z_ref, g_ref, dz_ref, st_ref, ds, dq):
        for i in range(blocks):

            @pl.when(pl.program_id(0) == i)
            def _(i=i):
                seen = (i + 1) * ROWS
                pr = p_ref[:, 0:seen].astype(F32)
                dp = col_inner(ao[...], vo[0:seen, :]) + col_inner(at[...], vt[0:seen, :])
                d = (pr * (dp - jnp.sum(pr * dp, axis=-1, keepdims=True))).astype(BF)
                ds[i * ROWS : (i + 1) * ROWS, 0:seen] = d
                dq[i * ROWS : (i + 1) * ROWS, :] = matmul(d, k_ref[0:seen, :]) * scale
                if i == blocks - 1:
                    sums = [jnp.zeros((1, zw), F32)] * 4
                    for j in range(blocks):
                        at_j = slice(j * ROWS, (j + 1) * ROWS)
                        dk = row_inner(ds[j * ROWS :, at_j], q_ref[j * ROWS :, :]) * scale
                        dqj = dq[at_j, :]
                        act, slope = silu_pair(z_ref[at_j, :])
                        dz_ref[at_j, :] = (slope * (dqj * g_ref[0:1, :] + dk * g_ref[1:2, :])).astype(BF)
                        for n_, v in enumerate((dqj * act, dk * act, dqj, dk)):
                            sums[n_] = sums[n_] + jnp.sum(v, axis=0, keepdims=True)
                    for n_ in range(4):
                        st_ref[n_ : n_ + 1, :] = sums[n_]
                    st_ref[4:8, :] = jnp.zeros((4, zw), F32)

    return run(
        body, (blocks,), scal, [p, da_own, da_oth, v_own, v_oth, q, k, z_pre, gain],
        [rows_of(n), rows_of(half), rows_of(half), whole((n, half)), whole((n, half)), whole((n, zw)),
         whole((n, zw)), whole((n, zw)), whole((2, zw))],
        [sds((n, zw)), sds((8, zw), F32)],
        [pl.BlockSpec((n, zw), lambda i, s: (0, 0)), pl.BlockSpec((8, zw), lambda i, s: (0, 0))],
        [pltpu.VMEM((n, n), BF), pltpu.VMEM((n, zw), F32)],
        flops=n * n * 2 * half * 1.25, name="score_back",
    )


def k_input_back(scal, dv_own, dv_oth, w_own, packs, rp, d_sig, tokens, direct):
    n, d = tokens.shape
    half = dv_own.shape[1]

    def body(s, vo, vt, wo, w0, w1, w2, w3, sg, x_ref, dir_ref, o_ref, w_scr):
        @pl.when(pl.program_id(0) == 0)
        def _():
            place(w_scr, s, (w0, w1, w2, w3))

        dn = col_inner(vo[...], wo[...]) + col_inner(vt[...], w_scr[...]) + sg[...]
        x = x_ref[...].astype(F32)
        r = lax.rsqrt(jnp.mean(x * x, axis=-1, keepdims=True) + norm_eps)
        n1 = x * r
        o_ref[...] = dir_ref[...].astype(F32) + r * (dn - n1 * jnp.mean(dn * n1, axis=-1, keepdims=True))

    return run(
        body, (n // ROWS,), scal, [dv_own, dv_oth, w_own, *packs, d_sig, tokens, direct],
        [rows_of(half), rows_of(half), whole((d, half))] + [piece_whole(rp, half, 0)] * 4 + [rows_of(d)] * 3,
        [sds((n, d), F32)], [rows_of(d)],
        [pltpu.VMEM((d, half), BF)],
        flops=4 * n * d * half, name="input_back",
    )[0]


def k_weight(scal, left, right, at, cols, tn, adds=(), name="weight"):
    n, d = left.shape
    steps = cols // tn

    def body(s, l_ref, r_ref, *refs):
        total = row_inner(l_ref[...], r_ref[...])
        for ref in refs[:-1]:
            total = total + ref[...].astype(F32)
        refs[-1][...] = total.astype(BF)

    ins = [left, right] + [a for a, _ in adds]
    specs = [whole((n, d)), pl.BlockSpec((n, tn), lambda i, s: (0, at(s) * steps + i))]
    specs += [pl.BlockSpec((d, tn), lambda i, s, o=o: (0, o * steps + i)) for _, o in adds]
    return run(
        body, (steps,), scal, ins, specs, [sds((d, cols))], [cols_of(d, tn)],
        flops=2 * n * d * cols, name=name,
    )[0]


def k_weight_mid(scal, ema_low, dh, df, gated_own, gated_oth, dg_own, dg_oth, part, got=None):
    n, d = ema_low.shape
    half = gated_own.shape[1] // 2
    qe = d // 4

    def body(s, e_ref, h_ref, f_ref, go, gt, do, dt, eo, et, *refs):
        adds = refs[:-2]
        own, oth = refs[-2:]

        def put(out, k, at, width, value):
            if adds:
                value = value + adds[k][:, at : at + width].astype(F32)
            out[:, at : at + width] = value.astype(BF)

        for i in range(3):

            @pl.when(pl.program_id(0) == i)
            def _(i=i):
                for k, (out, g, dg, e) in enumerate(((own, go, do, eo), (oth, gt, dt, et))):
                    if i == 0:
                        put(out, k, 0, half, row_inner(h_ref[...], g[...]))
                    elif i == 1:
                        put(out, k, 0, half, row_inner(e_ref[...], dg[...]))
                    else:
                        put(out, k, 0, qe, row_inner(h_ref[...], e[...]))
                        put(out, k, qe, qe, row_inner(f_ref[...], e[...]))

    at = pl.BlockSpec((n, half), lambda i, s: (0, s[part]), pipeline_mode=pl.Buffered(1))
    e_own = pl.BlockSpec((n, qe), lambda i, s: (0, s[6] * 2 + s[part]), pipeline_mode=pl.Buffered(1))
    e_oth = pl.BlockSpec((n, qe), lambda i, s: (0, s[7] * 2 + s[part]), pipeline_mode=pl.Buffered(1))
    adds = list(got) if got is not None else []
    return run(
        body, (3,), scal, [ema_low, dh, df, gated_own, gated_oth, dg_own, dg_oth, ema_low, ema_low] + adds,
        [whole((n, d))] * 3 + [at] * 4 + [e_own, e_oth] + [cols_of(d, half)] * len(adds),
        [sds((d, 3 * half))] * 2, [cols_of(d, half)] * 2,
        flops=2 * n * d * 6 * half, name="weight_mid",
    )


def k_weight_value(scal, normed, dv_own, dv_oth, part, got=None):
    n, d = normed.shape
    half = dv_own.shape[1] // 2

    def body(s, x_ref, vo, vt, *refs):
        adds = refs[:-2]
        for i, v in enumerate((vo, vt)):

            @pl.when(pl.program_id(0) == i)
            def _(i=i, v=v):
                total = row_inner(x_ref[...], v[...])
                if adds:
                    total = total + adds[i][...].astype(F32)
                refs[-2 + i][...] = total.astype(BF)

    at = pl.BlockSpec((n, half), lambda i, s: (0, s[part]), pipeline_mode=pl.Buffered(1))
    adds = list(got) if got is not None else []
    still = pl.BlockSpec((d, half), lambda i, s: (0, 0))
    return run(
        body, (2,), scal, [normed, dv_own, dv_oth] + adds,
        [whole((n, d)), at, at] + [whole((d, half))] * len(adds),
        [sds((d, half))] * 2, [still] * 2,
        flops=2 * n * d * 2 * half, name="weight_value",
    )


def swap(values, axis, bit, size):
    return lax.ppermute(values, axis, [(i, i ^ bit) for i in range(size)])


def pick(values, index, axis):
    return lax.dynamic_index_in_dim(values, index, axis, keepdims=False)


def one_sequence(
    tokens, alpha_logit, delta_logit, ema_beta, ema_eta, ema_omega, w_z, qk_gain, qk_bias,
    w_v, w_gamma, u_h, w_h, w_phi, w_up, w_down, cotangent,
):
    n, d = tokens.shape
    dp_size = lax.axis_size("dp")
    me = lax.axis_index("dp").astype(jnp.int32)
    t = lax.axis_index("tensor").astype(jnp.int32)
    core = me % 2
    x_pos = (me // 2) % 2
    z_pos = me // 4
    k0 = core * 2 + x_pos
    scal = jnp.stack([k0, k0 ^ 1, k0 ^ 2, k0 ^ 3, core, 1 - core, t, 1 - t])

    def after(*values):
        return lax.optimization_barrier((scal, *values))[0]

    def over_core(v):
        return swap(v, "dp", 1, dp_size)

    def over_x(v):
        return swap(v, "dp", 2, dp_size)

    def over_tensor(v):
        return swap(v, "tensor", 1, 2)

    def my_rows(w):
        rows = w.shape[0] // 4
        return lax.dynamic_slice_in_dim(w, k0 * rows, rows, 0)

    def fetch(values):
        by_y = over_tensor(values)
        by_x = over_x(by_y)
        return by_y, by_x, over_core(by_y), over_core(by_x)

    own_params = jnp.concatenate(
        [a.T for a in (alpha_logit, delta_logit, ema_beta, ema_eta)] + [ema_omega[None]], axis=0
    )
    oth_params = over_tensor(own_params)
    pv = fetch(my_rows(w_v))
    pg = fetch(my_rows(w_gamma))
    ph = fetch(jnp.concatenate([my_rows(u_h), my_rows(w_h), my_rows(w_phi)], axis=0))
    pu = fetch(my_rows(w_up))
    pd = fetch(my_rows(w_down))
    rv = w_v.shape[0] // 4
    rh = (u_h.shape[0] // 4, w_h.shape[0] // 4)

    params = jnp.where(
        t == 0,
        jnp.concatenate([own_params, oth_params], axis=1),
        jnp.concatenate([oth_params, own_params], axis=1),
    )
    al, de, be, et = (params[i * H : (i + 1) * H] for i in range(4))
    alpha_rate = jax.nn.sigmoid(al)
    decay = (1.0 - alpha_rate * jax.nn.sigmoid(de)).reshape(-1, 128)
    coef = (alpha_rate * be * et).reshape(-1, 128)
    omega = params[4 * H].reshape(-1, 128)

    normed, v_own, vs_own = k_value_own(scal, tokens, w_v)
    ema_low, e_slope = k_ema_forward(after(v_own), normed, decay, coef, omega)
    z_pre, query, key = k_query_key(scal, ema_low, w_z, qk_gain, qk_bias)
    g_own, gs_own = k_act_own(after(query), ema_low, w_gamma, 512)
    v_oth, vs_oth = k_act_other(after(g_own), normed, pv, rv, 0, 512)
    g_oth, gs_oth = k_act_other(after(v_oth), ema_low, pg, rv, 0, 512)
    gated_own, gated_oth, m_own, m_oth, probs = k_attend(
        scal, query, key, v_own, v_oth, g_own, g_oth, gs_own, gs_oth
    )
    mixed, lowered, fac_h, fac_f, keep = k_gate(
        scal, gated_own, gated_oth, ema_low, tokens, u_h, w_h, w_phi, ph, rh
    )
    acc, dl, ffn_so, ffn_ko = k_ffn(scal, lowered, cotangent, [w_up], [w_down], mixed, None, False)
    ffn_go = over_core(ffn_so)
    output, dl, ffn_st, ffn_kt = k_ffn(after(acc), lowered, cotangent, pu, pd, acc, dl, True)
    ffn_gt = over_core(ffn_st)
    dh, df, direct, da_own, da_oth, dg_own, dg_oth, de_part = k_mid_back(
        scal, dl, cotangent, mixed, fac_h, fac_f, keep, g_own, g_oth, m_own, m_oth,
        u_h, w_gamma, w_h, w_phi, pg, ph, rh,
    )
    mid_sent = k_weight_mid(after(dh), ema_low, dh, df, gated_own, gated_oth, dg_own, dg_oth, 5)
    mid_got = [over_core(v) for v in mid_sent]
    dv_own, dv_oth = k_value_back(after(*mid_sent), probs, da_own, da_oth, vs_own, vs_oth)
    val_sent = k_weight_value(after(dv_own), normed, dv_own, dv_oth, 5)
    val_got = [over_core(v) for v in val_sent]
    mid_own, mid_oth = k_weight_mid(
        after(*val_sent), ema_low, dh, df, gated_own, gated_oth, dg_own, dg_oth, 4, mid_got
    )
    dz, stats = k_score_back(
        after(mid_own), probs, da_own, da_oth, v_own, v_oth, query, key, z_pre, qk_gain
    )
    val_own, val_oth = k_weight_value(after(dz), normed, dv_own, dv_oth, 4, val_got)
    z_own = k_weight(after(dz), ema_low, dz, lambda s: 0, dz.shape[1], dz.shape[1])
    d_sig, sum_a, sum_b, sum_w = k_ema_backward(
        after(val_own, z_own), normed, de_part, dz, e_slope, w_z, decay, coef, omega
    )
    input_grad = k_input_back(scal, dv_own, dv_oth, w_v, pv, rv, d_sig, tokens, direct)

    def add(*values):
        total = values[0].astype(F32)
        for v in values[1:]:
            total = total + v.astype(F32)
        return total.astype(BF)

    def split_x(v):
        v = v.reshape(4, 2, d // 8, v.shape[-1])
        return pick(v, x_pos, 1), pick(v, 1 - x_pos, 1)

    def x_then_y(own_terms, oth_terms):
        own = [split_x(v) for v in own_terms]
        oth = [split_x(v) for v in oth_terms]
        got_own = over_x(add(*[v[1] for v in own]))
        got_oth = over_x(add(*[v[1] for v in oth]))
        got = over_tensor(add(*[v[0] for v in oth], got_oth))
        return [*[v[0] for v in own], got_own, got]

    def y_then_x(own_terms, oth_terms):
        got = over_tensor(add(*oth_terms))
        own = [split_x(v) for v in [*own_terms, got]]
        got = over_x(add(*[v[1] for v in own]))
        return [*[v[0] for v in own], got]

    def over_z(terms):
        total = add(*terms)
        by_z = total.reshape(2, 2, d // 8, total.shape[-1])
        got = swap(pick(by_z, 1 - z_pos % 2, 1), "dp", 4, dp_size)
        pair = add(pick(by_z, z_pos % 2, 1), got)
        got = swap(pick(pair, 1 - z_pos // 2, 0), "dp", 8, dp_size)
        return pick(pair, z_pos // 2, 0).astype(F32) + got.astype(F32)

    def finish(total):
        by_core = total.reshape(2, d // 16, total.shape[1])
        got = over_core(pick(by_core, 1 - core, 0).astype(BF)).astype(F32)
        kept = pick(by_core, core, 0)
        return jnp.where(core == 0, jnp.stack([kept, got]), jnp.stack([got, kept]))

    def joined(pair):
        return jnp.concatenate([pair[0], pair[1]], axis=1)

    down_terms = x_then_y([ffn_ko[0], ffn_go[0]], [ffn_kt[0], ffn_gt[0]])
    up_terms = y_then_x([ffn_ko[1], ffn_go[1]], [ffn_kt[1], ffn_gt[1]])
    ffn = finish(over_z([jnp.concatenate([add(*down_terms), add(*up_terms)], axis=-1)]))
    c = ffn.shape[2] // 2
    down_t, up = joined(ffn[:, :, :c]), joined(ffn[:, :, c:])

    c = mid_own.shape[1] // 2
    mid_a = x_then_y([mid_own[:, :c]], [mid_oth[:, :c]])
    mid_b = y_then_x([mid_own[:, c:]], [mid_oth[:, c:]])
    mid = finish(over_z([jnp.concatenate([add(*mid_a), add(*mid_b)], axis=-1)]))
    half = gated_own.shape[1] // 2
    uh_t, gamma = joined(mid[:, :, :half]), joined(mid[:, :, half : 2 * half])
    wh_t = joined(mid[:, :, 2 * half : 2 * half + d // 4])
    phi_t = joined(mid[:, :, 2 * half + d // 4 :])

    c = half // 2
    z_sum = add(z_own, over_core(z_own))
    z_sum = add(z_sum, over_tensor(z_sum))
    val_a = x_then_y([val_own[:, :c]], [val_oth[:, :c]])
    z_mine, z_sent = split_x(z_sum)
    val_b = y_then_x([val_own[:, c:]], [val_oth[:, c:]])
    z_total = add(z_mine, over_x(z_sent))
    val = over_z([jnp.concatenate([add(*val_a), add(*val_b), z_total], axis=-1)])
    z_grad = pick(val[:, half:].reshape(2, d // 16, -1), core, 0)
    value = joined(finish(val[:, :half]))

    sums = jnp.concatenate([sum_a, sum_b, sum_w, stats], axis=0)
    sums = sums + over_core(sums)
    sums = sums + over_tensor(sums)
    sums = sums + over_x(sums)
    sums = sums + swap(sums, "dp", 4, dp_size)
    sums = sums + swap(sums, "dp", 8, dp_size)
    gh = sum_a.shape[0]

    def own_half(v):
        return lax.dynamic_slice_in_dim(v, t * (d // 2), d // 2, 1).T

    tot_a = own_half(sums[:gh].reshape(H, d))
    tot_b = own_half(sums[gh : 2 * gh].reshape(H, d))
    omega_grad = lax.dynamic_slice_in_dim(sums[2 * gh : 2 * gh + d // 128].reshape(d), t * (d // 2), d // 2, 0)
    zsum = sums[2 * gh + d // 128 :]
    rate = jax.nn.sigmoid(alpha_logit)
    damp = jax.nn.sigmoid(delta_logit)
    feed = rate * ema_beta
    feed_grad = ema_eta * tot_a
    decay_grad = feed * ema_eta * tot_b
    alpha_grad = (feed_grad * ema_beta - decay_grad * damp) * rate * (1.0 - rate)
    delta_grad = -decay_grad * rate * damp * (1.0 - damp)
    return (
        output, input_grad, alpha_grad, delta_grad, feed_grad * rate, feed * tot_a, omega_grad,
        z_grad, zsum[0:2], zsum[2:4], value, gamma, uh_t.T, wh_t.T, phi_t.T, up, down_t.T,
    )


def solution(mesh):
    placed = (
        P(("dp", "tensor"), None),
        P("tensor", None),
        P("tensor", None),
        P("tensor", None),
        P("tensor", None),
        P("tensor"),
        P(),
        P(),
        P(),
        P(None, "tensor"),
        P(None, "tensor"),
        P("tensor", None),
        P("tensor", None),
        P("tensor", None),
        P(None, "tensor"),
        P("tensor", None),
        P(("dp", "tensor"), None),
    )

    def per_device(tokens, *rest):
        whole_sequence = tokens.shape[0] == LEN and dict(mesh.shape) == {"dp": 16, "tensor": 2}
        return (one_sequence if whole_sequence else shards)(tokens, *rest)

    return jax.shard_map(
        per_device,
        mesh=mesh,
        in_specs=placed,
        out_specs=(
            P(("dp", "tensor"), None),
            P(("dp", "tensor"), None),
            P("tensor", None),
            P("tensor", None),
            P("tensor", None),
            P("tensor", None),
            P("tensor"),
            P("dp", None),
            P(),
            P(),
            P("dp", "tensor"),
            P("dp", "tensor"),
            P("tensor", "dp"),
            P("tensor", "dp"),
            P("tensor", "dp"),
            P("dp", "tensor"),
            P("tensor", "dp"),
        ),
        check_vma=False,
    )
```

```python
import math

import jax
import jax.numpy as jnp
from jax import lax
from jax.experimental import pallas as pl
from jax.experimental.pallas import tpu as pltpu
from jax.sharding import PartitionSpec as P

H = 16
LEN = 1024
ATT_BLOCK = 512
EMA_BLOCK = 128


norm_eps = 1e-06
masked_value = -1e30


def rms_rows(values_in):
    return values_in * lax.rsqrt(jnp.mean(values_in * values_in, axis=-1, keepdims=True) + norm_eps)


def matmul(left, right):
    return jnp.dot(left, right, preferred_element_type=jnp.float32)


def row_inner(left, right):
    return lax.dot_general(
        left, right, (((0,), (0,)), ((), ())), preferred_element_type=jnp.float32
    )


def col_inner(left, right):
    return lax.dot_general(
        left, right, (((1,), (1,)), ((), ())), preferred_element_type=jnp.float32
    )


def silu_slope(pre_act):
    logistic = jax.nn.sigmoid(pre_act)
    return logistic * (1.0 + pre_act * (1.0 - logistic))


def gate_apply(h_pre, f_pre, x_rows):
    update = jax.nn.sigmoid(f_pre)
    return update * jax.nn.silu(h_pre) + (1.0 - update) * x_rows


def ema_apply(signal, ema_params):
    alpha_logit, delta_logit, ema_beta, ema_eta, ema_omega = ema_params
    alpha_rate = jax.nn.sigmoid(alpha_logit)
    decay_rate = 1.0 - alpha_rate * jax.nn.sigmoid(delta_logit)
    feed_rate = alpha_rate * ema_beta
    log_decay = jnp.log(decay_rate)
    total_rows, chan_count = signal.shape
    seq_count = total_rows // LEN
    block_count = LEN // EMA_BLOCK
    blocks = signal.reshape(seq_count, block_count, EMA_BLOCK, chan_count)
    steps_in = jnp.arange(EMA_BLOCK, dtype=jnp.float32)
    lag_power = jnp.exp(steps_in[:, None, None] * log_decay[None])
    kernel = jnp.sum(lag_power * (feed_rate * ema_eta)[None], axis=-1)
    offsets = steps_in[:, None] - steps_in[None, :]
    lag_index = jnp.clip(offsets, 0, EMA_BLOCK - 1).astype(jnp.int32)
    toeplitz = jnp.where((offsets >= 0)[:, :, None], kernel[lag_index], 0.0)
    local_part = jnp.einsum("ijc,snjc->snic", toeplitz, blocks)
    tail_power = lag_power[::-1] * feed_rate[None]
    block_state = jnp.einsum("jch,snjc->snch", tail_power, blocks)
    full_decay = jnp.exp(EMA_BLOCK * log_decay)

    def carry_step(state_in, incoming):
        return (full_decay * state_in + incoming, state_in)

    zero_state = jnp.zeros((seq_count, chan_count, H), jnp.float32)
    _, start_state = lax.scan(carry_step, zero_state, jnp.moveaxis(block_state, 1, 0))
    start_state = jnp.moveaxis(start_state, 0, 1)
    head_power = lag_power * decay_rate[None] * ema_eta[None]
    carried = jnp.einsum("ich,snch->snic", head_power, start_state)
    ema_pre = (local_part + carried).reshape(total_rows, chan_count) + ema_omega * signal
    return jax.nn.silu(ema_pre)


def masked_scores(q_rows, k_rows, first_row):
    raw_scores = col_inner(q_rows, k_rows) * q_rows.shape[1] ** (-0.5)
    row_pos = first_row + jnp.arange(q_rows.shape[0])[:, None]
    col_pos = jnp.arange(k_rows.shape[0])[None, :]
    return jnp.where(col_pos <= row_pos, raw_scores, masked_value)


def attend_forward(query_low, key_low, value_low):
    total_rows, value_width = value_low.shape
    seq_count = total_rows // LEN
    per_seq = LEN // ATT_BLOCK

    def attend_one_block(flat_index):
        seq_id = flat_index // per_seq
        blk_id = flat_index % per_seq
        seq_start = seq_id * LEN
        q_rows = lax.dynamic_slice_in_dim(query_low, seq_start + blk_id * ATT_BLOCK, ATT_BLOCK, 0)
        k_rows = lax.dynamic_slice_in_dim(key_low, seq_start, LEN, 0)
        v_rows = lax.dynamic_slice_in_dim(value_low, seq_start, LEN, 0)
        scores = masked_scores(q_rows, k_rows, blk_id * ATT_BLOCK)
        top_score = jnp.max(scores, axis=-1, keepdims=True)
        weights = jnp.exp(scores - top_score)
        total_weight = jnp.sum(weights, axis=-1, keepdims=True)
        probs = (weights / total_weight).astype(jnp.bfloat16)
        return (matmul(probs, v_rows), top_score[:, 0] + jnp.log(total_weight[:, 0]))

    outs, lse_all = lax.map(attend_one_block, jnp.arange(seq_count * per_seq))
    return (outs.reshape(total_rows, value_width), lse_all.reshape(total_rows))


def attend_backward(query_low, key_low, value_low, lse_rows, d_att):
    total_rows, value_width = value_low.shape
    head_width = query_low.shape[1]
    seq_count = total_rows // LEN
    per_seq = LEN // ATT_BLOCK
    scale = head_width ** (-0.5)

    def one_seq(seq_id):
        seq_start = seq_id * LEN
        k_rows = lax.dynamic_slice_in_dim(key_low, seq_start, LEN, 0)
        v_rows = lax.dynamic_slice_in_dim(value_low, seq_start, LEN, 0)

        def one_one_block(carry_in, blk_id):
            d_keys, d_vals = carry_in
            row_start = seq_start + blk_id * ATT_BLOCK
            q_rows = lax.dynamic_slice_in_dim(query_low, row_start, ATT_BLOCK, 0)
            g_rows = lax.dynamic_slice_in_dim(d_att, row_start, ATT_BLOCK, 0)
            lse_part = lax.dynamic_slice_in_dim(lse_rows, row_start, ATT_BLOCK, 0)
            probs = jnp.exp(masked_scores(q_rows, k_rows, blk_id * ATT_BLOCK) - lse_part[:, None])
            d_probs = col_inner(g_rows, v_rows)
            d_scores = (
                probs * (d_probs - jnp.sum(probs * d_probs, axis=-1, keepdims=True))
            ).astype(jnp.bfloat16)
            d_rows = matmul(d_scores, k_rows) * scale
            d_keys = d_keys + row_inner(d_scores, q_rows) * scale
            d_vals = d_vals + row_inner(probs.astype(jnp.bfloat16), g_rows)
            return ((d_keys, d_vals), d_rows)

        start_carry = (
            jnp.zeros((LEN, head_width), jnp.float32),
            jnp.zeros((LEN, value_width), jnp.float32),
        )
        (d_keys, d_vals), d_rows = lax.scan(one_one_block, start_carry, jnp.arange(per_seq))
        return (d_rows.reshape(LEN, head_width), d_keys, d_vals)

    d_query, d_key, d_value = lax.map(one_seq, jnp.arange(seq_count))
    return (
        d_query.reshape(total_rows, head_width),
        d_key.reshape(total_rows, head_width),
        d_value.reshape(total_rows, value_width),
    )


def shards(
    tokens,
    alpha_logit,
    delta_logit,
    ema_beta,
    ema_eta,
    ema_omega,
    w_z,
    qk_gain,
    qk_bias,
    w_v,
    w_gamma,
    u_h,
    w_h,
    w_phi,
    w_up,
    w_down,
    cotangent,
):
    tensor_pos = lax.axis_index("tensor")
    feature_count = tokens.shape[1]
    chan_count = ema_omega.shape[0]
    chan_start = tensor_pos * chan_count
    x_rows = tokens.astype(jnp.float32)
    normed_rows, norm_pull = jax.vjp(rms_rows, x_rows)
    normed, cot_full = (
        lax.all_gather(normed_rows.astype(jnp.bfloat16), "tensor", axis=0, tiled=True),
        lax.all_gather(cotangent, "tensor", axis=0, tiled=True),
    )
    signal = lax.dynamic_slice_in_dim(normed, chan_start, chan_count, 1).astype(jnp.float32)
    ema_params = (alpha_logit, delta_logit, ema_beta, ema_eta, ema_omega)
    ema_val, ema_pull = jax.vjp(ema_apply, signal, ema_params)
    ema_low = ema_val.astype(jnp.bfloat16)
    ema_full = lax.all_gather(ema_low, "tensor", axis=1, tiled=True)
    z_pre = matmul(ema_full, w_z)
    z_act = jax.nn.silu(z_pre)
    query_low = (z_act * qk_gain[0] + qk_bias[0]).astype(jnp.bfloat16)
    key_low = (z_act * qk_gain[1] + qk_bias[1]).astype(jnp.bfloat16)
    values_pre = matmul(normed, w_v)
    value_low = jax.nn.silu(values_pre).astype(jnp.bfloat16)
    gamma_pre = matmul(ema_full, w_gamma)
    gamma_act = jax.nn.silu(gamma_pre)
    attended, lse_rows = attend_forward(query_low, key_low, value_low)
    gated_low = (gamma_act * attended).astype(jnp.bfloat16)
    both_pre = lax.psum_scatter(
        jnp.concatenate(
            [matmul(gated_low, u_h) + matmul(ema_low, w_h), matmul(ema_low, w_phi)], axis=1
        ),
        "tensor",
        scatter_dimension=0,
        tiled=True,
    )
    h_pre = both_pre[:, :feature_count]
    f_pre = both_pre[:, feature_count:]
    mixed, gate_pull = jax.vjp(gate_apply, h_pre, f_pre, x_rows)
    normed_two, norm_two_pull = jax.vjp(rms_rows, mixed)
    lowered = lax.all_gather(normed_two.astype(jnp.bfloat16), "tensor", axis=0, tiled=True)
    up_pre = matmul(lowered, w_up)
    hidden = jax.nn.silu(up_pre).astype(jnp.bfloat16)
    down_rows = lax.psum_scatter(
        matmul(hidden, w_down).astype(jnp.bfloat16), "tensor", scatter_dimension=0, tiled=True
    ).astype(jnp.float32)
    output = (mixed + down_rows).astype(jnp.bfloat16)
    cot_rows = cotangent.astype(jnp.float32)
    d_hidden = col_inner(cot_full, w_down)
    d_up = (d_hidden * silu_slope(up_pre)).astype(jnp.bfloat16)
    down_grad = row_inner(hidden, cot_full)
    up_grad = row_inner(lowered, d_up)
    d_lowered = lax.psum_scatter(col_inner(d_up, w_up), "tensor", scatter_dimension=0, tiled=True)
    d_mixed = cot_rows + norm_two_pull(d_lowered)[0]
    d_hpre, d_fpre, d_direct = gate_pull(d_mixed)
    h_full_grad, f_full_grad = (
        lax.all_gather(d_hpre.astype(jnp.bfloat16), "tensor", axis=0, tiled=True),
        lax.all_gather(d_fpre.astype(jnp.bfloat16), "tensor", axis=0, tiled=True),
    )
    uh_grad = row_inner(gated_low, h_full_grad)
    wh_grad = row_inner(ema_low, h_full_grad)
    phi_grad = row_inner(ema_low, f_full_grad)
    d_gated = col_inner(h_full_grad, u_h)
    d_att = (d_gated * gamma_act).astype(jnp.bfloat16)
    d_gamma = (d_gated * attended * silu_slope(gamma_pre)).astype(jnp.bfloat16)
    d_query, d_key, d_value = attend_backward(query_low, key_low, value_low, lse_rows, d_att)
    d_query, d_key = lax.psum((d_query, d_key), "tensor")
    d_z = (silu_slope(z_pre) * (d_query * qk_gain[0] + d_key * qk_gain[1])).astype(jnp.bfloat16)
    gain_grad = jnp.stack([jnp.sum(d_query * z_act, axis=0), jnp.sum(d_key * z_act, axis=0)])
    bias_grad = jnp.stack([jnp.sum(d_query, axis=0), jnp.sum(d_key, axis=0)])
    z_grad = row_inner(ema_full, d_z)
    gamma_grad = row_inner(ema_full, d_gamma)
    d_value_pre = (d_value * silu_slope(values_pre)).astype(jnp.bfloat16)
    value_grad = row_inner(normed, d_value_pre)
    d_chan = lax.psum_scatter(
        col_inner(d_gamma, w_gamma).astype(jnp.bfloat16), "tensor", scatter_dimension=1, tiled=True
    ).astype(jnp.float32)
    z_rows = lax.dynamic_slice_in_dim(w_z, chan_start, chan_count, 0)
    d_chan = (
        d_chan
        + col_inner(d_z, z_rows)
        + col_inner(h_full_grad, w_h)
        + col_inner(f_full_grad, w_phi)
    )
    d_signal, d_params = ema_pull(d_chan)
    d_norm_part = col_inner(d_value_pre, w_v)
    own_cols = lax.dynamic_slice_in_dim(d_norm_part, chan_start, chan_count, 1)
    d_norm_part = lax.dynamic_update_slice_in_dim(d_norm_part, own_cols + d_signal, chan_start, 1)
    d_normed = lax.psum_scatter(
        d_norm_part.astype(jnp.bfloat16), "tensor", scatter_dimension=0, tiled=True
    ).astype(jnp.float32)
    input_grad = d_direct + norm_pull(d_normed)[0]
    weight_totals = (
        lax.psum_scatter(z_grad.astype(jnp.bfloat16), "dp", scatter_dimension=0, tiled=True).astype(
            jnp.float32
        ),
        lax.psum_scatter(
            value_grad.astype(jnp.bfloat16), "dp", scatter_dimension=0, tiled=True
        ).astype(jnp.float32),
        lax.psum_scatter(
            gamma_grad.astype(jnp.bfloat16), "dp", scatter_dimension=0, tiled=True
        ).astype(jnp.float32),
        lax.psum_scatter(
            uh_grad.astype(jnp.bfloat16), "dp", scatter_dimension=1, tiled=True
        ).astype(jnp.float32),
        lax.psum_scatter(
            wh_grad.astype(jnp.bfloat16), "dp", scatter_dimension=1, tiled=True
        ).astype(jnp.float32),
        lax.psum_scatter(
            phi_grad.astype(jnp.bfloat16), "dp", scatter_dimension=1, tiled=True
        ).astype(jnp.float32),
        lax.psum_scatter(
            up_grad.astype(jnp.bfloat16), "dp", scatter_dimension=0, tiled=True
        ).astype(jnp.float32),
        lax.psum_scatter(
            down_grad.astype(jnp.bfloat16), "dp", scatter_dimension=1, tiled=True
        ).astype(jnp.float32),
    )
    param_totals = lax.psum(
        (d_params[0], d_params[1], d_params[2], d_params[3], d_params[4], gain_grad, bias_grad),
        "dp",
    )
    return (
        output,
        input_grad,
        param_totals[0],
        param_totals[1],
        param_totals[2],
        param_totals[3],
        param_totals[4],
        weight_totals[0],
        param_totals[5],
        param_totals[6],
        weight_totals[1],
        weight_totals[2],
        weight_totals[3],
        weight_totals[4],
        weight_totals[5],
        weight_totals[6],
        weight_totals[7],
    )


CP = pltpu.CompilerParams(vmem_limit_bytes=56 * 1024 * 1024)
BF = jnp.bfloat16
F32 = jnp.float32
ROWS = 256
hint = 10


def sds(shape, dtype=BF):
    return jax.ShapeDtypeStruct(shape, dtype)


def whole(shape):
    return pl.BlockSpec(shape, lambda i, s: (0,) * len(shape), pipeline_mode=pl.Buffered(1))


def rows_of(cols, rows=ROWS):
    return pl.BlockSpec((rows, cols), lambda i, s: (i, 0))


def cols_of(rows, cols):
    return pl.BlockSpec((rows, cols), lambda i, s: (0, i))


def run(body, grid, scal, ins, in_specs, out_shape, out_specs, scratch=(), flops=0, name=None, aliases=None):
    moved = sum(a.size * a.dtype.itemsize for a in ins)
    moved += sum(math.prod(o.shape) * jnp.dtype(o.dtype).itemsize for o in out_shape)
    return pl.pallas_call(
        body,
        out_shape=out_shape,
        grid_spec=pltpu.PrefetchScalarGridSpec(
            num_scalar_prefetch=1,
            grid=grid,
            in_specs=in_specs,
            out_specs=out_specs,
            scratch_shapes=list(scratch),
        ),
        compiler_params=CP,
        cost_estimate=pl.CostEstimate(flops=int(flops * hint), bytes_accessed=int(moved * hint), transcendentals=0),
        name=name,
        input_output_aliases=aliases or {},
    )(scal, *ins)


def sig(u):
    return 1.0 / (1.0 + jnp.exp(-u))


def silu_pair(u):
    s = sig(u)
    return u * s, s * (1.0 + u * (1.0 - s))


def place(scr, s, pieces, base=0, table=0):
    rows = pieces[0].shape[0]
    for p in range(4):
        scr[pl.ds(pl.multiple_of(base + s[table + p] * rows, rows), rows), :] = pieces[p][...]


def piece_block(rows, cols, row_block):
    return pl.BlockSpec((rows, cols), lambda i, s: (row_block, i))


def piece_whole(rows, cols, row_block):
    return pl.BlockSpec((rows, cols), lambda i, s: (row_block, 0), pipeline_mode=pl.Buffered(1))


def k_value_own(scal, tokens, w_own):
    n, d = tokens.shape
    cols = w_own.shape[1]
    tn = 512

    def body(s, x_ref, w_ref, n_ref, v_ref, sl_ref):
        @pl.when(pl.program_id(0) == 0)
        def _():
            x = x_ref[...].astype(F32)
            n_ref[...] = (x * lax.rsqrt(jnp.mean(x * x, axis=-1, keepdims=True) + norm_eps)).astype(BF)

        act, slope = silu_pair(matmul(n_ref[...], w_ref[...]))
        v_ref[...] = act.astype(BF)
        sl_ref[...] = slope.astype(BF)

    return run(
        body, (cols // tn,), scal, [tokens, w_own],
        [whole((n, d)), cols_of(d, tn)],
        [sds((n, d)), sds((n, cols)), sds((n, cols))],
        [pl.BlockSpec((n, d), lambda i, s: (0, 0)), cols_of(n, tn), cols_of(n, tn)],
        flops=2 * n * d * cols, name="value_own",
    )


def k_act_own(scal, x, w_own, tn):
    n, d = x.shape
    cols = w_own.shape[1]

    def body(s, x_ref, w_ref, v_ref, sl_ref):
        act, slope = silu_pair(matmul(x_ref[...], w_ref[...]))
        v_ref[...] = act.astype(BF)
        sl_ref[...] = slope.astype(BF)

    return run(
        body, (cols // tn,), scal, [x, w_own],
        [whole((n, d)), cols_of(d, tn)],
        [sds((n, cols)), sds((n, cols))],
        [cols_of(n, tn), cols_of(n, tn)],
        flops=2 * n * d * cols, name="act_own",
    )


def k_act_other(scal, x, pieces, table, tn):
    n, d = x.shape
    rows, cols = pieces[0].shape

    def body(s, x_ref, p0, p1, p2, p3, v_ref, sl_ref, w_scr):
        place(w_scr, s, (p0, p1, p2, p3), table=table)
        act, slope = silu_pair(matmul(x_ref[...], w_scr[...]))
        v_ref[...] = act.astype(BF)
        sl_ref[...] = slope.astype(BF)

    return run(
        body, (cols // tn,), scal, [x, *pieces],
        [whole((n, d))] + [piece_block(rows, tn, 0)] * 4,
        [sds((n, cols)), sds((n, cols))],
        [cols_of(n, tn), cols_of(n, tn)],
        [pltpu.VMEM((d, tn), BF)],
        flops=2 * n * d * cols, name="act_other",
    )


def k_query_key(scal, ema_low, w_z, qk_gain, qk_bias):
    n, d = ema_low.shape
    zw = w_z.shape[1]

    def body(s, e_ref, w_ref, g_ref, b_ref, z_ref, q_ref, k_ref):
        z_pre = matmul(e_ref[...], w_ref[...])
        z_ref[...] = z_pre
        act = z_pre * sig(z_pre)
        q_ref[...] = (act * g_ref[0:1, :] + b_ref[0:1, :]).astype(BF)
        k_ref[...] = (act * g_ref[1:2, :] + b_ref[1:2, :]).astype(BF)

    return run(
        body, (2,), scal, [ema_low, w_z, qk_gain, qk_bias],
        [rows_of(d, n // 2), whole((d, zw)), whole((2, zw)), whole((2, zw))],
        [sds((n, zw), F32), sds((n, zw)), sds((n, zw))],
        [rows_of(zw, n // 2)] * 3,
        flops=2 * n * d * zw, name="query_key",
    )


def k_ema_forward(scal, normed, decay, coef, omega, first, count, before=None):
    n, d = normed.shape
    groups = d // 128
    tb = 128

    def body(s, x_ref, dec_ref, cf_ref, om_ref, *refs):
        e_ref, sl_ref, st, xs, ys = refs[-5:]

        @pl.when(pl.program_id(0) == 0)
        def _():
            st[...] = refs[0][...] if before else jnp.zeros_like(st)

        for g in range(groups):
            xs[pl.ds(g, tb, stride=groups), :] = x_ref[:, g * 128 : (g + 1) * 128].astype(F32)
        dec = [dec_ref[k * groups : (k + 1) * groups, :] for k in range(H)]
        cf = [cf_ref[k * groups : (k + 1) * groups, :] for k in range(H)]
        om = om_ref[...]

        def steps(b, carry):
            states = list(carry)
            for u in range(8):
                row = pl.multiple_of((b * 8 + u) * groups, groups)
                xt = xs[pl.ds(row, groups), :]
                parts = [om * xt, None, None, None]
                for k in range(H):
                    states[k] = dec[k] * states[k] + xt
                    term = cf[k] * states[k]
                    parts[k % 4] = term if parts[k % 4] is None else parts[k % 4] + term
                ys[pl.ds(row, groups), :] = (parts[0] + parts[1]) + (parts[2] + parts[3])
            return tuple(states)

        start = tuple(st[k * groups : (k + 1) * groups, :] for k in range(H))
        end = lax.fori_loop(0, tb // 8, steps, start)
        for k in range(H):
            st[k * groups : (k + 1) * groups, :] = end[k]
        for g in range(groups):
            act, slope = silu_pair(ys[pl.ds(g, tb, stride=groups), :])
            e_ref[:, g * 128 : (g + 1) * 128] = act.astype(BF)
            sl_ref[:, g * 128 : (g + 1) * 128] = slope.astype(BF)

    par = (H * groups, 128)
    at = pl.BlockSpec((tb, d), lambda i, s: (first + i, 0))
    more = list(before) if before else []
    return run(
        body, (count,), scal, [normed, decay, coef, omega, *more],
        [at, whole(par), whole(par), whole((groups, 128))]
        + ([whole(par), pl.BlockSpec(memory_space=pl.ANY), pl.BlockSpec(memory_space=pl.ANY)] if before else []),
        [sds((n, d)), sds((n, d)), sds(par, F32)],
        [at, at, pl.BlockSpec(par, lambda i, s: (0, 0))],
        [pltpu.VMEM((tb * groups, 128), F32), pltpu.VMEM((tb * groups, 128), F32)],
        flops=2.5e9 * count, name="ema_forward", aliases={6: 0, 7: 1} if before else {},
    )


def k_ema_backward(scal, normed, de_part, dz, slope, w_z, decay, coef, omega, first, count, before=None):
    n, d = normed.shape
    groups = d // 128
    tb = 128
    nb = n // tb
    half = H // 2
    gh = groups * half
    zw = dz.shape[1]

    def body(s, x_ref, de_ref, z_ref, sl_ref, wz_ref, dec_ref, cf_ref, om_ref, *refs):
        o_ref, back, deriv, a_ref, b_ref, w_ref, xs, gs, ys = refs[-9:]

        @pl.when(pl.program_id(0) == 0)
        def _():
            for i, ref in enumerate((back, deriv, a_ref, b_ref, w_ref)):
                ref[...] = refs[i][...] if before else jnp.zeros_like(ref)

        d_e = (de_ref[...] + col_inner(z_ref[...], wz_ref[...])) * sl_ref[...].astype(F32)
        for g in range(groups):
            xs[pl.ds(g, tb, stride=groups), :] = x_ref[:, g * 128 : (g + 1) * 128].astype(F32)
            gs[pl.ds(g, tb, stride=groups), :] = d_e[:, g * 128 : (g + 1) * 128]

        for part in range(2):
            low = part * gh
            at = [slice(low + k * groups, low + (k + 1) * groups) for k in range(half)]
            dec = [dec_ref[a, :] for a in at]

            def steps(b, carry, part=part, at=at, dec=dec):
                bk, dv, aa, bb, ww = (list(c) for c in carry)
                for u in range(4):
                    row = pl.multiple_of((tb - 1 - (b * 4 + u)) * groups, groups)
                    xt = xs[pl.ds(row, groups), :]
                    gt = gs[pl.ds(row, groups), :]
                    if part == 0:
                        outs = [om_ref[...] * gt, None]
                        ww[0] = ww[0] + xt * gt
                    else:
                        outs = [ys[pl.ds(row, groups), :], None]
                    for k in range(half):
                        dv[k] = dec[k] * dv[k] + bk[k]
                        bk[k] = dec[k] * bk[k] + gt
                        term = cf_ref[at[k], :] * bk[k]
                        outs[k % 2] = term if outs[k % 2] is None else outs[k % 2] + term
                        aa[k] = aa[k] + xt * bk[k]
                        bb[k] = bb[k] + xt * dv[k]
                    ys[pl.ds(row, groups), :] = outs[0] + outs[1]
                return tuple(bk), tuple(dv), tuple(aa), tuple(bb), tuple(ww)

            start = (
                tuple(back[a, :] for a in at),
                tuple(deriv[a, :] for a in at),
                tuple(a_ref[a, :] for a in at),
                tuple(b_ref[a, :] for a in at),
                (w_ref[...],),
            )
            bk, dv, aa, bb, ww = lax.fori_loop(0, tb // 4, steps, start)
            for k in range(half):
                back[at[k], :] = bk[k]
                deriv[at[k], :] = dv[k]
                a_ref[at[k], :] = aa[k]
                b_ref[at[k], :] = bb[k]
            w_ref[...] = ww[0]
        for g in range(groups):
            o_ref[:, g * 128 : (g + 1) * 128] = ys[pl.ds(g, tb, stride=groups), :]

    top = nb - 1 - first
    back_rows = pl.BlockSpec((tb, d), lambda i, s: (top - i, 0))
    par = (H * groups, 128)
    const = pl.BlockSpec(par, lambda i, s: (0, 0))
    small = (groups, 128)
    more = [*before[1:], before[0]] if before else []
    return run(
        body, (count,), scal, [normed, de_part, dz, slope, w_z, decay, coef, omega, *more],
        [back_rows, back_rows, pl.BlockSpec((tb, zw), lambda i, s: (top - i, 0)), back_rows, whole((d, zw)),
         whole(par), whole(par), whole(small)]
        + ([whole(par)] * 4 + [whole(small), pl.BlockSpec(memory_space=pl.ANY)] if before else []),
        [sds((n, d), F32)] + [sds(par, F32)] * 4 + [sds(small, F32)],
        [back_rows, const, const, const, const, pl.BlockSpec(small, lambda i, s: (0, 0))],
        [pltpu.VMEM((tb * groups, 128), F32)] * 3,
        flops=5e9 * count, name="ema_backward", aliases={14: 0} if before else {},
    )


def k_attend(scal, q, k, v_own, v_oth, g_own, g_oth, gs_own, gs_oth):
    n, zw = q.shape
    half = v_own.shape[1]
    blocks = n // ROWS
    scale = zw ** (-0.5)

    def body(s, q_ref, k_ref, vo, vt, go, gt, so, st, gated_o, gated_t, mo, mt, p_ref):
        for i in range(blocks):

            @pl.when(pl.program_id(0) == i)
            def _(i=i):
                seen = (i + 1) * ROWS
                sc = col_inner(q_ref[...], k_ref[0:seen, :]) * scale
                row = i * ROWS + lax.broadcasted_iota(jnp.int32, (ROWS, seen), 0)
                col = lax.broadcasted_iota(jnp.int32, (ROWS, seen), 1)
                sc = jnp.where(col <= row, sc, masked_value)
                e = jnp.exp(sc - jnp.max(sc, axis=-1, keepdims=True))
                p = (e * (1.0 / jnp.sum(e, axis=-1, keepdims=True))).astype(BF)
                p_ref[:, 0:seen] = p
                for v_ref, g_ref, sl_ref, gated, m in ((vo, go, so, gated_o, mo), (vt, gt, st, gated_t, mt)):
                    att = matmul(p, v_ref[0:seen, :])
                    gated[...] = (g_ref[...].astype(F32) * att).astype(BF)
                    m[...] = (sl_ref[...].astype(F32) * att).astype(BF)

    return run(
        body, (blocks,), scal, [q, k, v_own, v_oth, g_own, g_oth, gs_own, gs_oth],
        [rows_of(zw), whole((n, zw)), whole((n, half)), whole((n, half))] + [rows_of(half)] * 4,
        [sds((n, half))] * 4 + [sds((n, n))],
        [rows_of(half)] * 4 + [rows_of(n)],
        flops=n * n * (zw + 2 * half) * 1.25, name="attend",
    )


def k_gate(scal, gated_own, gated_oth, ema_low, tokens, u_own, h_own, f_own, packs_u, packs_h):
    n, d = tokens.shape
    half = u_own.shape[0]
    ch = h_own.shape[0]
    ru, rh = packs_u[0].shape[0], packs_h[0].shape[0] // 2

    def body(s, go, gt, e_ref, x_ref, uo, ho, fo, u0, u1, u2, u3, h0, h1, h2, h3, f0, f1, f2, f3,
             mix_ref, low_ref, a_ref, b_ref, up_ref, u_scr, h_scr, f_scr):
        @pl.when(pl.program_id(0) == 0)
        def _():
            place(u_scr, s, (u0, u1, u2, u3))
            own = pl.multiple_of(s[6] * ch, ch)
            oth = s[7] * ch
            h_scr[pl.ds(own, ch), :] = ho[...]
            f_scr[pl.ds(own, ch), :] = fo[...]
            place(h_scr, s, (h0, h1, h2, h3), oth, 8)
            place(f_scr, s, (f0, f1, f2, f3), oth, 8)

        h_pre = matmul(go[...], uo[...]) + matmul(gt[...], u_scr[...]) + matmul(e_ref[...], h_scr[...])
        f_pre = matmul(e_ref[...], f_scr[...])
        x = x_ref[...].astype(F32)
        act, slope = silu_pair(h_pre)
        update = sig(f_pre)
        mixed = update * act + (1.0 - update) * x
        mix_ref[...] = mixed
        low_ref[...] = (mixed * lax.rsqrt(jnp.mean(mixed * mixed, axis=-1, keepdims=True) + norm_eps)).astype(BF)
        a_ref[...] = (update * slope).astype(BF)
        b_ref[...] = ((act - x) * update * (1.0 - update)).astype(BF)
        up_ref[...] = (1.0 - update).astype(BF)

    ins = [gated_own, gated_oth, ema_low, tokens, u_own, h_own, f_own, *packs_u, *packs_h, *packs_h]
    specs = [rows_of(half), rows_of(half), rows_of(d), rows_of(d), whole((half, d)), whole((ch, d)), whole((ch, d))]
    specs += [piece_whole(ru, d, 0)] * 4 + [piece_whole(rh, d, 0)] * 4 + [piece_whole(rh, d, 1)] * 4
    return run(
        body, (n // ROWS,), scal, ins, specs,
        [sds((n, d), F32), sds((n, d)), sds((n, d)), sds((n, d)), sds((n, d))],
        [rows_of(d)] * 5,
        [pltpu.VMEM((half, d), BF), pltpu.VMEM((2 * ch, d), BF), pltpu.VMEM((2 * ch, d), BF)],
        flops=2 * n * d * (2 * half + 4 * ch), name="gate",
    )


def k_ffn(scal, lowered, cot, up, down, part):
    n, d = lowered.shape
    pieces = len(up) > 1
    tn = up[0].shape[1] // 4

    def body(s, low_ref, c_ref, *refs):
        step = pl.program_id(0)
        nu, nd = len(up), len(down)
        ups, downs = refs[:nu], refs[nu : nu + nd]
        out_ref, gl_ref, grads, acc, gl, u_scr = refs[nu + nd :]
        if pieces:
            place(u_scr, s, ups)
            wu = u_scr
        else:
            wu = ups[0]

        def work(wd, i):
            act, slope = silu_pair(matmul(low_ref[...], wu[...]))
            hid = act.astype(BF)
            out = matmul(hid, wd[...])
            du = (col_inner(c_ref[...], wd[...]) * slope).astype(BF)
            back = col_inner(du, wu[...])
            if i == 0:
                acc[...] = out
                gl[...] = back
            else:
                out_ref[...] = (acc[...] + out).astype(BF)
                gl_ref[...] = (gl[...] + back).astype(BF)
            grads[0] = row_inner(c_ref[...], hid).astype(BF)
            grads[1] = row_inner(low_ref[...], du).astype(BF)

        for i in range(2):

            @pl.when(step == i)
            def _(i=i):
                work(downs[i % nd], i)

    first = 8 + 2 * part
    if pieces:
        down = down[2 * part : 2 * part + 2]
        specs = [pl.BlockSpec((d // 4, tn), lambda i, s: (0, s[first + i]))] * 4 + [whole((tn, d))] * 2
    else:
        specs = [
            pl.BlockSpec((d, tn), lambda i, s: (0, s[first + i])),
            pl.BlockSpec((tn, d), lambda i, s: (s[first + i], 0)),
        ]
    still = pl.BlockSpec((n, d), lambda i, s: (0, 0))
    return run(
        body, (2,), scal, [lowered, cot, *up, *down],
        [whole((n, d)), whole((n, d))] + specs,
        [sds((n, d)), sds((n, d)), sds((2, d, 2 * tn))],
        [still, still, pl.BlockSpec((2, d, tn), lambda i, s: (0, 0, s[first + i] % 2))],
        [pltpu.VMEM((n, d), F32), pltpu.VMEM((n, d), F32), pltpu.VMEM((d, tn), BF)],
        flops=24 * n * d * tn, name="ffn",
    )


def k_mid_back(scal, dls, accs, cot, mixed, fac_h, fac_f, keep, g_own, g_oth, m_own, m_oth,
               u_own, wg_own, h_own, f_own, packs_g, packs_u, packs_h):
    n, d = cot.shape
    half = u_own.shape[0]
    ch = h_own.shape[0]
    ru, rh = packs_u[0].shape[0], packs_h[0].shape[0] // 2
    rg = packs_g[0].shape[0]

    def body(s, l0, l1, l2, l3, o0, o1, o2, o3, c_ref, x_ref, a_ref, b_ref, k_ref, go, gt, mo, mt, uo, wo, ho, fo,
             w0, w1, w2, w3, u0, u1, u2, u3, h0, h1, h2, h3, f0, f1, f2, f3,
             out_ref, dh_ref, df_ref, dir_ref, ao, at, do, dt, de_ref, u_scr, w_scr, h_scr, f_scr):
        @pl.when(pl.program_id(0) == 0)
        def _():
            place(u_scr, s, (u0, u1, u2, u3))
            place(w_scr, s, (w0, w1, w2, w3), table=8)
            own = pl.multiple_of(s[6] * ch, ch)
            oth = s[7] * ch
            h_scr[pl.ds(own, ch), :] = ho[...]
            f_scr[pl.ds(own, ch), :] = fo[...]
            place(h_scr, s, (h0, h1, h2, h3), oth, 8)
            place(f_scr, s, (f0, f1, f2, f3), oth, 8)

        dl = (l0[...].astype(F32) + l1[...].astype(F32)) + (l2[...].astype(F32) + l3[...].astype(F32))
        out = (o0[...].astype(F32) + o1[...].astype(F32)) + (o2[...].astype(F32) + o3[...].astype(F32))
        m = x_ref[...]
        out_ref[...] = (m + out).astype(BF)
        r = lax.rsqrt(jnp.mean(m * m, axis=-1, keepdims=True) + norm_eps)
        n2 = m * r
        dm = c_ref[...].astype(F32) + r * (dl - n2 * jnp.mean(dl * n2, axis=-1, keepdims=True))
        dh = (dm * a_ref[...].astype(F32)).astype(BF)
        df = (dm * b_ref[...].astype(F32)).astype(BF)
        dh_ref[...] = dh
        df_ref[...] = df
        dir_ref[...] = (dm * k_ref[...].astype(F32)).astype(BF)
        de = col_inner(dh, h_scr[...]) + col_inner(df, f_scr[...])
        for u, w, g_ref, m_ref, a_out, d_out in ((uo, wo, go, mo, ao, do), (u_scr, w_scr, gt, mt, at, dt)):
            dg = col_inner(dh, u[...])
            a_out[...] = (dg * g_ref[...].astype(F32)).astype(BF)
            low = (dg * m_ref[...].astype(F32)).astype(BF)
            d_out[...] = low
            de = de + col_inner(low, w[...])
        de_ref[...] = de

    ins = [*dls, *accs, cot, mixed, fac_h, fac_f, keep, g_own, g_oth, m_own, m_oth, u_own, wg_own, h_own, f_own]
    ins += [*packs_g, *packs_u, *packs_h, *packs_h]
    specs = [rows_of(d)] * 13 + [rows_of(half)] * 4
    specs += [whole((half, d)), whole((d, half)), whole((ch, d)), whole((ch, d))]
    specs += [piece_whole(rg, half, 0)] * 4 + [piece_whole(ru, d, 0)] * 4
    specs += [piece_whole(rh, d, 0)] * 4 + [piece_whole(rh, d, 1)] * 4
    return run(
        body, (n // ROWS,), scal, ins, specs,
        [sds((n, d))] * 4 + [sds((n, half))] * 4 + [sds((n, d), F32)],
        [rows_of(d)] * 4 + [rows_of(half)] * 4 + [rows_of(d)],
        [pltpu.VMEM((half, d), BF), pltpu.VMEM((d, half), BF), pltpu.VMEM((2 * ch, d), BF), pltpu.VMEM((2 * ch, d), BF)],
        flops=2 * n * d * (4 * half + 4 * ch), name="mid_back",
    )


def k_value_back(scal, p, da_own, da_oth, vs_own, vs_oth):
    n = p.shape[0]
    half = da_own.shape[1]
    blocks = n // ROWS

    def body(s, p_ref, ao, at, so, st, oo, ot):
        for j in range(blocks):

            @pl.when(pl.program_id(0) == j)
            def _(j=j):
                pj = p_ref[j * ROWS :, :]
                oo[...] = (row_inner(pj, ao[j * ROWS :, :]) * so[...].astype(F32)).astype(BF)
                ot[...] = (row_inner(pj, at[j * ROWS :, :]) * st[...].astype(F32)).astype(BF)

    return run(
        body, (blocks,), scal, [p, da_own, da_oth, vs_own, vs_oth],
        [cols_of(n, ROWS), whole((n, half)), whole((n, half)), rows_of(half), rows_of(half)],
        [sds((n, half))] * 2,
        [rows_of(half)] * 2,
        flops=n * n * 2 * half * 1.25, name="value_back",
    )


def k_score_back(scal, p, da_own, da_oth, v_own, v_oth, q, k, z_pre, gain):
    n, zw = q.shape
    half = da_own.shape[1]
    blocks = n // ROWS
    scale = zw ** (-0.5)

    def body(s, p_ref, ao, at, vo, vt, q_ref, k_ref, z_ref, g_ref, dz_ref, st_ref, ds, dq):
        for i in range(blocks):

            @pl.when(pl.program_id(0) == i)
            def _(i=i):
                seen = (i + 1) * ROWS
                pr = p_ref[:, 0:seen].astype(F32)
                dp = col_inner(ao[...], vo[0:seen, :]) + col_inner(at[...], vt[0:seen, :])
                d = (pr * (dp - jnp.sum(pr * dp, axis=-1, keepdims=True))).astype(BF)
                ds[i * ROWS : (i + 1) * ROWS, 0:seen] = d
                dq[i * ROWS : (i + 1) * ROWS, :] = matmul(d, k_ref[0:seen, :]) * scale
                if i == blocks - 1:
                    sums = [jnp.zeros((1, zw), F32)] * 4
                    for j in range(blocks):
                        at_j = slice(j * ROWS, (j + 1) * ROWS)
                        dk = row_inner(ds[j * ROWS :, at_j], q_ref[j * ROWS :, :]) * scale
                        dqj = dq[at_j, :]
                        act, slope = silu_pair(z_ref[at_j, :])
                        dz_ref[at_j, :] = (slope * (dqj * g_ref[0:1, :] + dk * g_ref[1:2, :])).astype(BF)
                        for n_, v in enumerate((dqj * act, dk * act, dqj, dk)):
                            sums[n_] = sums[n_] + jnp.sum(v, axis=0, keepdims=True)
                    for n_ in range(4):
                        st_ref[n_ : n_ + 1, :] = sums[n_]
                    st_ref[4:8, :] = jnp.zeros((4, zw), F32)

    return run(
        body, (blocks,), scal, [p, da_own, da_oth, v_own, v_oth, q, k, z_pre, gain],
        [rows_of(n), rows_of(half), rows_of(half), whole((n, half)), whole((n, half)), whole((n, zw)),
         whole((n, zw)), whole((n, zw)), whole((2, zw))],
        [sds((n, zw)), sds((8, zw), F32)],
        [pl.BlockSpec((n, zw), lambda i, s: (0, 0)), pl.BlockSpec((8, zw), lambda i, s: (0, 0))],
        [pltpu.VMEM((n, n), BF), pltpu.VMEM((n, zw), F32)],
        flops=n * n * 2 * half * 1.25, name="score_back",
    )


def k_input_back(scal, dv_own, dv_oth, w_own, packs, d_sig, tokens, direct):
    n, d = tokens.shape
    rp = packs[0].shape[0]
    half = dv_own.shape[1]

    def body(s, vo, vt, wo, w0, w1, w2, w3, sg, x_ref, dir_ref, o_ref, w_scr):
        @pl.when(pl.program_id(0) == 0)
        def _():
            place(w_scr, s, (w0, w1, w2, w3))

        dn = col_inner(vo[...], wo[...]) + col_inner(vt[...], w_scr[...]) + sg[...]
        x = x_ref[...].astype(F32)
        r = lax.rsqrt(jnp.mean(x * x, axis=-1, keepdims=True) + norm_eps)
        n1 = x * r
        o_ref[...] = dir_ref[...].astype(F32) + r * (dn - n1 * jnp.mean(dn * n1, axis=-1, keepdims=True))

    return run(
        body, (n // ROWS,), scal, [dv_own, dv_oth, w_own, *packs, d_sig, tokens, direct],
        [rows_of(half), rows_of(half), whole((d, half))] + [piece_whole(rp, half, 0)] * 4 + [rows_of(d)] * 3,
        [sds((n, d), F32)], [rows_of(d)],
        [pltpu.VMEM((d, half), BF)],
        flops=4 * n * d * half, name="input_back",
    )[0]


def k_weight(scal, left, right, at, cols, tn, adds=(), name="weight"):
    n, d = left.shape
    steps = cols // tn

    def body(s, l_ref, r_ref, *refs):
        total = row_inner(l_ref[...], r_ref[...])
        for ref in refs[:-1]:
            total = total + ref[...].astype(F32)
        refs[-1][...] = total.astype(BF)

    ins = [left, right] + [a for a, _ in adds]
    specs = [whole((n, d)), pl.BlockSpec((n, tn), lambda i, s: (0, at(s) * steps + i))]
    specs += [pl.BlockSpec((d, tn), lambda i, s, o=o: (0, o * steps + i)) for _, o in adds]
    return run(
        body, (steps,), scal, ins, specs, [sds((d, cols))], [cols_of(d, tn)],
        flops=2 * n * d * cols, name=name,
    )[0]


def k_weight_mid(scal, ema_low, dh, df, gated_own, gated_oth, dg_own, dg_oth, part, got=None):
    n, d = ema_low.shape
    half = gated_own.shape[1] // 2
    qe = d // 4

    def body(s, e_ref, h_ref, f_ref, go, gt, do, dt, eo, et, *refs):
        adds = refs[:-2]
        own, oth = refs[-2:]

        def put(out, k, at, width, value):
            if adds:
                value = value + adds[k][:, at : at + width].astype(F32)
            out[:, at : at + width] = value.astype(BF)

        for i in range(3):

            @pl.when(pl.program_id(0) == i)
            def _(i=i):
                for k, (out, g, dg, e) in enumerate(((own, go, do, eo), (oth, gt, dt, et))):
                    if i == 0:
                        put(out, k, 0, half, row_inner(h_ref[...], g[...]))
                    elif i == 1:
                        put(out, k, 0, half, row_inner(e_ref[...], dg[...]))
                    else:
                        put(out, k, 0, qe, row_inner(h_ref[...], e[...]))
                        put(out, k, qe, qe, row_inner(f_ref[...], e[...]))

    at = pl.BlockSpec((n, half), lambda i, s: (0, s[part]), pipeline_mode=pl.Buffered(1))
    e_own = pl.BlockSpec((n, qe), lambda i, s: (0, s[6] * 2 + s[part]), pipeline_mode=pl.Buffered(1))
    e_oth = pl.BlockSpec((n, qe), lambda i, s: (0, s[7] * 2 + s[part]), pipeline_mode=pl.Buffered(1))
    adds = list(got) if got is not None else []
    return run(
        body, (3,), scal, [ema_low, dh, df, gated_own, gated_oth, dg_own, dg_oth, ema_low, ema_low] + adds,
        [whole((n, d))] * 3 + [at] * 4 + [e_own, e_oth] + [cols_of(d, half)] * len(adds),
        [sds((d, 3 * half))] * 2, [cols_of(d, half)] * 2,
        flops=2 * n * d * 6 * half, name="weight_mid",
    )


def k_weight_value(scal, normed, dv_own, dv_oth, part, got=None):
    n, d = normed.shape
    half = dv_own.shape[1] // 2

    def body(s, x_ref, vo, vt, *refs):
        adds = refs[:-2]
        for i, v in enumerate((vo, vt)):

            @pl.when(pl.program_id(0) == i)
            def _(i=i, v=v):
                total = row_inner(x_ref[...], v[...])
                if adds:
                    total = total + adds[i][...].astype(F32)
                refs[-2 + i][...] = total.astype(BF)

    at = pl.BlockSpec((n, half), lambda i, s: (0, s[part]), pipeline_mode=pl.Buffered(1))
    adds = list(got) if got is not None else []
    still = pl.BlockSpec((d, half), lambda i, s: (0, 0))
    return run(
        body, (2,), scal, [normed, dv_own, dv_oth] + adds,
        [whole((n, d)), at, at] + [whole((d, half))] * len(adds),
        [sds((d, half))] * 2, [still] * 2,
        flops=2 * n * d * 2 * half, name="weight_value",
    )


def swap(values, axis, bit, size):
    return lax.ppermute(values, axis, [(i, i ^ bit) for i in range(size)])


def pick(values, index, axis):
    return lax.dynamic_index_in_dim(values, index, axis, keepdims=False)


def one_sequence(
    tokens, alpha_logit, delta_logit, ema_beta, ema_eta, ema_omega, w_z, qk_gain, qk_bias,
    w_v, w_gamma, u_h, w_h, w_phi, w_up, w_down, cotangent,
):
    n, d = tokens.shape
    dp_size = lax.axis_size("dp")
    me = lax.axis_index("dp").astype(jnp.int32)
    t = lax.axis_index("tensor").astype(jnp.int32)
    core = me % 2
    x_pos = (me // 2) % 2
    z_pos = me // 4
    kx = core * 2 + x_pos
    kz = core * 2 + z_pos % 2
    scal = jnp.stack([kx, kx ^ 1, kx ^ 2, kx ^ 3, core, 1 - core, t, 1 - t, kz, kz ^ 1, kz ^ 2, kz ^ 3])

    def held(values, *deps):
        return lax.optimization_barrier((values, deps))[0]

    def after(*deps):
        return held(scal, *deps)

    def over_core(v):
        return swap(v, "dp", 1, dp_size)

    def over_x(v):
        return swap(v, "dp", 2, dp_size)

    def over_z(v):
        return swap(v, "dp", 4, dp_size)

    def over_tensor(v):
        return swap(v, "tensor", 1, 2)

    def my_rows(w, k):
        rows = w.shape[0] // 4
        return lax.dynamic_slice_in_dim(w, k * rows, rows, 0)

    own_params = jnp.concatenate(
        [a.T for a in (alpha_logit, delta_logit, ema_beta, ema_eta)] + [ema_omega[None]], axis=0
    )
    oth_params = over_tensor(own_params)
    pv = [over_tensor(my_rows(w_v, kx))]
    params = jnp.where(
        t == 0,
        jnp.concatenate([own_params, oth_params], axis=1),
        jnp.concatenate([oth_params, own_params], axis=1),
    )
    al, de, be, et = (params[i * H : (i + 1) * H] for i in range(4))
    alpha_rate = jax.nn.sigmoid(al)
    decay = (1.0 - alpha_rate * jax.nn.sigmoid(de)).reshape(-1, 128)
    coef = (alpha_rate * be * et).reshape(-1, 128)
    omega = params[4 * H].reshape(-1, 128)

    normed, v_own, vs_own = k_value_own(scal, tokens, w_v)
    pg = [over_tensor(held(my_rows(w_gamma, kz), v_own))]
    blocks = n // 128
    ema_a = k_ema_forward(after(v_own), normed, decay, coef, omega, 0, blocks // 2)
    pv.append(over_x(held(pv[0], ema_a[0])))
    ema_low, e_slope, state = k_ema_forward(
        after(ema_a[0]), normed, decay, coef, omega, blocks // 2, blocks // 2, (ema_a[2], ema_a[0], ema_a[1])
    )
    pg.append(over_z(held(pg[0], state)))
    pu = [over_tensor(held(my_rows(u_h, kx), state))]
    z_pre, query, key = k_query_key(scal, ema_low, w_z, qk_gain, qk_bias)
    pv += [over_core(v) for v in held((pv[0], pv[1]), query)]
    g_own, gs_own = k_act_own(after(query), ema_low, w_gamma, 512)
    pg += [over_core(v) for v in held((pg[0], pg[1]), g_own)]
    pu.append(over_x(held(pu[0], g_own)))
    ph = [over_tensor(held(jnp.concatenate([my_rows(w_h, kz), my_rows(w_phi, kz)], axis=0), g_own))]
    v_oth, vs_oth = k_act_other(after(g_own), normed, pv, 0, 512)
    pup = [over_tensor(held(my_rows(w_up, kx), v_oth))]
    g_oth, gs_oth = k_act_other(after(v_oth), ema_low, pg, 8, 512)
    ph.append(over_z(held(ph[0], g_oth)))
    pu += [over_core(v) for v in held((pu[0], pu[1]), g_oth)]
    gated_own, gated_oth, m_own, m_oth, probs = k_attend(
        after(g_oth), query, key, v_own, v_oth, g_own, g_oth, gs_own, gs_oth
    )
    ph += [over_core(v) for v in held((ph[0], ph[1]), probs)]
    pdn = [over_tensor(held(my_rows(w_down, kz), probs))]
    mixed, lowered, fac_h, fac_f, keep = k_gate(
        after(probs), gated_own, gated_oth, ema_low, tokens, u_h, w_h, w_phi, pu, ph
    )
    pup.append(over_x(held(pup[0], mixed)))
    acc0, dl0, sent_o = k_ffn(after(mixed), lowered, cotangent, [w_up], [w_down], 1)
    pdn.append(over_z(held(pdn[0], acc0)))
    got_o = over_core(sent_o)
    acc1, dl1, kept_o = k_ffn(after(acc0), lowered, cotangent, [w_up], [w_down], 0)
    pup += [over_core(v) for v in held((pup[0], pup[1]), acc1)]
    pdn += [over_core(v) for v in held((pdn[0], pdn[1]), acc1)]

    def add(*values):
        total = values[0].astype(F32)
        for v in values[1:]:
            total = total + v.astype(F32)
        return total.astype(BF)

    def x_mine(v):
        return pick(v.reshape(4, 2, d // 8, v.shape[-1]), x_pos, 1)

    def x_theirs(v):
        return pick(v.reshape(4, 2, d // 8, v.shape[-1]), 1 - x_pos, 1)

    def z_first(terms):
        by_z = [v.reshape(2, 2, d // 8, v.shape[-1]) for v in terms]
        send = add(*[pick(v, 1 - z_pos % 2, 1) for v in by_z])
        return send, [pick(v, z_pos % 2, 1) for v in by_z]

    def z_second(terms):
        send = add(*[pick(v, 1 - z_pos // 2, 0) for v in terms])
        return send, [pick(v, z_pos // 2, 0) for v in terms]

    def over_z2(v):
        return swap(v, "dp", 8, dp_size)

    def core_rows(terms):
        by_core = [v.reshape(2, d // 16, v.shape[-1]) for v in terms]
        send = add(*[pick(v, 1 - core, 0) for v in by_core])
        return send, [pick(v, core, 0) for v in by_core]

    def total(terms):
        value = terms[0].astype(F32)
        for v in terms[1:]:
            value = value + v.astype(F32)
        return value

    def joined(kept, got):
        kept, got = kept.astype(F32), got.astype(F32)
        return jnp.where(
            core == 0, jnp.concatenate([kept, got], axis=1), jnp.concatenate([got, kept], axis=1)
        )

    dn_x1 = add(x_theirs(kept_o[0]), x_theirs(got_o[0]))
    dn_got_x1 = over_x(dn_x1)
    acc2, dl2, sent_t = k_ffn(after(acc1, dn_x1), lowered, cotangent, pup, pdn, 1)
    got_t = over_core(sent_t)
    acc3, dl3, kept_t = k_ffn(after(acc2), lowered, cotangent, pup, pdn, 0)
    dn_x2 = add(x_theirs(kept_t[0]), x_theirs(got_t[0]))
    up_y1 = add(kept_t[1], got_t[1])
    dn_got_x2 = over_x(dn_x2)
    up_got_y = over_tensor(up_y1)
    output, dh, df, direct, da_own, da_oth, dg_own, dg_oth, de_part = k_mid_back(
        after(acc3, dn_x2, up_y1), [dl0, dl1, dl2, dl3], [acc0, acc1, acc2, acc3], cotangent, mixed, fac_h, fac_f, keep,
        g_own, g_oth, m_own, m_oth, u_h, w_gamma, w_h, w_phi, pg, pu, ph,
    )
    dn_got_x2 = held(dn_got_x2, dh)
    dn_y = add(x_mine(kept_t[0]), x_mine(got_t[0]), dn_got_x2)
    dn_got_y = over_tensor(dn_y)
    mid_sent = k_weight_mid(after(dh, dn_y), ema_low, dh, df, gated_own, gated_oth, dg_own, dg_oth, 5)
    mid_got = [over_core(v) for v in mid_sent]
    dv_own, dv_oth = k_value_back(after(*mid_sent), probs, da_own, da_oth, vs_own, vs_oth)
    up_got_y = held(up_got_y, dv_own)
    up_terms = [kept_o[1], got_o[1], up_got_y]
    up_x = add(*[x_theirs(v) for v in up_terms])
    up_got_x = over_x(up_x)
    val_sent = k_weight_value(after(dv_own, up_x), normed, dv_own, dv_oth, 5)
    val_got = [over_core(v) for v in val_sent]
    mid_own, mid_oth = k_weight_mid(
        after(*val_sent), ema_low, dh, df, gated_own, gated_oth, dg_own, dg_oth, 4, mid_got
    )
    c = mid_own.shape[1] // 2
    ma_own, ma_oth, mb_own, mb_oth = mid_own[:, :c], mid_oth[:, :c], mid_own[:, c:], mid_oth[:, c:]
    ma_x = (x_theirs(ma_own), x_theirs(ma_oth))
    ma_got_x = [over_x(v) for v in ma_x]
    mb_got_y = over_tensor(mb_oth)
    dz, stats = k_score_back(
        after(mid_own, ma_x), probs, da_own, da_oth, v_own, v_oth, query, key, z_pre, qk_gain
    )
    dn_got_y, up_got_x = held((dn_got_y, up_got_x), dz)
    ffn_terms = [
        jnp.concatenate([x_mine(a), x_mine(b)], axis=-1)
        for a, b in ((kept_o[0], kept_o[1]), (got_o[0], got_o[1]))
    ] + [
        jnp.concatenate([dn_got_x1, x_mine(up_got_y)], axis=-1),
        jnp.concatenate([dn_got_y, up_got_x], axis=-1),
    ]
    ffn_z1, ffn_terms = z_first(ffn_terms)
    ffn_got_z1 = over_z(ffn_z1)
    z_own = k_weight(after(dz, ffn_z1), ema_low, dz, lambda s: 0, dz.shape[1], dz.shape[1])
    z_got = over_core(z_own)
    val_own, val_oth = k_weight_value(after(z_own), normed, dv_own, dv_oth, 4, val_got)
    c = val_own.shape[1] // 2
    va_own, va_oth, vb_own, vb_oth = val_own[:, :c], val_oth[:, :c], val_own[:, c:], val_oth[:, c:]
    va_x = (x_theirs(va_own), x_theirs(va_oth))
    va_got_x = [over_x(v) for v in va_x]
    z_sum = add(z_own, z_got)
    vb_y = jnp.concatenate([vb_oth, z_sum], axis=1)
    vb_got_y = over_tensor(vb_y)
    quarter = blocks // 4
    eb = k_ema_backward(
        after(val_own, va_x, vb_y), normed, de_part, dz, e_slope, w_z, decay, coef, omega, 0, quarter
    )
    ma_got_x, mb_got_y = held((ma_got_x, mb_got_y), eb[1])
    ma_y = add(x_mine(ma_oth), ma_got_x[1])
    mb_x = add(x_theirs(mb_own), x_theirs(mb_got_y))
    ma_got_y = over_tensor(ma_y)
    mb_got_x = over_x(mb_x)
    eb = k_ema_backward(
        after(eb[1], ma_y, mb_x), normed, de_part, dz, e_slope, w_z, decay, coef, omega, quarter, quarter, eb
    )
    ffn_got_z1 = held(ffn_got_z1, eb[1])
    ffn_z2, ffn_terms = z_second([*ffn_terms, ffn_got_z1])
    ffn_got_z2 = over_z2(ffn_z2)
    va_got_x, vb_got_y = held((va_got_x, vb_got_y), eb[1])
    va_y = add(x_mine(va_oth), va_got_x[1])
    vb_mine = jnp.concatenate([vb_own, z_sum], axis=1)
    vb_x = add(x_theirs(vb_mine), x_theirs(vb_got_y))
    va_got_y = over_tensor(va_y)
    vb_got_x = over_x(vb_x)
    eb = k_ema_backward(
        after(eb[1], ffn_z2, va_y, vb_x), normed, de_part, dz, e_slope, w_z, decay, coef, omega, 2 * quarter, quarter, eb
    )
    ma_got_y, mb_got_x = held((ma_got_y, mb_got_x), eb[1])
    mid_terms = [
        jnp.concatenate([x_mine(ma_own), x_mine(mb_own)], axis=-1),
        jnp.concatenate([ma_got_x[0], x_mine(mb_got_y)], axis=-1),
        jnp.concatenate([ma_got_y, mb_got_x], axis=-1),
    ]
    mid_z1, mid_terms = z_first(mid_terms)
    mid_got_z1 = over_z(mid_z1)
    eb = k_ema_backward(
        after(eb[1], mid_z1), normed, de_part, dz, e_slope, w_z, decay, coef, omega, 3 * quarter, quarter, eb
    )
    d_sig, _, _, sum_a, sum_b, sum_w = eb
    va_got_y, vb_got_x = held((va_got_y, vb_got_x), sum_a)
    val_terms = [
        jnp.concatenate([x_mine(va_own), x_mine(vb_mine)], axis=-1),
        jnp.concatenate([va_got_x[0], x_mine(vb_got_y)], axis=-1),
        jnp.concatenate([va_got_y, vb_got_x], axis=-1),
    ]
    val_z1, val_terms = z_first(val_terms)
    val_got_z1 = over_z(val_z1)
    sums = jnp.concatenate([sum_a, sum_b, sum_w, stats], axis=0)
    sums_core = over_core(sums)
    input_grad = k_input_back(
        after(sum_a, val_z1), dv_own, dv_oth, w_v, pv, d_sig, tokens, direct
    )
    mid_got_z1, ffn_got_z2, val_got_z1, sums_core = held(
        (mid_got_z1, ffn_got_z2, val_got_z1, sums_core), input_grad
    )
    mid_z2, mid_terms = z_second([*mid_terms, mid_got_z1])
    mid_got_z2 = over_z2(mid_z2)
    val_z2, val_terms = z_second([*val_terms, val_got_z1])
    val_got_z2 = over_z2(val_z2)
    sums = sums + sums_core
    sums = sums + over_tensor(sums)
    sums = sums + over_x(sums)
    sums = sums + over_z(sums)
    sums = sums + over_z2(sums)

    def finish(terms):
        send, terms = core_rows(terms)
        return total(terms), over_core(send)

    ffn_kept, ffn_got = finish([*ffn_terms, ffn_got_z2])
    c = ffn_kept.shape[1] // 2
    down_t, up = joined(ffn_kept[:, :c], ffn_got[:, :c]), joined(ffn_kept[:, c:], ffn_got[:, c:])
    mid_kept, mid_got = finish([*mid_terms, mid_got_z2])
    half = gated_own.shape[1] // 2
    cuts = (0, half, 2 * half, 2 * half + d // 4, 3 * half)
    uh_t, gamma, wh_t, phi_t = (
        joined(mid_kept[:, lo:hi], mid_got[:, lo:hi]) for lo, hi in zip(cuts[:-1], cuts[1:])
    )
    val_kept, val_got = finish([*val_terms, val_got_z2])
    value = joined(val_kept[:, :half], val_got[:, :half])
    z_grad = val_kept[:, half:]
    gh = sum_a.shape[0]

    def own_half(v):
        return lax.dynamic_slice_in_dim(v, t * (d // 2), d // 2, 1).T

    tot_a = own_half(sums[:gh].reshape(H, d))
    tot_b = own_half(sums[gh : 2 * gh].reshape(H, d))
    omega_grad = lax.dynamic_slice_in_dim(sums[2 * gh : 2 * gh + d // 128].reshape(d), t * (d // 2), d // 2, 0)
    zsum = sums[2 * gh + d // 128 :]
    rate = jax.nn.sigmoid(alpha_logit)
    damp = jax.nn.sigmoid(delta_logit)
    feed = rate * ema_beta
    feed_grad = ema_eta * tot_a
    decay_grad = feed * ema_eta * tot_b
    alpha_grad = (feed_grad * ema_beta - decay_grad * damp) * rate * (1.0 - rate)
    delta_grad = -decay_grad * rate * damp * (1.0 - damp)
    return (
        output, input_grad, alpha_grad, delta_grad, feed_grad * rate, feed * tot_a, omega_grad,
        z_grad, zsum[0:2], zsum[2:4], value, gamma, uh_t.T, wh_t.T, phi_t.T, up, down_t.T,
    )


def solution(mesh):
    placed = (
        P(("dp", "tensor"), None),
        P("tensor", None),
        P("tensor", None),
        P("tensor", None),
        P("tensor", None),
        P("tensor"),
        P(),
        P(),
        P(),
        P(None, "tensor"),
        P(None, "tensor"),
        P("tensor", None),
        P("tensor", None),
        P("tensor", None),
        P(None, "tensor"),
        P("tensor", None),
        P(("dp", "tensor"), None),
    )

    def per_device(tokens, *rest):
        whole_sequence = tokens.shape[0] == LEN and dict(mesh.shape) == {"dp": 16, "tensor": 2}
        return (one_sequence if whole_sequence else shards)(tokens, *rest)

    return jax.shard_map(
        per_device,
        mesh=mesh,
        in_specs=placed,
        out_specs=(
            P(("dp", "tensor"), None),
            P(("dp", "tensor"), None),
            P("tensor", None),
            P("tensor", None),
            P("tensor", None),
            P("tensor", None),
            P("tensor"),
            P("dp", None),
            P(),
            P(),
            P("dp", "tensor"),
            P("dp", "tensor"),
            P("tensor", "dp"),
            P("tensor", "dp"),
            P("tensor", "dp"),
            P("dp", "tensor"),
            P("tensor", "dp"),
        ),
        check_vma=False,
    )
```

```python
import math

import jax
import jax.numpy as jnp
from jax import lax
from jax.experimental import pallas as pl
from jax.experimental.pallas import tpu as pltpu
from jax.sharding import PartitionSpec as P

H = 16
LEN = 1024
ATT_BLOCK = 512
EMA_BLOCK = 128


norm_eps = 1e-06
masked_value = -1e30


def rms_rows(values_in):
    return values_in * lax.rsqrt(jnp.mean(values_in * values_in, axis=-1, keepdims=True) + norm_eps)


def matmul(left, right):
    return jnp.dot(left, right, preferred_element_type=jnp.float32)


def row_inner(left, right):
    return lax.dot_general(
        left, right, (((0,), (0,)), ((), ())), preferred_element_type=jnp.float32
    )


def col_inner(left, right):
    return lax.dot_general(
        left, right, (((1,), (1,)), ((), ())), preferred_element_type=jnp.float32
    )


def silu_slope(pre_act):
    logistic = jax.nn.sigmoid(pre_act)
    return logistic * (1.0 + pre_act * (1.0 - logistic))


def gate_apply(h_pre, f_pre, x_rows):
    update = jax.nn.sigmoid(f_pre)
    return update * jax.nn.silu(h_pre) + (1.0 - update) * x_rows


def ema_apply(signal, ema_params):
    alpha_logit, delta_logit, ema_beta, ema_eta, ema_omega = ema_params
    alpha_rate = jax.nn.sigmoid(alpha_logit)
    decay_rate = 1.0 - alpha_rate * jax.nn.sigmoid(delta_logit)
    feed_rate = alpha_rate * ema_beta
    log_decay = jnp.log(decay_rate)
    total_rows, chan_count = signal.shape
    seq_count = total_rows // LEN
    block_count = LEN // EMA_BLOCK
    blocks = signal.reshape(seq_count, block_count, EMA_BLOCK, chan_count)
    steps_in = jnp.arange(EMA_BLOCK, dtype=jnp.float32)
    lag_power = jnp.exp(steps_in[:, None, None] * log_decay[None])
    kernel = jnp.sum(lag_power * (feed_rate * ema_eta)[None], axis=-1)
    offsets = steps_in[:, None] - steps_in[None, :]
    lag_index = jnp.clip(offsets, 0, EMA_BLOCK - 1).astype(jnp.int32)
    toeplitz = jnp.where((offsets >= 0)[:, :, None], kernel[lag_index], 0.0)
    local_part = jnp.einsum("ijc,snjc->snic", toeplitz, blocks)
    tail_power = lag_power[::-1] * feed_rate[None]
    block_state = jnp.einsum("jch,snjc->snch", tail_power, blocks)
    full_decay = jnp.exp(EMA_BLOCK * log_decay)

    def carry_step(state_in, incoming):
        return (full_decay * state_in + incoming, state_in)

    zero_state = jnp.zeros((seq_count, chan_count, H), jnp.float32)
    _, start_state = lax.scan(carry_step, zero_state, jnp.moveaxis(block_state, 1, 0))
    start_state = jnp.moveaxis(start_state, 0, 1)
    head_power = lag_power * decay_rate[None] * ema_eta[None]
    carried = jnp.einsum("ich,snch->snic", head_power, start_state)
    ema_pre = (local_part + carried).reshape(total_rows, chan_count) + ema_omega * signal
    return jax.nn.silu(ema_pre)


def masked_scores(q_rows, k_rows, first_row):
    raw_scores = col_inner(q_rows, k_rows) * q_rows.shape[1] ** (-0.5)
    row_pos = first_row + jnp.arange(q_rows.shape[0])[:, None]
    col_pos = jnp.arange(k_rows.shape[0])[None, :]
    return jnp.where(col_pos <= row_pos, raw_scores, masked_value)


def attend_forward(query_low, key_low, value_low):
    total_rows, value_width = value_low.shape
    seq_count = total_rows // LEN
    per_seq = LEN // ATT_BLOCK

    def attend_one_block(flat_index):
        seq_id = flat_index // per_seq
        blk_id = flat_index % per_seq
        seq_start = seq_id * LEN
        q_rows = lax.dynamic_slice_in_dim(query_low, seq_start + blk_id * ATT_BLOCK, ATT_BLOCK, 0)
        k_rows = lax.dynamic_slice_in_dim(key_low, seq_start, LEN, 0)
        v_rows = lax.dynamic_slice_in_dim(value_low, seq_start, LEN, 0)
        scores = masked_scores(q_rows, k_rows, blk_id * ATT_BLOCK)
        top_score = jnp.max(scores, axis=-1, keepdims=True)
        weights = jnp.exp(scores - top_score)
        total_weight = jnp.sum(weights, axis=-1, keepdims=True)
        probs = (weights / total_weight).astype(jnp.bfloat16)
        return (matmul(probs, v_rows), top_score[:, 0] + jnp.log(total_weight[:, 0]))

    outs, lse_all = lax.map(attend_one_block, jnp.arange(seq_count * per_seq))
    return (outs.reshape(total_rows, value_width), lse_all.reshape(total_rows))


def attend_backward(query_low, key_low, value_low, lse_rows, d_att):
    total_rows, value_width = value_low.shape
    head_width = query_low.shape[1]
    seq_count = total_rows // LEN
    per_seq = LEN // ATT_BLOCK
    scale = head_width ** (-0.5)

    def one_seq(seq_id):
        seq_start = seq_id * LEN
        k_rows = lax.dynamic_slice_in_dim(key_low, seq_start, LEN, 0)
        v_rows = lax.dynamic_slice_in_dim(value_low, seq_start, LEN, 0)

        def one_one_block(carry_in, blk_id):
            d_keys, d_vals = carry_in
            row_start = seq_start + blk_id * ATT_BLOCK
            q_rows = lax.dynamic_slice_in_dim(query_low, row_start, ATT_BLOCK, 0)
            g_rows = lax.dynamic_slice_in_dim(d_att, row_start, ATT_BLOCK, 0)
            lse_part = lax.dynamic_slice_in_dim(lse_rows, row_start, ATT_BLOCK, 0)
            probs = jnp.exp(masked_scores(q_rows, k_rows, blk_id * ATT_BLOCK) - lse_part[:, None])
            d_probs = col_inner(g_rows, v_rows)
            d_scores = (
                probs * (d_probs - jnp.sum(probs * d_probs, axis=-1, keepdims=True))
            ).astype(jnp.bfloat16)
            d_rows = matmul(d_scores, k_rows) * scale
            d_keys = d_keys + row_inner(d_scores, q_rows) * scale
            d_vals = d_vals + row_inner(probs.astype(jnp.bfloat16), g_rows)
            return ((d_keys, d_vals), d_rows)

        start_carry = (
            jnp.zeros((LEN, head_width), jnp.float32),
            jnp.zeros((LEN, value_width), jnp.float32),
        )
        (d_keys, d_vals), d_rows = lax.scan(one_one_block, start_carry, jnp.arange(per_seq))
        return (d_rows.reshape(LEN, head_width), d_keys, d_vals)

    d_query, d_key, d_value = lax.map(one_seq, jnp.arange(seq_count))
    return (
        d_query.reshape(total_rows, head_width),
        d_key.reshape(total_rows, head_width),
        d_value.reshape(total_rows, value_width),
    )


def shards(
    tokens,
    alpha_logit,
    delta_logit,
    ema_beta,
    ema_eta,
    ema_omega,
    w_z,
    qk_gain,
    qk_bias,
    w_v,
    w_gamma,
    u_h,
    w_h,
    w_phi,
    w_up,
    w_down,
    cotangent,
):
    tensor_pos = lax.axis_index("tensor")
    feature_count = tokens.shape[1]
    chan_count = ema_omega.shape[0]
    chan_start = tensor_pos * chan_count
    x_rows = tokens.astype(jnp.float32)
    normed_rows, norm_pull = jax.vjp(rms_rows, x_rows)
    normed, cot_full = (
        lax.all_gather(normed_rows.astype(jnp.bfloat16), "tensor", axis=0, tiled=True),
        lax.all_gather(cotangent, "tensor", axis=0, tiled=True),
    )
    signal = lax.dynamic_slice_in_dim(normed, chan_start, chan_count, 1).astype(jnp.float32)
    ema_params = (alpha_logit, delta_logit, ema_beta, ema_eta, ema_omega)
    ema_val, ema_pull = jax.vjp(ema_apply, signal, ema_params)
    ema_low = ema_val.astype(jnp.bfloat16)
    ema_full = lax.all_gather(ema_low, "tensor", axis=1, tiled=True)
    z_pre = matmul(ema_full, w_z)
    z_act = jax.nn.silu(z_pre)
    query_low = (z_act * qk_gain[0] + qk_bias[0]).astype(jnp.bfloat16)
    key_low = (z_act * qk_gain[1] + qk_bias[1]).astype(jnp.bfloat16)
    values_pre = matmul(normed, w_v)
    value_low = jax.nn.silu(values_pre).astype(jnp.bfloat16)
    gamma_pre = matmul(ema_full, w_gamma)
    gamma_act = jax.nn.silu(gamma_pre)
    attended, lse_rows = attend_forward(query_low, key_low, value_low)
    gated_low = (gamma_act * attended).astype(jnp.bfloat16)
    both_pre = lax.psum_scatter(
        jnp.concatenate(
            [matmul(gated_low, u_h) + matmul(ema_low, w_h), matmul(ema_low, w_phi)], axis=1
        ),
        "tensor",
        scatter_dimension=0,
        tiled=True,
    )
    h_pre = both_pre[:, :feature_count]
    f_pre = both_pre[:, feature_count:]
    mixed, gate_pull = jax.vjp(gate_apply, h_pre, f_pre, x_rows)
    normed_two, norm_two_pull = jax.vjp(rms_rows, mixed)
    lowered = lax.all_gather(normed_two.astype(jnp.bfloat16), "tensor", axis=0, tiled=True)
    up_pre = matmul(lowered, w_up)
    hidden = jax.nn.silu(up_pre).astype(jnp.bfloat16)
    down_rows = lax.psum_scatter(
        matmul(hidden, w_down).astype(jnp.bfloat16), "tensor", scatter_dimension=0, tiled=True
    ).astype(jnp.float32)
    output = (mixed + down_rows).astype(jnp.bfloat16)
    cot_rows = cotangent.astype(jnp.float32)
    d_hidden = col_inner(cot_full, w_down)
    d_up = (d_hidden * silu_slope(up_pre)).astype(jnp.bfloat16)
    down_grad = row_inner(hidden, cot_full)
    up_grad = row_inner(lowered, d_up)
    d_lowered = lax.psum_scatter(col_inner(d_up, w_up), "tensor", scatter_dimension=0, tiled=True)
    d_mixed = cot_rows + norm_two_pull(d_lowered)[0]
    d_hpre, d_fpre, d_direct = gate_pull(d_mixed)
    h_full_grad, f_full_grad = (
        lax.all_gather(d_hpre.astype(jnp.bfloat16), "tensor", axis=0, tiled=True),
        lax.all_gather(d_fpre.astype(jnp.bfloat16), "tensor", axis=0, tiled=True),
    )
    uh_grad = row_inner(gated_low, h_full_grad)
    wh_grad = row_inner(ema_low, h_full_grad)
    phi_grad = row_inner(ema_low, f_full_grad)
    d_gated = col_inner(h_full_grad, u_h)
    d_att = (d_gated * gamma_act).astype(jnp.bfloat16)
    d_gamma = (d_gated * attended * silu_slope(gamma_pre)).astype(jnp.bfloat16)
    d_query, d_key, d_value = attend_backward(query_low, key_low, value_low, lse_rows, d_att)
    d_query, d_key = lax.psum((d_query, d_key), "tensor")
    d_z = (silu_slope(z_pre) * (d_query * qk_gain[0] + d_key * qk_gain[1])).astype(jnp.bfloat16)
    gain_grad = jnp.stack([jnp.sum(d_query * z_act, axis=0), jnp.sum(d_key * z_act, axis=0)])
    bias_grad = jnp.stack([jnp.sum(d_query, axis=0), jnp.sum(d_key, axis=0)])
    z_grad = row_inner(ema_full, d_z)
    gamma_grad = row_inner(ema_full, d_gamma)
    d_value_pre = (d_value * silu_slope(values_pre)).astype(jnp.bfloat16)
    value_grad = row_inner(normed, d_value_pre)
    d_chan = lax.psum_scatter(
        col_inner(d_gamma, w_gamma).astype(jnp.bfloat16), "tensor", scatter_dimension=1, tiled=True
    ).astype(jnp.float32)
    z_rows = lax.dynamic_slice_in_dim(w_z, chan_start, chan_count, 0)
    d_chan = (
        d_chan
        + col_inner(d_z, z_rows)
        + col_inner(h_full_grad, w_h)
        + col_inner(f_full_grad, w_phi)
    )
    d_signal, d_params = ema_pull(d_chan)
    d_norm_part = col_inner(d_value_pre, w_v)
    own_cols = lax.dynamic_slice_in_dim(d_norm_part, chan_start, chan_count, 1)
    d_norm_part = lax.dynamic_update_slice_in_dim(d_norm_part, own_cols + d_signal, chan_start, 1)
    d_normed = lax.psum_scatter(
        d_norm_part.astype(jnp.bfloat16), "tensor", scatter_dimension=0, tiled=True
    ).astype(jnp.float32)
    input_grad = d_direct + norm_pull(d_normed)[0]
    weight_totals = (
        lax.psum_scatter(z_grad.astype(jnp.bfloat16), "dp", scatter_dimension=0, tiled=True).astype(
            jnp.float32
        ),
        lax.psum_scatter(
            value_grad.astype(jnp.bfloat16), "dp", scatter_dimension=0, tiled=True
        ).astype(jnp.float32),
        lax.psum_scatter(
            gamma_grad.astype(jnp.bfloat16), "dp", scatter_dimension=0, tiled=True
        ).astype(jnp.float32),
        lax.psum_scatter(
            uh_grad.astype(jnp.bfloat16), "dp", scatter_dimension=1, tiled=True
        ).astype(jnp.float32),
        lax.psum_scatter(
            wh_grad.astype(jnp.bfloat16), "dp", scatter_dimension=1, tiled=True
        ).astype(jnp.float32),
        lax.psum_scatter(
            phi_grad.astype(jnp.bfloat16), "dp", scatter_dimension=1, tiled=True
        ).astype(jnp.float32),
        lax.psum_scatter(
            up_grad.astype(jnp.bfloat16), "dp", scatter_dimension=0, tiled=True
        ).astype(jnp.float32),
        lax.psum_scatter(
            down_grad.astype(jnp.bfloat16), "dp", scatter_dimension=1, tiled=True
        ).astype(jnp.float32),
    )
    param_totals = lax.psum(
        (d_params[0], d_params[1], d_params[2], d_params[3], d_params[4], gain_grad, bias_grad),
        "dp",
    )
    return (
        output,
        input_grad,
        param_totals[0],
        param_totals[1],
        param_totals[2],
        param_totals[3],
        param_totals[4],
        weight_totals[0],
        param_totals[5],
        param_totals[6],
        weight_totals[1],
        weight_totals[2],
        weight_totals[3],
        weight_totals[4],
        weight_totals[5],
        weight_totals[6],
        weight_totals[7],
    )


CP = pltpu.CompilerParams(vmem_limit_bytes=56 * 1024 * 1024)
BF = jnp.bfloat16
F32 = jnp.float32
ROWS = 256
hint = 10


def sds(shape, dtype=BF):
    return jax.ShapeDtypeStruct(shape, dtype)


def whole(shape):
    return pl.BlockSpec(shape, lambda i, s: (0,) * len(shape), pipeline_mode=pl.Buffered(1))


def rows_of(cols, rows=ROWS):
    return pl.BlockSpec((rows, cols), lambda i, s: (i, 0))


def cols_of(rows, cols):
    return pl.BlockSpec((rows, cols), lambda i, s: (0, i))


def run(body, grid, scal, ins, in_specs, out_shape, out_specs, scratch=(), flops=0, name=None, aliases=None):
    moved = sum(a.size * a.dtype.itemsize for a in ins)
    moved += sum(math.prod(o.shape) * jnp.dtype(o.dtype).itemsize for o in out_shape)
    return pl.pallas_call(
        body,
        out_shape=out_shape,
        grid_spec=pltpu.PrefetchScalarGridSpec(
            num_scalar_prefetch=1,
            grid=grid,
            in_specs=in_specs,
            out_specs=out_specs,
            scratch_shapes=list(scratch),
        ),
        compiler_params=CP,
        cost_estimate=pl.CostEstimate(flops=int(flops * hint), bytes_accessed=int(moved * hint), transcendentals=0),
        name=name,
        input_output_aliases=aliases or {},
    )(scal, *ins)


def sig(u):
    return 0.5 + 0.5 * jnp.tanh(0.5 * u)


def silu_pair(u):
    s = sig(u)
    return u * s, s * (1.0 + u * (1.0 - s))


def place(scr, s, pieces, base=0, table=0):
    rows = pieces[0].shape[0]
    for p in range(4):
        scr[pl.ds(pl.multiple_of(base + s[table + p] * rows, rows), rows), :] = pieces[p][...]


def piece_block(rows, cols, row_block):
    return pl.BlockSpec((rows, cols), lambda i, s: (row_block, i))


def piece_whole(rows, cols, row_block):
    return pl.BlockSpec((rows, cols), lambda i, s: (row_block, 0), pipeline_mode=pl.Buffered(1))


def k_value_own(scal, tokens, w_own):
    n, d = tokens.shape
    cols = w_own.shape[1]
    tn = 512

    def body(s, x_ref, w_ref, n_ref, v_ref, sl_ref):
        @pl.when(pl.program_id(0) == 0)
        def _():
            x = x_ref[...].astype(F32)
            n_ref[...] = (x * lax.rsqrt(jnp.mean(x * x, axis=-1, keepdims=True) + norm_eps)).astype(BF)

        act, slope = silu_pair(matmul(n_ref[...], w_ref[...]))
        v_ref[...] = act.astype(BF)
        sl_ref[...] = slope.astype(BF)

    return run(
        body, (cols // tn,), scal, [tokens, w_own],
        [whole((n, d)), cols_of(d, tn)],
        [sds((n, d)), sds((n, cols)), sds((n, cols))],
        [pl.BlockSpec((n, d), lambda i, s: (0, 0)), cols_of(n, tn), cols_of(n, tn)],
        flops=2 * n * d * cols, name="value_own",
    )


def k_act_own(scal, x, w_own, tn):
    n, d = x.shape
    cols = w_own.shape[1]

    def body(s, x_ref, w_ref, v_ref, sl_ref):
        act, slope = silu_pair(matmul(x_ref[...], w_ref[...]))
        v_ref[...] = act.astype(BF)
        sl_ref[...] = slope.astype(BF)

    return run(
        body, (cols // tn,), scal, [x, w_own],
        [whole((n, d)), cols_of(d, tn)],
        [sds((n, cols)), sds((n, cols))],
        [cols_of(n, tn), cols_of(n, tn)],
        flops=2 * n * d * cols, name="act_own",
    )


def k_act_other(scal, x, pieces, table, tn):
    n, d = x.shape
    rows, cols = pieces[0].shape

    def body(s, x_ref, p0, p1, p2, p3, v_ref, sl_ref, w_scr):
        place(w_scr, s, (p0, p1, p2, p3), table=table)
        act, slope = silu_pair(matmul(x_ref[...], w_scr[...]))
        v_ref[...] = act.astype(BF)
        sl_ref[...] = slope.astype(BF)

    return run(
        body, (cols // tn,), scal, [x, *pieces],
        [whole((n, d))] + [piece_block(rows, tn, 0)] * 4,
        [sds((n, cols)), sds((n, cols))],
        [cols_of(n, tn), cols_of(n, tn)],
        [pltpu.VMEM((d, tn), BF)],
        flops=2 * n * d * cols, name="act_other",
    )


def k_query_key(scal, ema_low, w_z, qk_gain, qk_bias):
    n, d = ema_low.shape
    zw = w_z.shape[1]

    def body(s, e_ref, w_ref, g_ref, b_ref, z_ref, q_ref, k_ref):
        z_pre = matmul(e_ref[...], w_ref[...])
        z_ref[...] = z_pre
        act = z_pre * sig(z_pre)
        q_ref[...] = (act * g_ref[0:1, :] + b_ref[0:1, :]).astype(BF)
        k_ref[...] = (act * g_ref[1:2, :] + b_ref[1:2, :]).astype(BF)

    return run(
        body, (2,), scal, [ema_low, w_z, qk_gain, qk_bias],
        [rows_of(d, n // 2), whole((d, zw)), whole((2, zw)), whole((2, zw))],
        [sds((n, zw), F32), sds((n, zw)), sds((n, zw))],
        [rows_of(zw, n // 2)] * 3,
        flops=2 * n * d * zw, name="query_key",
    )


def k_ema_params(scal, own, oth):
    ch, width = own.shape
    groups = 2 * ch // 128

    def body(s, own_ref, oth_ref, dec_ref, cf_ref, om_ref, scr):
        scr[pl.ds(pl.multiple_of(s[6] * ch, ch), ch), :] = own_ref[...]
        scr[pl.ds(pl.multiple_of(s[7] * ch, ch), ch), :] = oth_ref[...]
        v = scr[...].T
        rate = sig(v[0:H])
        dec = 1.0 - rate * sig(v[H : 2 * H])
        cf = rate * v[2 * H : 3 * H] * v[3 * H : 4 * H]
        for g in range(groups):
            lanes = slice(g * 128, (g + 1) * 128)
            dec_ref[pl.ds(g, H, stride=groups), :] = dec[:, lanes]
            cf_ref[pl.ds(g, H, stride=groups), :] = cf[:, lanes]
            om_ref[g : g + 1, :] = v[4 * H : 4 * H + 1, lanes]

    par = (H * groups, 128)
    return run(
        body, (1,), scal, [own, oth], [whole((ch, width))] * 2,
        [sds(par, F32), sds(par, F32), sds((groups, 128), F32)],
        [pl.BlockSpec(par, lambda i, s: (0, 0))] * 2 + [pl.BlockSpec((groups, 128), lambda i, s: (0, 0))],
        [pltpu.VMEM((2 * ch, width), F32)], flops=1e8, name="ema_params",
    )


def k_ema_forward(scal, normed, decay, coef, omega, first, count, before=None):
    n, d = normed.shape
    groups = d // 128
    tb = 128

    def body(s, x_ref, dec_ref, cf_ref, om_ref, *refs):
        e_ref, sl_ref, st, xs, ys = refs[-5:]

        @pl.when(pl.program_id(0) == 0)
        def _():
            st[...] = refs[0][...] if before else jnp.zeros_like(st)

        for g in range(groups):
            xs[pl.ds(g, tb, stride=groups), :] = x_ref[:, g * 128 : (g + 1) * 128].astype(F32)
        dec = [dec_ref[k * groups : (k + 1) * groups, :] for k in range(H)]
        cf = [cf_ref[k * groups : (k + 1) * groups, :] for k in range(H)]
        om = om_ref[...]

        def steps(b, carry):
            states = list(carry)
            for u in range(16):
                row = pl.multiple_of((b * 16 + u) * groups, groups)
                xt = xs[pl.ds(row, groups), :]
                parts = [om * xt, None, None, None]
                for k in range(H):
                    states[k] = dec[k] * states[k] + xt
                    term = cf[k] * states[k]
                    parts[k % 4] = term if parts[k % 4] is None else parts[k % 4] + term
                ys[pl.ds(row, groups), :] = (parts[0] + parts[1]) + (parts[2] + parts[3])
            return tuple(states)

        start = tuple(st[k * groups : (k + 1) * groups, :] for k in range(H))
        end = lax.fori_loop(0, tb // 16, steps, start)
        for k in range(H):
            st[k * groups : (k + 1) * groups, :] = end[k]
        for g in range(groups):
            act, slope = silu_pair(ys[pl.ds(g, tb, stride=groups), :])
            e_ref[:, g * 128 : (g + 1) * 128] = act.astype(BF)
            sl_ref[:, g * 128 : (g + 1) * 128] = slope.astype(BF)

    par = (H * groups, 128)
    at = pl.BlockSpec((tb, d), lambda i, s: (first + i, 0))
    more = list(before) if before else []
    return run(
        body, (count,), scal, [normed, decay, coef, omega, *more],
        [at, whole(par), whole(par), whole((groups, 128))]
        + ([whole(par), pl.BlockSpec(memory_space=pl.ANY), pl.BlockSpec(memory_space=pl.ANY)] if before else []),
        [sds((n, d)), sds((n, d)), sds(par, F32)],
        [at, at, pl.BlockSpec(par, lambda i, s: (0, 0))],
        [pltpu.VMEM((tb * groups, 128), F32), pltpu.VMEM((tb * groups, 128), F32)],
        flops=2.5e9 * count, name="ema_forward", aliases={6: 0, 7: 1} if before else {},
    )


def k_ema_backward(scal, normed, de_part, dz, slope, w_z, decay, coef, omega, first, count, before=None):
    n, d = normed.shape
    groups = d // 128
    tb = 128
    nb = n // tb
    half = H // 2
    gh = groups * half
    zw = dz.shape[1]

    def body(s, x_ref, de_ref, z_ref, sl_ref, wz_ref, dec_ref, cf_ref, om_ref, *refs):
        o_ref, back, deriv, a_ref, b_ref, w_ref, xs, gs, ys = refs[-9:]

        @pl.when(pl.program_id(0) == 0)
        def _():
            for i, ref in enumerate((back, deriv, a_ref, b_ref, w_ref)):
                ref[...] = refs[i][...] if before else jnp.zeros_like(ref)

        d_e = (de_ref[...].astype(F32) + col_inner(z_ref[...], wz_ref[...])) * sl_ref[...].astype(F32)
        for g in range(groups):
            xs[pl.ds(g, tb, stride=groups), :] = x_ref[:, g * 128 : (g + 1) * 128].astype(F32)
            gs[pl.ds(g, tb, stride=groups), :] = d_e[:, g * 128 : (g + 1) * 128]

        for part in range(2):
            low = part * gh
            at = [slice(low + k * groups, low + (k + 1) * groups) for k in range(half)]
            dec = [dec_ref[a, :] for a in at]

            def steps(b, carry, part=part, at=at, dec=dec):
                bk, dv, aa, bb, ww = (list(c) for c in carry)
                for u in range(8):
                    row = pl.multiple_of((tb - 1 - (b * 8 + u)) * groups, groups)
                    xt = xs[pl.ds(row, groups), :]
                    gt = gs[pl.ds(row, groups), :]
                    if part == 0:
                        outs = [om_ref[...] * gt, None]
                        ww[0] = ww[0] + xt * gt
                    else:
                        outs = [ys[pl.ds(row, groups), :], None]
                    for k in range(half):
                        dv[k] = dec[k] * dv[k] + bk[k]
                        bk[k] = dec[k] * bk[k] + gt
                        term = cf_ref[at[k], :] * bk[k]
                        outs[k % 2] = term if outs[k % 2] is None else outs[k % 2] + term
                        aa[k] = aa[k] + xt * bk[k]
                        bb[k] = bb[k] + xt * dv[k]
                    ys[pl.ds(row, groups), :] = outs[0] + outs[1]
                return tuple(bk), tuple(dv), tuple(aa), tuple(bb), tuple(ww)

            start = (
                tuple(back[a, :] for a in at),
                tuple(deriv[a, :] for a in at),
                tuple(a_ref[a, :] for a in at),
                tuple(b_ref[a, :] for a in at),
                (w_ref[...],),
            )
            bk, dv, aa, bb, ww = lax.fori_loop(0, tb // 8, steps, start)
            for k in range(half):
                back[at[k], :] = bk[k]
                deriv[at[k], :] = dv[k]
                a_ref[at[k], :] = aa[k]
                b_ref[at[k], :] = bb[k]
            w_ref[...] = ww[0]
        for g in range(groups):
            o_ref[:, g * 128 : (g + 1) * 128] = ys[pl.ds(g, tb, stride=groups), :]

    top = nb - 1 - first
    back_rows = pl.BlockSpec((tb, d), lambda i, s: (top - i, 0))
    par = (H * groups, 128)
    const = pl.BlockSpec(par, lambda i, s: (0, 0))
    small = (groups, 128)
    more = [*before[1:], before[0]] if before else []
    return run(
        body, (count,), scal, [normed, de_part, dz, slope, w_z, decay, coef, omega, *more],
        [back_rows, back_rows, pl.BlockSpec((tb, zw), lambda i, s: (top - i, 0)), back_rows, whole((d, zw)),
         whole(par), whole(par), whole(small)]
        + ([whole(par)] * 4 + [whole(small), pl.BlockSpec(memory_space=pl.ANY)] if before else []),
        [sds((n, d), F32)] + [sds(par, F32)] * 4 + [sds(small, F32)],
        [back_rows, const, const, const, const, pl.BlockSpec(small, lambda i, s: (0, 0))],
        [pltpu.VMEM((tb * groups, 128), F32)] * 3,
        flops=5e9 * count, name="ema_backward", aliases={14: 0} if before else {},
    )


def k_attend(scal, q, k, v_own, v_oth, ema_low, g_own, packs):
    n, zw = q.shape
    d, half = g_own.shape
    rp = packs[0].shape[0]
    blocks = n // ROWS
    scale = zw ** (-0.5)

    def body(s, q_ref, k_ref, vo, vt, e_ref, wo, w0, w1, w2, w3, gated_o, gated_t, go, gt, mo, mt, p_ref, w_scr):
        @pl.when(pl.program_id(0) == 0)
        def _():
            place(w_scr, s, (w0, w1, w2, w3), table=8)

        for i in range(blocks):

            @pl.when(pl.program_id(0) == i)
            def _(i=i):
                seen = (i + 1) * ROWS
                sc = col_inner(q_ref[...], k_ref[0:seen, :]) * scale
                row = i * ROWS + lax.broadcasted_iota(jnp.int32, (ROWS, seen), 0)
                col = lax.broadcasted_iota(jnp.int32, (ROWS, seen), 1)
                sc = jnp.where(col <= row, sc, masked_value)
                e = jnp.exp(sc - jnp.max(sc, axis=-1, keepdims=True))
                p = (e * (1.0 / jnp.sum(e, axis=-1, keepdims=True))).astype(BF)
                p_ref[:, 0:seen] = p
                if seen < n:
                    p_ref[:, seen:] = jnp.zeros((ROWS, n - seen), BF)
                for v_ref, w, gated, g, m in ((vo, wo, gated_o, go, mo), (vt, w_scr, gated_t, gt, mt)):
                    act, slope = silu_pair(matmul(e_ref[...], w[...]))
                    att = matmul(p, v_ref[0:seen, :])
                    gated[...] = (act * att).astype(BF)
                    g[...] = act.astype(BF)
                    m[...] = (slope * att).astype(BF)

    return run(
        body, (blocks,), scal, [q, k, v_own, v_oth, ema_low, g_own, *packs],
        [rows_of(zw), whole((n, zw)), whole((n, half)), whole((n, half)), rows_of(d), whole((d, half))]
        + [whole((rp, half))] * 4,
        [sds((n, half))] * 6 + [sds((n, n))],
        [rows_of(half)] * 6 + [rows_of(n)],
        [pltpu.VMEM((d, half), BF)],
        flops=n * n * (zw + 2 * half) * 1.25 + 4 * n * d * half, name="attend",
    )


def k_gate(scal, gated_own, gated_oth, ema_low, tokens, u_own, h_own, f_own, packs_u, packs_h):
    n, d = tokens.shape
    half = u_own.shape[0]
    ch = h_own.shape[0]
    ru, rh = packs_u[0].shape[0], packs_h[0].shape[0] // 2

    def body(s, go, gt, e_ref, x_ref, uo, ho, fo, u0, u1, u2, u3, h0, h1, h2, h3, f0, f1, f2, f3,
             mix_ref, low_ref, a_ref, b_ref, up_ref, u_scr, h_scr, f_scr):
        @pl.when(pl.program_id(0) == 0)
        def _():
            place(u_scr, s, (u0, u1, u2, u3))
            own = pl.multiple_of(s[6] * ch, ch)
            oth = s[7] * ch
            h_scr[pl.ds(own, ch), :] = ho[...]
            f_scr[pl.ds(own, ch), :] = fo[...]
            place(h_scr, s, (h0, h1, h2, h3), oth, 8)
            place(f_scr, s, (f0, f1, f2, f3), oth, 8)

        h_pre = matmul(go[...], uo[...]) + matmul(gt[...], u_scr[...]) + matmul(e_ref[...], h_scr[...])
        f_pre = matmul(e_ref[...], f_scr[...])
        x = x_ref[...].astype(F32)
        act, slope = silu_pair(h_pre)
        update = sig(f_pre)
        mixed = update * act + (1.0 - update) * x
        mix_ref[...] = mixed.astype(BF)
        low_ref[...] = (mixed * lax.rsqrt(jnp.mean(mixed * mixed, axis=-1, keepdims=True) + norm_eps)).astype(BF)
        a_ref[...] = (update * slope).astype(BF)
        b_ref[...] = ((act - x) * update * (1.0 - update)).astype(BF)
        up_ref[...] = (1.0 - update).astype(BF)

    ins = [gated_own, gated_oth, ema_low, tokens, u_own, h_own, f_own, *packs_u, *packs_h, *packs_h]
    specs = [rows_of(half), rows_of(half), rows_of(d), rows_of(d), whole((half, d)), whole((ch, d)), whole((ch, d))]
    specs += [piece_whole(ru, d, 0)] * 4 + [piece_whole(rh, d, 0)] * 4 + [piece_whole(rh, d, 1)] * 4
    return run(
        body, (n // ROWS,), scal, ins, specs,
        [sds((n, d))] * 5,
        [rows_of(d)] * 5,
        [pltpu.VMEM((half, d), BF), pltpu.VMEM((2 * ch, d), BF), pltpu.VMEM((2 * ch, d), BF)],
        flops=2 * n * d * (2 * half + 4 * ch), name="gate",
    )


def k_ffn(scal, lowered, cot, up, down, part, before=None):
    n, d = lowered.shape
    pieces = len(up) > 1
    tn = up[0].shape[1] // 4
    rows = d // 2

    def body(s, low_ref, c_ref, *refs):
        step = pl.program_id(0)
        nu, nd = len(up), len(down)
        ups, downs, refs = refs[:nu], refs[nu : nu + nd], refs[nu + nd :]
        if before:
            ins, refs = refs[:2], refs[2:]
            held, sems = refs[-2:]
            refs = refs[:-2]
            copies = [pltpu.make_async_copy(ins[i], held.at[i], sems.at[i]) for i in range(2)]
        out_ref, gl_ref, dn, up_ref, acc, gl, u_scr = refs
        if pieces:
            place(u_scr, s, ups)
            wu = u_scr
        else:
            wu = ups[0]

        def split(ref, grad):
            by_x = grad.reshape(4, 2, d // 8, tn)
            flip = s[12] == 0
            a, b = by_x[:, 0].reshape(rows, tn), by_x[:, 1].reshape(rows, tn)
            ref[0] = jnp.where(flip, a, b).astype(BF)
            ref[1] = jnp.where(flip, b, a).astype(BF)

        def work(wd, i):
            if before and i == 0:
                for c in copies:
                    c.start()
            act, slope = silu_pair(matmul(low_ref[...], wu[...]))
            hid = act.astype(BF)
            out = matmul(hid, wd[...])
            du = (col_inner(c_ref[...], wd[...]) * slope).astype(BF)
            back = col_inner(du, wu[...])
            if i == 0:
                acc[...] = out
                gl[...] = back
            else:
                if before:
                    for c in copies:
                        c.wait()
                    out = out + held[0].astype(F32)
                    back = back + held[1].astype(F32)
                out_ref[...] = (acc[...] + out).astype(BF)
                gl_ref[...] = (gl[...] + back).astype(BF)
            split(dn, row_inner(c_ref[...], hid))
            split(up_ref, row_inner(low_ref[...], du))

        for i in range(2):

            @pl.when(step == i)
            def _(i=i):
                work(downs[i % nd], i)

    first = 8 + 2 * part
    if pieces:
        down = down[2 * part : 2 * part + 2]
        specs = [pl.BlockSpec((d // 4, tn), lambda i, s: (0, s[first + i]))] * 4 + [whole((tn, d))] * 2
    else:
        specs = [
            pl.BlockSpec((d, tn), lambda i, s: (0, s[first + i])),
            pl.BlockSpec((tn, d), lambda i, s: (s[first + i], 0)),
        ]
    still = pl.BlockSpec((n, d), lambda i, s: (0, 0))
    grads = pl.BlockSpec((2, rows, tn), lambda i, s: (0, 0, s[first + i] % 2))
    more = list(before) if before else []
    return run(
        body, (2,), scal, [lowered, cot, *up, *down, *more],
        [whole((n, d)), whole((n, d))] + specs + [pl.BlockSpec(memory_space=pl.ANY)] * len(more),
        [sds((n, d)), sds((n, d)), sds((2, rows, 2 * tn)), sds((2, rows, 2 * tn))],
        [still, still, grads, grads],
        [pltpu.VMEM((n, d), F32), pltpu.VMEM((n, d), F32), pltpu.VMEM((d, tn), BF)]
        + ([pltpu.VMEM((2, n, d), BF), pltpu.SemaphoreType.DMA((2,))] if before else []),
        flops=24 * n * d * tn, name="ffn",
    )


def k_mid_back(scal, dl, acc, cot, mixed, fac_h, fac_f, keep, g_own, g_oth, m_own, m_oth,
               u_own, wg_own, h_own, f_own, packs_g, packs_u, packs_h):
    n, d = cot.shape
    half = u_own.shape[0]
    ch = h_own.shape[0]
    ru, rh = packs_u[0].shape[0], packs_h[0].shape[0] // 2
    rg = packs_g[0].shape[0]

    def body(s, l_ref, acc_ref, c_ref, x_ref, a_ref, b_ref, k_ref, go, gt, mo, mt, uo, wo, ho, fo,
             w0, w1, w2, w3, u0, u1, u2, u3, h0, h1, h2, h3, f0, f1, f2, f3,
             out_ref, dh_ref, df_ref, dir_ref, ao, at, do, dt, de_ref, u_scr, w_scr, h_scr, f_scr):
        @pl.when(pl.program_id(0) == 0)
        def _():
            place(u_scr, s, (u0, u1, u2, u3))
            place(w_scr, s, (w0, w1, w2, w3), table=8)
            own = pl.multiple_of(s[6] * ch, ch)
            oth = s[7] * ch
            h_scr[pl.ds(own, ch), :] = ho[...]
            f_scr[pl.ds(own, ch), :] = fo[...]
            place(h_scr, s, (h0, h1, h2, h3), oth, 8)
            place(f_scr, s, (f0, f1, f2, f3), oth, 8)

        dl = l_ref[...].astype(F32)
        m = x_ref[...].astype(F32)
        out_ref[...] = (m + acc_ref[...].astype(F32)).astype(BF)
        r = lax.rsqrt(jnp.mean(m * m, axis=-1, keepdims=True) + norm_eps)
        n2 = m * r
        dm = c_ref[...].astype(F32) + r * (dl - n2 * jnp.mean(dl * n2, axis=-1, keepdims=True))
        dh = (dm * a_ref[...].astype(F32)).astype(BF)
        df = (dm * b_ref[...].astype(F32)).astype(BF)
        dh_ref[...] = dh
        df_ref[...] = df
        dir_ref[...] = (dm * k_ref[...].astype(F32)).astype(BF)
        de = col_inner(dh, h_scr[...]) + col_inner(df, f_scr[...])
        for u, w, g_ref, m_ref, a_out, d_out in ((uo, wo, go, mo, ao, do), (u_scr, w_scr, gt, mt, at, dt)):
            dg = col_inner(dh, u[...])
            a_out[...] = (dg * g_ref[...].astype(F32)).astype(BF)
            low = (dg * m_ref[...].astype(F32)).astype(BF)
            d_out[...] = low
            de = de + col_inner(low, w[...])
        de_ref[...] = de.astype(BF)

    ins = [dl, acc, cot, mixed, fac_h, fac_f, keep, g_own, g_oth, m_own, m_oth, u_own, wg_own, h_own, f_own]
    ins += [*packs_g, *packs_u, *packs_h, *packs_h]
    specs = [rows_of(d)] * 7 + [rows_of(half)] * 4
    specs += [whole((half, d)), whole((d, half)), whole((ch, d)), whole((ch, d))]
    specs += [piece_whole(rg, half, 0)] * 4 + [piece_whole(ru, d, 0)] * 4
    specs += [piece_whole(rh, d, 0)] * 4 + [piece_whole(rh, d, 1)] * 4
    return run(
        body, (n // ROWS,), scal, ins, specs,
        [sds((n, d))] * 4 + [sds((n, half))] * 4 + [sds((n, d))],
        [rows_of(d)] * 4 + [rows_of(half)] * 4 + [rows_of(d)],
        [pltpu.VMEM((half, d), BF), pltpu.VMEM((d, half), BF), pltpu.VMEM((2 * ch, d), BF), pltpu.VMEM((2 * ch, d), BF)],
        flops=2 * n * d * (4 * half + 4 * ch), name="mid_back",
    )


def k_attend_back(scal, p, da_own, da_oth, v_own, v_oth, vs_own, vs_oth, q, k, z_pre, gain):
    n, zw = q.shape
    half = da_own.shape[1]
    blocks = n // ROWS
    scale = zw ** (-0.5)

    def body(s, p_ref, ao, at, vo, vt, so, st, q_ref, k_ref, z_ref, g_ref, oo, ot, dz_ref, sum_ref, dvo, dvt, dks):
        for step, i in enumerate(reversed(range(blocks))):

            @pl.when(pl.program_id(0) == step)
            def _(i=i):
                seen = (i + 1) * ROWS
                lo = i * ROWS
                last = i == blocks - 1
                pb = p_ref[:, 0:seen]
                pr = pb.astype(F32)
                dp = col_inner(ao[...], vo[0:seen, :]) + col_inner(at[...], vt[0:seen, :])
                ds = (pr * (dp - jnp.sum(pr * dp, axis=-1, keepdims=True))).astype(BF)
                dq = matmul(ds, k_ref[0:seen, :]) * scale
                dk = row_inner(ds, q_ref[...]) * scale
                if not last:
                    dk = dk + dks[0:seen, :]
                for a_ref, acc, sl, o_ref in ((ao, dvo, so, oo), (at, dvt, st, ot)):
                    dv = row_inner(pb, a_ref[...])
                    if not last:
                        dv = dv + acc[0:seen, :]
                    if i:
                        acc[0:lo, :] = dv[0:lo]
                    o_ref[...] = (dv[lo:seen] * sl[...].astype(F32)).astype(BF)
                if i:
                    dks[0:lo, :] = dk[0:lo]
                dk = dk[lo:seen]
                act, slope = silu_pair(z_ref[...])
                dz_ref[...] = (slope * (dq * g_ref[0:1, :] + dk * g_ref[1:2, :])).astype(BF)
                for j, v in enumerate((dq * act, dk * act, dq, dk)):
                    part = jnp.sum(v, axis=0, keepdims=True)
                    sum_ref[j : j + 1, :] = part if last else sum_ref[j : j + 1, :] + part
                if last:
                    sum_ref[4:8, :] = jnp.zeros((4, zw), F32)

    def back_rows(cols):
        return pl.BlockSpec((ROWS, cols), lambda i, s: (blocks - 1 - i, 0))

    low = n - ROWS
    return run(
        body, (blocks,), scal, [p, da_own, da_oth, v_own, v_oth, vs_own, vs_oth, q, k, z_pre, gain],
        [back_rows(n), back_rows(half), back_rows(half), whole((n, half)), whole((n, half)), back_rows(half),
         back_rows(half), back_rows(zw), whole((n, zw)), back_rows(zw), whole((2, zw))],
        [sds((n, half)), sds((n, half)), sds((n, zw)), sds((8, zw), F32)],
        [back_rows(half), back_rows(half), back_rows(zw), pl.BlockSpec((8, zw), lambda i, s: (0, 0))],
        [pltpu.VMEM((low, half), F32), pltpu.VMEM((low, half), F32), pltpu.VMEM((low, zw), F32)],
        flops=n * n * 4 * half * 1.25, name="attend_back",
    )


def k_input_back(scal, dv_own, dv_oth, w_own, packs, d_sig, tokens, direct):
    n, d = tokens.shape
    rp = packs[0].shape[0]
    half = dv_own.shape[1]

    def body(s, vo, vt, wo, w0, w1, w2, w3, sg, x_ref, dir_ref, o_ref, w_scr):
        @pl.when(pl.program_id(0) == 0)
        def _():
            place(w_scr, s, (w0, w1, w2, w3))

        dn = col_inner(vo[...], wo[...]) + col_inner(vt[...], w_scr[...]) + sg[...]
        x = x_ref[...].astype(F32)
        r = lax.rsqrt(jnp.mean(x * x, axis=-1, keepdims=True) + norm_eps)
        n1 = x * r
        o_ref[...] = dir_ref[...].astype(F32) + r * (dn - n1 * jnp.mean(dn * n1, axis=-1, keepdims=True))

    return run(
        body, (n // ROWS,), scal, [dv_own, dv_oth, w_own, *packs, d_sig, tokens, direct],
        [rows_of(half), rows_of(half), whole((d, half))] + [piece_whole(rp, half, 0)] * 4 + [rows_of(d)] * 3,
        [sds((n, d), F32)], [rows_of(d)],
        [pltpu.VMEM((d, half), BF)],
        flops=4 * n * d * half, name="input_back",
    )[0]


def split_rows(s, grad):
    d, c = grad.shape
    by_x = grad.reshape(4, 2, d // 8, c)
    flip = s[12] == 0
    a, b = by_x[:, 0].reshape(d // 2, c), by_x[:, 1].reshape(d // 2, c)
    return jnp.where(flip, a, b), jnp.where(flip, b, a)


def k_weight_mid(scal, ema_low, dh, df, gated_own, gated_oth, dg_own, dg_oth, part, got=None):
    n, d = ema_low.shape
    half = gated_own.shape[1] // 2
    tn = d // 4
    rows = d // 2

    def body(s, e_ref, h_ref, f_ref, go, gt, do, dt, eo, et, *refs):
        for i in range(3):

            @pl.when(pl.program_id(0) == i)
            def _(i=i):
                for k, (g, dg, e) in enumerate(((go, do, eo), (gt, dt, et))):
                    a = row_inner(h_ref[...], g[...] if i < 2 else e[...])
                    b = row_inner(e_ref[...], dg[...]) if i < 2 else row_inner(f_ref[...], e[...])
                    a, b = split_rows(s, a), split_rows(s, b)
                    if got is None:
                        for j in range(2):
                            refs[0][k, j] = a[j].astype(BF)
                            refs[1][k, j] = b[j].astype(BF)
                    else:
                        a = [a[j] + refs[0][k, j].astype(F32) for j in range(2)]
                        b = [b[j] + refs[1][k, j].astype(F32) for j in range(2)]
                        refs[2][k] = a[1].astype(BF)
                        refs[3][k] = a[0].astype(BF)
                        for j in range(2):
                            refs[4 + k][j] = b[j].astype(BF)

    at = pl.BlockSpec((n, tn), lambda i, s: (0, s[part] * 2 + jnp.minimum(i, 1)))
    e_own = pl.BlockSpec((n, tn), lambda i, s: (0, s[6] * 2 + s[part]), pipeline_mode=pl.Buffered(1))
    e_oth = pl.BlockSpec((n, tn), lambda i, s: (0, s[7] * 2 + s[part]), pipeline_mode=pl.Buffered(1))
    four = pl.BlockSpec((2, 2, rows, tn), lambda i, s: (0, 0, 0, i))
    two = pl.BlockSpec((2, rows, tn), lambda i, s: (0, 0, i))
    adds = list(got) if got is not None else []
    return run(
        body, (3,), scal, [ema_low, dh, df, gated_own, gated_oth, dg_own, dg_oth, ema_low, ema_low] + adds,
        [whole((n, d))] * 3 + [at] * 4 + [e_own, e_oth] + [four] * len(adds),
        [sds((2, rows, 3 * tn))] * 4 if adds else [sds((2, 2, rows, 3 * tn))] * 2,
        [two] * 4 if adds else [four] * 2,
        flops=2 * n * d * 6 * half, name="weight_mid",
    )


def k_weight_value(scal, normed, dv_own, dv_oth, part, got=None):
    n, d = normed.shape
    tn = dv_own.shape[1] // 4
    rows = d // 2

    def body(s, x_ref, vo, vt, *refs):
        for i in range(2):

            @pl.when(pl.program_id(0) == i)
            def _(i=i):
                for k, v in enumerate((vo, vt)):
                    a = split_rows(s, row_inner(x_ref[...], v[...]))
                    if got is None:
                        for j in range(2):
                            refs[0][k, j] = a[j].astype(BF)
                    else:
                        a = [a[j] + refs[0][k, j].astype(F32) for j in range(2)]
                        if i == 0:
                            refs[1][k] = a[1].astype(BF)
                            refs[2][k] = a[0].astype(BF)
                        else:
                            for j in range(2):
                                refs[3 + k][j] = a[j].astype(BF)

    at = pl.BlockSpec((n, tn), lambda i, s: (0, s[part] * 2 + i))
    four = pl.BlockSpec((2, 2, rows, tn), lambda i, s: (0, 0, 0, i))
    still = pl.BlockSpec((2, rows, tn), lambda i, s: (0, 0, 0))
    adds = [got] if got is not None else []
    return run(
        body, (2,), scal, [normed, dv_own, dv_oth] + adds,
        [whole((n, d)), at, at] + [four] * len(adds),
        [sds((2, rows, tn))] * 4 if adds else [sds((2, 2, rows, 2 * tn))],
        [still] * 4 if adds else [four],
        flops=2 * n * d * 4 * tn, name="weight_value",
    )


def k_weight_z(scal, ema_low, dz):
    n, d = ema_low.shape
    zw = dz.shape[1]

    def body(s, e_ref, z_ref, o_ref):
        a = split_rows(s, row_inner(e_ref[...], z_ref[...]))
        for j in range(2):
            o_ref[j] = a[j].astype(BF)

    return run(
        body, (1,), scal, [ema_low, dz], [whole((n, d)), whole((n, zw))],
        [sds((2, d // 2, zw))], [pl.BlockSpec((2, d // 2, zw), lambda i, s: (0, 0, 0))],
        flops=2 * n * d * zw, name="weight_z",
    )[0]


def swap(values, axis, bit, size):
    return lax.ppermute(values, axis, [(i, i ^ bit) for i in range(size)])


def pick(values, index, axis):
    return lax.dynamic_index_in_dim(values, index, axis, keepdims=False)


def one_sequence(
    tokens, alpha_logit, delta_logit, ema_beta, ema_eta, ema_omega, w_z, qk_gain, qk_bias,
    w_v, w_gamma, u_h, w_h, w_phi, w_up, w_down, cotangent,
):
    n, d = tokens.shape
    dp_size = lax.axis_size("dp")
    me = lax.axis_index("dp").astype(jnp.int32)
    t = lax.axis_index("tensor").astype(jnp.int32)
    core = me % 2
    x_pos = (me // 2) % 2
    z_pos = me // 4
    kx = core * 2 + x_pos
    kz = core * 2 + z_pos % 2
    scal = jnp.stack([kx, kx ^ 1, kx ^ 2, kx ^ 3, core, 1 - core, t, 1 - t, kz, kz ^ 1, kz ^ 2, kz ^ 3, x_pos])

    def held(values, *deps):
        return lax.optimization_barrier((values, deps))[0]

    def after(*deps):
        return held(scal, *deps)

    def over_core(v):
        return swap(v, "dp", 1, dp_size)

    def over_x(v):
        return swap(v, "dp", 2, dp_size)

    def over_z(v):
        return swap(v, "dp", 4, dp_size)

    def over_tensor(v):
        return swap(v, "tensor", 1, 2)

    def my_rows(w, k):
        rows = w.shape[0] // 4
        return lax.dynamic_slice_in_dim(w, k * rows, rows, 0)

    own_params = jnp.concatenate(
        [alpha_logit, delta_logit, ema_beta, ema_eta, ema_omega[:, None],
         jnp.zeros((ema_omega.shape[0], 128 - 4 * H - 1), F32)], axis=1
    )
    oth_params = over_tensor(own_params)
    pv = [over_tensor(my_rows(w_v, kx))]
    normed, v_own, vs_own = k_value_own(scal, tokens, w_v)
    pg = [over_tensor(held(my_rows(w_gamma, kz), v_own))]
    decay, coef, omega = k_ema_params(after(v_own), own_params, oth_params)
    blocks = n // 128
    ema_a = k_ema_forward(after(v_own), normed, decay, coef, omega, 0, blocks // 2)
    pv.append(over_x(held(pv[0], ema_a[0])))
    pu = [over_tensor(held(my_rows(u_h, kx), ema_a[0]))]
    ema_low, e_slope, state = k_ema_forward(
        after(ema_a[0]), normed, decay, coef, omega, blocks // 2, blocks // 2, (ema_a[2], ema_a[0], ema_a[1])
    )
    pg.append(over_z(held(pg[0], state)))
    ph = [over_tensor(held(jnp.concatenate([my_rows(w_h, kz), my_rows(w_phi, kz)], axis=0), state))]
    z_pre, query, key = k_query_key(scal, ema_low, w_z, qk_gain, qk_bias)
    pv += [over_core(v) for v in held((pv[0], pv[1]), query)]
    pu.append(over_x(held(pu[0], query)))
    pup = [over_tensor(held(my_rows(w_up, kx), query))]
    v_oth, vs_oth = k_act_other(after(query), normed, pv, 0, 512)
    pg += [over_core(v) for v in held((pg[0], pg[1]), v_oth)]
    ph.append(over_z(held(ph[0], v_oth)))
    pdn = [over_tensor(held(my_rows(w_down, kz), v_oth))]
    gated_own, gated_oth, g_own, g_oth, m_own, m_oth, probs = k_attend(
        after(v_oth), query, key, v_own, v_oth, ema_low, w_gamma, pg
    )
    pu += [over_core(v) for v in held((pu[0], pu[1]), probs)]
    ph += [over_core(v) for v in held((ph[0], ph[1]), probs)]
    pup.append(over_x(held(pup[0], probs)))
    mixed, lowered, fac_h, fac_f, keep = k_gate(
        after(probs), gated_own, gated_oth, ema_low, tokens, u_h, w_h, w_phi, pu, ph
    )
    acc, dl, *sent_o = k_ffn(after(mixed), lowered, cotangent, [w_up], [w_down], 1)
    pup += [over_core(v) for v in held((pup[0], pup[1]), acc)]
    pdn.append(over_z(held(pdn[0], acc)))
    dno_got, upo_got = [over_core(v) for v in sent_o]
    acc, dl, dno, upo = k_ffn(after(acc), lowered, cotangent, [w_up], [w_down], 0, (acc, dl))
    pdn += [over_core(v) for v in held((pdn[0], pdn[1]), acc)]

    def add(*values):
        value = values[0].astype(F32)
        for v in values[1:]:
            value = value + v.astype(F32)
        return value.astype(BF)

    def z_first(terms):
        by_z = [v.reshape(2, 2, d // 8, v.shape[-1]) for v in terms]
        send = add(*[pick(v, 1 - z_pos % 2, 1) for v in by_z])
        return send, [pick(v, z_pos % 2, 1) for v in by_z]

    def z_second(terms):
        send = add(*[pick(v, 1 - z_pos // 2, 0) for v in terms])
        return send, [pick(v, z_pos // 2, 0) for v in terms]

    def over_z2(v):
        return swap(v, "dp", 8, dp_size)

    def core_rows(terms):
        by_core = [v.reshape(2, d // 16, v.shape[-1]) for v in terms]
        send = add(*[pick(v, 1 - core, 0) for v in by_core])
        return send, [pick(v, core, 0) for v in by_core]

    def total(terms):
        value = terms[0].astype(F32)
        for v in terms[1:]:
            value = value + v.astype(F32)
        return value

    def joined(kept, got):
        kept, got = kept.astype(F32), got.astype(F32)
        return jnp.where(
            core == 0, jnp.concatenate([kept, got], axis=1), jnp.concatenate([got, kept], axis=1)
        )

    dn_x1 = add(dno[1], dno_got[1])
    dn_got_x1 = over_x(dn_x1)
    acc, dl, *sent_t = k_ffn(after(acc, dn_x1), lowered, cotangent, pup, pdn, 1, (acc, dl))
    dnt_got, upt_got = [over_core(v) for v in sent_t]
    acc, dl, dnt, upt = k_ffn(after(acc), lowered, cotangent, pup, pdn, 0, (acc, dl))
    dn_x2 = add(dnt[1], dnt_got[1])
    up_y1 = add(upt, upt_got)
    dn_got_x2 = over_x(dn_x2)
    up_got_y = over_tensor(up_y1)
    output, dh, df, direct, da_own, da_oth, dg_own, dg_oth, de_part = k_mid_back(
        after(acc, dn_x2, up_y1), dl, acc, cotangent, mixed, fac_h, fac_f, keep,
        g_own, g_oth, m_own, m_oth, u_h, w_gamma, w_h, w_phi, pg, pu, ph,
    )
    dn_got_x2 = held(dn_got_x2, dh)
    dn_y = add(dnt[0], dnt_got[0], dn_got_x2)
    dn_got_y = over_tensor(dn_y)
    mid_sent = k_weight_mid(after(dh, dn_y), ema_low, dh, df, gated_own, gated_oth, dg_own, dg_oth, 5)
    mid_got = [over_core(v) for v in mid_sent]
    dv_own, dv_oth, dz, stats = k_attend_back(
        after(*mid_sent), probs, da_own, da_oth, v_own, v_oth, vs_own, vs_oth, query, key, z_pre, qk_gain
    )
    up_got_y = held(up_got_y, dv_own)
    up_x = add(upo[1], upo_got[1], up_got_y[1])
    up_got_x = over_x(up_x)
    val_sent = k_weight_value(after(dv_own, up_x), normed, dv_own, dv_oth, 5)[0]
    val_got = over_core(val_sent)
    ma_theirs, ma_mine, mb_own, mb_oth = k_weight_mid(
        after(val_sent), ema_low, dh, df, gated_own, gated_oth, dg_own, dg_oth, 4, mid_got
    )
    ma_got_x = over_x(ma_theirs)
    mb_got_y = over_tensor(mb_oth)
    z_own = k_weight_z(after(ma_theirs), ema_low, dz)
    z_got = over_core(z_own)
    va_theirs, va_mine, vb_own, vb_oth = k_weight_value(after(z_own), normed, dv_own, dv_oth, 4, val_got)
    va_got_x = over_x(va_theirs)
    vb_got_y = over_tensor(vb_oth)
    dn_got_y, up_got_x = held((dn_got_y, up_got_x), va_theirs)
    dn_z, dn_terms = z_first([dno[0], dno_got[0], dn_got_x1, dn_got_y])
    up_z, up_terms = z_first([upo[0], upo_got[0], up_got_y[0], up_got_x])
    dn_got_z, up_got_z = over_z(dn_z), over_z(up_z)
    z_sum = add(z_own, z_got)
    z_got_y = over_tensor(z_sum)
    quarter = blocks // 4

    def ema_back(dep, first, count, before=None):
        return k_ema_backward(
            after(*dep), normed, de_part, dz, e_slope, w_z, decay, coef, omega, first, count, before
        )

    eb = ema_back((va_theirs, dn_z, up_z, z_sum), 0, quarter)
    ma_got_x, mb_got_y = held((ma_got_x, mb_got_y), eb[1])
    ma_y = add(ma_mine[1], ma_got_x[1])
    mb_x = add(mb_own[1], mb_got_y[1])
    ma_got_y = over_tensor(ma_y)
    mb_got_x = over_x(mb_x)
    eb = ema_back((eb[1], ma_y, mb_x), quarter, quarter, eb)
    dn_got_z, up_got_z, va_got_x, vb_got_y, z_got_y = held((dn_got_z, up_got_z, va_got_x, vb_got_y, z_got_y), eb[1])
    dn_z2, dn_terms = z_second([*dn_terms, dn_got_z])
    up_z2, up_terms = z_second([*up_terms, up_got_z])
    va_y = add(va_mine[1], va_got_x[1])
    zs = add(z_sum, z_got_y)
    vb_x = jnp.concatenate([add(vb_own[1], vb_got_y[1]), zs[1]], axis=-1)
    dn_got_z2, up_got_z2 = over_z2(dn_z2), over_z2(up_z2)
    va_got_y = over_tensor(va_y)
    vb_got_x = over_x(vb_x)
    eb = ema_back((eb[1], dn_z2, up_z2, va_y, vb_x), 2 * quarter, quarter, eb)
    ma_got_y, mb_got_x = held((ma_got_y, mb_got_x), eb[1])
    ma_z, ma_terms = z_first([ma_mine[0], ma_got_x[0], ma_got_y])
    mb_z, mb_terms = z_first([mb_own[0], mb_got_y[0], mb_got_x])
    ma_got_z, mb_got_z = over_z(ma_z), over_z(mb_z)
    eb = ema_back((eb[1], ma_z, mb_z), 3 * quarter, quarter, eb)
    d_sig, _, _, sum_a, sum_b, sum_w = eb
    sums = jnp.concatenate([sum_a, sum_b, sum_w, stats], axis=0)
    sums_got = over_core(sums)
    va_got_y, vb_got_x = held((va_got_y, vb_got_x), sum_a)
    c = va_mine.shape[-1]
    vb_terms = [jnp.concatenate([vb_own[0], zs[0]], axis=-1), jnp.pad(vb_got_y[0], ((0, 0), (0, zs.shape[-1]))), vb_got_x]
    val_z, val_terms = z_first([
        jnp.concatenate([add(va_mine[0], va_got_x[0], va_got_y), add(*vb_terms)], axis=-1)
    ])
    val_got_z = over_z(val_z)
    input_grad = k_input_back(
        after(sum_a, val_z, sums), dv_own, dv_oth, w_v, pv, d_sig, tokens, direct
    )
    ma_got_z, mb_got_z, val_got_z, sums_got = held((ma_got_z, mb_got_z, val_got_z, sums_got), input_grad)
    sums = sums + sums_got
    sums_got = over_tensor(sums)
    mid_z2, mid_terms = z_second([
        jnp.concatenate([add(*ma_terms, ma_got_z), add(*mb_terms, mb_got_z)], axis=-1)
    ])
    mid_got_z2 = over_z2(mid_z2)
    val_z2, val_terms = z_second([*val_terms, val_got_z])
    val_got_z2 = over_z2(val_z2)
    sums = sums + sums_got
    others = [over_x(sums), over_z(sums), lax.ppermute(sums, "dp", [(i, i ^ 6) for i in range(dp_size)])]
    sums = sums + others[0] + others[1] + others[2]
    sums = sums + over_z2(sums)

    def finish(terms):
        send, terms = core_rows(terms)
        return total(terms), over_core(send)

    down_t = joined(*finish([*dn_terms, dn_got_z2]))
    up = joined(*finish([*up_terms, up_got_z2]))
    mid_kept, mid_got = finish([*mid_terms, mid_got_z2])
    tn = d // 4
    uh_t, wh_t, gamma, phi_t = (
        joined(mid_kept[:, lo * tn : hi * tn], mid_got[:, lo * tn : hi * tn])
        for lo, hi in ((0, 2), (2, 3), (3, 5), (5, 6))
    )
    val_kept, val_got = finish([*val_terms, val_got_z2])
    value = joined(val_kept[:, : 2 * c], val_got[:, : 2 * c])
    z_grad = val_kept[:, 2 * c :]
    gh = sum_a.shape[0]

    def own_half(v):
        return lax.dynamic_slice_in_dim(v, t * (d // 2), d // 2, 1).T

    tot_a = own_half(sums[:gh].reshape(H, d))
    tot_b = own_half(sums[gh : 2 * gh].reshape(H, d))
    omega_grad = lax.dynamic_slice_in_dim(sums[2 * gh : 2 * gh + d // 128].reshape(d), t * (d // 2), d // 2, 0)
    zsum = sums[2 * gh + d // 128 :]
    rate = jax.nn.sigmoid(alpha_logit)
    damp = jax.nn.sigmoid(delta_logit)
    feed = rate * ema_beta
    feed_grad = ema_eta * tot_a
    decay_grad = feed * ema_eta * tot_b
    alpha_grad = (feed_grad * ema_beta - decay_grad * damp) * rate * (1.0 - rate)
    delta_grad = -decay_grad * rate * damp * (1.0 - damp)
    return (
        output, input_grad, alpha_grad, delta_grad, feed_grad * rate, feed * tot_a, omega_grad,
        z_grad, zsum[0:2], zsum[2:4], value, gamma, uh_t.T, wh_t.T, phi_t.T, up, down_t.T,
    )


def solution(mesh):
    placed = (
        P(("dp", "tensor"), None),
        P("tensor", None),
        P("tensor", None),
        P("tensor", None),
        P("tensor", None),
        P("tensor"),
        P(),
        P(),
        P(),
        P(None, "tensor"),
        P(None, "tensor"),
        P("tensor", None),
        P("tensor", None),
        P("tensor", None),
        P(None, "tensor"),
        P("tensor", None),
        P(("dp", "tensor"), None),
    )

    def per_device(tokens, *rest):
        whole_sequence = tokens.shape[0] == LEN and dict(mesh.shape) == {"dp": 16, "tensor": 2}
        return (one_sequence if whole_sequence else shards)(tokens, *rest)

    return jax.shard_map(
        per_device,
        mesh=mesh,
        in_specs=placed,
        out_specs=(
            P(("dp", "tensor"), None),
            P(("dp", "tensor"), None),
            P("tensor", None),
            P("tensor", None),
            P("tensor", None),
            P("tensor", None),
            P("tensor"),
            P("dp", None),
            P(),
            P(),
            P("dp", "tensor"),
            P("dp", "tensor"),
            P("tensor", "dp"),
            P("tensor", "dp"),
            P("tensor", "dp"),
            P("dp", "tensor"),
            P("tensor", "dp"),
        ),
        check_vma=False,
    )
```

```python
import math

import jax
import jax.numpy as jnp
from jax import lax
from jax.experimental import pallas as pl
from jax.experimental.pallas import tpu as pltpu
from jax.sharding import PartitionSpec as P

H = 16
LEN = 1024
ATT_BLOCK = 512
EMA_BLOCK = 128


norm_eps = 1e-06
masked_value = -1e30


def rms_rows(values_in):
    return values_in * lax.rsqrt(jnp.mean(values_in * values_in, axis=-1, keepdims=True) + norm_eps)


def matmul(left, right):
    return jnp.dot(left, right, preferred_element_type=jnp.float32)


def row_inner(left, right):
    return lax.dot_general(
        left, right, (((0,), (0,)), ((), ())), preferred_element_type=jnp.float32
    )


def col_inner(left, right):
    return lax.dot_general(
        left, right, (((1,), (1,)), ((), ())), preferred_element_type=jnp.float32
    )


def silu_slope(pre_act):
    logistic = jax.nn.sigmoid(pre_act)
    return logistic * (1.0 + pre_act * (1.0 - logistic))


def gate_apply(h_pre, f_pre, x_rows):
    update = jax.nn.sigmoid(f_pre)
    return update * jax.nn.silu(h_pre) + (1.0 - update) * x_rows


def ema_apply(signal, ema_params):
    alpha_logit, delta_logit, ema_beta, ema_eta, ema_omega = ema_params
    alpha_rate = jax.nn.sigmoid(alpha_logit)
    decay_rate = 1.0 - alpha_rate * jax.nn.sigmoid(delta_logit)
    feed_rate = alpha_rate * ema_beta
    log_decay = jnp.log(decay_rate)
    total_rows, chan_count = signal.shape
    seq_count = total_rows // LEN
    block_count = LEN // EMA_BLOCK
    blocks = signal.reshape(seq_count, block_count, EMA_BLOCK, chan_count)
    steps_in = jnp.arange(EMA_BLOCK, dtype=jnp.float32)
    lag_power = jnp.exp(steps_in[:, None, None] * log_decay[None])
    kernel = jnp.sum(lag_power * (feed_rate * ema_eta)[None], axis=-1)
    offsets = steps_in[:, None] - steps_in[None, :]
    lag_index = jnp.clip(offsets, 0, EMA_BLOCK - 1).astype(jnp.int32)
    toeplitz = jnp.where((offsets >= 0)[:, :, None], kernel[lag_index], 0.0)
    local_part = jnp.einsum("ijc,snjc->snic", toeplitz, blocks)
    tail_power = lag_power[::-1] * feed_rate[None]
    block_state = jnp.einsum("jch,snjc->snch", tail_power, blocks)
    full_decay = jnp.exp(EMA_BLOCK * log_decay)

    def carry_step(state_in, incoming):
        return (full_decay * state_in + incoming, state_in)

    zero_state = jnp.zeros((seq_count, chan_count, H), jnp.float32)
    _, start_state = lax.scan(carry_step, zero_state, jnp.moveaxis(block_state, 1, 0))
    start_state = jnp.moveaxis(start_state, 0, 1)
    head_power = lag_power * decay_rate[None] * ema_eta[None]
    carried = jnp.einsum("ich,snch->snic", head_power, start_state)
    ema_pre = (local_part + carried).reshape(total_rows, chan_count) + ema_omega * signal
    return jax.nn.silu(ema_pre)


def masked_scores(q_rows, k_rows, first_row):
    raw_scores = col_inner(q_rows, k_rows) * q_rows.shape[1] ** (-0.5)
    row_pos = first_row + jnp.arange(q_rows.shape[0])[:, None]
    col_pos = jnp.arange(k_rows.shape[0])[None, :]
    return jnp.where(col_pos <= row_pos, raw_scores, masked_value)


def attend_forward(query_low, key_low, value_low):
    total_rows, value_width = value_low.shape
    seq_count = total_rows // LEN
    per_seq = LEN // ATT_BLOCK

    def attend_one_block(flat_index):
        seq_id = flat_index // per_seq
        blk_id = flat_index % per_seq
        seq_start = seq_id * LEN
        q_rows = lax.dynamic_slice_in_dim(query_low, seq_start + blk_id * ATT_BLOCK, ATT_BLOCK, 0)
        k_rows = lax.dynamic_slice_in_dim(key_low, seq_start, LEN, 0)
        v_rows = lax.dynamic_slice_in_dim(value_low, seq_start, LEN, 0)
        scores = masked_scores(q_rows, k_rows, blk_id * ATT_BLOCK)
        top_score = jnp.max(scores, axis=-1, keepdims=True)
        weights = jnp.exp(scores - top_score)
        total_weight = jnp.sum(weights, axis=-1, keepdims=True)
        probs = (weights / total_weight).astype(jnp.bfloat16)
        return (matmul(probs, v_rows), top_score[:, 0] + jnp.log(total_weight[:, 0]))

    outs, lse_all = lax.map(attend_one_block, jnp.arange(seq_count * per_seq))
    return (outs.reshape(total_rows, value_width), lse_all.reshape(total_rows))


def attend_backward(query_low, key_low, value_low, lse_rows, d_att):
    total_rows, value_width = value_low.shape
    head_width = query_low.shape[1]
    seq_count = total_rows // LEN
    per_seq = LEN // ATT_BLOCK
    scale = head_width ** (-0.5)

    def one_seq(seq_id):
        seq_start = seq_id * LEN
        k_rows = lax.dynamic_slice_in_dim(key_low, seq_start, LEN, 0)
        v_rows = lax.dynamic_slice_in_dim(value_low, seq_start, LEN, 0)

        def one_one_block(carry_in, blk_id):
            d_keys, d_vals = carry_in
            row_start = seq_start + blk_id * ATT_BLOCK
            q_rows = lax.dynamic_slice_in_dim(query_low, row_start, ATT_BLOCK, 0)
            g_rows = lax.dynamic_slice_in_dim(d_att, row_start, ATT_BLOCK, 0)
            lse_part = lax.dynamic_slice_in_dim(lse_rows, row_start, ATT_BLOCK, 0)
            probs = jnp.exp(masked_scores(q_rows, k_rows, blk_id * ATT_BLOCK) - lse_part[:, None])
            d_probs = col_inner(g_rows, v_rows)
            d_scores = (
                probs * (d_probs - jnp.sum(probs * d_probs, axis=-1, keepdims=True))
            ).astype(jnp.bfloat16)
            d_rows = matmul(d_scores, k_rows) * scale
            d_keys = d_keys + row_inner(d_scores, q_rows) * scale
            d_vals = d_vals + row_inner(probs.astype(jnp.bfloat16), g_rows)
            return ((d_keys, d_vals), d_rows)

        start_carry = (
            jnp.zeros((LEN, head_width), jnp.float32),
            jnp.zeros((LEN, value_width), jnp.float32),
        )
        (d_keys, d_vals), d_rows = lax.scan(one_one_block, start_carry, jnp.arange(per_seq))
        return (d_rows.reshape(LEN, head_width), d_keys, d_vals)

    d_query, d_key, d_value = lax.map(one_seq, jnp.arange(seq_count))
    return (
        d_query.reshape(total_rows, head_width),
        d_key.reshape(total_rows, head_width),
        d_value.reshape(total_rows, value_width),
    )


def shards(
    tokens,
    alpha_logit,
    delta_logit,
    ema_beta,
    ema_eta,
    ema_omega,
    w_z,
    qk_gain,
    qk_bias,
    w_v,
    w_gamma,
    u_h,
    w_h,
    w_phi,
    w_up,
    w_down,
    cotangent,
):
    tensor_pos = lax.axis_index("tensor")
    feature_count = tokens.shape[1]
    chan_count = ema_omega.shape[0]
    chan_start = tensor_pos * chan_count
    x_rows = tokens.astype(jnp.float32)
    normed_rows, norm_pull = jax.vjp(rms_rows, x_rows)
    normed, cot_full = (
        lax.all_gather(normed_rows.astype(jnp.bfloat16), "tensor", axis=0, tiled=True),
        lax.all_gather(cotangent, "tensor", axis=0, tiled=True),
    )
    signal = lax.dynamic_slice_in_dim(normed, chan_start, chan_count, 1).astype(jnp.float32)
    ema_params = (alpha_logit, delta_logit, ema_beta, ema_eta, ema_omega)
    ema_val, ema_pull = jax.vjp(ema_apply, signal, ema_params)
    ema_low = ema_val.astype(jnp.bfloat16)
    ema_full = lax.all_gather(ema_low, "tensor", axis=1, tiled=True)
    z_pre = matmul(ema_full, w_z)
    z_act = jax.nn.silu(z_pre)
    query_low = (z_act * qk_gain[0] + qk_bias[0]).astype(jnp.bfloat16)
    key_low = (z_act * qk_gain[1] + qk_bias[1]).astype(jnp.bfloat16)
    values_pre = matmul(normed, w_v)
    value_low = jax.nn.silu(values_pre).astype(jnp.bfloat16)
    gamma_pre = matmul(ema_full, w_gamma)
    gamma_act = jax.nn.silu(gamma_pre)
    attended, lse_rows = attend_forward(query_low, key_low, value_low)
    gated_low = (gamma_act * attended).astype(jnp.bfloat16)
    both_pre = lax.psum_scatter(
        jnp.concatenate(
            [matmul(gated_low, u_h) + matmul(ema_low, w_h), matmul(ema_low, w_phi)], axis=1
        ),
        "tensor",
        scatter_dimension=0,
        tiled=True,
    )
    h_pre = both_pre[:, :feature_count]
    f_pre = both_pre[:, feature_count:]
    mixed, gate_pull = jax.vjp(gate_apply, h_pre, f_pre, x_rows)
    normed_two, norm_two_pull = jax.vjp(rms_rows, mixed)
    lowered = lax.all_gather(normed_two.astype(jnp.bfloat16), "tensor", axis=0, tiled=True)
    up_pre = matmul(lowered, w_up)
    hidden = jax.nn.silu(up_pre).astype(jnp.bfloat16)
    down_rows = lax.psum_scatter(
        matmul(hidden, w_down).astype(jnp.bfloat16), "tensor", scatter_dimension=0, tiled=True
    ).astype(jnp.float32)
    output = (mixed + down_rows).astype(jnp.bfloat16)
    cot_rows = cotangent.astype(jnp.float32)
    d_hidden = col_inner(cot_full, w_down)
    d_up = (d_hidden * silu_slope(up_pre)).astype(jnp.bfloat16)
    down_grad = row_inner(hidden, cot_full)
    up_grad = row_inner(lowered, d_up)
    d_lowered = lax.psum_scatter(col_inner(d_up, w_up), "tensor", scatter_dimension=0, tiled=True)
    d_mixed = cot_rows + norm_two_pull(d_lowered)[0]
    d_hpre, d_fpre, d_direct = gate_pull(d_mixed)
    h_full_grad, f_full_grad = (
        lax.all_gather(d_hpre.astype(jnp.bfloat16), "tensor", axis=0, tiled=True),
        lax.all_gather(d_fpre.astype(jnp.bfloat16), "tensor", axis=0, tiled=True),
    )
    uh_grad = row_inner(gated_low, h_full_grad)
    wh_grad = row_inner(ema_low, h_full_grad)
    phi_grad = row_inner(ema_low, f_full_grad)
    d_gated = col_inner(h_full_grad, u_h)
    d_att = (d_gated * gamma_act).astype(jnp.bfloat16)
    d_gamma = (d_gated * attended * silu_slope(gamma_pre)).astype(jnp.bfloat16)
    d_query, d_key, d_value = attend_backward(query_low, key_low, value_low, lse_rows, d_att)
    d_query, d_key = lax.psum((d_query, d_key), "tensor")
    d_z = (silu_slope(z_pre) * (d_query * qk_gain[0] + d_key * qk_gain[1])).astype(jnp.bfloat16)
    gain_grad = jnp.stack([jnp.sum(d_query * z_act, axis=0), jnp.sum(d_key * z_act, axis=0)])
    bias_grad = jnp.stack([jnp.sum(d_query, axis=0), jnp.sum(d_key, axis=0)])
    z_grad = row_inner(ema_full, d_z)
    gamma_grad = row_inner(ema_full, d_gamma)
    d_value_pre = (d_value * silu_slope(values_pre)).astype(jnp.bfloat16)
    value_grad = row_inner(normed, d_value_pre)
    d_chan = lax.psum_scatter(
        col_inner(d_gamma, w_gamma).astype(jnp.bfloat16), "tensor", scatter_dimension=1, tiled=True
    ).astype(jnp.float32)
    z_rows = lax.dynamic_slice_in_dim(w_z, chan_start, chan_count, 0)
    d_chan = (
        d_chan
        + col_inner(d_z, z_rows)
        + col_inner(h_full_grad, w_h)
        + col_inner(f_full_grad, w_phi)
    )
    d_signal, d_params = ema_pull(d_chan)
    d_norm_part = col_inner(d_value_pre, w_v)
    own_cols = lax.dynamic_slice_in_dim(d_norm_part, chan_start, chan_count, 1)
    d_norm_part = lax.dynamic_update_slice_in_dim(d_norm_part, own_cols + d_signal, chan_start, 1)
    d_normed = lax.psum_scatter(
        d_norm_part.astype(jnp.bfloat16), "tensor", scatter_dimension=0, tiled=True
    ).astype(jnp.float32)
    input_grad = d_direct + norm_pull(d_normed)[0]
    weight_totals = (
        lax.psum_scatter(z_grad.astype(jnp.bfloat16), "dp", scatter_dimension=0, tiled=True).astype(
            jnp.float32
        ),
        lax.psum_scatter(
            value_grad.astype(jnp.bfloat16), "dp", scatter_dimension=0, tiled=True
        ).astype(jnp.float32),
        lax.psum_scatter(
            gamma_grad.astype(jnp.bfloat16), "dp", scatter_dimension=0, tiled=True
        ).astype(jnp.float32),
        lax.psum_scatter(
            uh_grad.astype(jnp.bfloat16), "dp", scatter_dimension=1, tiled=True
        ).astype(jnp.float32),
        lax.psum_scatter(
            wh_grad.astype(jnp.bfloat16), "dp", scatter_dimension=1, tiled=True
        ).astype(jnp.float32),
        lax.psum_scatter(
            phi_grad.astype(jnp.bfloat16), "dp", scatter_dimension=1, tiled=True
        ).astype(jnp.float32),
        lax.psum_scatter(
            up_grad.astype(jnp.bfloat16), "dp", scatter_dimension=0, tiled=True
        ).astype(jnp.float32),
        lax.psum_scatter(
            down_grad.astype(jnp.bfloat16), "dp", scatter_dimension=1, tiled=True
        ).astype(jnp.float32),
    )
    param_totals = lax.psum(
        (d_params[0], d_params[1], d_params[2], d_params[3], d_params[4], gain_grad, bias_grad),
        "dp",
    )
    return (
        output,
        input_grad,
        param_totals[0],
        param_totals[1],
        param_totals[2],
        param_totals[3],
        param_totals[4],
        weight_totals[0],
        param_totals[5],
        param_totals[6],
        weight_totals[1],
        weight_totals[2],
        weight_totals[3],
        weight_totals[4],
        weight_totals[5],
        weight_totals[6],
        weight_totals[7],
    )


MIB = 1024 * 1024
BF = jnp.bfloat16
F32 = jnp.float32
ROWS = 256
hints = dict()
opt = dict(dn=0, m2=3, v2=5, z2=3, z1m=5, z1v=6)


def sds(shape, dtype=BF):
    return jax.ShapeDtypeStruct(shape, dtype)


def whole(shape):
    return pl.BlockSpec(shape, lambda i, s: (0,) * len(shape), pipeline_mode=pl.Buffered(1))


def rows_of(cols, rows=ROWS):
    return pl.BlockSpec((rows, cols), lambda i, s: (i, 0))


def cols_of(rows, cols):
    return pl.BlockSpec((rows, cols), lambda i, s: (0, i))


def run(body, grid, scal, ins, in_specs, out_shape, out_specs, scratch=(), flops=0, name=None, aliases=None, spare=12):
    moved = sum(a.size * a.dtype.itemsize for a in ins)
    moved += sum(math.prod(o.shape) * jnp.dtype(o.dtype).itemsize for o in out_shape)
    def held_bytes(spec, a):
        if spec.block_shape is None:
            return 0
        return math.prod(spec.block_shape) * jnp.dtype(a.dtype).itemsize * (1 if spec.pipeline_mode else 2)

    if name in ("attend", "gate", "ffn", "mid_back", "pack_params", "ema_params", "pieces"):
        spare = 56
    vmem = sum(map(held_bytes, in_specs, ins)) + sum(map(held_bytes, out_specs, out_shape))
    vmem += sum(math.prod(r.shape) * jnp.dtype(r.dtype).itemsize for r in scratch if r.memory_space == pltpu.VMEM)
    return pl.pallas_call(
        body,
        out_shape=out_shape,
        grid_spec=pltpu.PrefetchScalarGridSpec(
            num_scalar_prefetch=1,
            grid=grid,
            in_specs=in_specs,
            out_specs=out_specs,
            scratch_shapes=list(scratch),
        ),
        compiler_params=pltpu.CompilerParams(vmem_limit_bytes=min(vmem + spare * MIB, 56 * MIB)),
        cost_estimate=pl.CostEstimate(flops=int(flops * hints.get(name, 10)), bytes_accessed=int(moved * hints.get(name, 10)), transcendentals=0),
        name=name,
        input_output_aliases=aliases or {},
    )(scal, *ins)


def sig(u):
    return 0.5 + 0.5 * jnp.tanh(0.5 * u)


def silu_pair(u):
    s = sig(u)
    return u * s, s * (1.0 + u * (1.0 - s))


def place(scr, s, pieces, base=0, table=0):
    rows = pieces[0].shape[0]
    for p in range(4):
        scr[pl.ds(pl.multiple_of(base + s[table + p] * rows, rows), rows), :] = pieces[p][...]


def piece_block(rows, cols, row_block):
    return pl.BlockSpec((rows, cols), lambda i, s: (row_block, i))


def piece_whole(rows, cols, row_block):
    return pl.BlockSpec((rows, cols), lambda i, s: (row_block, 0), pipeline_mode=pl.Buffered(1))


def k_value_own(scal, tokens, w_own):
    n, d = tokens.shape
    cols = w_own.shape[1]
    tn = 512

    def body(s, x_ref, w_ref, n_ref, v_ref, sl_ref):
        @pl.when(pl.program_id(0) == 0)
        def _():
            x = x_ref[...].astype(F32)
            n_ref[...] = (x * lax.rsqrt(jnp.mean(x * x, axis=-1, keepdims=True) + norm_eps)).astype(BF)

        act, slope = silu_pair(matmul(n_ref[...], w_ref[...]))
        v_ref[...] = act.astype(BF)
        sl_ref[...] = slope.astype(BF)

    return run(
        body, (cols // tn,), scal, [tokens, w_own],
        [whole((n, d)), cols_of(d, tn)],
        [sds((n, d)), sds((n, cols)), sds((n, cols))],
        [pl.BlockSpec((n, d), lambda i, s: (0, 0)), cols_of(n, tn), cols_of(n, tn)],
        flops=2 * n * d * cols, name="value_own",
    )


def k_act_own(scal, x, w_own, tn):
    n, d = x.shape
    cols = w_own.shape[1]

    def body(s, x_ref, w_ref, v_ref, sl_ref):
        act, slope = silu_pair(matmul(x_ref[...], w_ref[...]))
        v_ref[...] = act.astype(BF)
        sl_ref[...] = slope.astype(BF)

    return run(
        body, (cols // tn,), scal, [x, w_own],
        [whole((n, d)), cols_of(d, tn)],
        [sds((n, cols)), sds((n, cols))],
        [cols_of(n, tn), cols_of(n, tn)],
        flops=2 * n * d * cols, name="act_own",
    )


def k_act_other(scal, x, pieces, table, tn):
    n, d = x.shape
    rows, cols = pieces[0].shape

    def body(s, x_ref, p0, p1, p2, p3, v_ref, sl_ref, w_scr):
        place(w_scr, s, (p0, p1, p2, p3), table=table)
        act, slope = silu_pair(matmul(x_ref[...], w_scr[...]))
        v_ref[...] = act.astype(BF)
        sl_ref[...] = slope.astype(BF)

    return run(
        body, (cols // tn,), scal, [x, *pieces],
        [whole((n, d))] + [piece_block(rows, tn, 0)] * 4,
        [sds((n, cols)), sds((n, cols))],
        [cols_of(n, tn), cols_of(n, tn)],
        [pltpu.VMEM((d, tn), BF)],
        flops=2 * n * d * cols, name="act_other",
    )


def k_query_key(scal, ema_low, w_z, qk_gain, qk_bias):
    n, d = ema_low.shape
    zw = w_z.shape[1]

    def body(s, e_ref, w_ref, g_ref, b_ref, z_ref, q_ref, k_ref):
        z_pre = matmul(e_ref[...], w_ref[...])
        z_ref[...] = z_pre
        act = z_pre * sig(z_pre)
        q_ref[...] = (act * g_ref[0:1, :] + b_ref[0:1, :]).astype(BF)
        k_ref[...] = (act * g_ref[1:2, :] + b_ref[1:2, :]).astype(BF)

    return run(
        body, (2,), scal, [ema_low, w_z, qk_gain, qk_bias],
        [rows_of(d, n // 2), whole((d, zw)), whole((2, zw)), whole((2, zw))],
        [sds((n, zw), F32), sds((n, zw)), sds((n, zw))],
        [rows_of(zw, n // 2)] * 3,
        flops=2 * n * d * zw, name="query_key",
    )


def k_pack_params(scal, arrays, omega):
    ch = omega.shape[1]

    def body(s, a0, a1, a2, a3, w_ref, o_ref):
        for i, ref in enumerate((a0, a1, a2, a3)):
            o_ref[i * H : (i + 1) * H, :] = ref[...]
        o_ref[4 * H : 4 * H + 8, :] = jnp.broadcast_to(w_ref[...], (8, ch))

    return run(
        body, (1,), scal, [*arrays, omega], [whole((H, ch))] * 4 + [whole((1, ch))],
        [sds((4 * H + 8, ch), F32)], [pl.BlockSpec((4 * H + 8, ch), lambda i, s: (0, 0))], flops=1e7, name="pack_params",
    )[0]


def k_ema_params(scal, own, oth):
    height, ch = own.shape
    groups = 2 * ch // 128

    def body(s, own_ref, oth_ref, dec_ref, cf_ref, om_ref):
        for j in range(2):
            for src, ref in ((0, own_ref), (1, oth_ref)):

                @pl.when(s[6 + src] == j)
                def _(j=j, ref=ref):
                    v = ref[...]
                    rate = sig(v[0:H])
                    dec = 1.0 - rate * sig(v[H : 2 * H])
                    cf = rate * v[2 * H : 3 * H] * v[3 * H : 4 * H]
                    for g in range(groups // 2):
                        lanes = slice(g * 128, (g + 1) * 128)
                        at = j * (groups // 2) + g
                        dec_ref[pl.ds(at, H, stride=groups), :] = dec[:, lanes]
                        cf_ref[pl.ds(at, H, stride=groups), :] = cf[:, lanes]
                        om_ref[at : at + 1, :] = v[4 * H : 4 * H + 1, lanes]

    par = (H * groups, 128)
    return run(
        body, (1,), scal, [own, oth], [whole((height, ch))] * 2,
        [sds(par, F32), sds(par, F32), sds((groups, 128), F32)],
        [pl.BlockSpec(par, lambda i, s: (0, 0))] * 2 + [pl.BlockSpec((groups, 128), lambda i, s: (0, 0))],
        flops=1e8, name="ema_params",
    )


def k_pieces(scal, takes):
    parts = [(w, at) for take in takes for w, at in take]

    def body(s, *refs):
        ins, outs = refs[: len(parts)], refs[len(parts) :]
        n = 0
        for take, out in zip(takes, outs):
            low = 0
            for w, _ in take:
                rows = w.shape[0] // 4
                out[low : low + rows, :] = ins[n][...]
                low += rows
                n += 1

    return run(
        body, (1,), scal, [w for w, _ in parts],
        [pl.BlockSpec((w.shape[0] // 4, w.shape[1]), lambda i, s, at=at: (s[at], 0)) for w, at in parts],
        [sds((sum(w.shape[0] // 4 for w, _ in take), take[0][0].shape[1])) for take in takes],
        [pl.BlockSpec((sum(w.shape[0] // 4 for w, _ in take), take[0][0].shape[1]), lambda i, s: (0, 0)) for take in takes],
        flops=1e7, name="pieces",
    )


def k_ema_forward(scal, normed, decay, coef, omega, first, count, before=None):
    n, d = normed.shape
    groups = d // 128
    tb = 128

    def body(s, x_ref, dec_ref, cf_ref, om_ref, *refs):
        e_ref, sl_ref, st, xs, ys = refs[-5:]

        @pl.when(pl.program_id(0) == 0)
        def _():
            st[...] = refs[0][...] if before else jnp.zeros_like(st)

        for g in range(groups):
            xs[pl.ds(g, tb, stride=groups), :] = x_ref[:, g * 128 : (g + 1) * 128].astype(F32)
        dec = [dec_ref[k * groups : (k + 1) * groups, :] for k in range(H)]
        cf = [cf_ref[k * groups : (k + 1) * groups, :] for k in range(H)]
        om = om_ref[...]

        def steps(b, carry):
            states = list(carry)
            for u in range(16):
                row = pl.multiple_of((b * 16 + u) * groups, groups)
                xt = xs[pl.ds(row, groups), :]
                parts = [om * xt, None, None, None]
                for k in range(H):
                    states[k] = dec[k] * states[k] + xt
                    term = cf[k] * states[k]
                    parts[k % 4] = term if parts[k % 4] is None else parts[k % 4] + term
                ys[pl.ds(row, groups), :] = (parts[0] + parts[1]) + (parts[2] + parts[3])
            return tuple(states)

        start = tuple(st[k * groups : (k + 1) * groups, :] for k in range(H))
        end = lax.fori_loop(0, tb // 16, steps, start)
        for k in range(H):
            st[k * groups : (k + 1) * groups, :] = end[k]
        for g in range(groups):
            act, slope = silu_pair(ys[pl.ds(g, tb, stride=groups), :])
            e_ref[:, g * 128 : (g + 1) * 128] = act.astype(BF)
            sl_ref[:, g * 128 : (g + 1) * 128] = slope.astype(BF)

    par = (H * groups, 128)
    at = pl.BlockSpec((tb, d), lambda i, s: (first + i, 0))
    more = list(before) if before else []
    return run(
        body, (count,), scal, [normed, decay, coef, omega, *more],
        [at, whole(par), whole(par), whole((groups, 128))]
        + ([whole(par), pl.BlockSpec(memory_space=pltpu.HBM), pl.BlockSpec(memory_space=pltpu.HBM)] if before else []),
        [sds((n, d)), sds((n, d)), sds(par, F32)],
        [at, at, pl.BlockSpec(par, lambda i, s: (0, 0))],
        [pltpu.VMEM((tb * groups, 128), F32), pltpu.VMEM((tb * groups, 128), F32)],
        flops=2.5e9 * count, name="ema_forward", aliases={6: 0, 7: 1} if before else {},
    )


def k_ema_backward(scal, normed, de_part, dz, slope, w_z, decay, coef, omega, first, count, before=None):
    n, d = normed.shape
    groups = d // 128
    tb = 128
    nb = n // tb
    half = H // 2
    gh = groups * half
    zw = dz.shape[1]

    def body(s, x_ref, de_ref, z_ref, sl_ref, wz_ref, dec_ref, cf_ref, om_ref, *refs):
        o_ref, back, deriv, a_ref, b_ref, w_ref, xs, gs, ys = refs[-9:]

        @pl.when(pl.program_id(0) == 0)
        def _():
            for i, ref in enumerate((back, deriv, a_ref, b_ref, w_ref)):
                ref[...] = refs[i][...] if before else jnp.zeros_like(ref)

        d_e = (de_ref[...].astype(F32) + col_inner(z_ref[...], wz_ref[...])) * sl_ref[...].astype(F32)
        for g in range(groups):
            xs[pl.ds(g, tb, stride=groups), :] = x_ref[:, g * 128 : (g + 1) * 128].astype(F32)
            gs[pl.ds(g, tb, stride=groups), :] = d_e[:, g * 128 : (g + 1) * 128]

        for part in range(2):
            low = part * gh
            at = [slice(low + k * groups, low + (k + 1) * groups) for k in range(half)]
            dec = [dec_ref[a, :] for a in at]

            def steps(b, carry, part=part, at=at, dec=dec):
                bk, dv, aa, bb, ww = (list(c) for c in carry)
                for u in range(8):
                    row = pl.multiple_of((tb - 1 - (b * 8 + u)) * groups, groups)
                    xt = xs[pl.ds(row, groups), :]
                    gt = gs[pl.ds(row, groups), :]
                    if part == 0:
                        outs = [om_ref[...] * gt, None]
                        ww[0] = ww[0] + xt * gt
                    else:
                        outs = [ys[pl.ds(row, groups), :], None]
                    for k in range(half):
                        dv[k] = dec[k] * dv[k] + bk[k]
                        bk[k] = dec[k] * bk[k] + gt
                        term = cf_ref[at[k], :] * bk[k]
                        outs[k % 2] = term if outs[k % 2] is None else outs[k % 2] + term
                        aa[k] = aa[k] + xt * bk[k]
                        bb[k] = bb[k] + xt * dv[k]
                    ys[pl.ds(row, groups), :] = outs[0] + outs[1]
                return tuple(bk), tuple(dv), tuple(aa), tuple(bb), tuple(ww)

            start = (
                tuple(back[a, :] for a in at),
                tuple(deriv[a, :] for a in at),
                tuple(a_ref[a, :] for a in at),
                tuple(b_ref[a, :] for a in at),
                (w_ref[...],),
            )
            bk, dv, aa, bb, ww = lax.fori_loop(0, tb // 8, steps, start)
            for k in range(half):
                back[at[k], :] = bk[k]
                deriv[at[k], :] = dv[k]
                a_ref[at[k], :] = aa[k]
                b_ref[at[k], :] = bb[k]
            w_ref[...] = ww[0]
        for g in range(groups):
            o_ref[:, g * 128 : (g + 1) * 128] = ys[pl.ds(g, tb, stride=groups), :]

    top = nb - 1 - first
    back_rows = pl.BlockSpec((tb, d), lambda i, s: (top - i, 0))
    par = (H * groups, 128)
    const = pl.BlockSpec(par, lambda i, s: (0, 0))
    small = (groups, 128)
    more = [*before[1:], before[0]] if before else []
    return run(
        body, (count,), scal, [normed, de_part, dz, slope, w_z, decay, coef, omega, *more],
        [back_rows, back_rows, pl.BlockSpec((tb, zw), lambda i, s: (top - i, 0)), back_rows, whole((d, zw)),
         whole(par), whole(par), whole(small)]
        + ([whole(par)] * 4 + [whole(small), pl.BlockSpec(memory_space=pltpu.HBM)] if before else []),
        [sds((n, d), F32)] + [sds(par, F32)] * 4 + [sds(small, F32)],
        [back_rows, const, const, const, const, pl.BlockSpec(small, lambda i, s: (0, 0))],
        [pltpu.VMEM((tb * groups, 128), F32)] * 3,
        flops=5e9 * count, name="ema_backward", aliases={14: 0} if before else {},
    )


def k_attend(scal, q, k, v_own, v_oth, ema_low, g_own, packs):
    n, zw = q.shape
    d, half = g_own.shape
    rp = packs[0].shape[0]
    blocks = n // ROWS
    scale = zw ** (-0.5)

    def body(s, q_ref, k_ref, vo, vt, e_ref, wo, w0, w1, w2, w3, gated_o, gated_t, go, gt, mo, mt, p_ref, w_scr):
        @pl.when(pl.program_id(0) == 0)
        def _():
            place(w_scr, s, (w0, w1, w2, w3), table=8)

        for i in range(blocks):

            @pl.when(pl.program_id(0) == i)
            def _(i=i):
                seen = (i + 1) * ROWS
                sc = col_inner(q_ref[...], k_ref[0:seen, :]) * scale
                row = i * ROWS + lax.broadcasted_iota(jnp.int32, (ROWS, seen), 0)
                col = lax.broadcasted_iota(jnp.int32, (ROWS, seen), 1)
                sc = jnp.where(col <= row, sc, masked_value)
                e = jnp.exp(sc - jnp.max(sc, axis=-1, keepdims=True))
                p = (e * (1.0 / jnp.sum(e, axis=-1, keepdims=True))).astype(BF)
                p_ref[:, 0:seen] = p
                if seen < n:
                    p_ref[:, seen:] = jnp.zeros((ROWS, n - seen), BF)
                for v_ref, w, gated, g, m in ((vo, wo, gated_o, go, mo), (vt, w_scr, gated_t, gt, mt)):
                    act, slope = silu_pair(matmul(e_ref[...], w[...]))
                    att = matmul(p, v_ref[0:seen, :])
                    gated[...] = (act * att).astype(BF)
                    g[...] = act.astype(BF)
                    m[...] = (slope * att).astype(BF)

    return run(
        body, (blocks,), scal, [q, k, v_own, v_oth, ema_low, g_own, *packs],
        [rows_of(zw), whole((n, zw)), whole((n, half)), whole((n, half)), rows_of(d), whole((d, half))]
        + [whole((rp, half))] * 4,
        [sds((n, half))] * 6 + [sds((n, n))],
        [rows_of(half)] * 6 + [rows_of(n)],
        [pltpu.VMEM((d, half), BF)],
        flops=n * n * (zw + 2 * half) * 1.25 + 4 * n * d * half, name="attend",
    )


def k_gate(scal, gated_own, gated_oth, ema_low, tokens, u_own, h_own, f_own, packs_u, packs_h):
    n, d = tokens.shape
    half = u_own.shape[0]
    ch = h_own.shape[0]
    ru, rh = packs_u[0].shape[0], packs_h[0].shape[0] // 2

    def body(s, go, gt, e_ref, x_ref, uo, ho, fo, u0, u1, u2, u3, h0, h1, h2, h3, f0, f1, f2, f3,
             mix_ref, low_ref, a_ref, b_ref, up_ref, u_scr, h_scr, f_scr):
        @pl.when(pl.program_id(0) == 0)
        def _():
            place(u_scr, s, (u0, u1, u2, u3))
            own = pl.multiple_of(s[6] * ch, ch)
            oth = s[7] * ch
            h_scr[pl.ds(own, ch), :] = ho[...]
            f_scr[pl.ds(own, ch), :] = fo[...]
            place(h_scr, s, (h0, h1, h2, h3), oth, 8)
            place(f_scr, s, (f0, f1, f2, f3), oth, 8)

        h_pre = matmul(go[...], uo[...]) + matmul(gt[...], u_scr[...]) + matmul(e_ref[...], h_scr[...])
        f_pre = matmul(e_ref[...], f_scr[...])
        x = x_ref[...].astype(F32)
        act, slope = silu_pair(h_pre)
        update = sig(f_pre)
        mixed = update * act + (1.0 - update) * x
        mix_ref[...] = mixed.astype(BF)
        low_ref[...] = (mixed * lax.rsqrt(jnp.mean(mixed * mixed, axis=-1, keepdims=True) + norm_eps)).astype(BF)
        a_ref[...] = (update * slope).astype(BF)
        b_ref[...] = ((act - x) * update * (1.0 - update)).astype(BF)
        up_ref[...] = (1.0 - update).astype(BF)

    ins = [gated_own, gated_oth, ema_low, tokens, u_own, h_own, f_own, *packs_u, *packs_h, *packs_h]
    specs = [rows_of(half), rows_of(half), rows_of(d), rows_of(d), whole((half, d)), whole((ch, d)), whole((ch, d))]
    specs += [piece_whole(ru, d, 0)] * 4 + [piece_whole(rh, d, 0)] * 4 + [piece_whole(rh, d, 1)] * 4
    return run(
        body, (n // ROWS,), scal, ins, specs,
        [sds((n, d))] * 5,
        [rows_of(d)] * 5,
        [pltpu.VMEM((half, d), BF), pltpu.VMEM((2 * ch, d), BF), pltpu.VMEM((2 * ch, d), BF)],
        flops=2 * n * d * (2 * half + 4 * ch), name="gate",
    )


def split_rows(s, grad):
    d, c = grad.shape
    by_x = grad.reshape(4, 2, d // 8, c)
    flip = s[12] == 0
    a, b = by_x[:, 0].reshape(d // 2, c), by_x[:, 1].reshape(d // 2, c)
    return jnp.where(flip, a, b), jnp.where(flip, b, a)


def put_rows(s, ref, value, lead=(), add=None):
    rows = value.shape[0] // 4
    for z in range(4):
        at = pl.ds(pl.multiple_of((s[13] ^ z) * rows, rows), rows)
        part = value[z * rows : (z + 1) * rows]
        if add is not None:
            part = part + add[0][(*add[1], at, slice(None))].astype(F32)
        ref[(*lead, at, slice(None))] = part.astype(BF)


def k_ffn(scal, lowered, cot, up, down, part, before=None, form="sent"):
    n, d = lowered.shape
    pieces = len(up) > 1
    tn = up[0].shape[1] // 4
    rows = d // 2

    def body(s, low_ref, c_ref, *refs):
        step = pl.program_id(0)
        nu = len(up)
        ups, wd, refs = refs[:nu], refs[nu], refs[nu + 1 :]
        if before:
            ins, refs = refs[:2], refs[2:]
            held, sems = refs[-2:]
            refs = refs[:-2]
            copies = [pltpu.make_async_copy(ins[i], held.at[i], sems.at[i]) for i in range(2)]
        out_ref, gl_ref, *grads, acc, gl, u_scr = refs
        if pieces:
            place(u_scr, s, ups)
            wu = u_scr
        else:
            wu = ups[0]

        def work(wd, i):
            if before and i == 0:
                for c in copies:
                    c.start()
            act, slope = silu_pair(matmul(low_ref[...], wu[...]))
            hid = act.astype(BF)
            out = matmul(hid, wd[...])
            du = (col_inner(c_ref[...], wd[...]) * slope).astype(BF)
            back = col_inner(du, wu[...])
            if i == 0:
                acc[...] = out
                gl[...] = back
            else:
                if before:
                    for c in copies:
                        c.wait()
                    out = out + held[0].astype(F32)
                    back = back + held[1].astype(F32)
                out_ref[...] = (acc[...] + out).astype(BF)
                gl_ref[...] = (gl[...] + back).astype(BF)
            for k, grad in enumerate((row_inner(c_ref[...], hid), row_inner(low_ref[...], du))):
                for j, rows_j in enumerate(split_rows(s, grad)):
                    if form == "sent":
                        put_rows(s, grads[0], rows_j, (k, j))
                    elif form == "own" or k == 0:
                        put_rows(s, grads[2 * k + j], rows_j)
                    else:
                        put_rows(s, grads[2], rows_j, (j,))

        for i in range(2):

            @pl.when(step == i)
            def _(i=i):
                work(wd, i)

    if pieces:
        down = [down[part]]
        specs = [pl.BlockSpec((d // 4, tn), lambda i, s: (0, s[4 + part] * 2 + i))] * 4
        specs += [pl.BlockSpec((tn, d), lambda i, s: (i, 0))]
    else:
        specs = [
            pl.BlockSpec((d, tn), lambda i, s: (0, s[4 + part] * 2 + i)),
            pl.BlockSpec((tn, d), lambda i, s: (s[4 + part] * 2 + i, 0)),
        ]
    still = pl.BlockSpec((n, d), lambda i, s: (0, 0))
    one = pl.BlockSpec((rows, tn), lambda i, s: (0, i))
    two = pl.BlockSpec((2, rows, tn), lambda i, s: (0, 0, i))
    four = pl.BlockSpec((2, 2, rows, tn), lambda i, s: (0, 0, 0, i))
    grad_specs = dict(sent=[four], own=[one] * 4, other=[one, one, two])[form]
    grad_shapes = [sds((*g.block_shape[:-1], 2 * tn)) for g in grad_specs]
    more = list(before) if before else []
    return run(
        body, (2,), scal, [lowered, cot, *up, *down, *more],
        [whole((n, d)), whole((n, d))] + specs + [pl.BlockSpec(memory_space=pltpu.HBM)] * len(more),
        [sds((n, d)), sds((n, d)), *grad_shapes],
        [still, still, *grad_specs],
        [pltpu.VMEM((n, d), F32), pltpu.VMEM((n, d), F32), pltpu.VMEM((d, tn), BF)]
        + ([pltpu.VMEM((2, n, d), BF), pltpu.SemaphoreType.DMA((2,))] if before else []),
        flops=24 * n * d * tn, name="ffn",
    )


def k_mid_back(scal, dl, acc, cot, mixed, fac_h, fac_f, keep, g_own, g_oth, m_own, m_oth,
               u_own, wg_own, h_own, f_own, packs_g, packs_u, packs_h):
    n, d = cot.shape
    half = u_own.shape[0]
    ch = h_own.shape[0]
    ru, rh = packs_u[0].shape[0], packs_h[0].shape[0] // 2
    rg = packs_g[0].shape[0]

    def body(s, l_ref, acc_ref, c_ref, x_ref, a_ref, b_ref, k_ref, go, gt, mo, mt, uo, wo, ho, fo,
             w0, w1, w2, w3, u0, u1, u2, u3, h0, h1, h2, h3, f0, f1, f2, f3,
             out_ref, dh_ref, df_ref, dir_ref, ao, at, do, dt, de_ref, u_scr, w_scr, h_scr, f_scr):
        @pl.when(pl.program_id(0) == 0)
        def _():
            place(u_scr, s, (u0, u1, u2, u3))
            place(w_scr, s, (w0, w1, w2, w3), table=8)
            own = pl.multiple_of(s[6] * ch, ch)
            oth = s[7] * ch
            h_scr[pl.ds(own, ch), :] = ho[...]
            f_scr[pl.ds(own, ch), :] = fo[...]
            place(h_scr, s, (h0, h1, h2, h3), oth, 8)
            place(f_scr, s, (f0, f1, f2, f3), oth, 8)

        dl = l_ref[...].astype(F32)
        m = x_ref[...].astype(F32)
        out_ref[...] = (m + acc_ref[...].astype(F32)).astype(BF)
        r = lax.rsqrt(jnp.mean(m * m, axis=-1, keepdims=True) + norm_eps)
        n2 = m * r
        dm = c_ref[...].astype(F32) + r * (dl - n2 * jnp.mean(dl * n2, axis=-1, keepdims=True))
        dh = (dm * a_ref[...].astype(F32)).astype(BF)
        df = (dm * b_ref[...].astype(F32)).astype(BF)
        dh_ref[...] = dh
        df_ref[...] = df
        dir_ref[...] = (dm * k_ref[...].astype(F32)).astype(BF)
        de = col_inner(dh, h_scr[...]) + col_inner(df, f_scr[...])
        for u, w, g_ref, m_ref, a_out, d_out in ((uo, wo, go, mo, ao, do), (u_scr, w_scr, gt, mt, at, dt)):
            dg = col_inner(dh, u[...])
            a_out[...] = (dg * g_ref[...].astype(F32)).astype(BF)
            low = (dg * m_ref[...].astype(F32)).astype(BF)
            d_out[...] = low
            de = de + col_inner(low, w[...])
        de_ref[...] = de.astype(BF)

    ins = [dl, acc, cot, mixed, fac_h, fac_f, keep, g_own, g_oth, m_own, m_oth, u_own, wg_own, h_own, f_own]
    ins += [*packs_g, *packs_u, *packs_h, *packs_h]
    specs = [rows_of(d)] * 7 + [rows_of(half)] * 4
    specs += [whole((half, d)), whole((d, half)), whole((ch, d)), whole((ch, d))]
    specs += [piece_whole(rg, half, 0)] * 4 + [piece_whole(ru, d, 0)] * 4
    specs += [piece_whole(rh, d, 0)] * 4 + [piece_whole(rh, d, 1)] * 4
    return run(
        body, (n // ROWS,), scal, ins, specs,
        [sds((n, d))] * 4 + [sds((n, half))] * 4 + [sds((n, d))],
        [rows_of(d)] * 4 + [rows_of(half)] * 4 + [rows_of(d)],
        [pltpu.VMEM((half, d), BF), pltpu.VMEM((d, half), BF), pltpu.VMEM((2 * ch, d), BF), pltpu.VMEM((2 * ch, d), BF)],
        flops=2 * n * d * (4 * half + 4 * ch), name="mid_back",
    )


def k_attend_back(scal, p, da_own, da_oth, v_own, v_oth, vs_own, vs_oth, q, k, z_pre, gain):
    n, zw = q.shape
    half = da_own.shape[1]
    blocks = n // ROWS
    scale = zw ** (-0.5)

    def body(s, p_ref, ao, at, vo, vt, so, st, q_ref, k_ref, z_ref, g_ref, oo, ot, dz_ref, sum_ref, dvo, dvt, dks):
        for step, i in enumerate(reversed(range(blocks))):

            @pl.when(pl.program_id(0) == step)
            def _(i=i):
                seen = (i + 1) * ROWS
                lo = i * ROWS
                last = i == blocks - 1
                pb = p_ref[:, 0:seen]
                pr = pb.astype(F32)
                dp = col_inner(ao[...], vo[0:seen, :]) + col_inner(at[...], vt[0:seen, :])
                ds = (pr * (dp - jnp.sum(pr * dp, axis=-1, keepdims=True))).astype(BF)
                dq = matmul(ds, k_ref[0:seen, :]) * scale
                dk = row_inner(ds, q_ref[...]) * scale
                if not last:
                    dk = dk + dks[0:seen, :]
                for a_ref, acc, sl, o_ref in ((ao, dvo, so, oo), (at, dvt, st, ot)):
                    dv = row_inner(pb, a_ref[...])
                    if not last:
                        dv = dv + acc[0:seen, :]
                    if i:
                        acc[0:lo, :] = dv[0:lo]
                    o_ref[...] = (dv[lo:seen] * sl[...].astype(F32)).astype(BF)
                if i:
                    dks[0:lo, :] = dk[0:lo]
                dk = dk[lo:seen]
                act, slope = silu_pair(z_ref[...])
                dz_ref[...] = (slope * (dq * g_ref[0:1, :] + dk * g_ref[1:2, :])).astype(BF)
                for j, v in enumerate((dq * act, dk * act, dq, dk)):
                    part = jnp.sum(v, axis=0, keepdims=True)
                    sum_ref[j : j + 1, :] = part if last else sum_ref[j : j + 1, :] + part
                if last:
                    sum_ref[4:8, :] = jnp.zeros((4, zw), F32)

    def back_rows(cols):
        return pl.BlockSpec((ROWS, cols), lambda i, s: (blocks - 1 - i, 0))

    low = n - ROWS
    return run(
        body, (blocks,), scal, [p, da_own, da_oth, v_own, v_oth, vs_own, vs_oth, q, k, z_pre, gain],
        [back_rows(n), back_rows(half), back_rows(half), whole((n, half)), whole((n, half)), back_rows(half),
         back_rows(half), back_rows(zw), whole((n, zw)), back_rows(zw), whole((2, zw))],
        [sds((n, half)), sds((n, half)), sds((n, zw)), sds((8, zw), F32)],
        [back_rows(half), back_rows(half), back_rows(zw), pl.BlockSpec((8, zw), lambda i, s: (0, 0))],
        [pltpu.VMEM((low, half), F32), pltpu.VMEM((low, half), F32), pltpu.VMEM((low, zw), F32)],
        flops=n * n * 4 * half * 1.25, name="attend_back",
    )


def k_input_back(scal, dv_own, dv_oth, w_own, packs, d_sig, tokens, direct, first, count, before=None):
    n, d = tokens.shape
    rp = packs[0].shape[0]
    half = dv_own.shape[1]

    def body(s, vo, vt, wo, w0, w1, w2, w3, sg, x_ref, dir_ref, *refs):
        o_ref, w_scr = refs[-2:]

        @pl.when(pl.program_id(0) == 0)
        def _():
            place(w_scr, s, (w0, w1, w2, w3))

        dn = col_inner(vo[...], wo[...]) + col_inner(vt[...], w_scr[...]) + sg[...]
        x = x_ref[...].astype(F32)
        r = lax.rsqrt(jnp.mean(x * x, axis=-1, keepdims=True) + norm_eps)
        n1 = x * r
        o_ref[...] = dir_ref[...].astype(F32) + r * (dn - n1 * jnp.mean(dn * n1, axis=-1, keepdims=True))

    def at(cols):
        return pl.BlockSpec((ROWS, cols), lambda i, s: (first + i, 0))

    more = [before] if before is not None else []
    return run(
        body, (count,), scal, [dv_own, dv_oth, w_own, *packs, d_sig, tokens, direct, *more],
        [at(half), at(half), whole((d, half))] + [piece_whole(rp, half, 0)] * 4 + [at(d)] * 3
        + [pl.BlockSpec(memory_space=pltpu.HBM)] * len(more),
        [sds((n, d), F32)], [at(d)],
        [pltpu.VMEM((d, half), BF)],
        flops=4 * ROWS * count * d * half, name="input_back", aliases={11: 0} if more else {},
    )[0]


def k_weight_mid(scal, ema_low, left, right_own, right_oth, gate, part, got=None):
    n, d = ema_low.shape
    tn = d // 4
    rows = d // 2

    def body(s, *refs):
        if gate:
            e_ref, *refs = refs
        l_ref, ro, rt, eo, et, *refs = refs
        for i in range(3):

            @pl.when(pl.program_id(0) == i)
            def _(i=i):
                for k, (r, e) in enumerate(((ro, eo), (rt, et))):
                    lhs = e_ref if gate and i < 2 else l_ref
                    grad = split_rows(s, row_inner(lhs[...], r[...] if i < 2 else e[...]))
                    for j in range(2):
                        if got is None:
                            put_rows(s, refs[0], grad[j], (k, j))
                        elif gate:
                            put_rows(s, refs[1 + k], grad[j], (j,), (refs[0], (k, j)))
                        else:
                            put_rows(s, refs[2 - j], grad[j], (k,), (refs[0], (k, j)))

    at = pl.BlockSpec((n, tn), lambda i, s: (0, s[part] * 2 + jnp.minimum(i, 1)))
    e_own = pl.BlockSpec((n, tn), lambda i, s: (0, s[6] * 2 + s[part]), pipeline_mode=pl.Buffered(1))
    e_oth = pl.BlockSpec((n, tn), lambda i, s: (0, s[7] * 2 + s[part]), pipeline_mode=pl.Buffered(1))
    four = pl.BlockSpec((2, 2, rows, tn), lambda i, s: (0, 0, 0, i))
    two = pl.BlockSpec((2, rows, tn), lambda i, s: (0, 0, i))
    adds = [got] if got is not None else []
    lead = [ema_low] if gate else []
    return run(
        body, (3,), scal, [*lead, left, right_own, right_oth, ema_low, ema_low] + adds,
        [whole((n, d))] * (1 + len(lead)) + [at] * 2 + [e_own, e_oth] + [four] * len(adds),
        [sds((2, rows, 3 * tn))] * 2 if adds else [sds((2, 2, rows, 3 * tn))],
        [two] * 2 if adds else [four],
        flops=2 * n * d * 6 * tn, name="weight_mid",
    )


def k_weight_value(scal, normed, dv_own, dv_oth, ema_low, dz, part, got=None):
    n, d = normed.shape
    tn = dv_own.shape[1] // 4
    zw = dz.shape[1]
    rows = d // 2

    def body(s, x_ref, vo, vt, e_ref, z_ref, *refs):
        for k, v in enumerate((vo, vt)):
            grad = split_rows(s, row_inner(x_ref[...], v[...]))
            for j in range(2):
                if got is None:
                    put_rows(s, refs[0].at[:, :, :, 0 : 2 * tn], grad[j], (k, j))
                else:
                    add = (refs[0].at[:, :, :, 0 : 2 * tn], (k, j))
                    put_rows(s, refs[5], grad[j], (j,), add)
                    whole_rows = refs[5][j]
                    refs[2 - j][k] = whole_rows[:, 0:tn]
                    refs[3 + k][j, :, 0:tn] = whole_rows[:, tn:]
        grad = split_rows(s, row_inner(e_ref[...], z_ref[...]))
        for j in range(2):
            for k in range(2):
                if got is None:
                    put_rows(s, refs[0].at[:, :, :, 2 * tn :], grad[j], (k, j))
                else:
                    put_rows(s, refs[3 + k].at[:, :, tn:], grad[j], (j,), (refs[0].at[:, :, :, 2 * tn :], (k, j)))

    at = pl.BlockSpec((n, 2 * tn), lambda i, s: (0, s[part]))
    adds = [got] if got is not None else []
    if adds:
        shapes = [(2, rows, tn)] * 2 + [(2, rows, tn + zw)] * 2
    else:
        shapes = [(2, 2, rows, 2 * tn + zw)]
    return run(
        body, (1,), scal, [normed, dv_own, dv_oth, ema_low, dz] + adds,
        [whole((n, d)), at, at, whole((n, d)), whole((n, zw))] + [whole(a.shape) for a in adds],
        [sds(o) for o in shapes],
        [pl.BlockSpec(o, lambda i, s, r=len(o): (0,) * r) for o in shapes],
        [pltpu.VMEM((2, rows, 2 * tn), BF)] if adds else [],
        flops=2 * n * d * (4 * tn + zw), name="weight_value",
    )


def swap(values, axis, bit, size):
    return lax.ppermute(values, axis, [(i, i ^ bit) for i in range(size)])


def pick(values, index, axis):
    return lax.dynamic_index_in_dim(values, index, axis, keepdims=False)


def one_sequence(
    tokens, alpha_logit, delta_logit, ema_beta, ema_eta, ema_omega, w_z, qk_gain, qk_bias,
    w_v, w_gamma, u_h, w_h, w_phi, w_up, w_down, cotangent,
):
    n, d = tokens.shape
    dp_size = lax.axis_size("dp")
    me = lax.axis_index("dp").astype(jnp.int32)
    t = lax.axis_index("tensor").astype(jnp.int32)
    core = me % 2
    x_pos = (me // 2) % 2
    z_pos = me // 4
    kx = core * 2 + x_pos
    kz = core * 2 + z_pos % 2
    scal = jnp.stack(
        [kx, kx ^ 1, kx ^ 2, kx ^ 3, core, 1 - core, t, 1 - t, kz, kz ^ 1, kz ^ 2, kz ^ 3, x_pos, z_pos, 2 * core, 2 * core + 1]
    )

    def held(values, *deps):
        return lax.optimization_barrier((values, deps))[0]

    def after(*deps):
        return held(scal, *deps)

    def over_core(v):
        return swap(v, "dp", 1, dp_size)

    def over_x(v):
        return swap(v, "dp", 2, dp_size)

    def over_z(v):
        return swap(v, "dp", 4, dp_size)

    def over_tensor(v):
        return swap(v, "tensor", 1, 2)

    def my_rows(w, k):
        rows = w.shape[0] // 4
        return lax.dynamic_slice_in_dim(w, k * rows, rows, 0)

    piece_v = my_rows(w_v, kx)
    pv = [over_tensor(piece_v)]
    own_params = k_pack_params(
        after(piece_v), [a.T for a in (alpha_logit, delta_logit, ema_beta, ema_eta)], ema_omega[None]
    )
    oth_params = over_tensor(own_params)
    piece_g, piece_u, piece_h, piece_up, piece_dn = k_pieces(
        after(own_params),
        [[(w_gamma, 8)], [(u_h, 0)], [(w_h, 8), (w_phi, 8)], [(w_up, 0)], [(w_down, 14), (w_down, 15)]],
    )
    normed, v_own, vs_own = k_value_own(after(piece_g), tokens, w_v)
    pg = [over_tensor(held(piece_g, v_own))]
    decay, coef, omega = k_ema_params(after(v_own), own_params, oth_params)
    blocks = n // 128
    ema_a = k_ema_forward(after(v_own), normed, decay, coef, omega, 0, blocks // 2)
    pv.append(over_x(held(pv[0], ema_a[0])))
    pu = [over_tensor(held(piece_u, ema_a[0]))]
    ema_low, e_slope, state = k_ema_forward(
        after(ema_a[0]), normed, decay, coef, omega, blocks // 2, blocks // 2, (ema_a[2], ema_a[0], ema_a[1])
    )
    pg.append(over_z(held(pg[0], state)))
    ph = [over_tensor(held(piece_h, state))]
    z_pre, query, key = k_query_key(scal, ema_low, w_z, qk_gain, qk_bias)
    pv += [over_core(v) for v in held((pv[0], pv[1]), query)]
    pu.append(over_x(held(pu[0], query)))
    pup = [over_tensor(held(piece_up, query))]
    v_oth, vs_oth = k_act_other(after(query), normed, pv, 0, 512)
    pg += [over_core(v) for v in held((pg[0], pg[1]), v_oth)]
    ph.append(over_z(held(ph[0], v_oth)))
    pdn = [over_tensor(held(piece_dn, v_oth))]
    gated_own, gated_oth, g_own, g_oth, m_own, m_oth, probs = k_attend(
        after(v_oth), query, key, v_own, v_oth, ema_low, w_gamma, pg
    )
    pu += [over_core(v) for v in held((pu[0], pu[1]), probs)]
    ph += [over_core(v) for v in held((ph[0], ph[1]), probs)]
    pup.append(over_x(held(pup[0], probs)))
    mixed, lowered, fac_h, fac_f, keep = k_gate(
        after(probs), gated_own, gated_oth, ema_low, tokens, u_h, w_h, w_phi, pu, ph
    )
    acc, dl, sent_o = k_ffn(after(mixed), lowered, cotangent, [w_up], [w_down], 1)
    pup += [over_core(v) for v in held((pup[0], pup[1]), acc)]
    got_o = over_core(sent_o)
    acc, dl, dno, dno_x, upo, upo_x = k_ffn(
        after(acc), lowered, cotangent, [w_up], [w_down], 0, (acc, dl), "own"
    )
    pdn.append(over_core(held(pdn[0], acc)))

    def total(*values):
        value = values[0].astype(F32)
        for v in values[1:]:
            value = value + v.astype(F32)
        return value

    def add(*values):
        return total(*values).astype(BF)

    def by_z(v):
        return v.reshape(2, 2, d // 8, v.shape[-1])

    def z_send(terms):
        return add(*[by_z(v)[:, 1] for v in terms])

    def z_keep(terms):
        return [by_z(v)[:, 0] for v in terms]

    def over_z2(v):
        return swap(v, "dp", 8, dp_size)

    def core_split(value):
        rows = value.reshape(2, d // 16, value.shape[-1])
        return pick(rows, 1 - core, 0).astype(BF), pick(rows, core, 0)

    def joined(kept, got):
        kept, got = kept.astype(F32), got.astype(F32)
        return jnp.where(
            core == 0, jnp.concatenate([kept, got], axis=1), jnp.concatenate([got, kept], axis=1)
        )

    dn_x1 = add(dno_x, got_o[0, 1])
    dn_got_x1 = over_x(dn_x1)
    acc, dl, sent_t = k_ffn(after(acc, dn_x1), lowered, cotangent, pup, pdn, 1, (acc, dl))
    got_t = over_core(sent_t)
    acc, dl, dnt, dnt_x, upt = k_ffn(after(acc), lowered, cotangent, pup, pdn, 0, (acc, dl), "other")
    dn_x2 = add(dnt_x, got_t[0, 1])
    up_y1 = add(upt, got_t[1])
    dn_got_x2 = over_x(dn_x2)
    up_got_y = over_tensor(up_y1)
    output, dh, df, direct, da_own, da_oth, dg_own, dg_oth, de_part = k_mid_back(
        after(acc, dn_x2, up_y1, dn_got_x1), dl, acc, cotangent, mixed, fac_h, fac_f, keep,
        g_own, g_oth, m_own, m_oth, u_h, w_gamma, w_h, w_phi, pg, pu, ph,
    )
    dn_y = {}

    def start_dn(place, dep):
        if opt["dn"] == place:
            dn_y[0] = add(dnt, got_t[0, 0], held(dn_got_x2, dep))
            dn_y[1] = over_tensor(dn_y[0])
            return (dn_y[0],)
        return ()

    ma_sent = k_weight_mid(after(dh, *start_dn(0, dh)), ema_low, dh, gated_own, gated_oth, False, 5)[0]
    ma_got = over_core(ma_sent)
    mb_sent = k_weight_mid(after(ma_sent, *start_dn(1, ma_sent)), ema_low, df, dg_own, dg_oth, True, 5)[0]
    mb_got = over_core(mb_sent)
    dv_own, dv_oth, dz, stats = k_attend_back(
        after(mb_sent, *start_dn(2, mb_sent)), probs, da_own, da_oth, v_own, v_oth, vs_own, vs_oth, query, key, z_pre, qk_gain
    )
    up_got_y = held(up_got_y, dv_own)
    up_x = add(upo_x, got_o[1, 1], up_got_y[1])
    up_got_x = over_x(up_x)
    val_sent = k_weight_value(after(dv_own, up_x), normed, dv_own, dv_oth, ema_low, dz, 5)[0]
    val_got = over_core(val_sent)
    ma_theirs, ma_mine = k_weight_mid(after(val_sent), ema_low, dh, gated_own, gated_oth, False, 4, ma_got)
    ma_got_x = over_x(ma_theirs)
    mb_own, mb_oth = k_weight_mid(after(ma_theirs), ema_low, df, dg_own, dg_oth, True, 4, mb_got)
    mb_got_y = over_tensor(mb_oth)
    dn_got_y = dn_y[1]
    up_got_x, dn_got_y = held((up_got_x, dn_got_y), mb_own)
    dn_terms = [dno, got_o[0, 0], dn_got_x1, dn_got_y]
    up_terms = [upo, got_o[1, 0], up_got_y[0], up_got_x]
    ffn_z = jnp.stack([z_send(dn_terms), z_send(up_terms)])
    dn_terms, up_terms = z_keep(dn_terms), z_keep(up_terms)
    ffn_got_z = over_z(ffn_z)
    quarter = blocks // 4

    def ema_back(dep, first, count, before=None):
        return k_ema_backward(
            after(*dep), normed, de_part, dz, e_slope, w_z, decay, coef, omega, first, count, before
        )

    eb = ema_back((mb_own, ffn_z), 0, quarter)
    va_theirs, va_mine, vb_own, vb_oth = k_weight_value(
        after(eb[1]), normed, dv_own, dv_oth, ema_low, dz, 4, val_got
    )
    va_got_x = over_x(va_theirs)
    vb_got_y = over_tensor(vb_oth)
    eb = ema_back((va_theirs,), quarter, quarter, eb)
    done = {}

    def second(place, dep):
        forced = []
        if opt["m2"] == place:
            gx, gy = held((ma_got_x, mb_got_y), dep)
            ma_y, mb_x = add(ma_mine[1], gx[1]), add(mb_own[1], gy[1])
            done["m"] = (gx, gy, over_tensor(ma_y), over_x(mb_x))
            forced += [ma_y, mb_x]
        if opt.get("z2", opt["m2"]) == place:
            gz = held(ffn_got_z, dep)
            done["z"] = [*dn_terms, gz[0]], [*up_terms, gz[1]]
            ffn_z2 = jnp.stack([add(*[v[1] for v in ts]) for ts in done["z"]])
            done["z2"] = over_z2(ffn_z2)
            forced.append(ffn_z2)
        if opt["v2"] == place:
            gx, gy = held((va_got_x, vb_got_y), dep)
            va_y, vb_x = add(va_mine[1], gx[1]), add(vb_own[1], gy[1])
            done["v"] = (gx, gy, over_tensor(va_y), over_x(vb_x))
            forced += [va_y, vb_x]
        if opt.get("z1m", 6) == place:
            gy, gx = held((done["m"][2], done["m"][3]), dep)
            a_terms = [ma_mine[0], done["m"][0][0], gy]
            b_terms = [mb_own[0], done["m"][1][0], gx]
            mid_z = jnp.stack([z_send(a_terms), z_send(b_terms)])
            done["mz"] = (z_keep(a_terms), z_keep(b_terms), over_z(mid_z))
            forced.append(mid_z)
        if opt.get("z1v", 6) == place:
            gy, gx = held((done["v"][2], done["v"][3]), dep)
            a_terms = [va_mine[0], done["v"][0][0], gy]
            b_terms = [vb_own[0], done["v"][1][0], gx]
            val_z = jnp.concatenate([z_send(a_terms), z_send(b_terms)], axis=-1)
            done["vz"] = (z_keep(a_terms), z_keep(b_terms), over_z(val_z))
            forced.append(val_z)
        return forced

    f2 = second(2, eb[1])
    eb = ema_back((eb[1], *f2), 2 * quarter, quarter, eb)
    f3 = second(3, eb[1])
    eb = ema_back((eb[1], *f3), 3 * quarter, quarter, eb)
    d_sig, _, _, sum_a, sum_b, sum_w = eb
    f4 = second(4, sum_a)
    sums = jnp.concatenate([sum_a, sum_b, sum_w, stats], axis=0)
    others = over_core(sums)
    halves = n // ROWS // 2
    part = k_input_back(
        after(sum_a, sums, *f4), dv_own, dv_oth, w_v, pv, d_sig, tokens, direct, 0, halves
    )
    f5 = second(5, part)
    sums = sums + held(others, part)
    others = over_tensor(sums)
    input_grad = k_input_back(
        after(part, sums, *f5), dv_own, dv_oth, w_v, pv, d_sig, tokens, direct, halves, halves, part
    )
    second(6, input_grad)
    sums = sums + held(others, input_grad)
    sums = sums + over_x(sums)
    sums = sums + over_z(sums)
    sums = sums + over_z2(sums)
    c = va_mine.shape[-1]
    dn_terms, up_terms = done["z"]
    ffn_got_z2 = done["z2"]
    ma_terms, mb_terms, mid_got_z = done["mz"]
    va_terms, vb_terms, val_got_z = done["vz"]
    ma_terms, mb_terms = [*ma_terms, mid_got_z[0]], [*mb_terms, mid_got_z[1]]
    mid_z2 = jnp.stack([add(*[v[1] for v in ma_terms]), add(*[v[1] for v in mb_terms])])
    mid_got_z2 = over_z2(mid_z2)
    va_terms, vb_terms = [*va_terms, val_got_z[..., :c]], [*vb_terms, val_got_z[..., c:]]
    val_z2 = jnp.concatenate([add(*[v[1] for v in ts]) for ts in (va_terms, vb_terms)], axis=-1)
    val_got_z2 = over_z2(val_z2)

    def last(terms):
        return total(*[v[0] for v in terms])

    ffn_total = jnp.stack([total(last(dn_terms), ffn_got_z2[0]), total(last(up_terms), ffn_got_z2[1])])
    ffn_rows = ffn_total.reshape(2, 2, d // 16, -1)
    ffn_got = over_core(pick(ffn_rows, 1 - core, 1).astype(BF))
    ffn_kept = pick(ffn_rows, core, 1)
    mid_total = jnp.stack([total(last(ma_terms), mid_got_z2[0]), total(last(mb_terms), mid_got_z2[1])])
    mid_rows = mid_total.reshape(2, 2, d // 16, -1)
    mid_got = over_core(pick(mid_rows, 1 - core, 1).astype(BF))
    mid_kept = pick(mid_rows, core, 1)
    val_total = jnp.concatenate([last(va_terms), last(vb_terms)], axis=-1) + val_got_z2.astype(F32)
    val_sent, val_kept = core_split(val_total)
    val_got = over_core(val_sent)
    down_t, up = joined(ffn_kept[0], ffn_got[0]), joined(ffn_kept[1], ffn_got[1])
    tn = d // 4
    uh_t, gamma = (joined(mid_kept[i][:, : 2 * tn], mid_got[i][:, : 2 * tn]) for i in range(2))
    wh_t, phi_t = (joined(mid_kept[i][:, 2 * tn :], mid_got[i][:, 2 * tn :]) for i in range(2))
    value = joined(val_kept[:, : 2 * c], val_got[:, : 2 * c])
    z_grad = val_kept[:, 2 * c :]
    gh = sum_a.shape[0]

    def own_half(v):
        return lax.dynamic_slice_in_dim(v, t * (d // 2), d // 2, 1).T

    tot_a = own_half(sums[:gh].reshape(H, d))
    tot_b = own_half(sums[gh : 2 * gh].reshape(H, d))
    omega_grad = lax.dynamic_slice_in_dim(sums[2 * gh : 2 * gh + d // 128].reshape(d), t * (d // 2), d // 2, 0)
    zsum = sums[2 * gh + d // 128 :]
    rate = jax.nn.sigmoid(alpha_logit)
    damp = jax.nn.sigmoid(delta_logit)
    feed = rate * ema_beta
    feed_grad = ema_eta * tot_a
    decay_grad = feed * ema_eta * tot_b
    alpha_grad = (feed_grad * ema_beta - decay_grad * damp) * rate * (1.0 - rate)
    delta_grad = -decay_grad * rate * damp * (1.0 - damp)
    return (
        output, input_grad, alpha_grad, delta_grad, feed_grad * rate, feed * tot_a, omega_grad,
        z_grad, zsum[0:2], zsum[2:4], value, gamma, uh_t.T, wh_t.T, phi_t.T, up, down_t.T,
    )


def solution(mesh):
    placed = (
        P(("dp", "tensor"), None),
        P("tensor", None),
        P("tensor", None),
        P("tensor", None),
        P("tensor", None),
        P("tensor"),
        P(),
        P(),
        P(),
        P(None, "tensor"),
        P(None, "tensor"),
        P("tensor", None),
        P("tensor", None),
        P("tensor", None),
        P(None, "tensor"),
        P("tensor", None),
        P(("dp", "tensor"), None),
    )

    def per_device(tokens, *rest):
        whole_sequence = tokens.shape[0] == LEN and dict(mesh.shape) == {"dp": 16, "tensor": 2}
        return (one_sequence if whole_sequence else shards)(tokens, *rest)

    return jax.shard_map(
        per_device,
        mesh=mesh,
        in_specs=placed,
        out_specs=(
            P(("dp", "tensor"), None),
            P(("dp", "tensor"), None),
            P("tensor", None),
            P("tensor", None),
            P("tensor", None),
            P("tensor", None),
            P("tensor"),
            P("dp", None),
            P(),
            P(),
            P("dp", "tensor"),
            P("dp", "tensor"),
            P("tensor", "dp"),
            P("tensor", "dp"),
            P("tensor", "dp"),
            P("dp", "tensor"),
            P("tensor", "dp"),
        ),
        check_vma=False,
    )
```

```python
import math

import jax
import jax.numpy as jnp
from jax import lax
from jax.experimental import pallas as pl
from jax.experimental.pallas import tpu as pltpu
from jax.sharding import PartitionSpec as P

H = 16
LEN = 1024
ATT_BLOCK = 512
EMA_BLOCK = 128


norm_eps = 1e-06
masked_value = -1e30


def rms_rows(values_in):
    return values_in * lax.rsqrt(jnp.mean(values_in * values_in, axis=-1, keepdims=True) + norm_eps)


def matmul(left, right):
    return jnp.dot(left, right, preferred_element_type=jnp.float32)


def row_inner(left, right):
    return lax.dot_general(
        left, right, (((0,), (0,)), ((), ())), preferred_element_type=jnp.float32
    )


def col_inner(left, right):
    return lax.dot_general(
        left, right, (((1,), (1,)), ((), ())), preferred_element_type=jnp.float32
    )


def silu_slope(pre_act):
    logistic = jax.nn.sigmoid(pre_act)
    return logistic * (1.0 + pre_act * (1.0 - logistic))


def gate_apply(h_pre, f_pre, x_rows):
    update = jax.nn.sigmoid(f_pre)
    return update * jax.nn.silu(h_pre) + (1.0 - update) * x_rows


def ema_apply(signal, ema_params):
    alpha_logit, delta_logit, ema_beta, ema_eta, ema_omega = ema_params
    alpha_rate = jax.nn.sigmoid(alpha_logit)
    decay_rate = 1.0 - alpha_rate * jax.nn.sigmoid(delta_logit)
    feed_rate = alpha_rate * ema_beta
    log_decay = jnp.log(decay_rate)
    total_rows, chan_count = signal.shape
    seq_count = total_rows // LEN
    block_count = LEN // EMA_BLOCK
    blocks = signal.reshape(seq_count, block_count, EMA_BLOCK, chan_count)
    steps_in = jnp.arange(EMA_BLOCK, dtype=jnp.float32)
    lag_power = jnp.exp(steps_in[:, None, None] * log_decay[None])
    kernel = jnp.sum(lag_power * (feed_rate * ema_eta)[None], axis=-1)
    offsets = steps_in[:, None] - steps_in[None, :]
    lag_index = jnp.clip(offsets, 0, EMA_BLOCK - 1).astype(jnp.int32)
    toeplitz = jnp.where((offsets >= 0)[:, :, None], kernel[lag_index], 0.0)
    local_part = jnp.einsum("ijc,snjc->snic", toeplitz, blocks)
    tail_power = lag_power[::-1] * feed_rate[None]
    block_state = jnp.einsum("jch,snjc->snch", tail_power, blocks)
    full_decay = jnp.exp(EMA_BLOCK * log_decay)

    def carry_step(state_in, incoming):
        return (full_decay * state_in + incoming, state_in)

    zero_state = jnp.zeros((seq_count, chan_count, H), jnp.float32)
    _, start_state = lax.scan(carry_step, zero_state, jnp.moveaxis(block_state, 1, 0))
    start_state = jnp.moveaxis(start_state, 0, 1)
    head_power = lag_power * decay_rate[None] * ema_eta[None]
    carried = jnp.einsum("ich,snch->snic", head_power, start_state)
    ema_pre = (local_part + carried).reshape(total_rows, chan_count) + ema_omega * signal
    return jax.nn.silu(ema_pre)


def masked_scores(q_rows, k_rows, first_row):
    raw_scores = col_inner(q_rows, k_rows) * q_rows.shape[1] ** (-0.5)
    row_pos = first_row + jnp.arange(q_rows.shape[0])[:, None]
    col_pos = jnp.arange(k_rows.shape[0])[None, :]
    return jnp.where(col_pos <= row_pos, raw_scores, masked_value)


def attend_forward(query_low, key_low, value_low):
    total_rows, value_width = value_low.shape
    seq_count = total_rows // LEN
    per_seq = LEN // ATT_BLOCK

    def attend_one_block(flat_index):
        seq_id = flat_index // per_seq
        blk_id = flat_index % per_seq
        seq_start = seq_id * LEN
        q_rows = lax.dynamic_slice_in_dim(query_low, seq_start + blk_id * ATT_BLOCK, ATT_BLOCK, 0)
        k_rows = lax.dynamic_slice_in_dim(key_low, seq_start, LEN, 0)
        v_rows = lax.dynamic_slice_in_dim(value_low, seq_start, LEN, 0)
        scores = masked_scores(q_rows, k_rows, blk_id * ATT_BLOCK)
        top_score = jnp.max(scores, axis=-1, keepdims=True)
        weights = jnp.exp(scores - top_score)
        total_weight = jnp.sum(weights, axis=-1, keepdims=True)
        probs = (weights / total_weight).astype(jnp.bfloat16)
        return (matmul(probs, v_rows), top_score[:, 0] + jnp.log(total_weight[:, 0]))

    outs, lse_all = lax.map(attend_one_block, jnp.arange(seq_count * per_seq))
    return (outs.reshape(total_rows, value_width), lse_all.reshape(total_rows))


def attend_backward(query_low, key_low, value_low, lse_rows, d_att):
    total_rows, value_width = value_low.shape
    head_width = query_low.shape[1]
    seq_count = total_rows // LEN
    per_seq = LEN // ATT_BLOCK
    scale = head_width ** (-0.5)

    def one_seq(seq_id):
        seq_start = seq_id * LEN
        k_rows = lax.dynamic_slice_in_dim(key_low, seq_start, LEN, 0)
        v_rows = lax.dynamic_slice_in_dim(value_low, seq_start, LEN, 0)

        def one_one_block(carry_in, blk_id):
            d_keys, d_vals = carry_in
            row_start = seq_start + blk_id * ATT_BLOCK
            q_rows = lax.dynamic_slice_in_dim(query_low, row_start, ATT_BLOCK, 0)
            g_rows = lax.dynamic_slice_in_dim(d_att, row_start, ATT_BLOCK, 0)
            lse_part = lax.dynamic_slice_in_dim(lse_rows, row_start, ATT_BLOCK, 0)
            probs = jnp.exp(masked_scores(q_rows, k_rows, blk_id * ATT_BLOCK) - lse_part[:, None])
            d_probs = col_inner(g_rows, v_rows)
            d_scores = (
                probs * (d_probs - jnp.sum(probs * d_probs, axis=-1, keepdims=True))
            ).astype(jnp.bfloat16)
            d_rows = matmul(d_scores, k_rows) * scale
            d_keys = d_keys + row_inner(d_scores, q_rows) * scale
            d_vals = d_vals + row_inner(probs.astype(jnp.bfloat16), g_rows)
            return ((d_keys, d_vals), d_rows)

        start_carry = (
            jnp.zeros((LEN, head_width), jnp.float32),
            jnp.zeros((LEN, value_width), jnp.float32),
        )
        (d_keys, d_vals), d_rows = lax.scan(one_one_block, start_carry, jnp.arange(per_seq))
        return (d_rows.reshape(LEN, head_width), d_keys, d_vals)

    d_query, d_key, d_value = lax.map(one_seq, jnp.arange(seq_count))
    return (
        d_query.reshape(total_rows, head_width),
        d_key.reshape(total_rows, head_width),
        d_value.reshape(total_rows, value_width),
    )


def shards(
    tokens,
    alpha_logit,
    delta_logit,
    ema_beta,
    ema_eta,
    ema_omega,
    w_z,
    qk_gain,
    qk_bias,
    w_v,
    w_gamma,
    u_h,
    w_h,
    w_phi,
    w_up,
    w_down,
    cotangent,
):
    tensor_pos = lax.axis_index("tensor")
    feature_count = tokens.shape[1]
    chan_count = ema_omega.shape[0]
    chan_start = tensor_pos * chan_count
    x_rows = tokens.astype(jnp.float32)
    normed_rows, norm_pull = jax.vjp(rms_rows, x_rows)
    normed, cot_full = (
        lax.all_gather(normed_rows.astype(jnp.bfloat16), "tensor", axis=0, tiled=True),
        lax.all_gather(cotangent, "tensor", axis=0, tiled=True),
    )
    signal = lax.dynamic_slice_in_dim(normed, chan_start, chan_count, 1).astype(jnp.float32)
    ema_params = (alpha_logit, delta_logit, ema_beta, ema_eta, ema_omega)
    ema_val, ema_pull = jax.vjp(ema_apply, signal, ema_params)
    ema_low = ema_val.astype(jnp.bfloat16)
    ema_full = lax.all_gather(ema_low, "tensor", axis=1, tiled=True)
    z_pre = matmul(ema_full, w_z)
    z_act = jax.nn.silu(z_pre)
    query_low = (z_act * qk_gain[0] + qk_bias[0]).astype(jnp.bfloat16)
    key_low = (z_act * qk_gain[1] + qk_bias[1]).astype(jnp.bfloat16)
    values_pre = matmul(normed, w_v)
    value_low = jax.nn.silu(values_pre).astype(jnp.bfloat16)
    gamma_pre = matmul(ema_full, w_gamma)
    gamma_act = jax.nn.silu(gamma_pre)
    attended, lse_rows = attend_forward(query_low, key_low, value_low)
    gated_low = (gamma_act * attended).astype(jnp.bfloat16)
    both_pre = lax.psum_scatter(
        jnp.concatenate(
            [matmul(gated_low, u_h) + matmul(ema_low, w_h), matmul(ema_low, w_phi)], axis=1
        ),
        "tensor",
        scatter_dimension=0,
        tiled=True,
    )
    h_pre = both_pre[:, :feature_count]
    f_pre = both_pre[:, feature_count:]
    mixed, gate_pull = jax.vjp(gate_apply, h_pre, f_pre, x_rows)
    normed_two, norm_two_pull = jax.vjp(rms_rows, mixed)
    lowered = lax.all_gather(normed_two.astype(jnp.bfloat16), "tensor", axis=0, tiled=True)
    up_pre = matmul(lowered, w_up)
    hidden = jax.nn.silu(up_pre).astype(jnp.bfloat16)
    down_rows = lax.psum_scatter(
        matmul(hidden, w_down).astype(jnp.bfloat16), "tensor", scatter_dimension=0, tiled=True
    ).astype(jnp.float32)
    output = (mixed + down_rows).astype(jnp.bfloat16)
    cot_rows = cotangent.astype(jnp.float32)
    d_hidden = col_inner(cot_full, w_down)
    d_up = (d_hidden * silu_slope(up_pre)).astype(jnp.bfloat16)
    down_grad = row_inner(hidden, cot_full)
    up_grad = row_inner(lowered, d_up)
    d_lowered = lax.psum_scatter(col_inner(d_up, w_up), "tensor", scatter_dimension=0, tiled=True)
    d_mixed = cot_rows + norm_two_pull(d_lowered)[0]
    d_hpre, d_fpre, d_direct = gate_pull(d_mixed)
    h_full_grad, f_full_grad = (
        lax.all_gather(d_hpre.astype(jnp.bfloat16), "tensor", axis=0, tiled=True),
        lax.all_gather(d_fpre.astype(jnp.bfloat16), "tensor", axis=0, tiled=True),
    )
    uh_grad = row_inner(gated_low, h_full_grad)
    wh_grad = row_inner(ema_low, h_full_grad)
    phi_grad = row_inner(ema_low, f_full_grad)
    d_gated = col_inner(h_full_grad, u_h)
    d_att = (d_gated * gamma_act).astype(jnp.bfloat16)
    d_gamma = (d_gated * attended * silu_slope(gamma_pre)).astype(jnp.bfloat16)
    d_query, d_key, d_value = attend_backward(query_low, key_low, value_low, lse_rows, d_att)
    d_query, d_key = lax.psum((d_query, d_key), "tensor")
    d_z = (silu_slope(z_pre) * (d_query * qk_gain[0] + d_key * qk_gain[1])).astype(jnp.bfloat16)
    gain_grad = jnp.stack([jnp.sum(d_query * z_act, axis=0), jnp.sum(d_key * z_act, axis=0)])
    bias_grad = jnp.stack([jnp.sum(d_query, axis=0), jnp.sum(d_key, axis=0)])
    z_grad = row_inner(ema_full, d_z)
    gamma_grad = row_inner(ema_full, d_gamma)
    d_value_pre = (d_value * silu_slope(values_pre)).astype(jnp.bfloat16)
    value_grad = row_inner(normed, d_value_pre)
    d_chan = lax.psum_scatter(
        col_inner(d_gamma, w_gamma).astype(jnp.bfloat16), "tensor", scatter_dimension=1, tiled=True
    ).astype(jnp.float32)
    z_rows = lax.dynamic_slice_in_dim(w_z, chan_start, chan_count, 0)
    d_chan = (
        d_chan
        + col_inner(d_z, z_rows)
        + col_inner(h_full_grad, w_h)
        + col_inner(f_full_grad, w_phi)
    )
    d_signal, d_params = ema_pull(d_chan)
    d_norm_part = col_inner(d_value_pre, w_v)
    own_cols = lax.dynamic_slice_in_dim(d_norm_part, chan_start, chan_count, 1)
    d_norm_part = lax.dynamic_update_slice_in_dim(d_norm_part, own_cols + d_signal, chan_start, 1)
    d_normed = lax.psum_scatter(
        d_norm_part.astype(jnp.bfloat16), "tensor", scatter_dimension=0, tiled=True
    ).astype(jnp.float32)
    input_grad = d_direct + norm_pull(d_normed)[0]
    weight_totals = (
        lax.psum_scatter(z_grad.astype(jnp.bfloat16), "dp", scatter_dimension=0, tiled=True).astype(
            jnp.float32
        ),
        lax.psum_scatter(
            value_grad.astype(jnp.bfloat16), "dp", scatter_dimension=0, tiled=True
        ).astype(jnp.float32),
        lax.psum_scatter(
            gamma_grad.astype(jnp.bfloat16), "dp", scatter_dimension=0, tiled=True
        ).astype(jnp.float32),
        lax.psum_scatter(
            uh_grad.astype(jnp.bfloat16), "dp", scatter_dimension=1, tiled=True
        ).astype(jnp.float32),
        lax.psum_scatter(
            wh_grad.astype(jnp.bfloat16), "dp", scatter_dimension=1, tiled=True
        ).astype(jnp.float32),
        lax.psum_scatter(
            phi_grad.astype(jnp.bfloat16), "dp", scatter_dimension=1, tiled=True
        ).astype(jnp.float32),
        lax.psum_scatter(
            up_grad.astype(jnp.bfloat16), "dp", scatter_dimension=0, tiled=True
        ).astype(jnp.float32),
        lax.psum_scatter(
            down_grad.astype(jnp.bfloat16), "dp", scatter_dimension=1, tiled=True
        ).astype(jnp.float32),
    )
    param_totals = lax.psum(
        (d_params[0], d_params[1], d_params[2], d_params[3], d_params[4], gain_grad, bias_grad),
        "dp",
    )
    return (
        output,
        input_grad,
        param_totals[0],
        param_totals[1],
        param_totals[2],
        param_totals[3],
        param_totals[4],
        weight_totals[0],
        param_totals[5],
        param_totals[6],
        weight_totals[1],
        weight_totals[2],
        weight_totals[3],
        weight_totals[4],
        weight_totals[5],
        weight_totals[6],
        weight_totals[7],
    )


MIB = 1024 * 1024
BF = jnp.bfloat16
F32 = jnp.float32
ROWS = 256
hints = dict()
opt = dict(dn=0, m2=3, v2=4, z2=3, z1m=5)


def sds(shape, dtype=BF):
    return jax.ShapeDtypeStruct(shape, dtype)


def whole(shape):
    return pl.BlockSpec(shape, lambda i, s: (0,) * len(shape), pipeline_mode=pl.Buffered(1))


def rows_of(cols, rows=ROWS):
    return pl.BlockSpec((rows, cols), lambda i, s: (i, 0))


def cols_of(rows, cols):
    return pl.BlockSpec((rows, cols), lambda i, s: (0, i))


def run(body, grid, scal, ins, in_specs, out_shape, out_specs, scratch=(), flops=0, name=None, aliases=None, spare=12):
    moved = sum(a.size * a.dtype.itemsize for a in ins)
    moved += sum(math.prod(o.shape) * jnp.dtype(o.dtype).itemsize for o in out_shape)
    def held_bytes(spec, a):
        if spec.block_shape is None:
            return 0
        return math.prod(spec.block_shape) * jnp.dtype(a.dtype).itemsize * (1 if spec.pipeline_mode else 2)

    if name in ("attend", "gate", "ffn", "mid_back", "pack_params", "ema_params", "pieces"):
        spare = 56
    vmem = sum(map(held_bytes, in_specs, ins)) + sum(map(held_bytes, out_specs, out_shape))
    vmem += sum(math.prod(r.shape) * jnp.dtype(r.dtype).itemsize for r in scratch if r.memory_space == pltpu.VMEM)
    return pl.pallas_call(
        body,
        out_shape=out_shape,
        grid_spec=pltpu.PrefetchScalarGridSpec(
            num_scalar_prefetch=1,
            grid=grid,
            in_specs=in_specs,
            out_specs=out_specs,
            scratch_shapes=list(scratch),
        ),
        compiler_params=pltpu.CompilerParams(vmem_limit_bytes=min(vmem + spare * MIB, 56 * MIB)),
        cost_estimate=pl.CostEstimate(flops=int(flops * hints.get(name, 10)), bytes_accessed=int(moved * hints.get(name, 10)), transcendentals=0),
        name=name,
        input_output_aliases=aliases or {},
    )(scal, *ins)


def sig(u):
    return 0.5 + 0.5 * jnp.tanh(0.5 * u)


def silu_pair(u):
    s = sig(u)
    return u * s, s * (1.0 + u * (1.0 - s))


def place(scr, s, pieces, base=0, table=0):
    rows = pieces[0].shape[0]
    for p in range(4):
        scr[pl.ds(pl.multiple_of(base + s[table + p] * rows, rows), rows), :] = pieces[p][...]


def piece_block(rows, cols, row_block):
    return pl.BlockSpec((rows, cols), lambda i, s: (row_block, i))


def piece_whole(rows, cols, row_block):
    return pl.BlockSpec((rows, cols), lambda i, s: (row_block, 0), pipeline_mode=pl.Buffered(1))


def k_value_own(scal, tokens, w_own):
    n, d = tokens.shape
    cols = w_own.shape[1]
    tn = 512

    def body(s, x_ref, w_ref, n_ref, v_ref, sl_ref):
        @pl.when(pl.program_id(0) == 0)
        def _():
            x = x_ref[...].astype(F32)
            n_ref[...] = (x * lax.rsqrt(jnp.mean(x * x, axis=-1, keepdims=True) + norm_eps)).astype(BF)

        act, slope = silu_pair(matmul(n_ref[...], w_ref[...]))
        v_ref[...] = act.astype(BF)
        sl_ref[...] = slope.astype(BF)

    return run(
        body, (cols // tn,), scal, [tokens, w_own],
        [whole((n, d)), cols_of(d, tn)],
        [sds((n, d)), sds((n, cols)), sds((n, cols))],
        [pl.BlockSpec((n, d), lambda i, s: (0, 0)), cols_of(n, tn), cols_of(n, tn)],
        flops=2 * n * d * cols, name="value_own",
    )


def k_act_own(scal, x, w_own, tn):
    n, d = x.shape
    cols = w_own.shape[1]

    def body(s, x_ref, w_ref, v_ref, sl_ref):
        act, slope = silu_pair(matmul(x_ref[...], w_ref[...]))
        v_ref[...] = act.astype(BF)
        sl_ref[...] = slope.astype(BF)

    return run(
        body, (cols // tn,), scal, [x, w_own],
        [whole((n, d)), cols_of(d, tn)],
        [sds((n, cols)), sds((n, cols))],
        [cols_of(n, tn), cols_of(n, tn)],
        flops=2 * n * d * cols, name="act_own",
    )


def k_act_other(scal, x, pieces, table, tn):
    n, d = x.shape
    rows, cols = pieces[0].shape

    def body(s, x_ref, p0, p1, p2, p3, v_ref, sl_ref, w_scr):
        place(w_scr, s, (p0, p1, p2, p3), table=table)
        act, slope = silu_pair(matmul(x_ref[...], w_scr[...]))
        v_ref[...] = act.astype(BF)
        sl_ref[...] = slope.astype(BF)

    return run(
        body, (cols // tn,), scal, [x, *pieces],
        [whole((n, d))] + [piece_block(rows, tn, 0)] * 4,
        [sds((n, cols)), sds((n, cols))],
        [cols_of(n, tn), cols_of(n, tn)],
        [pltpu.VMEM((d, tn), BF)],
        flops=2 * n * d * cols, name="act_other",
    )


def k_query_key(scal, ema_low, w_z, qk_gain, qk_bias):
    n, d = ema_low.shape
    zw = w_z.shape[1]

    def body(s, e_ref, w_ref, g_ref, b_ref, z_ref, q_ref, k_ref):
        z_pre = matmul(e_ref[...], w_ref[...])
        z_ref[...] = z_pre
        act = z_pre * sig(z_pre)
        q_ref[...] = (act * g_ref[0:1, :] + b_ref[0:1, :]).astype(BF)
        k_ref[...] = (act * g_ref[1:2, :] + b_ref[1:2, :]).astype(BF)

    return run(
        body, (2,), scal, [ema_low, w_z, qk_gain, qk_bias],
        [rows_of(d, n // 2), whole((d, zw)), whole((2, zw)), whole((2, zw))],
        [sds((n, zw), F32), sds((n, zw)), sds((n, zw))],
        [rows_of(zw, n // 2)] * 3,
        flops=2 * n * d * zw, name="query_key",
    )


def k_pack_params(scal, arrays, omega):
    ch = omega.shape[1]

    def body(s, a0, a1, a2, a3, w_ref, o_ref):
        for i, ref in enumerate((a0, a1, a2, a3)):
            o_ref[i * H : (i + 1) * H, :] = ref[...]
        o_ref[4 * H : 4 * H + 8, :] = jnp.broadcast_to(w_ref[...], (8, ch))

    return run(
        body, (1,), scal, [*arrays, omega], [whole((H, ch))] * 4 + [whole((1, ch))],
        [sds((4 * H + 8, ch), F32)], [pl.BlockSpec((4 * H + 8, ch), lambda i, s: (0, 0))], flops=1e7, name="pack_params",
    )[0]


def k_ema_params(scal, own, oth):
    height, ch = own.shape
    groups = 2 * ch // 128

    def body(s, own_ref, oth_ref, dec_ref, cf_ref, om_ref):
        for j in range(2):
            for src, ref in ((0, own_ref), (1, oth_ref)):

                @pl.when(s[6 + src] == j)
                def _(j=j, ref=ref):
                    v = ref[...]
                    rate = sig(v[0:H])
                    dec = 1.0 - rate * sig(v[H : 2 * H])
                    cf = rate * v[2 * H : 3 * H] * v[3 * H : 4 * H]
                    for g in range(groups // 2):
                        lanes = slice(g * 128, (g + 1) * 128)
                        at = j * (groups // 2) + g
                        dec_ref[pl.ds(at, H, stride=groups), :] = dec[:, lanes]
                        cf_ref[pl.ds(at, H, stride=groups), :] = cf[:, lanes]
                        om_ref[at : at + 1, :] = v[4 * H : 4 * H + 1, lanes]

    par = (H * groups, 128)
    return run(
        body, (1,), scal, [own, oth], [whole((height, ch))] * 2,
        [sds(par, F32), sds(par, F32), sds((groups, 128), F32)],
        [pl.BlockSpec(par, lambda i, s: (0, 0))] * 2 + [pl.BlockSpec((groups, 128), lambda i, s: (0, 0))],
        flops=1e8, name="ema_params",
    )


def k_pieces(scal, takes):
    parts = [(w, at) for take in takes for w, at in take]

    def body(s, *refs):
        ins, outs = refs[: len(parts)], refs[len(parts) :]
        n = 0
        for take, out in zip(takes, outs):
            low = 0
            for w, _ in take:
                rows = w.shape[0] // 4
                out[low : low + rows, :] = ins[n][...]
                low += rows
                n += 1

    return run(
        body, (1,), scal, [w for w, _ in parts],
        [pl.BlockSpec((w.shape[0] // 4, w.shape[1]), lambda i, s, at=at: (s[at], 0)) for w, at in parts],
        [sds((sum(w.shape[0] // 4 for w, _ in take), take[0][0].shape[1])) for take in takes],
        [pl.BlockSpec((sum(w.shape[0] // 4 for w, _ in take), take[0][0].shape[1]), lambda i, s: (0, 0)) for take in takes],
        flops=1e7, name="pieces",
    )


def k_ema_forward(scal, normed, decay, coef, omega, first, count, before=None):
    n, d = normed.shape
    groups = d // 128
    tb = 128

    def body(s, x_ref, dec_ref, cf_ref, om_ref, *refs):
        e_ref, sl_ref, st, xs, ys = refs[-5:]

        @pl.when(pl.program_id(0) == 0)
        def _():
            st[...] = refs[0][...] if before else jnp.zeros_like(st)

        for g in range(groups):
            xs[pl.ds(g, tb, stride=groups), :] = x_ref[:, g * 128 : (g + 1) * 128].astype(F32)
        dec = [dec_ref[k * groups : (k + 1) * groups, :] for k in range(H)]
        cf = [cf_ref[k * groups : (k + 1) * groups, :] for k in range(H)]
        om = om_ref[...]

        def steps(b, carry):
            states = list(carry)
            for u in range(16):
                row = pl.multiple_of((b * 16 + u) * groups, groups)
                xt = xs[pl.ds(row, groups), :]
                parts = [om * xt, None, None, None]
                for k in range(H):
                    states[k] = dec[k] * states[k] + xt
                    term = cf[k] * states[k]
                    parts[k % 4] = term if parts[k % 4] is None else parts[k % 4] + term
                ys[pl.ds(row, groups), :] = (parts[0] + parts[1]) + (parts[2] + parts[3])
            return tuple(states)

        start = tuple(st[k * groups : (k + 1) * groups, :] for k in range(H))
        end = lax.fori_loop(0, tb // 16, steps, start)
        for k in range(H):
            st[k * groups : (k + 1) * groups, :] = end[k]
        for g in range(groups):
            act, slope = silu_pair(ys[pl.ds(g, tb, stride=groups), :])
            e_ref[:, g * 128 : (g + 1) * 128] = act.astype(BF)
            sl_ref[:, g * 128 : (g + 1) * 128] = slope.astype(BF)

    par = (H * groups, 128)
    at = pl.BlockSpec((tb, d), lambda i, s: (first + i, 0))
    more = list(before) if before else []
    return run(
        body, (count,), scal, [normed, decay, coef, omega, *more],
        [at, whole(par), whole(par), whole((groups, 128))]
        + ([whole(par), pl.BlockSpec(memory_space=pltpu.HBM), pl.BlockSpec(memory_space=pltpu.HBM)] if before else []),
        [sds((n, d)), sds((n, d)), sds(par, F32)],
        [at, at, pl.BlockSpec(par, lambda i, s: (0, 0))],
        [pltpu.VMEM((tb * groups, 128), F32), pltpu.VMEM((tb * groups, 128), F32)],
        flops=2.5e9 * count, name="ema_forward", aliases={6: 0, 7: 1} if before else {},
    )


def k_ema_backward(scal, normed, de_part, dz, slope, w_z, decay, coef, omega, first, count, before=None):
    n, d = normed.shape
    groups = d // 128
    tb = 128
    nb = n // tb
    half = H // 2
    gh = groups * half
    zw = dz.shape[1]

    def body(s, x_ref, de_ref, z_ref, sl_ref, wz_ref, dec_ref, cf_ref, om_ref, *refs):
        o_ref, back, deriv, a_ref, b_ref, w_ref, xs, gs, ys = refs[-9:]

        @pl.when(pl.program_id(0) == 0)
        def _():
            for i, ref in enumerate((back, deriv, a_ref, b_ref, w_ref)):
                ref[...] = refs[i][...] if before else jnp.zeros_like(ref)

        d_e = (de_ref[...].astype(F32) + col_inner(z_ref[...], wz_ref[...])) * sl_ref[...].astype(F32)
        for g in range(groups):
            xs[pl.ds(g, tb, stride=groups), :] = x_ref[:, g * 128 : (g + 1) * 128].astype(F32)
            gs[pl.ds(g, tb, stride=groups), :] = d_e[:, g * 128 : (g + 1) * 128]

        for part in range(2):
            low = part * gh
            at = [slice(low + k * groups, low + (k + 1) * groups) for k in range(half)]
            dec = [dec_ref[a, :] for a in at]

            def steps(b, carry, part=part, at=at, dec=dec):
                bk, dv, aa, bb, ww = (list(c) for c in carry)
                for u in range(8):
                    row = pl.multiple_of((tb - 1 - (b * 8 + u)) * groups, groups)
                    xt = xs[pl.ds(row, groups), :]
                    gt = gs[pl.ds(row, groups), :]
                    if part == 0:
                        outs = [om_ref[...] * gt, None]
                        ww[0] = ww[0] + xt * gt
                    else:
                        outs = [ys[pl.ds(row, groups), :], None]
                    for k in range(half):
                        dv[k] = dec[k] * dv[k] + bk[k]
                        bk[k] = dec[k] * bk[k] + gt
                        term = cf_ref[at[k], :] * bk[k]
                        outs[k % 2] = term if outs[k % 2] is None else outs[k % 2] + term
                        aa[k] = aa[k] + xt * bk[k]
                        bb[k] = bb[k] + xt * dv[k]
                    ys[pl.ds(row, groups), :] = outs[0] + outs[1]
                return tuple(bk), tuple(dv), tuple(aa), tuple(bb), tuple(ww)

            start = (
                tuple(back[a, :] for a in at),
                tuple(deriv[a, :] for a in at),
                tuple(a_ref[a, :] for a in at),
                tuple(b_ref[a, :] for a in at),
                (w_ref[...],),
            )
            bk, dv, aa, bb, ww = lax.fori_loop(0, tb // 8, steps, start)
            for k in range(half):
                back[at[k], :] = bk[k]
                deriv[at[k], :] = dv[k]
                a_ref[at[k], :] = aa[k]
                b_ref[at[k], :] = bb[k]
            w_ref[...] = ww[0]
        for g in range(groups):
            o_ref[:, g * 128 : (g + 1) * 128] = ys[pl.ds(g, tb, stride=groups), :]

    top = nb - 1 - first
    back_rows = pl.BlockSpec((tb, d), lambda i, s: (top - i, 0))
    par = (H * groups, 128)
    const = pl.BlockSpec(par, lambda i, s: (0, 0))
    small = (groups, 128)
    more = [*before[1:], before[0]] if before else []
    return run(
        body, (count,), scal, [normed, de_part, dz, slope, w_z, decay, coef, omega, *more],
        [back_rows, back_rows, pl.BlockSpec((tb, zw), lambda i, s: (top - i, 0)), back_rows, whole((d, zw)),
         whole(par), whole(par), whole(small)]
        + ([whole(par)] * 4 + [whole(small), pl.BlockSpec(memory_space=pltpu.HBM)] if before else []),
        [sds((n, d), F32)] + [sds(par, F32)] * 4 + [sds(small, F32)],
        [back_rows, const, const, const, const, pl.BlockSpec(small, lambda i, s: (0, 0))],
        [pltpu.VMEM((tb * groups, 128), F32)] * 3,
        flops=5e9 * count, name="ema_backward", aliases={14: 0} if before else {},
    )


def k_attend(scal, q, k, v_own, v_oth, ema_low, g_own, packs):
    n, zw = q.shape
    d, half = g_own.shape
    rp = packs[0].shape[0]
    blocks = n // ROWS
    scale = zw ** (-0.5)

    def body(s, q_ref, k_ref, vo, vt, e_ref, wo, w0, w1, w2, w3, gated_o, gated_t, go, gt, mo, mt, p_ref, w_scr):
        @pl.when(pl.program_id(0) == 0)
        def _():
            place(w_scr, s, (w0, w1, w2, w3), table=8)

        for i in range(blocks):

            @pl.when(pl.program_id(0) == i)
            def _(i=i):
                seen = (i + 1) * ROWS
                sc = col_inner(q_ref[...], k_ref[0:seen, :]) * scale
                row = i * ROWS + lax.broadcasted_iota(jnp.int32, (ROWS, seen), 0)
                col = lax.broadcasted_iota(jnp.int32, (ROWS, seen), 1)
                sc = jnp.where(col <= row, sc, masked_value)
                e = jnp.exp(sc - jnp.max(sc, axis=-1, keepdims=True))
                p = (e * (1.0 / jnp.sum(e, axis=-1, keepdims=True))).astype(BF)
                p_ref[:, 0:seen] = p
                if seen < n:
                    p_ref[:, seen:] = jnp.zeros((ROWS, n - seen), BF)
                for v_ref, w, gated, g, m in ((vo, wo, gated_o, go, mo), (vt, w_scr, gated_t, gt, mt)):
                    act, slope = silu_pair(matmul(e_ref[...], w[...]))
                    att = matmul(p, v_ref[0:seen, :])
                    gated[...] = (act * att).astype(BF)
                    g[...] = act.astype(BF)
                    m[...] = (slope * att).astype(BF)

    return run(
        body, (blocks,), scal, [q, k, v_own, v_oth, ema_low, g_own, *packs],
        [rows_of(zw), whole((n, zw)), whole((n, half)), whole((n, half)), rows_of(d), whole((d, half))]
        + [whole((rp, half))] * 4,
        [sds((n, half))] * 6 + [sds((n, n))],
        [rows_of(half)] * 6 + [rows_of(n)],
        [pltpu.VMEM((d, half), BF)],
        flops=n * n * (zw + 2 * half) * 1.25 + 4 * n * d * half, name="attend",
    )


def k_gate(scal, gated_own, gated_oth, ema_low, tokens, u_own, h_own, f_own, packs_u, packs_h):
    n, d = tokens.shape
    half = u_own.shape[0]
    ch = h_own.shape[0]
    ru, rh = packs_u[0].shape[0], packs_h[0].shape[0] // 2

    def body(s, go, gt, e_ref, x_ref, uo, ho, fo, u0, u1, u2, u3, h0, h1, h2, h3, f0, f1, f2, f3,
             mix_ref, low_ref, a_ref, b_ref, up_ref, u_scr, h_scr, f_scr):
        @pl.when(pl.program_id(0) == 0)
        def _():
            place(u_scr, s, (u0, u1, u2, u3))
            own = pl.multiple_of(s[6] * ch, ch)
            oth = s[7] * ch
            h_scr[pl.ds(own, ch), :] = ho[...]
            f_scr[pl.ds(own, ch), :] = fo[...]
            place(h_scr, s, (h0, h1, h2, h3), oth, 8)
            place(f_scr, s, (f0, f1, f2, f3), oth, 8)

        h_pre = matmul(go[...], uo[...]) + matmul(gt[...], u_scr[...]) + matmul(e_ref[...], h_scr[...])
        f_pre = matmul(e_ref[...], f_scr[...])
        x = x_ref[...].astype(F32)
        act, slope = silu_pair(h_pre)
        update = sig(f_pre)
        mixed = update * act + (1.0 - update) * x
        mix_ref[...] = mixed.astype(BF)
        low_ref[...] = (mixed * lax.rsqrt(jnp.mean(mixed * mixed, axis=-1, keepdims=True) + norm_eps)).astype(BF)
        a_ref[...] = (update * slope).astype(BF)
        b_ref[...] = ((act - x) * update * (1.0 - update)).astype(BF)
        up_ref[...] = (1.0 - update).astype(BF)

    ins = [gated_own, gated_oth, ema_low, tokens, u_own, h_own, f_own, *packs_u, *packs_h, *packs_h]
    specs = [rows_of(half), rows_of(half), rows_of(d), rows_of(d), whole((half, d)), whole((ch, d)), whole((ch, d))]
    specs += [piece_whole(ru, d, 0)] * 4 + [piece_whole(rh, d, 0)] * 4 + [piece_whole(rh, d, 1)] * 4
    return run(
        body, (n // ROWS,), scal, ins, specs,
        [sds((n, d))] * 5,
        [rows_of(d)] * 5,
        [pltpu.VMEM((half, d), BF), pltpu.VMEM((2 * ch, d), BF), pltpu.VMEM((2 * ch, d), BF)],
        flops=2 * n * d * (2 * half + 4 * ch), name="gate",
    )


def split_rows(s, grad):
    d, c = grad.shape
    by_x = grad.reshape(4, 2, d // 8, c)
    flip = s[12] == 0
    a, b = by_x[:, 0].reshape(d // 2, c), by_x[:, 1].reshape(d // 2, c)
    return jnp.where(flip, a, b), jnp.where(flip, b, a)


def put_rows(s, ref, value, lead=(), add=None):
    rows = value.shape[0] // 4
    for z in range(4):
        at = pl.ds(pl.multiple_of((s[13] ^ z) * rows, rows), rows)
        part = value[z * rows : (z + 1) * rows]
        if add is not None:
            part = part + add[0][(*add[1], at, slice(None))].astype(F32)
        ref[(*lead, at, slice(None))] = part.astype(BF)


def k_ffn(scal, lowered, cot, up, down, part, before=None, form="sent"):
    n, d = lowered.shape
    pieces = len(up) > 1
    tn = up[0].shape[1] // 4
    rows = d // 2

    def body(s, low_ref, c_ref, *refs):
        step = pl.program_id(0)
        nu = len(up)
        ups, wd, refs = refs[:nu], refs[nu], refs[nu + 1 :]
        if before:
            ins, refs = refs[:2], refs[2:]
            held, sems = refs[-2:]
            refs = refs[:-2]
            copies = [pltpu.make_async_copy(ins[i], held.at[i], sems.at[i]) for i in range(2)]
        out_ref, gl_ref, *grads, acc, gl, u_scr = refs
        if pieces:
            place(u_scr, s, ups)
            wu = u_scr
        else:
            wu = ups[0]

        def work(wd, i):
            if before and i == 0:
                for c in copies:
                    c.start()
            act, slope = silu_pair(matmul(low_ref[...], wu[...]))
            hid = act.astype(BF)
            out = matmul(hid, wd[...])
            du = (col_inner(c_ref[...], wd[...]) * slope).astype(BF)
            back = col_inner(du, wu[...])
            if i == 0:
                acc[...] = out
                gl[...] = back
            else:
                if before:
                    for c in copies:
                        c.wait()
                    out = out + held[0].astype(F32)
                    back = back + held[1].astype(F32)
                out_ref[...] = (acc[...] + out).astype(BF)
                gl_ref[...] = (gl[...] + back).astype(BF)
            for k, grad in enumerate((row_inner(c_ref[...], hid), row_inner(low_ref[...], du))):
                for j, rows_j in enumerate(split_rows(s, grad)):
                    if form == "sent":
                        put_rows(s, grads[0], rows_j, (k, j))
                    elif form == "own" or k == 0:
                        put_rows(s, grads[2 * k + j], rows_j)
                    else:
                        put_rows(s, grads[2], rows_j, (j,))

        for i in range(2):

            @pl.when(step == i)
            def _(i=i):
                work(wd, i)

    if pieces:
        down = [down[part]]
        specs = [pl.BlockSpec((d // 4, tn), lambda i, s: (0, s[4 + part] * 2 + i))] * 4
        specs += [pl.BlockSpec((tn, d), lambda i, s: (i, 0))]
    else:
        specs = [
            pl.BlockSpec((d, tn), lambda i, s: (0, s[4 + part] * 2 + i)),
            pl.BlockSpec((tn, d), lambda i, s: (s[4 + part] * 2 + i, 0)),
        ]
    still = pl.BlockSpec((n, d), lambda i, s: (0, 0))
    one = pl.BlockSpec((rows, tn), lambda i, s: (0, i))
    two = pl.BlockSpec((2, rows, tn), lambda i, s: (0, 0, i))
    four = pl.BlockSpec((2, 2, rows, tn), lambda i, s: (0, 0, 0, i))
    grad_specs = dict(sent=[four], own=[one] * 4, other=[one, one, two])[form]
    grad_shapes = [sds((*g.block_shape[:-1], 2 * tn)) for g in grad_specs]
    more = list(before) if before else []
    return run(
        body, (2,), scal, [lowered, cot, *up, *down, *more],
        [whole((n, d)), whole((n, d))] + specs + [pl.BlockSpec(memory_space=pltpu.HBM)] * len(more),
        [sds((n, d)), sds((n, d)), *grad_shapes],
        [still, still, *grad_specs],
        [pltpu.VMEM((n, d), F32), pltpu.VMEM((n, d), F32), pltpu.VMEM((d, tn), BF)]
        + ([pltpu.VMEM((2, n, d), BF), pltpu.SemaphoreType.DMA((2,))] if before else []),
        flops=24 * n * d * tn, name="ffn",
    )


def k_mid_back(scal, dl, acc, cot, mixed, fac_h, fac_f, keep, g_own, g_oth, m_own, m_oth,
               u_own, wg_own, h_own, f_own, packs_g, packs_u, packs_h):
    n, d = cot.shape
    half = u_own.shape[0]
    ch = h_own.shape[0]
    ru, rh = packs_u[0].shape[0], packs_h[0].shape[0] // 2
    rg = packs_g[0].shape[0]

    def body(s, l_ref, acc_ref, c_ref, x_ref, a_ref, b_ref, k_ref, go, gt, mo, mt, uo, wo, ho, fo,
             w0, w1, w2, w3, u0, u1, u2, u3, h0, h1, h2, h3, f0, f1, f2, f3,
             out_ref, dh_ref, df_ref, dir_ref, ao, at, do, dt, de_ref, u_scr, w_scr, h_scr, f_scr):
        @pl.when(pl.program_id(0) == 0)
        def _():
            place(u_scr, s, (u0, u1, u2, u3))
            place(w_scr, s, (w0, w1, w2, w3), table=8)
            own = pl.multiple_of(s[6] * ch, ch)
            oth = s[7] * ch
            h_scr[pl.ds(own, ch), :] = ho[...]
            f_scr[pl.ds(own, ch), :] = fo[...]
            place(h_scr, s, (h0, h1, h2, h3), oth, 8)
            place(f_scr, s, (f0, f1, f2, f3), oth, 8)

        dl = l_ref[...].astype(F32)
        m = x_ref[...].astype(F32)
        out_ref[...] = (m + acc_ref[...].astype(F32)).astype(BF)
        r = lax.rsqrt(jnp.mean(m * m, axis=-1, keepdims=True) + norm_eps)
        n2 = m * r
        dm = c_ref[...].astype(F32) + r * (dl - n2 * jnp.mean(dl * n2, axis=-1, keepdims=True))
        dh = (dm * a_ref[...].astype(F32)).astype(BF)
        df = (dm * b_ref[...].astype(F32)).astype(BF)
        dh_ref[...] = dh
        df_ref[...] = df
        dir_ref[...] = (dm * k_ref[...].astype(F32)).astype(BF)
        de = col_inner(dh, h_scr[...]) + col_inner(df, f_scr[...])
        for u, w, g_ref, m_ref, a_out, d_out in ((uo, wo, go, mo, ao, do), (u_scr, w_scr, gt, mt, at, dt)):
            dg = col_inner(dh, u[...])
            a_out[...] = (dg * g_ref[...].astype(F32)).astype(BF)
            low = (dg * m_ref[...].astype(F32)).astype(BF)
            d_out[...] = low
            de = de + col_inner(low, w[...])
        de_ref[...] = de.astype(BF)

    ins = [dl, acc, cot, mixed, fac_h, fac_f, keep, g_own, g_oth, m_own, m_oth, u_own, wg_own, h_own, f_own]
    ins += [*packs_g, *packs_u, *packs_h, *packs_h]
    specs = [rows_of(d)] * 7 + [rows_of(half)] * 4
    specs += [whole((half, d)), whole((d, half)), whole((ch, d)), whole((ch, d))]
    specs += [piece_whole(rg, half, 0)] * 4 + [piece_whole(ru, d, 0)] * 4
    specs += [piece_whole(rh, d, 0)] * 4 + [piece_whole(rh, d, 1)] * 4
    return run(
        body, (n // ROWS,), scal, ins, specs,
        [sds((n, d))] * 4 + [sds((n, half))] * 4 + [sds((n, d))],
        [rows_of(d)] * 4 + [rows_of(half)] * 4 + [rows_of(d)],
        [pltpu.VMEM((half, d), BF), pltpu.VMEM((d, half), BF), pltpu.VMEM((2 * ch, d), BF), pltpu.VMEM((2 * ch, d), BF)],
        flops=2 * n * d * (4 * half + 4 * ch), name="mid_back",
    )


def k_attend_back(scal, p, da_own, da_oth, v_own, v_oth, vs_own, vs_oth, q, k, z_pre, gain):
    n, zw = q.shape
    half = da_own.shape[1]
    blocks = n // ROWS
    scale = zw ** (-0.5)

    def body(s, p_ref, ao, at, vo, vt, so, st, q_ref, k_ref, z_ref, g_ref, oo, ot, dz_ref, sum_ref, dvo, dvt, dks):
        for step, i in enumerate(reversed(range(blocks))):

            @pl.when(pl.program_id(0) == step)
            def _(i=i):
                seen = (i + 1) * ROWS
                lo = i * ROWS
                last = i == blocks - 1
                pb = p_ref[:, 0:seen]
                pr = pb.astype(F32)
                dp = col_inner(ao[...], vo[0:seen, :]) + col_inner(at[...], vt[0:seen, :])
                ds = (pr * (dp - jnp.sum(pr * dp, axis=-1, keepdims=True))).astype(BF)
                dq = matmul(ds, k_ref[0:seen, :]) * scale
                dk = row_inner(ds, q_ref[...]) * scale
                if not last:
                    dk = dk + dks[0:seen, :]
                for a_ref, acc, sl, o_ref in ((ao, dvo, so, oo), (at, dvt, st, ot)):
                    dv = row_inner(pb, a_ref[...])
                    if not last:
                        dv = dv + acc[0:seen, :]
                    if i:
                        acc[0:lo, :] = dv[0:lo]
                    o_ref[...] = (dv[lo:seen] * sl[...].astype(F32)).astype(BF)
                if i:
                    dks[0:lo, :] = dk[0:lo]
                dk = dk[lo:seen]
                act, slope = silu_pair(z_ref[...])
                dz_ref[...] = (slope * (dq * g_ref[0:1, :] + dk * g_ref[1:2, :])).astype(BF)
                for j, v in enumerate((dq * act, dk * act, dq, dk)):
                    part = jnp.sum(v, axis=0, keepdims=True)
                    sum_ref[j : j + 1, :] = part if last else sum_ref[j : j + 1, :] + part
                if last:
                    sum_ref[4:8, :] = jnp.zeros((4, zw), F32)

    def back_rows(cols):
        return pl.BlockSpec((ROWS, cols), lambda i, s: (blocks - 1 - i, 0))

    low = n - ROWS
    return run(
        body, (blocks,), scal, [p, da_own, da_oth, v_own, v_oth, vs_own, vs_oth, q, k, z_pre, gain],
        [back_rows(n), back_rows(half), back_rows(half), whole((n, half)), whole((n, half)), back_rows(half),
         back_rows(half), back_rows(zw), whole((n, zw)), back_rows(zw), whole((2, zw))],
        [sds((n, half)), sds((n, half)), sds((n, zw)), sds((8, zw), F32)],
        [back_rows(half), back_rows(half), back_rows(zw), pl.BlockSpec((8, zw), lambda i, s: (0, 0))],
        [pltpu.VMEM((low, half), F32), pltpu.VMEM((low, half), F32), pltpu.VMEM((low, zw), F32)],
        flops=n * n * 4 * half * 1.25, name="attend_back",
    )


def k_input_back(scal, dv_own, dv_oth, w_own, packs, d_sig, tokens, direct, first, count, before=None):
    n, d = tokens.shape
    rp = packs[0].shape[0]
    half = dv_own.shape[1]

    def body(s, vo, vt, wo, w0, w1, w2, w3, sg, x_ref, dir_ref, *refs):
        o_ref, w_scr = refs[-2:]

        @pl.when(pl.program_id(0) == 0)
        def _():
            place(w_scr, s, (w0, w1, w2, w3))

        dn = col_inner(vo[...], wo[...]) + col_inner(vt[...], w_scr[...]) + sg[...]
        x = x_ref[...].astype(F32)
        r = lax.rsqrt(jnp.mean(x * x, axis=-1, keepdims=True) + norm_eps)
        n1 = x * r
        o_ref[...] = dir_ref[...].astype(F32) + r * (dn - n1 * jnp.mean(dn * n1, axis=-1, keepdims=True))

    def at(cols):
        return pl.BlockSpec((ROWS, cols), lambda i, s: (first + i, 0))

    more = [before] if before is not None else []
    return run(
        body, (count,), scal, [dv_own, dv_oth, w_own, *packs, d_sig, tokens, direct, *more],
        [at(half), at(half), whole((d, half))] + [piece_whole(rp, half, 0)] * 4 + [at(d)] * 3
        + [pl.BlockSpec(memory_space=pltpu.HBM)] * len(more),
        [sds((n, d), F32)], [at(d)],
        [pltpu.VMEM((d, half), BF)],
        flops=4 * ROWS * count * d * half, name="input_back", aliases={11: 0} if more else {},
    )[0]


def k_weight_mid(scal, ema_low, left, right_own, right_oth, gate, part, got=None):
    n, d = ema_low.shape
    tn = d // 4
    rows = d // 2

    def body(s, *refs):
        if gate:
            e_ref, *refs = refs
        l_ref, ro, rt, eo, et, *refs = refs
        for i in range(3):

            @pl.when(pl.program_id(0) == i)
            def _(i=i):
                for k, (r, e) in enumerate(((ro, eo), (rt, et))):
                    lhs = e_ref if gate and i < 2 else l_ref
                    grad = split_rows(s, row_inner(lhs[...], r[...] if i < 2 else e[...]))
                    for j in range(2):
                        if got is None:
                            put_rows(s, refs[0], grad[j], (k, j))
                        elif gate:
                            put_rows(s, refs[1 + k], grad[j], (j,), (refs[0], (k, j)))
                        else:
                            put_rows(s, refs[2 - j], grad[j], (k,), (refs[0], (k, j)))

    at = pl.BlockSpec((n, tn), lambda i, s: (0, s[part] * 2 + jnp.minimum(i, 1)))
    e_own = pl.BlockSpec((n, tn), lambda i, s: (0, s[6] * 2 + s[part]), pipeline_mode=pl.Buffered(1))
    e_oth = pl.BlockSpec((n, tn), lambda i, s: (0, s[7] * 2 + s[part]), pipeline_mode=pl.Buffered(1))
    four = pl.BlockSpec((2, 2, rows, tn), lambda i, s: (0, 0, 0, i))
    two = pl.BlockSpec((2, rows, tn), lambda i, s: (0, 0, i))
    adds = [got] if got is not None else []
    lead = [ema_low] if gate else []
    return run(
        body, (3,), scal, [*lead, left, right_own, right_oth, ema_low, ema_low] + adds,
        [whole((n, d))] * (1 + len(lead)) + [at] * 2 + [e_own, e_oth] + [four] * len(adds),
        [sds((2, rows, 3 * tn))] * 2 if adds else [sds((2, 2, rows, 3 * tn))],
        [two] * 2 if adds else [four],
        flops=2 * n * d * 6 * tn, name="weight_mid",
    )


def k_weight_value(scal, normed, dv_own, dv_oth, ema_low, dz, part, got=None):
    n, d = normed.shape
    width = dv_own.shape[1] // 2
    zw = dz.shape[1]
    shape = (2, 2, d // 2, width + zw)

    def body(s, x_ref, vo, vt, e_ref, z_ref, *refs):
        def put(lanes, value, k, j):
            add = (refs[0].at[:, :, :, lanes], (k, j)) if got is not None else None
            put_rows(s, refs[-1].at[:, :, :, lanes], value, (k, j), add)

        for k, v in enumerate((vo, vt)):
            grad = split_rows(s, row_inner(x_ref[...], v[...]))
            for j in range(2):
                put(slice(0, width), grad[j], k, j)
        grad = split_rows(s, row_inner(e_ref[...], z_ref[...]))
        for j in range(2):
            for k in range(2):
                put(slice(width, width + zw), grad[j], k, j)

    at = pl.BlockSpec((n, width), lambda i, s: (0, s[part]))
    adds = [got] if got is not None else []
    return run(
        body, (1,), scal, [normed, dv_own, dv_oth, ema_low, dz] + adds,
        [whole((n, d)), at, at, whole((n, d)), whole((n, zw))] + [whole(shape)] * len(adds),
        [sds(shape)], [pl.BlockSpec(shape, lambda i, s: (0, 0, 0, 0))],
        flops=2 * n * d * (2 * width + zw), name="weight_value",
    )[0]


def swap(values, axis, bit, size):
    return lax.ppermute(values, axis, [(i, i ^ bit) for i in range(size)])


def pick(values, index, axis):
    return lax.dynamic_index_in_dim(values, index, axis, keepdims=False)


def one_sequence(
    tokens, alpha_logit, delta_logit, ema_beta, ema_eta, ema_omega, w_z, qk_gain, qk_bias,
    w_v, w_gamma, u_h, w_h, w_phi, w_up, w_down, cotangent,
):
    n, d = tokens.shape
    dp_size = lax.axis_size("dp")
    me = lax.axis_index("dp").astype(jnp.int32)
    t = lax.axis_index("tensor").astype(jnp.int32)
    core = me % 2
    x_pos = (me // 2) % 2
    z_pos = me // 4
    kx = core * 2 + x_pos
    kz = core * 2 + z_pos % 2
    scal = jnp.stack(
        [kx, kx ^ 1, kx ^ 2, kx ^ 3, core, 1 - core, t, 1 - t, kz, kz ^ 1, kz ^ 2, kz ^ 3, x_pos, z_pos, 2 * core, 2 * core + 1]
    )

    def held(values, *deps):
        return lax.optimization_barrier((values, deps))[0]

    def after(*deps):
        return held(scal, *deps)

    def over_core(v):
        return swap(v, "dp", 1, dp_size)

    def over_x(v):
        return swap(v, "dp", 2, dp_size)

    def over_z(v):
        return swap(v, "dp", 4, dp_size)

    def over_tensor(v):
        return swap(v, "tensor", 1, 2)

    def my_rows(w, k):
        rows = w.shape[0] // 4
        return lax.dynamic_slice_in_dim(w, k * rows, rows, 0)

    piece_v = my_rows(w_v, kx)
    pv = [over_tensor(piece_v)]
    own_params = k_pack_params(
        after(piece_v), [a.T for a in (alpha_logit, delta_logit, ema_beta, ema_eta)], ema_omega[None]
    )
    oth_params = over_tensor(own_params)
    piece_g, piece_u, piece_h, piece_up, piece_dn = k_pieces(
        after(own_params),
        [[(w_gamma, 8)], [(u_h, 0)], [(w_h, 8), (w_phi, 8)], [(w_up, 0)], [(w_down, 14), (w_down, 15)]],
    )
    normed, v_own, vs_own = k_value_own(after(piece_g), tokens, w_v)
    pg = [over_tensor(held(piece_g, v_own))]
    decay, coef, omega = k_ema_params(after(v_own), own_params, oth_params)
    blocks = n // 128
    ema_a = k_ema_forward(after(v_own), normed, decay, coef, omega, 0, blocks // 2)
    pv.append(over_x(held(pv[0], ema_a[0])))
    pu = [over_tensor(held(piece_u, ema_a[0]))]
    ema_low, e_slope, state = k_ema_forward(
        after(ema_a[0]), normed, decay, coef, omega, blocks // 2, blocks // 2, (ema_a[2], ema_a[0], ema_a[1])
    )
    pg.append(over_z(held(pg[0], state)))
    ph = [over_tensor(held(piece_h, state))]
    z_pre, query, key = k_query_key(scal, ema_low, w_z, qk_gain, qk_bias)
    pv += [over_core(v) for v in held((pv[0], pv[1]), query)]
    pu.append(over_x(held(pu[0], query)))
    pup = [over_tensor(held(piece_up, query))]
    v_oth, vs_oth = k_act_other(after(query), normed, pv, 0, 512)
    pg += [over_core(v) for v in held((pg[0], pg[1]), v_oth)]
    ph.append(over_z(held(ph[0], v_oth)))
    pdn = [over_tensor(held(piece_dn, v_oth))]
    gated_own, gated_oth, g_own, g_oth, m_own, m_oth, probs = k_attend(
        after(v_oth), query, key, v_own, v_oth, ema_low, w_gamma, pg
    )
    pu += [over_core(v) for v in held((pu[0], pu[1]), probs)]
    ph += [over_core(v) for v in held((ph[0], ph[1]), probs)]
    pup.append(over_x(held(pup[0], probs)))
    mixed, lowered, fac_h, fac_f, keep = k_gate(
        after(probs), gated_own, gated_oth, ema_low, tokens, u_h, w_h, w_phi, pu, ph
    )
    acc, dl, sent_o = k_ffn(after(mixed), lowered, cotangent, [w_up], [w_down], 1)
    pup += [over_core(v) for v in held((pup[0], pup[1]), acc)]
    got_o = over_core(sent_o)
    acc, dl, dno, dno_x, upo, upo_x = k_ffn(
        after(acc), lowered, cotangent, [w_up], [w_down], 0, (acc, dl), "own"
    )
    pdn.append(over_core(held(pdn[0], acc)))

    def total(*values):
        value = values[0].astype(F32)
        for v in values[1:]:
            value = value + v.astype(F32)
        return value

    def add(*values):
        return total(*values).astype(BF)

    def by_z(v):
        return v.reshape(2, 2, d // 8, v.shape[-1])

    def z_send(terms):
        return add(*[by_z(v)[:, 1] for v in terms])

    def z_keep(terms):
        return [by_z(v)[:, 0] for v in terms]

    def over_z2(v):
        return swap(v, "dp", 8, dp_size)

    def core_split(value):
        rows = value.reshape(2, d // 16, value.shape[-1])
        return pick(rows, 1 - core, 0).astype(BF), pick(rows, core, 0)

    def joined(kept, got):
        kept, got = kept.astype(F32), got.astype(F32)
        return jnp.where(
            core == 0, jnp.concatenate([kept, got], axis=1), jnp.concatenate([got, kept], axis=1)
        )

    dn_x1 = add(dno_x, got_o[0, 1])
    dn_got_x1 = over_x(dn_x1)
    acc, dl, sent_t = k_ffn(after(acc, dn_x1), lowered, cotangent, pup, pdn, 1, (acc, dl))
    got_t = over_core(sent_t)
    acc, dl, dnt, dnt_x, upt = k_ffn(after(acc), lowered, cotangent, pup, pdn, 0, (acc, dl), "other")
    dn_x2 = add(dnt_x, got_t[0, 1])
    up_y1 = add(upt, got_t[1])
    dn_got_x2 = over_x(dn_x2)
    up_got_y = over_tensor(up_y1)
    output, dh, df, direct, da_own, da_oth, dg_own, dg_oth, de_part = k_mid_back(
        after(acc, dn_x2, up_y1, dn_got_x1), dl, acc, cotangent, mixed, fac_h, fac_f, keep,
        g_own, g_oth, m_own, m_oth, u_h, w_gamma, w_h, w_phi, pg, pu, ph,
    )
    dn_y = {}

    def start_dn(place, dep):
        if opt["dn"] == place:
            dn_y[0] = add(dnt, got_t[0, 0], held(dn_got_x2, dep))
            dn_y[1] = over_tensor(dn_y[0])
            return (dn_y[0],)
        return ()

    ma_sent = k_weight_mid(after(dh, *start_dn(0, dh)), ema_low, dh, gated_own, gated_oth, False, 5)[0]
    ma_got = over_core(ma_sent)
    mb_sent = k_weight_mid(after(ma_sent, *start_dn(1, ma_sent)), ema_low, df, dg_own, dg_oth, True, 5)[0]
    mb_got = over_core(mb_sent)
    dv_own, dv_oth, dz, stats = k_attend_back(
        after(mb_sent, *start_dn(2, mb_sent)), probs, da_own, da_oth, v_own, v_oth, vs_own, vs_oth, query, key, z_pre, qk_gain
    )
    up_got_y = held(up_got_y, dv_own)
    up_x = add(upo_x, got_o[1, 1], up_got_y[1])
    up_got_x = over_x(up_x)
    ma_theirs, ma_mine = k_weight_mid(after(dv_own, up_x), ema_low, dh, gated_own, gated_oth, False, 4, ma_got)
    ma_got_x = over_x(ma_theirs)
    mb_own, mb_oth = k_weight_mid(after(ma_theirs), ema_low, df, dg_own, dg_oth, True, 4, mb_got)
    mb_got_y = over_tensor(mb_oth)
    val_sent = k_weight_value(after(mb_own), normed, dv_own, dv_oth, ema_low, dz, 5)
    val_got = over_core(val_sent)
    dn_got_y = dn_y[1]
    up_got_x, dn_got_y = held((up_got_x, dn_got_y), val_sent)
    dn_terms = [dno, got_o[0, 0], dn_got_x1, dn_got_y]
    up_terms = [upo, got_o[1, 0], up_got_y[0], up_got_x]
    ffn_z = jnp.stack([z_send(dn_terms), z_send(up_terms)])
    dn_terms, up_terms = z_keep(dn_terms), z_keep(up_terms)
    ffn_got_z = over_z(ffn_z)
    quarter = blocks // 4

    def ema_back(dep, first, count, before=None):
        return k_ema_backward(
            after(*dep), normed, de_part, dz, e_slope, w_z, decay, coef, omega, first, count, before
        )

    eb = ema_back((val_sent, ffn_z), 0, quarter)
    val = k_weight_value(
        after(eb[1]), normed, dv_own, dv_oth, ema_low, dz, 4, val_got
    )
    val = val.reshape(2, 2, 2, 2, d // 8, val.shape[-1])
    val_z1 = val[:, :, :, 1]
    val_kept = val[:, :, :, 0]
    val_got_z1 = over_z(val_z1)
    eb = ema_back((val_z1,), quarter, quarter, eb)
    done = {}

    def second(place, dep):
        forced = []
        if opt["m2"] == place:
            gx, gy = held((ma_got_x, mb_got_y), dep)
            ma_y, mb_x = add(ma_mine[1], gx[1]), add(mb_own[1], gy[1])
            done["m"] = (gx, gy, over_tensor(ma_y), over_x(mb_x))
            forced += [ma_y, mb_x]
        if opt.get("z2", opt["m2"]) == place:
            gz = held(ffn_got_z, dep)
            done["z"] = [*dn_terms, gz[0]], [*up_terms, gz[1]]
            ffn_z2 = jnp.stack([add(*[v[1] for v in ts]) for ts in done["z"]])
            done["z2"] = over_z2(ffn_z2)
            forced.append(ffn_z2)
        if opt["v2"] == place:
            gz = held(val_got_z1, dep)
            val_x = add(val_kept[:, 1], gz[:, 1])
            done["v"] = (gz, over_x(val_x))
            forced.append(val_x)
        if opt.get("z1m", 6) == place:
            gy, gx = held((done["m"][2], done["m"][3]), dep)
            a_terms = [ma_mine[0], done["m"][0][0], gy]
            b_terms = [mb_own[0], done["m"][1][0], gx]
            mid_z = jnp.stack([z_send(a_terms), z_send(b_terms)])
            done["mz"] = (z_keep(a_terms), z_keep(b_terms), over_z(mid_z))
            forced.append(mid_z)
        return forced

    f2 = second(2, eb[1])
    eb = ema_back((eb[1], *f2), 2 * quarter, quarter, eb)
    f3 = second(3, eb[1])
    eb = ema_back((eb[1], *f3), 3 * quarter, quarter, eb)
    d_sig, _, _, sum_a, sum_b, sum_w = eb
    f4 = second(4, sum_a)
    sums = jnp.concatenate([sum_a, sum_b, sum_w, stats], axis=0)
    others = over_z(sums)
    halves = n // ROWS // 2
    part = k_input_back(
        after(sum_a, sums, done["z2"], *f4), dv_own, dv_oth, w_v, pv, d_sig, tokens, direct, 0, halves
    )
    ffn_got_z2 = held(done["z2"], part)
    ffn_total = jnp.stack([total(*[v[0] for v in ts], ffn_got_z2[i]) for i, ts in enumerate(done["z"])])
    ffn_rows = ffn_total.reshape(2, 2, d // 16, -1)
    ffn_got = over_core(pick(ffn_rows, 1 - core, 1).astype(BF))
    ffn_kept = pick(ffn_rows, core, 1)
    f5 = second(5, part)
    sums = sums + held(others, part)
    others = over_z2(sums)
    input_grad = k_input_back(
        after(part, sums, *f5), dv_own, dv_oth, w_v, pv, d_sig, tokens, direct, halves, halves, part
    )
    gz, gx = held(done["v"], input_grad)
    val_y = add(val_kept[1, 0], gz[1, 0], gx[1])
    val_terms = [val_kept[0, 0], gz[0, 0], gx[0], over_tensor(val_y)]
    dn_terms, up_terms = done["z"]
    ma_terms, mb_terms, mid_got_z = done["mz"]

    def last(terms):
        return total(*[v[0] for v in terms])

    sums = sums + held(others, input_grad)
    sums = sums + over_core(sums)
    sums = sums + over_x(sums)
    mid_got_z = held(mid_got_z, sums)
    ma_terms, mb_terms = [*ma_terms, mid_got_z[0]], [*mb_terms, mid_got_z[1]]
    mid_z2 = jnp.stack([add(*[v[1] for v in ma_terms]), add(*[v[1] for v in mb_terms])])
    mid_got_z2 = over_z2(mid_z2)
    sums_got = over_tensor(held(sums, mid_z2))
    val_terms[-1] = held(val_terms[-1], sums_got)
    val_z2 = add(*[v[1] for v in val_terms])
    val_got_z2 = over_z2(val_z2)
    sums = held(sums + sums_got, val_z2)
    down_t, up = joined(ffn_kept[0], ffn_got[0]), joined(ffn_kept[1], ffn_got[1])
    gh = sum_a.shape[0]

    def own_half(v):
        return lax.dynamic_slice_in_dim(v, t * (d // 2), d // 2, 1).T

    tot_a = own_half(sums[:gh].reshape(H, d))
    tot_b = own_half(sums[gh : 2 * gh].reshape(H, d))
    omega_grad = lax.dynamic_slice_in_dim(sums[2 * gh : 2 * gh + d // 128].reshape(d), t * (d // 2), d // 2, 0)
    zsum = sums[2 * gh + d // 128 :]
    rate = jax.nn.sigmoid(alpha_logit)
    damp = jax.nn.sigmoid(delta_logit)
    feed = rate * ema_beta
    feed_grad = ema_eta * tot_a
    decay_grad = feed * ema_eta * tot_b
    alpha_grad = (feed_grad * ema_beta - decay_grad * damp) * rate * (1.0 - rate)
    delta_grad = -decay_grad * rate * damp * (1.0 - damp)
    params = (alpha_grad, delta_grad, feed_grad * rate, feed * tot_a, omega_grad)
    down_grad = down_t.T
    mid_got_z2, val_got_z2 = held((mid_got_z2, val_got_z2), params, down_grad, up)
    mid_total = jnp.stack([total(last(ma_terms), mid_got_z2[0]), total(last(mb_terms), mid_got_z2[1])])
    mid_rows = mid_total.reshape(2, 2, d // 16, -1)
    mid_got = over_core(pick(mid_rows, 1 - core, 1).astype(BF))
    mid_kept = pick(mid_rows, core, 1)
    val_total = last(val_terms) + val_got_z2.astype(F32)
    val_sent, val_rows = core_split(val_total)
    zw = dz.shape[1]
    val_got = over_core(val_sent)
    tn = d // 4
    uh_t, gamma = (joined(mid_kept[i][:, : 2 * tn], mid_got[i][:, : 2 * tn]) for i in range(2))
    wh_t, phi_t = (joined(mid_kept[i][:, 2 * tn :], mid_got[i][:, 2 * tn :]) for i in range(2))
    value = joined(val_rows[:, :-zw], val_got[:, :-zw])
    z_grad = val_rows[:, -zw:]
    return (
        output, input_grad, *params,
        z_grad, zsum[0:2], zsum[2:4], value, gamma, uh_t.T, wh_t.T, phi_t.T, up, down_grad,
    )


def solution(mesh):
    placed = (
        P(("dp", "tensor"), None),
        P("tensor", None),
        P("tensor", None),
        P("tensor", None),
        P("tensor", None),
        P("tensor"),
        P(),
        P(),
        P(),
        P(None, "tensor"),
        P(None, "tensor"),
        P("tensor", None),
        P("tensor", None),
        P("tensor", None),
        P(None, "tensor"),
        P("tensor", None),
        P(("dp", "tensor"), None),
    )

    def per_device(tokens, *rest):
        whole_sequence = tokens.shape[0] == LEN and dict(mesh.shape) == {"dp": 16, "tensor": 2}
        return (one_sequence if whole_sequence else shards)(tokens, *rest)

    return jax.shard_map(
        per_device,
        mesh=mesh,
        in_specs=placed,
        out_specs=(
            P(("dp", "tensor"), None),
            P(("dp", "tensor"), None),
            P("tensor", None),
            P("tensor", None),
            P("tensor", None),
            P("tensor", None),
            P("tensor"),
            P("dp", None),
            P(),
            P(),
            P("dp", "tensor"),
            P("dp", "tensor"),
            P("tensor", "dp"),
            P("tensor", "dp"),
            P("tensor", "dp"),
            P("dp", "tensor"),
            P("tensor", "dp"),
        ),
        check_vma=False,
    )
```

```python
import math

import jax
import jax.numpy as jnp
from jax import lax
from jax.experimental import pallas as pl
from jax.experimental.pallas import tpu as pltpu
from jax.sharding import PartitionSpec as P

H = 16
LEN = 1024
ATT_BLOCK = 512
EMA_BLOCK = 128


norm_eps = 1e-06
masked_value = -1e30


def rms_rows(values_in):
    return values_in * lax.rsqrt(jnp.mean(values_in * values_in, axis=-1, keepdims=True) + norm_eps)


def matmul(left, right):
    return jnp.dot(left, right, preferred_element_type=jnp.float32)


def row_inner(left, right):
    return lax.dot_general(
        left, right, (((0,), (0,)), ((), ())), preferred_element_type=jnp.float32
    )


def col_inner(left, right):
    return lax.dot_general(
        left, right, (((1,), (1,)), ((), ())), preferred_element_type=jnp.float32
    )


def silu_slope(pre_act):
    logistic = jax.nn.sigmoid(pre_act)
    return logistic * (1.0 + pre_act * (1.0 - logistic))


def gate_apply(h_pre, f_pre, x_rows):
    update = jax.nn.sigmoid(f_pre)
    return update * jax.nn.silu(h_pre) + (1.0 - update) * x_rows


def ema_apply(signal, ema_params):
    alpha_logit, delta_logit, ema_beta, ema_eta, ema_omega = ema_params
    alpha_rate = jax.nn.sigmoid(alpha_logit)
    decay_rate = 1.0 - alpha_rate * jax.nn.sigmoid(delta_logit)
    feed_rate = alpha_rate * ema_beta
    log_decay = jnp.log(decay_rate)
    total_rows, chan_count = signal.shape
    seq_count = total_rows // LEN
    block_count = LEN // EMA_BLOCK
    blocks = signal.reshape(seq_count, block_count, EMA_BLOCK, chan_count)
    steps_in = jnp.arange(EMA_BLOCK, dtype=jnp.float32)
    lag_power = jnp.exp(steps_in[:, None, None] * log_decay[None])
    kernel = jnp.sum(lag_power * (feed_rate * ema_eta)[None], axis=-1)
    offsets = steps_in[:, None] - steps_in[None, :]
    lag_index = jnp.clip(offsets, 0, EMA_BLOCK - 1).astype(jnp.int32)
    toeplitz = jnp.where((offsets >= 0)[:, :, None], kernel[lag_index], 0.0)
    local_part = jnp.einsum("ijc,snjc->snic", toeplitz, blocks)
    tail_power = lag_power[::-1] * feed_rate[None]
    block_state = jnp.einsum("jch,snjc->snch", tail_power, blocks)
    full_decay = jnp.exp(EMA_BLOCK * log_decay)

    def carry_step(state_in, incoming):
        return (full_decay * state_in + incoming, state_in)

    zero_state = jnp.zeros((seq_count, chan_count, H), jnp.float32)
    _, start_state = lax.scan(carry_step, zero_state, jnp.moveaxis(block_state, 1, 0))
    start_state = jnp.moveaxis(start_state, 0, 1)
    head_power = lag_power * decay_rate[None] * ema_eta[None]
    carried = jnp.einsum("ich,snch->snic", head_power, start_state)
    ema_pre = (local_part + carried).reshape(total_rows, chan_count) + ema_omega * signal
    return jax.nn.silu(ema_pre)


def masked_scores(q_rows, k_rows, first_row):
    raw_scores = col_inner(q_rows, k_rows) * q_rows.shape[1] ** (-0.5)
    row_pos = first_row + jnp.arange(q_rows.shape[0])[:, None]
    col_pos = jnp.arange(k_rows.shape[0])[None, :]
    return jnp.where(col_pos <= row_pos, raw_scores, masked_value)


def attend_forward(query_low, key_low, value_low):
    total_rows, value_width = value_low.shape
    seq_count = total_rows // LEN
    per_seq = LEN // ATT_BLOCK

    def attend_one_block(flat_index):
        seq_id = flat_index // per_seq
        blk_id = flat_index % per_seq
        seq_start = seq_id * LEN
        q_rows = lax.dynamic_slice_in_dim(query_low, seq_start + blk_id * ATT_BLOCK, ATT_BLOCK, 0)
        k_rows = lax.dynamic_slice_in_dim(key_low, seq_start, LEN, 0)
        v_rows = lax.dynamic_slice_in_dim(value_low, seq_start, LEN, 0)
        scores = masked_scores(q_rows, k_rows, blk_id * ATT_BLOCK)
        top_score = jnp.max(scores, axis=-1, keepdims=True)
        weights = jnp.exp(scores - top_score)
        total_weight = jnp.sum(weights, axis=-1, keepdims=True)
        probs = (weights / total_weight).astype(jnp.bfloat16)
        return (matmul(probs, v_rows), top_score[:, 0] + jnp.log(total_weight[:, 0]))

    outs, lse_all = lax.map(attend_one_block, jnp.arange(seq_count * per_seq))
    return (outs.reshape(total_rows, value_width), lse_all.reshape(total_rows))


def attend_backward(query_low, key_low, value_low, lse_rows, d_att):
    total_rows, value_width = value_low.shape
    head_width = query_low.shape[1]
    seq_count = total_rows // LEN
    per_seq = LEN // ATT_BLOCK
    scale = head_width ** (-0.5)

    def one_seq(seq_id):
        seq_start = seq_id * LEN
        k_rows = lax.dynamic_slice_in_dim(key_low, seq_start, LEN, 0)
        v_rows = lax.dynamic_slice_in_dim(value_low, seq_start, LEN, 0)

        def one_one_block(carry_in, blk_id):
            d_keys, d_vals = carry_in
            row_start = seq_start + blk_id * ATT_BLOCK
            q_rows = lax.dynamic_slice_in_dim(query_low, row_start, ATT_BLOCK, 0)
            g_rows = lax.dynamic_slice_in_dim(d_att, row_start, ATT_BLOCK, 0)
            lse_part = lax.dynamic_slice_in_dim(lse_rows, row_start, ATT_BLOCK, 0)
            probs = jnp.exp(masked_scores(q_rows, k_rows, blk_id * ATT_BLOCK) - lse_part[:, None])
            d_probs = col_inner(g_rows, v_rows)
            d_scores = (
                probs * (d_probs - jnp.sum(probs * d_probs, axis=-1, keepdims=True))
            ).astype(jnp.bfloat16)
            d_rows = matmul(d_scores, k_rows) * scale
            d_keys = d_keys + row_inner(d_scores, q_rows) * scale
            d_vals = d_vals + row_inner(probs.astype(jnp.bfloat16), g_rows)
            return ((d_keys, d_vals), d_rows)

        start_carry = (
            jnp.zeros((LEN, head_width), jnp.float32),
            jnp.zeros((LEN, value_width), jnp.float32),
        )
        (d_keys, d_vals), d_rows = lax.scan(one_one_block, start_carry, jnp.arange(per_seq))
        return (d_rows.reshape(LEN, head_width), d_keys, d_vals)

    d_query, d_key, d_value = lax.map(one_seq, jnp.arange(seq_count))
    return (
        d_query.reshape(total_rows, head_width),
        d_key.reshape(total_rows, head_width),
        d_value.reshape(total_rows, value_width),
    )


def shards(
    tokens,
    alpha_logit,
    delta_logit,
    ema_beta,
    ema_eta,
    ema_omega,
    w_z,
    qk_gain,
    qk_bias,
    w_v,
    w_gamma,
    u_h,
    w_h,
    w_phi,
    w_up,
    w_down,
    cotangent,
):
    tensor_pos = lax.axis_index("tensor")
    feature_count = tokens.shape[1]
    chan_count = ema_omega.shape[0]
    chan_start = tensor_pos * chan_count
    x_rows = tokens.astype(jnp.float32)
    normed_rows, norm_pull = jax.vjp(rms_rows, x_rows)
    normed, cot_full = (
        lax.all_gather(normed_rows.astype(jnp.bfloat16), "tensor", axis=0, tiled=True),
        lax.all_gather(cotangent, "tensor", axis=0, tiled=True),
    )
    signal = lax.dynamic_slice_in_dim(normed, chan_start, chan_count, 1).astype(jnp.float32)
    ema_params = (alpha_logit, delta_logit, ema_beta, ema_eta, ema_omega)
    ema_val, ema_pull = jax.vjp(ema_apply, signal, ema_params)
    ema_low = ema_val.astype(jnp.bfloat16)
    ema_full = lax.all_gather(ema_low, "tensor", axis=1, tiled=True)
    z_pre = matmul(ema_full, w_z)
    z_act = jax.nn.silu(z_pre)
    query_low = (z_act * qk_gain[0] + qk_bias[0]).astype(jnp.bfloat16)
    key_low = (z_act * qk_gain[1] + qk_bias[1]).astype(jnp.bfloat16)
    values_pre = matmul(normed, w_v)
    value_low = jax.nn.silu(values_pre).astype(jnp.bfloat16)
    gamma_pre = matmul(ema_full, w_gamma)
    gamma_act = jax.nn.silu(gamma_pre)
    attended, lse_rows = attend_forward(query_low, key_low, value_low)
    gated_low = (gamma_act * attended).astype(jnp.bfloat16)
    both_pre = lax.psum_scatter(
        jnp.concatenate(
            [matmul(gated_low, u_h) + matmul(ema_low, w_h), matmul(ema_low, w_phi)], axis=1
        ),
        "tensor",
        scatter_dimension=0,
        tiled=True,
    )
    h_pre = both_pre[:, :feature_count]
    f_pre = both_pre[:, feature_count:]
    mixed, gate_pull = jax.vjp(gate_apply, h_pre, f_pre, x_rows)
    normed_two, norm_two_pull = jax.vjp(rms_rows, mixed)
    lowered = lax.all_gather(normed_two.astype(jnp.bfloat16), "tensor", axis=0, tiled=True)
    up_pre = matmul(lowered, w_up)
    hidden = jax.nn.silu(up_pre).astype(jnp.bfloat16)
    down_rows = lax.psum_scatter(
        matmul(hidden, w_down).astype(jnp.bfloat16), "tensor", scatter_dimension=0, tiled=True
    ).astype(jnp.float32)
    output = (mixed + down_rows).astype(jnp.bfloat16)
    cot_rows = cotangent.astype(jnp.float32)
    d_hidden = col_inner(cot_full, w_down)
    d_up = (d_hidden * silu_slope(up_pre)).astype(jnp.bfloat16)
    down_grad = row_inner(hidden, cot_full)
    up_grad = row_inner(lowered, d_up)
    d_lowered = lax.psum_scatter(col_inner(d_up, w_up), "tensor", scatter_dimension=0, tiled=True)
    d_mixed = cot_rows + norm_two_pull(d_lowered)[0]
    d_hpre, d_fpre, d_direct = gate_pull(d_mixed)
    h_full_grad, f_full_grad = (
        lax.all_gather(d_hpre.astype(jnp.bfloat16), "tensor", axis=0, tiled=True),
        lax.all_gather(d_fpre.astype(jnp.bfloat16), "tensor", axis=0, tiled=True),
    )
    uh_grad = row_inner(gated_low, h_full_grad)
    wh_grad = row_inner(ema_low, h_full_grad)
    phi_grad = row_inner(ema_low, f_full_grad)
    d_gated = col_inner(h_full_grad, u_h)
    d_att = (d_gated * gamma_act).astype(jnp.bfloat16)
    d_gamma = (d_gated * attended * silu_slope(gamma_pre)).astype(jnp.bfloat16)
    d_query, d_key, d_value = attend_backward(query_low, key_low, value_low, lse_rows, d_att)
    d_query, d_key = lax.psum((d_query, d_key), "tensor")
    d_z = (silu_slope(z_pre) * (d_query * qk_gain[0] + d_key * qk_gain[1])).astype(jnp.bfloat16)
    gain_grad = jnp.stack([jnp.sum(d_query * z_act, axis=0), jnp.sum(d_key * z_act, axis=0)])
    bias_grad = jnp.stack([jnp.sum(d_query, axis=0), jnp.sum(d_key, axis=0)])
    z_grad = row_inner(ema_full, d_z)
    gamma_grad = row_inner(ema_full, d_gamma)
    d_value_pre = (d_value * silu_slope(values_pre)).astype(jnp.bfloat16)
    value_grad = row_inner(normed, d_value_pre)
    d_chan = lax.psum_scatter(
        col_inner(d_gamma, w_gamma).astype(jnp.bfloat16), "tensor", scatter_dimension=1, tiled=True
    ).astype(jnp.float32)
    z_rows = lax.dynamic_slice_in_dim(w_z, chan_start, chan_count, 0)
    d_chan = (
        d_chan
        + col_inner(d_z, z_rows)
        + col_inner(h_full_grad, w_h)
        + col_inner(f_full_grad, w_phi)
    )
    d_signal, d_params = ema_pull(d_chan)
    d_norm_part = col_inner(d_value_pre, w_v)
    own_cols = lax.dynamic_slice_in_dim(d_norm_part, chan_start, chan_count, 1)
    d_norm_part = lax.dynamic_update_slice_in_dim(d_norm_part, own_cols + d_signal, chan_start, 1)
    d_normed = lax.psum_scatter(
        d_norm_part.astype(jnp.bfloat16), "tensor", scatter_dimension=0, tiled=True
    ).astype(jnp.float32)
    input_grad = d_direct + norm_pull(d_normed)[0]
    weight_totals = (
        lax.psum_scatter(z_grad.astype(jnp.bfloat16), "dp", scatter_dimension=0, tiled=True).astype(
            jnp.float32
        ),
        lax.psum_scatter(
            value_grad.astype(jnp.bfloat16), "dp", scatter_dimension=0, tiled=True
        ).astype(jnp.float32),
        lax.psum_scatter(
            gamma_grad.astype(jnp.bfloat16), "dp", scatter_dimension=0, tiled=True
        ).astype(jnp.float32),
        lax.psum_scatter(
            uh_grad.astype(jnp.bfloat16), "dp", scatter_dimension=1, tiled=True
        ).astype(jnp.float32),
        lax.psum_scatter(
            wh_grad.astype(jnp.bfloat16), "dp", scatter_dimension=1, tiled=True
        ).astype(jnp.float32),
        lax.psum_scatter(
            phi_grad.astype(jnp.bfloat16), "dp", scatter_dimension=1, tiled=True
        ).astype(jnp.float32),
        lax.psum_scatter(
            up_grad.astype(jnp.bfloat16), "dp", scatter_dimension=0, tiled=True
        ).astype(jnp.float32),
        lax.psum_scatter(
            down_grad.astype(jnp.bfloat16), "dp", scatter_dimension=1, tiled=True
        ).astype(jnp.float32),
    )
    param_totals = lax.psum(
        (d_params[0], d_params[1], d_params[2], d_params[3], d_params[4], gain_grad, bias_grad),
        "dp",
    )
    return (
        output,
        input_grad,
        param_totals[0],
        param_totals[1],
        param_totals[2],
        param_totals[3],
        param_totals[4],
        weight_totals[0],
        param_totals[5],
        param_totals[6],
        weight_totals[1],
        weight_totals[2],
        weight_totals[3],
        weight_totals[4],
        weight_totals[5],
        weight_totals[6],
        weight_totals[7],
    )


MIB = 1024 * 1024
BF = jnp.bfloat16
F32 = jnp.float32
ROWS = 256
hints = dict(ema_backward2=0.3, weight_value=0.3)
opt = dict(dn=0, m2=3, v2=4, z2=3, z1m=5)


def sds(shape, dtype=BF):
    return jax.ShapeDtypeStruct(shape, dtype)


def whole(shape):
    return pl.BlockSpec(shape, lambda i, s: (0,) * len(shape), pipeline_mode=pl.Buffered(1))


def rows_of(cols, rows=ROWS):
    return pl.BlockSpec((rows, cols), lambda i, s: (i, 0))


def cols_of(rows, cols):
    return pl.BlockSpec((rows, cols), lambda i, s: (0, i))


def run(body, grid, scal, ins, in_specs, out_shape, out_specs, scratch=(), flops=0, name=None, aliases=None, spare=12):
    moved = sum(a.size * a.dtype.itemsize for a in ins)
    moved += sum(math.prod(o.shape) * jnp.dtype(o.dtype).itemsize for o in out_shape)
    def held_bytes(spec, a):
        if spec.block_shape is None:
            return 0
        return math.prod(spec.block_shape) * jnp.dtype(a.dtype).itemsize * (1 if spec.pipeline_mode else 2)

    if name in ("attend", "gate", "ffn", "mid_back", "pack_params", "ema_params", "pieces"):
        spare = 56
    vmem = sum(map(held_bytes, in_specs, ins)) + sum(map(held_bytes, out_specs, out_shape))
    vmem += sum(math.prod(r.shape) * jnp.dtype(r.dtype).itemsize for r in scratch if r.memory_space == pltpu.VMEM)
    return pl.pallas_call(
        body,
        out_shape=out_shape,
        grid_spec=pltpu.PrefetchScalarGridSpec(
            num_scalar_prefetch=1,
            grid=grid,
            in_specs=in_specs,
            out_specs=out_specs,
            scratch_shapes=list(scratch),
        ),
        compiler_params=pltpu.CompilerParams(vmem_limit_bytes=min(vmem + spare * MIB, 56 * MIB)),
        cost_estimate=pl.CostEstimate(flops=int(flops * hints.get(name, 10)), bytes_accessed=int(moved * hints.get(name, 10)), transcendentals=0),
        name=name,
        input_output_aliases=aliases or {},
    )(scal, *ins)


def sig(u):
    return 0.5 + 0.5 * jnp.tanh(0.5 * u)


def silu_pair(u):
    s = sig(u)
    return u * s, s * (1.0 + u * (1.0 - s))


def place(scr, s, pieces, base=0, table=0):
    rows = pieces[0].shape[0]
    for p in range(4):
        scr[pl.ds(pl.multiple_of(base + s[table + p] * rows, rows), rows), :] = pieces[p][...]


def piece_block(rows, cols, row_block):
    return pl.BlockSpec((rows, cols), lambda i, s: (row_block, i))


def piece_whole(rows, cols, row_block):
    return pl.BlockSpec((rows, cols), lambda i, s: (row_block, 0), pipeline_mode=pl.Buffered(1))


def k_value_own(scal, tokens, w_own):
    n, d = tokens.shape
    cols = w_own.shape[1]
    tn = 512

    def body(s, x_ref, w_ref, n_ref, v_ref, sl_ref):
        @pl.when(pl.program_id(0) == 0)
        def _():
            x = x_ref[...].astype(F32)
            n_ref[...] = (x * lax.rsqrt(jnp.mean(x * x, axis=-1, keepdims=True) + norm_eps)).astype(BF)

        act, slope = silu_pair(matmul(n_ref[...], w_ref[...]))
        v_ref[...] = act.astype(BF)
        sl_ref[...] = slope.astype(BF)

    return run(
        body, (cols // tn,), scal, [tokens, w_own],
        [whole((n, d)), cols_of(d, tn)],
        [sds((n, d)), sds((n, cols)), sds((n, cols))],
        [pl.BlockSpec((n, d), lambda i, s: (0, 0)), cols_of(n, tn), cols_of(n, tn)],
        flops=2 * n * d * cols, name="value_own",
    )


def k_act_own(scal, x, w_own, tn):
    n, d = x.shape
    cols = w_own.shape[1]

    def body(s, x_ref, w_ref, v_ref, sl_ref):
        act, slope = silu_pair(matmul(x_ref[...], w_ref[...]))
        v_ref[...] = act.astype(BF)
        sl_ref[...] = slope.astype(BF)

    return run(
        body, (cols // tn,), scal, [x, w_own],
        [whole((n, d)), cols_of(d, tn)],
        [sds((n, cols)), sds((n, cols))],
        [cols_of(n, tn), cols_of(n, tn)],
        flops=2 * n * d * cols, name="act_own",
    )


def k_act_other(scal, x, pieces, table, tn):
    n, d = x.shape
    rows, cols = pieces[0].shape

    def body(s, x_ref, p0, p1, p2, p3, v_ref, sl_ref, w_scr):
        place(w_scr, s, (p0, p1, p2, p3), table=table)
        act, slope = silu_pair(matmul(x_ref[...], w_scr[...]))
        v_ref[...] = act.astype(BF)
        sl_ref[...] = slope.astype(BF)

    return run(
        body, (cols // tn,), scal, [x, *pieces],
        [whole((n, d))] + [piece_block(rows, tn, 0)] * 4,
        [sds((n, cols)), sds((n, cols))],
        [cols_of(n, tn), cols_of(n, tn)],
        [pltpu.VMEM((d, tn), BF)],
        flops=2 * n * d * cols, name="act_other",
    )


def k_query_key(scal, ema_low, w_z, qk_gain, qk_bias):
    n, d = ema_low.shape
    zw = w_z.shape[1]

    def body(s, e_ref, w_ref, g_ref, b_ref, z_ref, q_ref, k_ref):
        z_pre = matmul(e_ref[...], w_ref[...])
        z_ref[...] = z_pre
        act = z_pre * sig(z_pre)
        q_ref[...] = (act * g_ref[0:1, :] + b_ref[0:1, :]).astype(BF)
        k_ref[...] = (act * g_ref[1:2, :] + b_ref[1:2, :]).astype(BF)

    return run(
        body, (2,), scal, [ema_low, w_z, qk_gain, qk_bias],
        [rows_of(d, n // 2), whole((d, zw)), whole((2, zw)), whole((2, zw))],
        [sds((n, zw), F32), sds((n, zw)), sds((n, zw))],
        [rows_of(zw, n // 2)] * 3,
        flops=2 * n * d * zw, name="query_key",
    )


def k_pack_params(scal, arrays, omega):
    ch = omega.shape[1]

    def body(s, a0, a1, a2, a3, w_ref, o_ref):
        for i, ref in enumerate((a0, a1, a2, a3)):
            o_ref[i * H : (i + 1) * H, :] = ref[...]
        o_ref[4 * H : 4 * H + 8, :] = jnp.broadcast_to(w_ref[...], (8, ch))

    return run(
        body, (1,), scal, [*arrays, omega], [whole((H, ch))] * 4 + [whole((1, ch))],
        [sds((4 * H + 8, ch), F32)], [pl.BlockSpec((4 * H + 8, ch), lambda i, s: (0, 0))], flops=1e7, name="pack_params",
    )[0]


def k_ema_params(scal, own, oth):
    height, ch = own.shape
    groups = 2 * ch // 128

    def body(s, own_ref, oth_ref, dec_ref, cf_ref, om_ref):
        for j in range(2):
            for src, ref in ((0, own_ref), (1, oth_ref)):

                @pl.when(s[6 + src] == j)
                def _(j=j, ref=ref):
                    v = ref[...]
                    rate = sig(v[0:H])
                    dec = 1.0 - rate * sig(v[H : 2 * H])
                    cf = rate * v[2 * H : 3 * H] * v[3 * H : 4 * H]
                    for g in range(groups // 2):
                        lanes = slice(g * 128, (g + 1) * 128)
                        at = j * (groups // 2) + g
                        dec_ref[pl.ds(at, H, stride=groups), :] = dec[:, lanes]
                        cf_ref[pl.ds(at, H, stride=groups), :] = cf[:, lanes]
                        om_ref[at : at + 1, :] = v[4 * H : 4 * H + 1, lanes]

    par = (H * groups, 128)
    return run(
        body, (1,), scal, [own, oth], [whole((height, ch))] * 2,
        [sds(par, F32), sds(par, F32), sds((groups, 128), F32)],
        [pl.BlockSpec(par, lambda i, s: (0, 0))] * 2 + [pl.BlockSpec((groups, 128), lambda i, s: (0, 0))],
        flops=1e8, name="ema_params",
    )


def k_pieces(scal, takes):
    parts = [(w, at) for take in takes for w, at in take]

    def body(s, *refs):
        ins, outs = refs[: len(parts)], refs[len(parts) :]
        n = 0
        for take, out in zip(takes, outs):
            low = 0
            for w, _ in take:
                rows = w.shape[0] // 4
                out[low : low + rows, :] = ins[n][...]
                low += rows
                n += 1

    return run(
        body, (1,), scal, [w for w, _ in parts],
        [pl.BlockSpec((w.shape[0] // 4, w.shape[1]), lambda i, s, at=at: (s[at], 0)) for w, at in parts],
        [sds((sum(w.shape[0] // 4 for w, _ in take), take[0][0].shape[1])) for take in takes],
        [pl.BlockSpec((sum(w.shape[0] // 4 for w, _ in take), take[0][0].shape[1]), lambda i, s: (0, 0)) for take in takes],
        flops=1e7, name="pieces",
    )


def k_ema_forward(scal, normed, decay, coef, omega, first, count, before=None):
    n, d = normed.shape
    groups = d // 128
    tb = 128

    def body(s, x_ref, dec_ref, cf_ref, om_ref, *refs):
        e_ref, sl_ref, st, xs, ys = refs[-5:]

        @pl.when(pl.program_id(0) == 0)
        def _():
            st[...] = refs[0][...] if before else jnp.zeros_like(st)

        for g in range(groups):
            xs[pl.ds(g, tb, stride=groups), :] = x_ref[:, g * 128 : (g + 1) * 128].astype(F32)
        dec = [dec_ref[k * groups : (k + 1) * groups, :] for k in range(H)]
        cf = [cf_ref[k * groups : (k + 1) * groups, :] for k in range(H)]
        om = om_ref[...]

        def steps(b, carry):
            states = list(carry)
            for u in range(16):
                row = pl.multiple_of((b * 16 + u) * groups, groups)
                xt = xs[pl.ds(row, groups), :]
                parts = [om * xt, None, None, None]
                for k in range(H):
                    states[k] = dec[k] * states[k] + xt
                    term = cf[k] * states[k]
                    parts[k % 4] = term if parts[k % 4] is None else parts[k % 4] + term
                ys[pl.ds(row, groups), :] = (parts[0] + parts[1]) + (parts[2] + parts[3])
            return tuple(states)

        start = tuple(st[k * groups : (k + 1) * groups, :] for k in range(H))
        end = lax.fori_loop(0, tb // 16, steps, start)
        for k in range(H):
            st[k * groups : (k + 1) * groups, :] = end[k]
        for g in range(groups):
            act, slope = silu_pair(ys[pl.ds(g, tb, stride=groups), :])
            e_ref[:, g * 128 : (g + 1) * 128] = act.astype(BF)
            sl_ref[:, g * 128 : (g + 1) * 128] = slope.astype(BF)

    par = (H * groups, 128)
    at = pl.BlockSpec((tb, d), lambda i, s: (first + i, 0))
    more = list(before) if before else []
    return run(
        body, (count,), scal, [normed, decay, coef, omega, *more],
        [at, whole(par), whole(par), whole((groups, 128))]
        + ([whole(par), pl.BlockSpec(memory_space=pltpu.HBM), pl.BlockSpec(memory_space=pltpu.HBM)] if before else []),
        [sds((n, d)), sds((n, d)), sds(par, F32)],
        [at, at, pl.BlockSpec(par, lambda i, s: (0, 0))],
        [pltpu.VMEM((tb * groups, 128), F32), pltpu.VMEM((tb * groups, 128), F32)],
        flops=2.5e9 * count, name="ema_forward", aliases={6: 0, 7: 1} if before else {},
    )


def k_ema_backward(scal, normed, de_part, dz, slope, w_z, decay, coef, omega, first, count, before=None):
    n, d = normed.shape
    groups = d // 128
    tb = 128
    nb = n // tb
    half = H // 2
    gh = groups * half
    zw = dz.shape[1]

    def body(s, x_ref, de_ref, z_ref, sl_ref, wz_ref, dec_ref, cf_ref, om_ref, *refs):
        o_ref, back, deriv, a_ref, b_ref, w_ref, xs, gs, ys = refs[-9:]

        @pl.when(pl.program_id(0) == 0)
        def _():
            for i, ref in enumerate((back, deriv, a_ref, b_ref, w_ref)):
                ref[...] = refs[i][...] if before else jnp.zeros_like(ref)

        d_e = (de_ref[...].astype(F32) + col_inner(z_ref[...], wz_ref[...])) * sl_ref[...].astype(F32)
        for g in range(groups):
            xs[pl.ds(g, tb, stride=groups), :] = x_ref[:, g * 128 : (g + 1) * 128].astype(F32)
            gs[pl.ds(g, tb, stride=groups), :] = d_e[:, g * 128 : (g + 1) * 128]

        for part in range(2):
            low = part * gh
            at = [slice(low + k * groups, low + (k + 1) * groups) for k in range(half)]
            dec = [dec_ref[a, :] for a in at]

            def steps(b, carry, part=part, at=at, dec=dec):
                bk, dv, aa, bb, ww = (list(c) for c in carry)
                for u in range(8):
                    row = pl.multiple_of((tb - 1 - (b * 8 + u)) * groups, groups)
                    xt = xs[pl.ds(row, groups), :]
                    gt = gs[pl.ds(row, groups), :]
                    if part == 0:
                        outs = [om_ref[...] * gt, None]
                        ww[0] = ww[0] + xt * gt
                    else:
                        outs = [ys[pl.ds(row, groups), :], None]
                    for k in range(half):
                        dv[k] = dec[k] * dv[k] + bk[k]
                        bk[k] = dec[k] * bk[k] + gt
                        term = cf_ref[at[k], :] * bk[k]
                        outs[k % 2] = term if outs[k % 2] is None else outs[k % 2] + term
                        aa[k] = aa[k] + xt * bk[k]
                        bb[k] = bb[k] + xt * dv[k]
                    ys[pl.ds(row, groups), :] = outs[0] + outs[1]
                return tuple(bk), tuple(dv), tuple(aa), tuple(bb), tuple(ww)

            start = (
                tuple(back[a, :] for a in at),
                tuple(deriv[a, :] for a in at),
                tuple(a_ref[a, :] for a in at),
                tuple(b_ref[a, :] for a in at),
                (w_ref[...],),
            )
            bk, dv, aa, bb, ww = lax.fori_loop(0, tb // 8, steps, start)
            for k in range(half):
                back[at[k], :] = bk[k]
                deriv[at[k], :] = dv[k]
                a_ref[at[k], :] = aa[k]
                b_ref[at[k], :] = bb[k]
            w_ref[...] = ww[0]
        for g in range(groups):
            o_ref[:, g * 128 : (g + 1) * 128] = ys[pl.ds(g, tb, stride=groups), :]

    top = nb - 1 - first
    back_rows = pl.BlockSpec((tb, d), lambda i, s: (top - i, 0))
    par = (H * groups, 128)
    const = pl.BlockSpec(par, lambda i, s: (0, 0))
    small = (groups, 128)
    more = [*before[1:], before[0]] if before else []
    return run(
        body, (count,), scal, [normed, de_part, dz, slope, w_z, decay, coef, omega, *more],
        [back_rows, back_rows, pl.BlockSpec((tb, zw), lambda i, s: (top - i, 0)), back_rows, whole((d, zw)),
         whole(par), whole(par), whole(small)]
        + ([whole(par)] * 4 + [whole(small), pl.BlockSpec(memory_space=pltpu.HBM)] if before else []),
        [sds((n, d), F32)] + [sds(par, F32)] * 4 + [sds(small, F32)],
        [back_rows, const, const, const, const, pl.BlockSpec(small, lambda i, s: (0, 0))],
        [pltpu.VMEM((tb * groups, 128), F32)] * 3,
        flops=5e9 * count, name=f"ema_backward{first}", aliases={14: 0} if before else {},
    )


def k_attend(scal, q, k, v_own, v_oth, ema_low, g_own, packs):
    n, zw = q.shape
    d, half = g_own.shape
    rp = packs[0].shape[0]
    blocks = n // ROWS
    scale = zw ** (-0.5)

    def body(s, q_ref, k_ref, vo, vt, e_ref, wo, w0, w1, w2, w3, gated_o, gated_t, go, gt, mo, mt, p_ref, w_scr):
        @pl.when(pl.program_id(0) == 0)
        def _():
            place(w_scr, s, (w0, w1, w2, w3), table=8)

        for i in range(blocks):

            @pl.when(pl.program_id(0) == i)
            def _(i=i):
                seen = (i + 1) * ROWS
                sc = col_inner(q_ref[...], k_ref[0:seen, :]) * scale
                row = i * ROWS + lax.broadcasted_iota(jnp.int32, (ROWS, seen), 0)
                col = lax.broadcasted_iota(jnp.int32, (ROWS, seen), 1)
                sc = jnp.where(col <= row, sc, masked_value)
                e = jnp.exp(sc - jnp.max(sc, axis=-1, keepdims=True))
                p = (e * (1.0 / jnp.sum(e, axis=-1, keepdims=True))).astype(BF)
                p_ref[:, 0:seen] = p
                if seen < n:
                    p_ref[:, seen:] = jnp.zeros((ROWS, n - seen), BF)
                for v_ref, w, gated, g, m in ((vo, wo, gated_o, go, mo), (vt, w_scr, gated_t, gt, mt)):
                    act, slope = silu_pair(matmul(e_ref[...], w[...]))
                    att = matmul(p, v_ref[0:seen, :])
                    gated[...] = (act * att).astype(BF)
                    g[...] = act.astype(BF)
                    m[...] = (slope * att).astype(BF)

    return run(
        body, (blocks,), scal, [q, k, v_own, v_oth, ema_low, g_own, *packs],
        [rows_of(zw), whole((n, zw)), whole((n, half)), whole((n, half)), rows_of(d), whole((d, half))]
        + [whole((rp, half))] * 4,
        [sds((n, half))] * 6 + [sds((n, n))],
        [rows_of(half)] * 6 + [rows_of(n)],
        [pltpu.VMEM((d, half), BF)],
        flops=n * n * (zw + 2 * half) * 1.25 + 4 * n * d * half, name="attend",
    )


def k_gate(scal, gated_own, gated_oth, ema_low, tokens, u_own, h_own, f_own, packs_u, packs_h):
    n, d = tokens.shape
    half = u_own.shape[0]
    ch = h_own.shape[0]
    ru, rh = packs_u[0].shape[0], packs_h[0].shape[0] // 2

    def body(s, go, gt, e_ref, x_ref, uo, ho, fo, u0, u1, u2, u3, h0, h1, h2, h3, f0, f1, f2, f3,
             mix_ref, low_ref, a_ref, b_ref, up_ref, u_scr, h_scr, f_scr):
        @pl.when(pl.program_id(0) == 0)
        def _():
            place(u_scr, s, (u0, u1, u2, u3))
            own = pl.multiple_of(s[6] * ch, ch)
            oth = s[7] * ch
            h_scr[pl.ds(own, ch), :] = ho[...]
            f_scr[pl.ds(own, ch), :] = fo[...]
            place(h_scr, s, (h0, h1, h2, h3), oth, 8)
            place(f_scr, s, (f0, f1, f2, f3), oth, 8)

        h_pre = matmul(go[...], uo[...]) + matmul(gt[...], u_scr[...]) + matmul(e_ref[...], h_scr[...])
        f_pre = matmul(e_ref[...], f_scr[...])
        x = x_ref[...].astype(F32)
        act, slope = silu_pair(h_pre)
        update = sig(f_pre)
        mixed = update * act + (1.0 - update) * x
        mix_ref[...] = mixed.astype(BF)
        low_ref[...] = (mixed * lax.rsqrt(jnp.mean(mixed * mixed, axis=-1, keepdims=True) + norm_eps)).astype(BF)
        a_ref[...] = (update * slope).astype(BF)
        b_ref[...] = ((act - x) * update * (1.0 - update)).astype(BF)
        up_ref[...] = (1.0 - update).astype(BF)

    ins = [gated_own, gated_oth, ema_low, tokens, u_own, h_own, f_own, *packs_u, *packs_h, *packs_h]
    specs = [rows_of(half), rows_of(half), rows_of(d), rows_of(d), whole((half, d)), whole((ch, d)), whole((ch, d))]
    specs += [piece_whole(ru, d, 0)] * 4 + [piece_whole(rh, d, 0)] * 4 + [piece_whole(rh, d, 1)] * 4
    return run(
        body, (n // ROWS,), scal, ins, specs,
        [sds((n, d))] * 5,
        [rows_of(d)] * 5,
        [pltpu.VMEM((half, d), BF), pltpu.VMEM((2 * ch, d), BF), pltpu.VMEM((2 * ch, d), BF)],
        flops=2 * n * d * (2 * half + 4 * ch), name="gate",
    )


def split_rows(s, grad):
    d, c = grad.shape
    by_x = grad.reshape(4, 2, d // 8, c)
    flip = s[12] == 0
    a, b = by_x[:, 0].reshape(d // 2, c), by_x[:, 1].reshape(d // 2, c)
    return jnp.where(flip, a, b), jnp.where(flip, b, a)


def put_rows(s, ref, value, lead=(), add=None):
    rows = value.shape[0] // 4
    for z in range(4):
        at = pl.ds(pl.multiple_of((s[13] ^ z) * rows, rows), rows)
        part = value[z * rows : (z + 1) * rows]
        if add is not None:
            part = part + add[0][(*add[1], at, slice(None))].astype(F32)
        ref[(*lead, at, slice(None))] = part.astype(BF)


def k_ffn(scal, lowered, cot, up, down, part, before=None, form="sent"):
    n, d = lowered.shape
    pieces = len(up) > 1
    tn = up[0].shape[1] // 4
    rows = d // 2

    def body(s, low_ref, c_ref, *refs):
        step = pl.program_id(0)
        nu = len(up)
        ups, wd, refs = refs[:nu], refs[nu], refs[nu + 1 :]
        if before:
            ins, refs = refs[:2], refs[2:]
            held, sems = refs[-2:]
            refs = refs[:-2]
            copies = [pltpu.make_async_copy(ins[i], held.at[i], sems.at[i]) for i in range(2)]
        out_ref, gl_ref, *grads, acc, gl, u_scr = refs
        if pieces:
            place(u_scr, s, ups)
            wu = u_scr
        else:
            wu = ups[0]

        def work(wd, i):
            if before and i == 0:
                for c in copies:
                    c.start()
            act, slope = silu_pair(matmul(low_ref[...], wu[...]))
            hid = act.astype(BF)
            out = matmul(hid, wd[...])
            du = (col_inner(c_ref[...], wd[...]) * slope).astype(BF)
            back = col_inner(du, wu[...])
            if i == 0:
                acc[...] = out
                gl[...] = back
            else:
                if before:
                    for c in copies:
                        c.wait()
                    out = out + held[0].astype(F32)
                    back = back + held[1].astype(F32)
                out_ref[...] = (acc[...] + out).astype(BF)
                gl_ref[...] = (gl[...] + back).astype(BF)
            for k, grad in enumerate((row_inner(c_ref[...], hid), row_inner(low_ref[...], du))):
                for j, rows_j in enumerate(split_rows(s, grad)):
                    if form == "sent":
                        put_rows(s, grads[0], rows_j, (k, j))
                    elif form == "own" or k == 0:
                        put_rows(s, grads[2 * k + j], rows_j)
                    else:
                        put_rows(s, grads[2], rows_j, (j,))

        for i in range(2):

            @pl.when(step == i)
            def _(i=i):
                work(wd, i)

    if pieces:
        down = [down[part]]
        specs = [pl.BlockSpec((d // 4, tn), lambda i, s: (0, s[4 + part] * 2 + i))] * 4
        specs += [pl.BlockSpec((tn, d), lambda i, s: (i, 0))]
    else:
        specs = [
            pl.BlockSpec((d, tn), lambda i, s: (0, s[4 + part] * 2 + i)),
            pl.BlockSpec((tn, d), lambda i, s: (s[4 + part] * 2 + i, 0)),
        ]
    still = pl.BlockSpec((n, d), lambda i, s: (0, 0))
    one = pl.BlockSpec((rows, tn), lambda i, s: (0, i))
    two = pl.BlockSpec((2, rows, tn), lambda i, s: (0, 0, i))
    four = pl.BlockSpec((2, 2, rows, tn), lambda i, s: (0, 0, 0, i))
    grad_specs = dict(sent=[four], own=[one] * 4, other=[one, one, two])[form]
    grad_shapes = [sds((*g.block_shape[:-1], 2 * tn)) for g in grad_specs]
    more = list(before) if before else []
    return run(
        body, (2,), scal, [lowered, cot, *up, *down, *more],
        [whole((n, d)), whole((n, d))] + specs + [pl.BlockSpec(memory_space=pltpu.HBM)] * len(more),
        [sds((n, d)), sds((n, d)), *grad_shapes],
        [still, still, *grad_specs],
        [pltpu.VMEM((n, d), F32), pltpu.VMEM((n, d), F32), pltpu.VMEM((d, tn), BF)]
        + ([pltpu.VMEM((2, n, d), BF), pltpu.SemaphoreType.DMA((2,))] if before else []),
        flops=24 * n * d * tn, name="ffn",
    )


def k_mid_back(scal, dl, acc, cot, mixed, fac_h, fac_f, keep, g_own, g_oth, m_own, m_oth,
               u_own, wg_own, h_own, f_own, packs_g, packs_u, packs_h):
    n, d = cot.shape
    half = u_own.shape[0]
    ch = h_own.shape[0]
    ru, rh = packs_u[0].shape[0], packs_h[0].shape[0] // 2
    rg = packs_g[0].shape[0]

    def body(s, l_ref, acc_ref, c_ref, x_ref, a_ref, b_ref, k_ref, go, gt, mo, mt, uo, wo, ho, fo,
             w0, w1, w2, w3, u0, u1, u2, u3, h0, h1, h2, h3, f0, f1, f2, f3,
             out_ref, dh_ref, df_ref, dir_ref, ao, at, do, dt, de_ref, u_scr, w_scr, h_scr, f_scr):
        @pl.when(pl.program_id(0) == 0)
        def _():
            place(u_scr, s, (u0, u1, u2, u3))
            place(w_scr, s, (w0, w1, w2, w3), table=8)
            own = pl.multiple_of(s[6] * ch, ch)
            oth = s[7] * ch
            h_scr[pl.ds(own, ch), :] = ho[...]
            f_scr[pl.ds(own, ch), :] = fo[...]
            place(h_scr, s, (h0, h1, h2, h3), oth, 8)
            place(f_scr, s, (f0, f1, f2, f3), oth, 8)

        dl = l_ref[...].astype(F32)
        m = x_ref[...].astype(F32)
        out_ref[...] = (m + acc_ref[...].astype(F32)).astype(BF)
        r = lax.rsqrt(jnp.mean(m * m, axis=-1, keepdims=True) + norm_eps)
        n2 = m * r
        dm = c_ref[...].astype(F32) + r * (dl - n2 * jnp.mean(dl * n2, axis=-1, keepdims=True))
        dh = (dm * a_ref[...].astype(F32)).astype(BF)
        df = (dm * b_ref[...].astype(F32)).astype(BF)
        dh_ref[...] = dh
        df_ref[...] = df
        dir_ref[...] = (dm * k_ref[...].astype(F32)).astype(BF)
        de = col_inner(dh, h_scr[...]) + col_inner(df, f_scr[...])
        for u, w, g_ref, m_ref, a_out, d_out in ((uo, wo, go, mo, ao, do), (u_scr, w_scr, gt, mt, at, dt)):
            dg = col_inner(dh, u[...])
            a_out[...] = (dg * g_ref[...].astype(F32)).astype(BF)
            low = (dg * m_ref[...].astype(F32)).astype(BF)
            d_out[...] = low
            de = de + col_inner(low, w[...])
        de_ref[...] = de.astype(BF)

    ins = [dl, acc, cot, mixed, fac_h, fac_f, keep, g_own, g_oth, m_own, m_oth, u_own, wg_own, h_own, f_own]
    ins += [*packs_g, *packs_u, *packs_h, *packs_h]
    specs = [rows_of(d)] * 7 + [rows_of(half)] * 4
    specs += [whole((half, d)), whole((d, half)), whole((ch, d)), whole((ch, d))]
    specs += [piece_whole(rg, half, 0)] * 4 + [piece_whole(ru, d, 0)] * 4
    specs += [piece_whole(rh, d, 0)] * 4 + [piece_whole(rh, d, 1)] * 4
    return run(
        body, (n // ROWS,), scal, ins, specs,
        [sds((n, d))] * 4 + [sds((n, half))] * 4 + [sds((n, d))],
        [rows_of(d)] * 4 + [rows_of(half)] * 4 + [rows_of(d)],
        [pltpu.VMEM((half, d), BF), pltpu.VMEM((d, half), BF), pltpu.VMEM((2 * ch, d), BF), pltpu.VMEM((2 * ch, d), BF)],
        flops=2 * n * d * (4 * half + 4 * ch), name="mid_back",
    )


def k_attend_back(scal, p, da_own, da_oth, v_own, v_oth, vs_own, vs_oth, q, k, z_pre, gain):
    n, zw = q.shape
    half = da_own.shape[1]
    blocks = n // ROWS
    scale = zw ** (-0.5)

    def body(s, p_ref, ao, at, vo, vt, so, st, q_ref, k_ref, z_ref, g_ref, oo, ot, dz_ref, sum_ref, dvo, dvt, dks):
        for step, i in enumerate(reversed(range(blocks))):

            @pl.when(pl.program_id(0) == step)
            def _(i=i):
                seen = (i + 1) * ROWS
                lo = i * ROWS
                last = i == blocks - 1
                pb = p_ref[:, 0:seen]
                pr = pb.astype(F32)
                dp = col_inner(ao[...], vo[0:seen, :]) + col_inner(at[...], vt[0:seen, :])
                ds = (pr * (dp - jnp.sum(pr * dp, axis=-1, keepdims=True))).astype(BF)
                dq = matmul(ds, k_ref[0:seen, :]) * scale
                dk = row_inner(ds, q_ref[...]) * scale
                if not last:
                    dk = dk + dks[0:seen, :]
                for a_ref, acc, sl, o_ref in ((ao, dvo, so, oo), (at, dvt, st, ot)):
                    dv = row_inner(pb, a_ref[...])
                    if not last:
                        dv = dv + acc[0:seen, :]
                    if i:
                        acc[0:lo, :] = dv[0:lo]
                    o_ref[...] = (dv[lo:seen] * sl[...].astype(F32)).astype(BF)
                if i:
                    dks[0:lo, :] = dk[0:lo]
                dk = dk[lo:seen]
                act, slope = silu_pair(z_ref[...])
                dz_ref[...] = (slope * (dq * g_ref[0:1, :] + dk * g_ref[1:2, :])).astype(BF)
                for j, v in enumerate((dq * act, dk * act, dq, dk)):
                    part = jnp.sum(v, axis=0, keepdims=True)
                    sum_ref[j : j + 1, :] = part if last else sum_ref[j : j + 1, :] + part
                if last:
                    sum_ref[4:8, :] = jnp.zeros((4, zw), F32)

    def back_rows(cols):
        return pl.BlockSpec((ROWS, cols), lambda i, s: (blocks - 1 - i, 0))

    low = n - ROWS
    return run(
        body, (blocks,), scal, [p, da_own, da_oth, v_own, v_oth, vs_own, vs_oth, q, k, z_pre, gain],
        [back_rows(n), back_rows(half), back_rows(half), whole((n, half)), whole((n, half)), back_rows(half),
         back_rows(half), back_rows(zw), whole((n, zw)), back_rows(zw), whole((2, zw))],
        [sds((n, half)), sds((n, half)), sds((n, zw)), sds((8, zw), F32)],
        [back_rows(half), back_rows(half), back_rows(zw), pl.BlockSpec((8, zw), lambda i, s: (0, 0))],
        [pltpu.VMEM((low, half), F32), pltpu.VMEM((low, half), F32), pltpu.VMEM((low, zw), F32)],
        flops=n * n * 4 * half * 1.25, name="attend_back",
    )


def k_input_back(scal, dv_own, dv_oth, w_own, packs, d_sig, tokens, direct, first, count, before=None):
    n, d = tokens.shape
    rp = packs[0].shape[0]
    half = dv_own.shape[1]

    def body(s, vo, vt, wo, w0, w1, w2, w3, sg, x_ref, dir_ref, *refs):
        o_ref, w_scr = refs[-2:]

        @pl.when(pl.program_id(0) == 0)
        def _():
            place(w_scr, s, (w0, w1, w2, w3))

        dn = col_inner(vo[...], wo[...]) + col_inner(vt[...], w_scr[...]) + sg[...]
        x = x_ref[...].astype(F32)
        r = lax.rsqrt(jnp.mean(x * x, axis=-1, keepdims=True) + norm_eps)
        n1 = x * r
        o_ref[...] = dir_ref[...].astype(F32) + r * (dn - n1 * jnp.mean(dn * n1, axis=-1, keepdims=True))

    def at(cols):
        return pl.BlockSpec((ROWS, cols), lambda i, s: (first + i, 0))

    more = [before] if before is not None else []
    return run(
        body, (count,), scal, [dv_own, dv_oth, w_own, *packs, d_sig, tokens, direct, *more],
        [at(half), at(half), whole((d, half))] + [piece_whole(rp, half, 0)] * 4 + [at(d)] * 3
        + [pl.BlockSpec(memory_space=pltpu.HBM)] * len(more),
        [sds((n, d), F32)], [at(d)],
        [pltpu.VMEM((d, half), BF)],
        flops=4 * ROWS * count * d * half, name="input_back", aliases={11: 0} if more else {},
    )[0]


def k_weight_mid(scal, ema_low, left, right_own, right_oth, gate, part, got=None):
    n, d = ema_low.shape
    tn = d // 4
    rows = d // 2

    def body(s, *refs):
        if gate:
            e_ref, *refs = refs
        l_ref, ro, rt, eo, et, *refs = refs
        for i in range(3):

            @pl.when(pl.program_id(0) == i)
            def _(i=i):
                for k, (r, e) in enumerate(((ro, eo), (rt, et))):
                    lhs = e_ref if gate and i < 2 else l_ref
                    grad = split_rows(s, row_inner(lhs[...], r[...] if i < 2 else e[...]))
                    for j in range(2):
                        if got is None:
                            put_rows(s, refs[0], grad[j], (k, j))
                        elif gate:
                            put_rows(s, refs[1 + k], grad[j], (j,), (refs[0], (k, j)))
                        else:
                            put_rows(s, refs[2 - j], grad[j], (k,), (refs[0], (k, j)))

    at = pl.BlockSpec((n, tn), lambda i, s: (0, s[part] * 2 + jnp.minimum(i, 1)))
    e_own = pl.BlockSpec((n, tn), lambda i, s: (0, s[6] * 2 + s[part]), pipeline_mode=pl.Buffered(1))
    e_oth = pl.BlockSpec((n, tn), lambda i, s: (0, s[7] * 2 + s[part]), pipeline_mode=pl.Buffered(1))
    four = pl.BlockSpec((2, 2, rows, tn), lambda i, s: (0, 0, 0, i))
    two = pl.BlockSpec((2, rows, tn), lambda i, s: (0, 0, i))
    adds = [got] if got is not None else []
    lead = [ema_low] if gate else []
    return run(
        body, (3,), scal, [*lead, left, right_own, right_oth, ema_low, ema_low] + adds,
        [whole((n, d))] * (1 + len(lead)) + [at] * 2 + [e_own, e_oth] + [four] * len(adds),
        [sds((2, rows, 3 * tn))] * 2 if adds else [sds((2, 2, rows, 3 * tn))],
        [two] * 2 if adds else [four],
        flops=2 * n * d * 6 * tn, name="weight_mid",
    )


def k_weight_value(scal, normed, dv_own, dv_oth, ema_low, dz, part, got=None):
    n, d = normed.shape
    width = dv_own.shape[1] // 2
    zw = dz.shape[1]
    shape = (2, 2, d // 2, width + zw)

    def body(s, x_ref, vo, vt, e_ref, z_ref, *refs):
        def put(lanes, value, k, j):
            add = (refs[0].at[:, :, :, lanes], (k, j)) if got is not None else None
            put_rows(s, refs[-1].at[:, :, :, lanes], value, (k, j), add)

        for k, v in enumerate((vo, vt)):
            grad = split_rows(s, row_inner(x_ref[...], v[...]))
            for j in range(2):
                put(slice(0, width), grad[j], k, j)
        grad = split_rows(s, row_inner(e_ref[...], z_ref[...]))
        for j in range(2):
            for k in range(2):
                put(slice(width, width + zw), grad[j], k, j)

    at = pl.BlockSpec((n, width), lambda i, s: (0, s[part]))
    adds = [got] if got is not None else []
    return run(
        body, (1,), scal, [normed, dv_own, dv_oth, ema_low, dz] + adds,
        [whole((n, d)), at, at, whole((n, d)), whole((n, zw))] + [whole(shape)] * len(adds),
        [sds(shape)], [pl.BlockSpec(shape, lambda i, s: (0, 0, 0, 0))],
        flops=2 * n * d * (2 * width + zw), name="weight_value",
    )[0]


def swap(values, axis, bit, size):
    return lax.ppermute(values, axis, [(i, i ^ bit) for i in range(size)])


def pick(values, index, axis):
    return lax.dynamic_index_in_dim(values, index, axis, keepdims=False)


def one_sequence(
    tokens, alpha_logit, delta_logit, ema_beta, ema_eta, ema_omega, w_z, qk_gain, qk_bias,
    w_v, w_gamma, u_h, w_h, w_phi, w_up, w_down, cotangent,
):
    n, d = tokens.shape
    dp_size = lax.axis_size("dp")
    me = lax.axis_index("dp").astype(jnp.int32)
    t = lax.axis_index("tensor").astype(jnp.int32)
    core = me % 2
    x_pos = (me // 2) % 2
    z_pos = me // 4
    kx = core * 2 + x_pos
    kz = core * 2 + z_pos % 2
    scal = jnp.stack(
        [kx, kx ^ 1, kx ^ 2, kx ^ 3, core, 1 - core, t, 1 - t, kz, kz ^ 1, kz ^ 2, kz ^ 3, x_pos, z_pos, 2 * core, 2 * core + 1]
    )

    def held(values, *deps):
        return lax.optimization_barrier((values, deps))[0]

    def after(*deps):
        return held(scal, *deps)

    def over_core(v):
        return swap(v, "dp", 1, dp_size)

    def over_x(v):
        return swap(v, "dp", 2, dp_size)

    def over_z(v):
        return swap(v, "dp", 4, dp_size)

    def over_tensor(v):
        return swap(v, "tensor", 1, 2)

    def my_rows(w, k):
        rows = w.shape[0] // 4
        return lax.dynamic_slice_in_dim(w, k * rows, rows, 0)

    piece_v = my_rows(w_v, kx)
    pv = [over_tensor(piece_v)]
    own_params = k_pack_params(
        after(piece_v), [a.T for a in (alpha_logit, delta_logit, ema_beta, ema_eta)], ema_omega[None]
    )
    oth_params = over_tensor(own_params)
    piece_g, piece_u, piece_h, piece_up, piece_dn = k_pieces(
        after(own_params),
        [[(w_gamma, 8)], [(u_h, 0)], [(w_h, 8), (w_phi, 8)], [(w_up, 0)], [(w_down, 14), (w_down, 15)]],
    )
    normed, v_own, vs_own = k_value_own(after(piece_g), tokens, w_v)
    pg = [over_tensor(held(piece_g, v_own))]
    decay, coef, omega = k_ema_params(after(v_own), own_params, oth_params)
    blocks = n // 128
    ema_a = k_ema_forward(after(v_own), normed, decay, coef, omega, 0, blocks // 2)
    pv.append(over_x(held(pv[0], ema_a[0])))
    pu = [over_tensor(held(piece_u, ema_a[0]))]
    ema_low, e_slope, state = k_ema_forward(
        after(ema_a[0]), normed, decay, coef, omega, blocks // 2, blocks // 2, (ema_a[2], ema_a[0], ema_a[1])
    )
    pg.append(over_z(held(pg[0], ema_a[0])))
    ph = [over_tensor(held(piece_h, state))]
    z_pre, query, key = k_query_key(scal, ema_low, w_z, qk_gain, qk_bias)
    pv += [over_core(v) for v in held((pv[0], pv[1]), query)]
    pu.append(over_x(held(pu[0], query)))
    pup = [over_tensor(held(piece_up, query))]
    v_oth, vs_oth = k_act_other(after(query, pu[0], pg[1]), normed, pv, 0, 512)
    pg += [over_core(v) for v in held((pg[0], pg[1]), v_oth)]
    ph.append(over_z(held(ph[0], v_oth)))
    pdn = [over_tensor(held(piece_dn, v_oth))]
    gated_own, gated_oth, g_own, g_oth, m_own, m_oth, probs = k_attend(
        after(v_oth), query, key, v_own, v_oth, ema_low, w_gamma, pg
    )
    pu += [over_core(v) for v in held((pu[0], pu[1]), probs)]
    ph += [over_core(v) for v in held((ph[0], ph[1]), probs)]
    pup.append(over_x(held(pup[0], probs)))
    mixed, lowered, fac_h, fac_f, keep = k_gate(
        after(probs), gated_own, gated_oth, ema_low, tokens, u_h, w_h, w_phi, pu, ph
    )
    acc, dl, sent_o = k_ffn(after(mixed), lowered, cotangent, [w_up], [w_down], 1)
    pup += [over_core(v) for v in held((pup[0], pup[1]), acc)]
    got_o = over_core(sent_o)
    acc, dl, dno, dno_x, upo, upo_x = k_ffn(
        after(acc), lowered, cotangent, [w_up], [w_down], 0, (acc, dl), "own"
    )
    pdn.append(over_core(held(pdn[0], acc)))

    def total(*values):
        value = values[0].astype(F32)
        for v in values[1:]:
            value = value + v.astype(F32)
        return value

    def add(*values):
        return total(*values).astype(BF)

    def by_z(v):
        return v.reshape(2, 2, d // 8, v.shape[-1])

    def z_send(terms):
        return add(*[by_z(v)[:, 1] for v in terms])

    def z_keep(terms):
        return [by_z(v)[:, 0] for v in terms]

    def over_z2(v):
        return swap(v, "dp", 8, dp_size)

    def core_split(value):
        rows = value.reshape(2, d // 16, value.shape[-1])
        return pick(rows, 1 - core, 0).astype(BF), pick(rows, core, 0)

    def joined(kept, got):
        kept, got = kept.astype(F32), got.astype(F32)
        return jnp.where(
            core == 0, jnp.concatenate([kept, got], axis=1), jnp.concatenate([got, kept], axis=1)
        )

    dn_x1 = add(dno_x, got_o[0, 1])
    dn_got_x1 = over_x(dn_x1)
    acc, dl, sent_t = k_ffn(after(acc, dn_x1), lowered, cotangent, pup, pdn, 1, (acc, dl))
    got_t = over_core(sent_t)
    acc, dl, dnt, dnt_x, upt = k_ffn(after(acc), lowered, cotangent, pup, pdn, 0, (acc, dl), "other")
    dn_x2 = add(dnt_x, got_t[0, 1])
    up_y1 = add(upt, got_t[1])
    dn_got_x2 = over_x(dn_x2)
    up_got_y = over_tensor(up_y1)
    output, dh, df, direct, da_own, da_oth, dg_own, dg_oth, de_part = k_mid_back(
        after(acc, dn_x2, up_y1, dn_got_x1), dl, acc, cotangent, mixed, fac_h, fac_f, keep,
        g_own, g_oth, m_own, m_oth, u_h, w_gamma, w_h, w_phi, pg, pu, ph,
    )
    dn_y = {}

    def start_dn(place, dep):
        if opt["dn"] == place:
            dn_y[0] = add(dnt, got_t[0, 0], held(dn_got_x2, dep))
            dn_y[1] = over_tensor(dn_y[0])
            return (dn_y[0],)
        return ()

    ma_sent = k_weight_mid(after(dh, *start_dn(0, dh)), ema_low, dh, gated_own, gated_oth, False, 5)[0]
    ma_got = over_core(ma_sent)
    mb_sent = k_weight_mid(after(ma_sent, *start_dn(1, ma_sent)), ema_low, df, dg_own, dg_oth, True, 5)[0]
    mb_got = over_core(mb_sent)
    dv_own, dv_oth, dz, stats = k_attend_back(
        after(mb_sent, *start_dn(2, mb_sent)), probs, da_own, da_oth, v_own, v_oth, vs_own, vs_oth, query, key, z_pre, qk_gain
    )
    up_got_y = held(up_got_y, dv_own)
    up_x = add(upo_x, got_o[1, 1], up_got_y[1])
    up_got_x = over_x(up_x)
    ma_theirs, ma_mine = k_weight_mid(after(dv_own, up_x), ema_low, dh, gated_own, gated_oth, False, 4, ma_got)
    ma_got_x = over_x(ma_theirs)
    mb_own, mb_oth = k_weight_mid(after(ma_theirs), ema_low, df, dg_own, dg_oth, True, 4, mb_got)
    mb_got_y = over_tensor(mb_oth)
    val_sent = k_weight_value(after(mb_own), normed, dv_own, dv_oth, ema_low, dz, 5)
    val_got = over_core(val_sent)
    dn_got_y = dn_y[1]
    up_got_x, dn_got_y = held((up_got_x, dn_got_y), val_sent)
    dn_terms = [dno, got_o[0, 0], dn_got_x1, dn_got_y]
    up_terms = [upo, got_o[1, 0], up_got_y[0], up_got_x]
    ffn_z = jnp.stack([z_send(dn_terms), z_send(up_terms)])
    dn_terms, up_terms = z_keep(dn_terms), z_keep(up_terms)
    ffn_got_z = over_z(ffn_z)
    quarter = blocks // 4

    def ema_back(dep, first, count, before=None):
        return k_ema_backward(
            after(*dep), normed, de_part, dz, e_slope, w_z, decay, coef, omega, first, count, before
        )

    eb = ema_back((val_sent, ffn_z), 0, quarter)
    val = k_weight_value(
        after(eb[1]), normed, dv_own, dv_oth, ema_low, dz, 4, val_got
    )
    val = val.reshape(2, 2, 2, 2, d // 8, val.shape[-1])
    val_z1 = val[:, :, :, 1]
    val_kept = val[:, :, :, 0]
    val_got_z1 = over_z(val_z1)
    eb = ema_back((val_z1,), quarter, quarter, eb)
    done = {}

    def second(place, dep):
        forced = []
        if opt["m2"] == place:
            gx, gy = held((ma_got_x, mb_got_y), dep)
            ma_y, mb_x = add(ma_mine[1], gx[1]), add(mb_own[1], gy[1])
            done["m"] = (gx, gy, over_tensor(ma_y), over_x(mb_x))
            forced += [ma_y, mb_x]
        if opt.get("z2", opt["m2"]) == place:
            gz = held(ffn_got_z, dep)
            done["z"] = [*dn_terms, gz[0]], [*up_terms, gz[1]]
            ffn_z2 = jnp.stack([add(*[v[1] for v in ts]) for ts in done["z"]])
            done["z2"] = over_z2(ffn_z2)
            forced.append(ffn_z2)
        if opt["v2"] == place:
            gz = held(val_got_z1, dep)
            val_x = add(val_kept[:, 1], gz[:, 1])
            done["v"] = (gz, over_x(val_x))
            forced.append(val_x)
        if opt.get("z1m", 6) == place:
            gy, gx = held((done["m"][2], done["m"][3]), dep)
            a_terms = [ma_mine[0], done["m"][0][0], gy]
            b_terms = [mb_own[0], done["m"][1][0], gx]
            mid_z = jnp.stack([z_send(a_terms), z_send(b_terms)])
            done["mz"] = (z_keep(a_terms), z_keep(b_terms), over_z(mid_z))
            forced.append(mid_z)
        return forced

    f2 = second(2, eb[1])
    eb = ema_back((eb[1], *f2), 2 * quarter, quarter, eb)
    f3 = second(3, eb[1])
    eb = ema_back((eb[1], *f3), 3 * quarter, quarter, eb)
    d_sig, _, _, sum_a, sum_b, sum_w = eb
    f4 = second(4, sum_a)
    sums = jnp.concatenate([sum_a, sum_b, sum_w, stats], axis=0)
    others = over_z(sums)
    halves = n // ROWS // 2
    part = k_input_back(
        after(sum_a, sums, done["z2"], *f4), dv_own, dv_oth, w_v, pv, d_sig, tokens, direct, 0, halves
    )
    ffn_got_z2 = held(done["z2"], part)
    ffn_total = jnp.stack([total(*[v[0] for v in ts], ffn_got_z2[i]) for i, ts in enumerate(done["z"])])
    ffn_rows = ffn_total.reshape(2, 2, d // 16, -1)
    ffn_got = over_core(pick(ffn_rows, 1 - core, 1).astype(BF))
    ffn_kept = pick(ffn_rows, core, 1)
    f5 = second(5, part)
    sums = sums + held(others, part)
    others = over_z2(sums)
    input_grad = k_input_back(
        after(part, sums, *f5), dv_own, dv_oth, w_v, pv, d_sig, tokens, direct, halves, halves, part
    )
    gz, gx = held(done["v"], input_grad)
    val_y = add(val_kept[1, 0], gz[1, 0], gx[1])
    val_terms = [val_kept[0, 0], gz[0, 0], gx[0], over_tensor(val_y)]
    dn_terms, up_terms = done["z"]
    ma_terms, mb_terms, mid_got_z = done["mz"]

    def last(terms):
        return total(*[v[0] for v in terms])

    sums = sums + held(others, input_grad)
    sums = sums + over_core(sums)
    sums = sums + over_x(sums)
    mid_got_z = held(mid_got_z, sums)
    ma_terms, mb_terms = [*ma_terms, mid_got_z[0]], [*mb_terms, mid_got_z[1]]
    mid_z2 = jnp.stack([add(*[v[1] for v in ma_terms]), add(*[v[1] for v in mb_terms])])
    mid_got_z2 = over_z2(mid_z2)
    sums_got = over_tensor(held(sums, mid_z2))
    val_terms[-1] = held(val_terms[-1], sums_got)
    val_z2 = add(*[v[1] for v in val_terms])
    val_got_z2 = over_z2(val_z2)
    sums = held(sums + sums_got, val_z2)
    down_t, up = joined(ffn_kept[0], ffn_got[0]), joined(ffn_kept[1], ffn_got[1])
    gh = sum_a.shape[0]

    def own_half(v):
        return lax.dynamic_slice_in_dim(v, t * (d // 2), d // 2, 1).T

    tot_a = own_half(sums[:gh].reshape(H, d))
    tot_b = own_half(sums[gh : 2 * gh].reshape(H, d))
    omega_grad = lax.dynamic_slice_in_dim(sums[2 * gh : 2 * gh + d // 128].reshape(d), t * (d // 2), d // 2, 0)
    zsum = sums[2 * gh + d // 128 :]
    rate = jax.nn.sigmoid(alpha_logit)
    damp = jax.nn.sigmoid(delta_logit)
    feed = rate * ema_beta
    feed_grad = ema_eta * tot_a
    decay_grad = feed * ema_eta * tot_b
    alpha_grad = (feed_grad * ema_beta - decay_grad * damp) * rate * (1.0 - rate)
    delta_grad = -decay_grad * rate * damp * (1.0 - damp)
    params = (alpha_grad, delta_grad, feed_grad * rate, feed * tot_a, omega_grad)
    down_grad = down_t.T
    mid_got_z2, val_got_z2 = held((mid_got_z2, val_got_z2), params, down_grad, up)
    mid_total = jnp.stack([total(last(ma_terms), mid_got_z2[0]), total(last(mb_terms), mid_got_z2[1])])
    mid_rows = mid_total.reshape(2, 2, d // 16, -1)
    mid_got = over_core(pick(mid_rows, 1 - core, 1).astype(BF))
    mid_kept = pick(mid_rows, core, 1)
    val_total = last(val_terms) + val_got_z2.astype(F32)
    val_sent, val_rows = core_split(val_total)
    zw = dz.shape[1]
    val_got = over_core(val_sent)
    tn = d // 4
    uh_t, gamma = (joined(mid_kept[i][:, : 2 * tn], mid_got[i][:, : 2 * tn]) for i in range(2))
    wh_t, phi_t = (joined(mid_kept[i][:, 2 * tn :], mid_got[i][:, 2 * tn :]) for i in range(2))
    value = joined(val_rows[:, :-zw], val_got[:, :-zw])
    z_grad = val_rows[:, -zw:]
    return (
        output, input_grad, *params,
        z_grad, zsum[0:2], zsum[2:4], value, gamma, uh_t.T, wh_t.T, phi_t.T, up, down_grad,
    )


def solution(mesh):
    placed = (
        P(("dp", "tensor"), None),
        P("tensor", None),
        P("tensor", None),
        P("tensor", None),
        P("tensor", None),
        P("tensor"),
        P(),
        P(),
        P(),
        P(None, "tensor"),
        P(None, "tensor"),
        P("tensor", None),
        P("tensor", None),
        P("tensor", None),
        P(None, "tensor"),
        P("tensor", None),
        P(("dp", "tensor"), None),
    )

    def per_device(tokens, *rest):
        whole_sequence = tokens.shape[0] == LEN and dict(mesh.shape) == {"dp": 16, "tensor": 2}
        return (one_sequence if whole_sequence else shards)(tokens, *rest)

    return jax.shard_map(
        per_device,
        mesh=mesh,
        in_specs=placed,
        out_specs=(
            P(("dp", "tensor"), None),
            P(("dp", "tensor"), None),
            P("tensor", None),
            P("tensor", None),
            P("tensor", None),
            P("tensor", None),
            P("tensor"),
            P("dp", None),
            P(),
            P(),
            P("dp", "tensor"),
            P("dp", "tensor"),
            P("tensor", "dp"),
            P("tensor", "dp"),
            P("tensor", "dp"),
            P("dp", "tensor"),
            P("tensor", "dp"),
        ),
        check_vma=False,
    )
```

```python
import math

import jax
import jax.numpy as jnp
from jax import lax
from jax.experimental import pallas as pl
from jax.experimental.pallas import tpu as pltpu
from jax.sharding import PartitionSpec as P

H = 16
LEN = 1024
ATT_BLOCK = 512
EMA_BLOCK = 128


norm_eps = 1e-06
masked_value = -1e30


def rms_rows(values_in):
    return values_in * lax.rsqrt(jnp.mean(values_in * values_in, axis=-1, keepdims=True) + norm_eps)


def matmul(left, right):
    return jnp.dot(left, right, preferred_element_type=jnp.float32)


def row_inner(left, right):
    return lax.dot_general(
        left, right, (((0,), (0,)), ((), ())), preferred_element_type=jnp.float32
    )


def col_inner(left, right):
    return lax.dot_general(
        left, right, (((1,), (1,)), ((), ())), preferred_element_type=jnp.float32
    )


def silu_slope(pre_act):
    logistic = jax.nn.sigmoid(pre_act)
    return logistic * (1.0 + pre_act * (1.0 - logistic))


def gate_apply(h_pre, f_pre, x_rows):
    update = jax.nn.sigmoid(f_pre)
    return update * jax.nn.silu(h_pre) + (1.0 - update) * x_rows


def ema_apply(signal, ema_params):
    alpha_logit, delta_logit, ema_beta, ema_eta, ema_omega = ema_params
    alpha_rate = jax.nn.sigmoid(alpha_logit)
    decay_rate = 1.0 - alpha_rate * jax.nn.sigmoid(delta_logit)
    feed_rate = alpha_rate * ema_beta
    log_decay = jnp.log(decay_rate)
    total_rows, chan_count = signal.shape
    seq_count = total_rows // LEN
    block_count = LEN // EMA_BLOCK
    blocks = signal.reshape(seq_count, block_count, EMA_BLOCK, chan_count)
    steps_in = jnp.arange(EMA_BLOCK, dtype=jnp.float32)
    lag_power = jnp.exp(steps_in[:, None, None] * log_decay[None])
    kernel = jnp.sum(lag_power * (feed_rate * ema_eta)[None], axis=-1)
    offsets = steps_in[:, None] - steps_in[None, :]
    lag_index = jnp.clip(offsets, 0, EMA_BLOCK - 1).astype(jnp.int32)
    toeplitz = jnp.where((offsets >= 0)[:, :, None], kernel[lag_index], 0.0)
    local_part = jnp.einsum("ijc,snjc->snic", toeplitz, blocks)
    tail_power = lag_power[::-1] * feed_rate[None]
    block_state = jnp.einsum("jch,snjc->snch", tail_power, blocks)
    full_decay = jnp.exp(EMA_BLOCK * log_decay)

    def carry_step(state_in, incoming):
        return (full_decay * state_in + incoming, state_in)

    zero_state = jnp.zeros((seq_count, chan_count, H), jnp.float32)
    _, start_state = lax.scan(carry_step, zero_state, jnp.moveaxis(block_state, 1, 0))
    start_state = jnp.moveaxis(start_state, 0, 1)
    head_power = lag_power * decay_rate[None] * ema_eta[None]
    carried = jnp.einsum("ich,snch->snic", head_power, start_state)
    ema_pre = (local_part + carried).reshape(total_rows, chan_count) + ema_omega * signal
    return jax.nn.silu(ema_pre)


def masked_scores(q_rows, k_rows, first_row):
    raw_scores = col_inner(q_rows, k_rows) * q_rows.shape[1] ** (-0.5)
    row_pos = first_row + jnp.arange(q_rows.shape[0])[:, None]
    col_pos = jnp.arange(k_rows.shape[0])[None, :]
    return jnp.where(col_pos <= row_pos, raw_scores, masked_value)


def attend_forward(query_low, key_low, value_low):
    total_rows, value_width = value_low.shape
    seq_count = total_rows // LEN
    per_seq = LEN // ATT_BLOCK

    def attend_one_block(flat_index):
        seq_id = flat_index // per_seq
        blk_id = flat_index % per_seq
        seq_start = seq_id * LEN
        q_rows = lax.dynamic_slice_in_dim(query_low, seq_start + blk_id * ATT_BLOCK, ATT_BLOCK, 0)
        k_rows = lax.dynamic_slice_in_dim(key_low, seq_start, LEN, 0)
        v_rows = lax.dynamic_slice_in_dim(value_low, seq_start, LEN, 0)
        scores = masked_scores(q_rows, k_rows, blk_id * ATT_BLOCK)
        top_score = jnp.max(scores, axis=-1, keepdims=True)
        weights = jnp.exp(scores - top_score)
        total_weight = jnp.sum(weights, axis=-1, keepdims=True)
        probs = (weights / total_weight).astype(jnp.bfloat16)
        return (matmul(probs, v_rows), top_score[:, 0] + jnp.log(total_weight[:, 0]))

    outs, lse_all = lax.map(attend_one_block, jnp.arange(seq_count * per_seq))
    return (outs.reshape(total_rows, value_width), lse_all.reshape(total_rows))


def attend_backward(query_low, key_low, value_low, lse_rows, d_att):
    total_rows, value_width = value_low.shape
    head_width = query_low.shape[1]
    seq_count = total_rows // LEN
    per_seq = LEN // ATT_BLOCK
    scale = head_width ** (-0.5)

    def one_seq(seq_id):
        seq_start = seq_id * LEN
        k_rows = lax.dynamic_slice_in_dim(key_low, seq_start, LEN, 0)
        v_rows = lax.dynamic_slice_in_dim(value_low, seq_start, LEN, 0)

        def one_one_block(carry_in, blk_id):
            d_keys, d_vals = carry_in
            row_start = seq_start + blk_id * ATT_BLOCK
            q_rows = lax.dynamic_slice_in_dim(query_low, row_start, ATT_BLOCK, 0)
            g_rows = lax.dynamic_slice_in_dim(d_att, row_start, ATT_BLOCK, 0)
            lse_part = lax.dynamic_slice_in_dim(lse_rows, row_start, ATT_BLOCK, 0)
            probs = jnp.exp(masked_scores(q_rows, k_rows, blk_id * ATT_BLOCK) - lse_part[:, None])
            d_probs = col_inner(g_rows, v_rows)
            d_scores = (
                probs * (d_probs - jnp.sum(probs * d_probs, axis=-1, keepdims=True))
            ).astype(jnp.bfloat16)
            d_rows = matmul(d_scores, k_rows) * scale
            d_keys = d_keys + row_inner(d_scores, q_rows) * scale
            d_vals = d_vals + row_inner(probs.astype(jnp.bfloat16), g_rows)
            return ((d_keys, d_vals), d_rows)

        start_carry = (
            jnp.zeros((LEN, head_width), jnp.float32),
            jnp.zeros((LEN, value_width), jnp.float32),
        )
        (d_keys, d_vals), d_rows = lax.scan(one_one_block, start_carry, jnp.arange(per_seq))
        return (d_rows.reshape(LEN, head_width), d_keys, d_vals)

    d_query, d_key, d_value = lax.map(one_seq, jnp.arange(seq_count))
    return (
        d_query.reshape(total_rows, head_width),
        d_key.reshape(total_rows, head_width),
        d_value.reshape(total_rows, value_width),
    )


def shards(
    tokens,
    alpha_logit,
    delta_logit,
    ema_beta,
    ema_eta,
    ema_omega,
    w_z,
    qk_gain,
    qk_bias,
    w_v,
    w_gamma,
    u_h,
    w_h,
    w_phi,
    w_up,
    w_down,
    cotangent,
):
    tensor_pos = lax.axis_index("tensor")
    feature_count = tokens.shape[1]
    chan_count = ema_omega.shape[0]
    chan_start = tensor_pos * chan_count
    x_rows = tokens.astype(jnp.float32)
    normed_rows, norm_pull = jax.vjp(rms_rows, x_rows)
    normed, cot_full = (
        lax.all_gather(normed_rows.astype(jnp.bfloat16), "tensor", axis=0, tiled=True),
        lax.all_gather(cotangent, "tensor", axis=0, tiled=True),
    )
    signal = lax.dynamic_slice_in_dim(normed, chan_start, chan_count, 1).astype(jnp.float32)
    ema_params = (alpha_logit, delta_logit, ema_beta, ema_eta, ema_omega)
    ema_val, ema_pull = jax.vjp(ema_apply, signal, ema_params)
    ema_low = ema_val.astype(jnp.bfloat16)
    ema_full = lax.all_gather(ema_low, "tensor", axis=1, tiled=True)
    z_pre = matmul(ema_full, w_z)
    z_act = jax.nn.silu(z_pre)
    query_low = (z_act * qk_gain[0] + qk_bias[0]).astype(jnp.bfloat16)
    key_low = (z_act * qk_gain[1] + qk_bias[1]).astype(jnp.bfloat16)
    values_pre = matmul(normed, w_v)
    value_low = jax.nn.silu(values_pre).astype(jnp.bfloat16)
    gamma_pre = matmul(ema_full, w_gamma)
    gamma_act = jax.nn.silu(gamma_pre)
    attended, lse_rows = attend_forward(query_low, key_low, value_low)
    gated_low = (gamma_act * attended).astype(jnp.bfloat16)
    both_pre = lax.psum_scatter(
        jnp.concatenate(
            [matmul(gated_low, u_h) + matmul(ema_low, w_h), matmul(ema_low, w_phi)], axis=1
        ),
        "tensor",
        scatter_dimension=0,
        tiled=True,
    )
    h_pre = both_pre[:, :feature_count]
    f_pre = both_pre[:, feature_count:]
    mixed, gate_pull = jax.vjp(gate_apply, h_pre, f_pre, x_rows)
    normed_two, norm_two_pull = jax.vjp(rms_rows, mixed)
    lowered = lax.all_gather(normed_two.astype(jnp.bfloat16), "tensor", axis=0, tiled=True)
    up_pre = matmul(lowered, w_up)
    hidden = jax.nn.silu(up_pre).astype(jnp.bfloat16)
    down_rows = lax.psum_scatter(
        matmul(hidden, w_down).astype(jnp.bfloat16), "tensor", scatter_dimension=0, tiled=True
    ).astype(jnp.float32)
    output = (mixed + down_rows).astype(jnp.bfloat16)
    cot_rows = cotangent.astype(jnp.float32)
    d_hidden = col_inner(cot_full, w_down)
    d_up = (d_hidden * silu_slope(up_pre)).astype(jnp.bfloat16)
    down_grad = row_inner(hidden, cot_full)
    up_grad = row_inner(lowered, d_up)
    d_lowered = lax.psum_scatter(col_inner(d_up, w_up), "tensor", scatter_dimension=0, tiled=True)
    d_mixed = cot_rows + norm_two_pull(d_lowered)[0]
    d_hpre, d_fpre, d_direct = gate_pull(d_mixed)
    h_full_grad, f_full_grad = (
        lax.all_gather(d_hpre.astype(jnp.bfloat16), "tensor", axis=0, tiled=True),
        lax.all_gather(d_fpre.astype(jnp.bfloat16), "tensor", axis=0, tiled=True),
    )
    uh_grad = row_inner(gated_low, h_full_grad)
    wh_grad = row_inner(ema_low, h_full_grad)
    phi_grad = row_inner(ema_low, f_full_grad)
    d_gated = col_inner(h_full_grad, u_h)
    d_att = (d_gated * gamma_act).astype(jnp.bfloat16)
    d_gamma = (d_gated * attended * silu_slope(gamma_pre)).astype(jnp.bfloat16)
    d_query, d_key, d_value = attend_backward(query_low, key_low, value_low, lse_rows, d_att)
    d_query, d_key = lax.psum((d_query, d_key), "tensor")
    d_z = (silu_slope(z_pre) * (d_query * qk_gain[0] + d_key * qk_gain[1])).astype(jnp.bfloat16)
    gain_grad = jnp.stack([jnp.sum(d_query * z_act, axis=0), jnp.sum(d_key * z_act, axis=0)])
    bias_grad = jnp.stack([jnp.sum(d_query, axis=0), jnp.sum(d_key, axis=0)])
    z_grad = row_inner(ema_full, d_z)
    gamma_grad = row_inner(ema_full, d_gamma)
    d_value_pre = (d_value * silu_slope(values_pre)).astype(jnp.bfloat16)
    value_grad = row_inner(normed, d_value_pre)
    d_chan = lax.psum_scatter(
        col_inner(d_gamma, w_gamma).astype(jnp.bfloat16), "tensor", scatter_dimension=1, tiled=True
    ).astype(jnp.float32)
    z_rows = lax.dynamic_slice_in_dim(w_z, chan_start, chan_count, 0)
    d_chan = (
        d_chan
        + col_inner(d_z, z_rows)
        + col_inner(h_full_grad, w_h)
        + col_inner(f_full_grad, w_phi)
    )
    d_signal, d_params = ema_pull(d_chan)
    d_norm_part = col_inner(d_value_pre, w_v)
    own_cols = lax.dynamic_slice_in_dim(d_norm_part, chan_start, chan_count, 1)
    d_norm_part = lax.dynamic_update_slice_in_dim(d_norm_part, own_cols + d_signal, chan_start, 1)
    d_normed = lax.psum_scatter(
        d_norm_part.astype(jnp.bfloat16), "tensor", scatter_dimension=0, tiled=True
    ).astype(jnp.float32)
    input_grad = d_direct + norm_pull(d_normed)[0]
    weight_totals = (
        lax.psum_scatter(z_grad.astype(jnp.bfloat16), "dp", scatter_dimension=0, tiled=True).astype(
            jnp.float32
        ),
        lax.psum_scatter(
            value_grad.astype(jnp.bfloat16), "dp", scatter_dimension=0, tiled=True
        ).astype(jnp.float32),
        lax.psum_scatter(
            gamma_grad.astype(jnp.bfloat16), "dp", scatter_dimension=0, tiled=True
        ).astype(jnp.float32),
        lax.psum_scatter(
            uh_grad.astype(jnp.bfloat16), "dp", scatter_dimension=1, tiled=True
        ).astype(jnp.float32),
        lax.psum_scatter(
            wh_grad.astype(jnp.bfloat16), "dp", scatter_dimension=1, tiled=True
        ).astype(jnp.float32),
        lax.psum_scatter(
            phi_grad.astype(jnp.bfloat16), "dp", scatter_dimension=1, tiled=True
        ).astype(jnp.float32),
        lax.psum_scatter(
            up_grad.astype(jnp.bfloat16), "dp", scatter_dimension=0, tiled=True
        ).astype(jnp.float32),
        lax.psum_scatter(
            down_grad.astype(jnp.bfloat16), "dp", scatter_dimension=1, tiled=True
        ).astype(jnp.float32),
    )
    param_totals = lax.psum(
        (d_params[0], d_params[1], d_params[2], d_params[3], d_params[4], gain_grad, bias_grad),
        "dp",
    )
    return (
        output,
        input_grad,
        param_totals[0],
        param_totals[1],
        param_totals[2],
        param_totals[3],
        param_totals[4],
        weight_totals[0],
        param_totals[5],
        param_totals[6],
        weight_totals[1],
        weight_totals[2],
        weight_totals[3],
        weight_totals[4],
        weight_totals[5],
        weight_totals[6],
        weight_totals[7],
    )


MIB = 1024 * 1024
BF = jnp.bfloat16
F32 = jnp.float32
ROWS = 256
hints = dict(ema_backward2=0.3, weight_value=0.3)
opt = dict(dn=0, m2=3, v2=4, z2=3, z1m=5)


def sds(shape, dtype=BF):
    return jax.ShapeDtypeStruct(shape, dtype)


def whole(shape):
    return pl.BlockSpec(shape, lambda i, s: (0,) * len(shape), pipeline_mode=pl.Buffered(1))


def rows_of(cols, rows=ROWS):
    return pl.BlockSpec((rows, cols), lambda i, s: (i, 0))


def cols_of(rows, cols):
    return pl.BlockSpec((rows, cols), lambda i, s: (0, i))


def run(body, grid, scal, ins, in_specs, out_shape, out_specs, scratch=(), flops=0, name=None, aliases=None, spare=12):
    moved = sum(a.size * a.dtype.itemsize for a in ins)
    moved += sum(math.prod(o.shape) * jnp.dtype(o.dtype).itemsize for o in out_shape)
    def held_bytes(spec, a):
        if spec.block_shape is None:
            return 0
        return math.prod(spec.block_shape) * jnp.dtype(a.dtype).itemsize * (1 if spec.pipeline_mode else 2)

    if name in ("attend", "gate", "ffn", "mid_back", "pack_params", "ema_params", "pieces"):
        spare = 56
    vmem = sum(map(held_bytes, in_specs, ins)) + sum(map(held_bytes, out_specs, out_shape))
    vmem += sum(math.prod(r.shape) * jnp.dtype(r.dtype).itemsize for r in scratch if r.memory_space == pltpu.VMEM)
    return pl.pallas_call(
        body,
        out_shape=out_shape,
        grid_spec=pltpu.PrefetchScalarGridSpec(
            num_scalar_prefetch=1,
            grid=grid,
            in_specs=in_specs,
            out_specs=out_specs,
            scratch_shapes=list(scratch),
        ),
        compiler_params=pltpu.CompilerParams(vmem_limit_bytes=min(vmem + spare * MIB, 56 * MIB)),
        cost_estimate=pl.CostEstimate(flops=int(flops * hints.get(name, 10)), bytes_accessed=int(moved * hints.get(name, 10)), transcendentals=0),
        name=name,
        input_output_aliases=aliases or {},
    )(scal, *ins)


def sig(u):
    return 0.5 + 0.5 * jnp.tanh(0.5 * u)


def silu_pair(u):
    s = sig(u)
    return u * s, s * (1.0 + u * (1.0 - s))


def place(scr, s, pieces, base=0, table=0):
    rows = pieces[0].shape[0]
    for p in range(4):
        scr[pl.ds(pl.multiple_of(base + s[table + p] * rows, rows), rows), :] = pieces[p][...]


def piece_block(rows, cols, row_block):
    return pl.BlockSpec((rows, cols), lambda i, s: (row_block, i))


def piece_whole(rows, cols, row_block):
    return pl.BlockSpec((rows, cols), lambda i, s: (row_block, 0), pipeline_mode=pl.Buffered(1))


def k_value_own(scal, tokens, w_own):
    n, d = tokens.shape
    cols = w_own.shape[1]
    tn = 512

    def body(s, x_ref, w_ref, n_ref, v_ref, sl_ref):
        @pl.when(pl.program_id(0) == 0)
        def _():
            x = x_ref[...].astype(F32)
            n_ref[...] = (x * lax.rsqrt(jnp.mean(x * x, axis=-1, keepdims=True) + norm_eps)).astype(BF)

        act, slope = silu_pair(matmul(n_ref[...], w_ref[...]))
        v_ref[...] = act.astype(BF)
        sl_ref[...] = slope.astype(BF)

    return run(
        body, (cols // tn,), scal, [tokens, w_own],
        [whole((n, d)), cols_of(d, tn)],
        [sds((n, d)), sds((n, cols)), sds((n, cols))],
        [pl.BlockSpec((n, d), lambda i, s: (0, 0)), cols_of(n, tn), cols_of(n, tn)],
        flops=2 * n * d * cols, name="value_own",
    )


def k_act_own(scal, x, w_own, tn):
    n, d = x.shape
    cols = w_own.shape[1]

    def body(s, x_ref, w_ref, v_ref, sl_ref):
        act, slope = silu_pair(matmul(x_ref[...], w_ref[...]))
        v_ref[...] = act.astype(BF)
        sl_ref[...] = slope.astype(BF)

    return run(
        body, (cols // tn,), scal, [x, w_own],
        [whole((n, d)), cols_of(d, tn)],
        [sds((n, cols)), sds((n, cols))],
        [cols_of(n, tn), cols_of(n, tn)],
        flops=2 * n * d * cols, name="act_own",
    )


def k_act_other(scal, x, pieces, table, tn):
    n, d = x.shape
    rows, cols = pieces[0].shape

    def body(s, x_ref, p0, p1, p2, p3, v_ref, sl_ref, w_scr):
        place(w_scr, s, (p0, p1, p2, p3), table=table)
        act, slope = silu_pair(matmul(x_ref[...], w_scr[...]))
        v_ref[...] = act.astype(BF)
        sl_ref[...] = slope.astype(BF)

    return run(
        body, (cols // tn,), scal, [x, *pieces],
        [whole((n, d))] + [piece_block(rows, tn, 0)] * 4,
        [sds((n, cols)), sds((n, cols))],
        [cols_of(n, tn), cols_of(n, tn)],
        [pltpu.VMEM((d, tn), BF)],
        flops=2 * n * d * cols, name="act_other",
    )


def k_query_key(scal, ema_low, w_z, qk_gain, qk_bias):
    n, d = ema_low.shape
    zw = w_z.shape[1]

    def body(s, e_ref, w_ref, g_ref, b_ref, z_ref, q_ref, k_ref):
        z_pre = matmul(e_ref[...], w_ref[...])
        z_ref[...] = z_pre
        act = z_pre * sig(z_pre)
        q_ref[...] = (act * g_ref[0:1, :] + b_ref[0:1, :]).astype(BF)
        k_ref[...] = (act * g_ref[1:2, :] + b_ref[1:2, :]).astype(BF)

    return run(
        body, (2,), scal, [ema_low, w_z, qk_gain, qk_bias],
        [rows_of(d, n // 2), whole((d, zw)), whole((2, zw)), whole((2, zw))],
        [sds((n, zw), F32), sds((n, zw)), sds((n, zw))],
        [rows_of(zw, n // 2)] * 3,
        flops=2 * n * d * zw, name="query_key",
    )


def k_pack_params(scal, arrays, omega):
    ch = omega.shape[1]

    def body(s, a0, a1, a2, a3, w_ref, o_ref):
        for i, ref in enumerate((a0, a1, a2, a3)):
            o_ref[i * H : (i + 1) * H, :] = ref[...]
        o_ref[4 * H : 4 * H + 8, :] = jnp.broadcast_to(w_ref[...], (8, ch))

    return run(
        body, (1,), scal, [*arrays, omega], [whole((H, ch))] * 4 + [whole((1, ch))],
        [sds((4 * H + 8, ch), F32)], [pl.BlockSpec((4 * H + 8, ch), lambda i, s: (0, 0))], flops=1e7, name="pack_params",
    )[0]


def k_ema_params(scal, own, oth):
    height, ch = own.shape
    groups = 2 * ch // 128

    def body(s, own_ref, oth_ref, dec_ref, cf_ref, om_ref):
        for j in range(2):
            for src, ref in ((0, own_ref), (1, oth_ref)):

                @pl.when(s[6 + src] == j)
                def _(j=j, ref=ref):
                    v = ref[...]
                    rate = sig(v[0:H])
                    dec = 1.0 - rate * sig(v[H : 2 * H])
                    cf = rate * v[2 * H : 3 * H] * v[3 * H : 4 * H]
                    for g in range(groups // 2):
                        lanes = slice(g * 128, (g + 1) * 128)
                        at = j * (groups // 2) + g
                        dec_ref[pl.ds(at, H, stride=groups), :] = dec[:, lanes]
                        cf_ref[pl.ds(at, H, stride=groups), :] = cf[:, lanes]
                        om_ref[at : at + 1, :] = v[4 * H : 4 * H + 1, lanes]

    par = (H * groups, 128)
    return run(
        body, (1,), scal, [own, oth], [whole((height, ch))] * 2,
        [sds(par, F32), sds(par, F32), sds((groups, 128), F32)],
        [pl.BlockSpec(par, lambda i, s: (0, 0))] * 2 + [pl.BlockSpec((groups, 128), lambda i, s: (0, 0))],
        flops=1e8, name="ema_params",
    )


def k_pieces(scal, takes):
    parts = [(w, at) for take in takes for w, at in take]

    def body(s, *refs):
        ins, outs = refs[: len(parts)], refs[len(parts) :]
        n = 0
        for take, out in zip(takes, outs):
            low = 0
            for w, _ in take:
                rows = w.shape[0] // 4
                out[low : low + rows, :] = ins[n][...]
                low += rows
                n += 1

    return run(
        body, (1,), scal, [w for w, _ in parts],
        [pl.BlockSpec((w.shape[0] // 4, w.shape[1]), lambda i, s, at=at: (s[at], 0)) for w, at in parts],
        [sds((sum(w.shape[0] // 4 for w, _ in take), take[0][0].shape[1])) for take in takes],
        [pl.BlockSpec((sum(w.shape[0] // 4 for w, _ in take), take[0][0].shape[1]), lambda i, s: (0, 0)) for take in takes],
        flops=1e7, name="pieces",
    )


def k_ema_forward(scal, normed, decay, coef, omega, first, count, before=None):
    n, d = normed.shape
    groups = d // 128
    tb = 128

    def body(s, x_ref, dec_ref, cf_ref, om_ref, *refs):
        e_ref, sl_ref, st, xs, ys = refs[-5:]

        @pl.when(pl.program_id(0) == 0)
        def _():
            st[...] = refs[0][...] if before else jnp.zeros_like(st)

        for g in range(groups):
            xs[pl.ds(g, tb, stride=groups), :] = x_ref[:, g * 128 : (g + 1) * 128].astype(F32)
        dec = [dec_ref[k * groups : (k + 1) * groups, :] for k in range(H)]
        cf = [cf_ref[k * groups : (k + 1) * groups, :] for k in range(H)]
        om = om_ref[...]

        def steps(b, carry):
            states = list(carry)
            for u in range(16):
                row = pl.multiple_of((b * 16 + u) * groups, groups)
                xt = xs[pl.ds(row, groups), :]
                parts = [om * xt, None, None, None]
                for k in range(H):
                    states[k] = dec[k] * states[k] + xt
                    term = cf[k] * states[k]
                    parts[k % 4] = term if parts[k % 4] is None else parts[k % 4] + term
                ys[pl.ds(row, groups), :] = (parts[0] + parts[1]) + (parts[2] + parts[3])
            return tuple(states)

        start = tuple(st[k * groups : (k + 1) * groups, :] for k in range(H))
        end = lax.fori_loop(0, tb // 16, steps, start)
        for k in range(H):
            st[k * groups : (k + 1) * groups, :] = end[k]
        for g in range(groups):
            act, slope = silu_pair(ys[pl.ds(g, tb, stride=groups), :])
            e_ref[:, g * 128 : (g + 1) * 128] = act.astype(BF)
            sl_ref[:, g * 128 : (g + 1) * 128] = slope.astype(BF)

    par = (H * groups, 128)
    at = pl.BlockSpec((tb, d), lambda i, s: (first + i, 0))
    more = list(before) if before else []
    return run(
        body, (count,), scal, [normed, decay, coef, omega, *more],
        [at, whole(par), whole(par), whole((groups, 128))]
        + ([whole(par), pl.BlockSpec(memory_space=pltpu.HBM), pl.BlockSpec(memory_space=pltpu.HBM)] if before else []),
        [sds((n, d)), sds((n, d)), sds(par, F32)],
        [at, at, pl.BlockSpec(par, lambda i, s: (0, 0))],
        [pltpu.VMEM((tb * groups, 128), F32), pltpu.VMEM((tb * groups, 128), F32)],
        flops=2.5e9 * count, name="ema_forward", aliases={6: 0, 7: 1} if before else {},
    )


def k_ema_backward(scal, normed, de_part, dz, slope, w_z, decay, coef, omega, first, count, before=None):
    n, d = normed.shape
    groups = d // 128
    tb = 128
    nb = n // tb
    half = H // 2
    gh = groups * half
    zw = dz.shape[1]

    def body(s, x_ref, de_ref, z_ref, sl_ref, wz_ref, dec_ref, cf_ref, om_ref, *refs):
        o_ref, back, deriv, a_ref, b_ref, w_ref, xs, gs, ys = refs[-9:]

        @pl.when(pl.program_id(0) == 0)
        def _():
            for i, ref in enumerate((back, deriv, a_ref, b_ref, w_ref)):
                ref[...] = refs[i][...] if before else jnp.zeros_like(ref)

        d_e = (de_ref[...].astype(F32) + col_inner(z_ref[...], wz_ref[...])) * sl_ref[...].astype(F32)
        for g in range(groups):
            xs[pl.ds(g, tb, stride=groups), :] = x_ref[:, g * 128 : (g + 1) * 128].astype(F32)
            gs[pl.ds(g, tb, stride=groups), :] = d_e[:, g * 128 : (g + 1) * 128]

        for part in range(2):
            low = part * gh
            at = [slice(low + k * groups, low + (k + 1) * groups) for k in range(half)]
            dec = [dec_ref[a, :] for a in at]

            def steps(b, carry, part=part, at=at, dec=dec):
                bk, dv, aa, bb, ww = (list(c) for c in carry)
                for u in range(8):
                    row = pl.multiple_of((tb - 1 - (b * 8 + u)) * groups, groups)
                    xt = xs[pl.ds(row, groups), :]
                    gt = gs[pl.ds(row, groups), :]
                    if part == 0:
                        outs = [om_ref[...] * gt, None]
                        ww[0] = ww[0] + xt * gt
                    else:
                        outs = [ys[pl.ds(row, groups), :], None]
                    for k in range(half):
                        dv[k] = dec[k] * dv[k] + bk[k]
                        bk[k] = dec[k] * bk[k] + gt
                        term = cf_ref[at[k], :] * bk[k]
                        outs[k % 2] = term if outs[k % 2] is None else outs[k % 2] + term
                        aa[k] = aa[k] + xt * bk[k]
                        bb[k] = bb[k] + xt * dv[k]
                    ys[pl.ds(row, groups), :] = outs[0] + outs[1]
                return tuple(bk), tuple(dv), tuple(aa), tuple(bb), tuple(ww)

            start = (
                tuple(back[a, :] for a in at),
                tuple(deriv[a, :] for a in at),
                tuple(a_ref[a, :] for a in at),
                tuple(b_ref[a, :] for a in at),
                (w_ref[...],),
            )
            bk, dv, aa, bb, ww = lax.fori_loop(0, tb // 8, steps, start)
            for k in range(half):
                back[at[k], :] = bk[k]
                deriv[at[k], :] = dv[k]
                a_ref[at[k], :] = aa[k]
                b_ref[at[k], :] = bb[k]
            w_ref[...] = ww[0]
        for g in range(groups):
            o_ref[:, g * 128 : (g + 1) * 128] = ys[pl.ds(g, tb, stride=groups), :]

    top = nb - 1 - first
    back_rows = pl.BlockSpec((tb, d), lambda i, s: (top - i, 0))
    par = (H * groups, 128)
    const = pl.BlockSpec(par, lambda i, s: (0, 0))
    small = (groups, 128)
    more = [*before[1:], before[0]] if before else []
    return run(
        body, (count,), scal, [normed, de_part, dz, slope, w_z, decay, coef, omega, *more],
        [back_rows, back_rows, pl.BlockSpec((tb, zw), lambda i, s: (top - i, 0)), back_rows, whole((d, zw)),
         whole(par), whole(par), whole(small)]
        + ([whole(par)] * 4 + [whole(small), pl.BlockSpec(memory_space=pltpu.HBM)] if before else []),
        [sds((n, d), F32)] + [sds(par, F32)] * 4 + [sds(small, F32)],
        [back_rows, const, const, const, const, pl.BlockSpec(small, lambda i, s: (0, 0))],
        [pltpu.VMEM((tb * groups, 128), F32)] * 3,
        flops=5e9 * count, name=f"ema_backward{first}", aliases={14: 0} if before else {},
    )


def k_attend(scal, q, k, v_own, v_oth, ema_low, g_own, packs):
    n, zw = q.shape
    d, half = g_own.shape
    rp = packs[0].shape[0]
    blocks = n // ROWS
    scale = zw ** (-0.5)

    def body(s, q_ref, k_ref, vo, vt, e_ref, wo, w0, w1, w2, w3, gated_o, gated_t, go, gt, mo, mt, p_ref, w_scr):
        @pl.when(pl.program_id(0) == 0)
        def _():
            place(w_scr, s, (w0, w1, w2, w3), table=8)

        for i in range(blocks):

            @pl.when(pl.program_id(0) == i)
            def _(i=i):
                seen = (i + 1) * ROWS
                sc = col_inner(q_ref[...], k_ref[0:seen, :]) * scale
                row = i * ROWS + lax.broadcasted_iota(jnp.int32, (ROWS, seen), 0)
                col = lax.broadcasted_iota(jnp.int32, (ROWS, seen), 1)
                sc = jnp.where(col <= row, sc, masked_value)
                e = jnp.exp(sc - jnp.max(sc, axis=-1, keepdims=True))
                p = (e * (1.0 / jnp.sum(e, axis=-1, keepdims=True))).astype(BF)
                p_ref[:, 0:seen] = p
                if seen < n:
                    p_ref[:, seen:] = jnp.zeros((ROWS, n - seen), BF)
                for v_ref, w, gated, g, m in ((vo, wo, gated_o, go, mo), (vt, w_scr, gated_t, gt, mt)):
                    act, slope = silu_pair(matmul(e_ref[...], w[...]))
                    att = matmul(p, v_ref[0:seen, :])
                    gated[...] = (act * att).astype(BF)
                    g[...] = act.astype(BF)
                    m[...] = (slope * att).astype(BF)

    return run(
        body, (blocks,), scal, [q, k, v_own, v_oth, ema_low, g_own, *packs],
        [rows_of(zw), whole((n, zw)), whole((n, half)), whole((n, half)), rows_of(d), whole((d, half))]
        + [whole((rp, half))] * 4,
        [sds((n, half))] * 6 + [sds((n, n))],
        [rows_of(half)] * 6 + [rows_of(n)],
        [pltpu.VMEM((d, half), BF)],
        flops=n * n * (zw + 2 * half) * 1.25 + 4 * n * d * half, name="attend",
    )


def k_gate(scal, gated_own, gated_oth, ema_low, tokens, u_own, h_own, f_own, packs_u, packs_h):
    n, d = tokens.shape
    half = u_own.shape[0]
    ch = h_own.shape[0]
    ru, rh = packs_u[0].shape[0], packs_h[0].shape[0] // 2

    def body(s, go, gt, e_ref, x_ref, uo, ho, fo, u0, u1, u2, u3, h0, h1, h2, h3, f0, f1, f2, f3,
             mix_ref, low_ref, a_ref, b_ref, up_ref, u_scr, h_scr, f_scr):
        @pl.when(pl.program_id(0) == 0)
        def _():
            place(u_scr, s, (u0, u1, u2, u3))
            own = pl.multiple_of(s[6] * ch, ch)
            oth = s[7] * ch
            h_scr[pl.ds(own, ch), :] = ho[...]
            f_scr[pl.ds(own, ch), :] = fo[...]
            place(h_scr, s, (h0, h1, h2, h3), oth, 8)
            place(f_scr, s, (f0, f1, f2, f3), oth, 8)

        h_pre = matmul(go[...], uo[...]) + matmul(gt[...], u_scr[...]) + matmul(e_ref[...], h_scr[...])
        f_pre = matmul(e_ref[...], f_scr[...])
        x = x_ref[...].astype(F32)
        act, slope = silu_pair(h_pre)
        update = sig(f_pre)
        mixed = update * act + (1.0 - update) * x
        mix_ref[...] = mixed.astype(BF)
        low_ref[...] = (mixed * lax.rsqrt(jnp.mean(mixed * mixed, axis=-1, keepdims=True) + norm_eps)).astype(BF)
        a_ref[...] = (update * slope).astype(BF)
        b_ref[...] = ((act - x) * update * (1.0 - update)).astype(BF)
        up_ref[...] = (1.0 - update).astype(BF)

    ins = [gated_own, gated_oth, ema_low, tokens, u_own, h_own, f_own, *packs_u, *packs_h, *packs_h]
    specs = [rows_of(half), rows_of(half), rows_of(d), rows_of(d), whole((half, d)), whole((ch, d)), whole((ch, d))]
    specs += [piece_whole(ru, d, 0)] * 4 + [piece_whole(rh, d, 0)] * 4 + [piece_whole(rh, d, 1)] * 4
    return run(
        body, (n // ROWS,), scal, ins, specs,
        [sds((n, d))] * 5,
        [rows_of(d)] * 5,
        [pltpu.VMEM((half, d), BF), pltpu.VMEM((2 * ch, d), BF), pltpu.VMEM((2 * ch, d), BF)],
        flops=2 * n * d * (2 * half + 4 * ch), name="gate",
    )


def split_rows(s, grad):
    d, c = grad.shape
    by_x = grad.reshape(4, 2, d // 8, c)
    flip = s[12] == 0
    a, b = by_x[:, 0].reshape(d // 2, c), by_x[:, 1].reshape(d // 2, c)
    return jnp.where(flip, a, b), jnp.where(flip, b, a)


def put_rows(s, ref, value, lead=(), add=None):
    rows = value.shape[0] // 4
    for z in range(4):
        at = pl.ds(pl.multiple_of((s[13] ^ z) * rows, rows), rows)
        part = value[z * rows : (z + 1) * rows]
        if add is not None:
            part = part + add[0][(*add[1], at, slice(None))].astype(F32)
        ref[(*lead, at, slice(None))] = part.astype(BF)


def k_ffn(scal, lowered, cot, up, down, part, before=None, form="sent"):
    n, d = lowered.shape
    pieces = len(up) > 1
    tn = up[0].shape[1] // 4
    rows = d // 2

    def body(s, low_ref, c_ref, *refs):
        step = pl.program_id(0)
        nu = len(up)
        ups, wd, refs = refs[:nu], refs[nu], refs[nu + 1 :]
        if before:
            ins, refs = refs[:2], refs[2:]
            held, sems = refs[-2:]
            refs = refs[:-2]
            copies = [pltpu.make_async_copy(ins[i], held.at[i], sems.at[i]) for i in range(2)]
        out_ref, gl_ref, *grads, acc, gl, u_scr = refs
        if pieces:
            place(u_scr, s, ups)
            wu = u_scr
        else:
            wu = ups[0]

        def work(wd, i):
            if before and i == 0:
                for c in copies:
                    c.start()
            act, slope = silu_pair(matmul(low_ref[...], wu[...]))
            hid = act.astype(BF)
            out = matmul(hid, wd[...])
            du = (col_inner(c_ref[...], wd[...]) * slope).astype(BF)
            back = col_inner(du, wu[...])
            if i == 0:
                acc[...] = out
                gl[...] = back
            else:
                if before:
                    for c in copies:
                        c.wait()
                    out = out + held[0].astype(F32)
                    back = back + held[1].astype(F32)
                out_ref[...] = (acc[...] + out).astype(BF)
                gl_ref[...] = (gl[...] + back).astype(BF)
            for k, grad in enumerate((row_inner(c_ref[...], hid), row_inner(low_ref[...], du))):
                for j, rows_j in enumerate(split_rows(s, grad)):
                    if form == "sent":
                        put_rows(s, grads[0], rows_j, (k, j))
                    elif form == "own" or k == 0:
                        put_rows(s, grads[2 * k + j], rows_j)
                    else:
                        put_rows(s, grads[2], rows_j, (j,))

        for i in range(2):

            @pl.when(step == i)
            def _(i=i):
                work(wd, i)

    if pieces:
        down = [down[part]]
        specs = [pl.BlockSpec((d // 4, tn), lambda i, s: (0, s[4 + part] * 2 + i))] * 4
        specs += [pl.BlockSpec((tn, d), lambda i, s: (i, 0))]
    else:
        specs = [
            pl.BlockSpec((d, tn), lambda i, s: (0, s[4 + part] * 2 + i)),
            pl.BlockSpec((tn, d), lambda i, s: (s[4 + part] * 2 + i, 0)),
        ]
    still = pl.BlockSpec((n, d), lambda i, s: (0, 0))
    one = pl.BlockSpec((rows, tn), lambda i, s: (0, i))
    two = pl.BlockSpec((2, rows, tn), lambda i, s: (0, 0, i))
    four = pl.BlockSpec((2, 2, rows, tn), lambda i, s: (0, 0, 0, i))
    grad_specs = dict(sent=[four], own=[one] * 4, other=[one, one, two])[form]
    grad_shapes = [sds((*g.block_shape[:-1], 2 * tn)) for g in grad_specs]
    more = list(before) if before else []
    return run(
        body, (2,), scal, [lowered, cot, *up, *down, *more],
        [whole((n, d)), whole((n, d))] + specs + [pl.BlockSpec(memory_space=pltpu.HBM)] * len(more),
        [sds((n, d)), sds((n, d)), *grad_shapes],
        [still, still, *grad_specs],
        [pltpu.VMEM((n, d), F32), pltpu.VMEM((n, d), F32), pltpu.VMEM((d, tn), BF)]
        + ([pltpu.VMEM((2, n, d), BF), pltpu.SemaphoreType.DMA((2,))] if before else []),
        flops=24 * n * d * tn, name="ffn",
    )


def k_mid_back(scal, dl, acc, cot, mixed, fac_h, fac_f, keep, g_own, g_oth, m_own, m_oth,
               u_own, wg_own, h_own, f_own, packs_g, packs_u, packs_h):
    n, d = cot.shape
    half = u_own.shape[0]
    ch = h_own.shape[0]
    ru, rh = packs_u[0].shape[0], packs_h[0].shape[0] // 2
    rg = packs_g[0].shape[0]

    def body(s, l_ref, acc_ref, c_ref, x_ref, a_ref, b_ref, k_ref, go, gt, mo, mt, uo, wo, ho, fo,
             w0, w1, w2, w3, u0, u1, u2, u3, h0, h1, h2, h3, f0, f1, f2, f3,
             out_ref, dh_ref, df_ref, dir_ref, ao, at, do, dt, de_ref, u_scr, w_scr, h_scr, f_scr):
        @pl.when(pl.program_id(0) == 0)
        def _():
            place(u_scr, s, (u0, u1, u2, u3))
            place(w_scr, s, (w0, w1, w2, w3), table=8)
            own = pl.multiple_of(s[6] * ch, ch)
            oth = s[7] * ch
            h_scr[pl.ds(own, ch), :] = ho[...]
            f_scr[pl.ds(own, ch), :] = fo[...]
            place(h_scr, s, (h0, h1, h2, h3), oth, 8)
            place(f_scr, s, (f0, f1, f2, f3), oth, 8)

        dl = l_ref[...].astype(F32)
        m = x_ref[...].astype(F32)
        out_ref[...] = (m + acc_ref[...].astype(F32)).astype(BF)
        r = lax.rsqrt(jnp.mean(m * m, axis=-1, keepdims=True) + norm_eps)
        n2 = m * r
        dm = c_ref[...].astype(F32) + r * (dl - n2 * jnp.mean(dl * n2, axis=-1, keepdims=True))
        dh = (dm * a_ref[...].astype(F32)).astype(BF)
        df = (dm * b_ref[...].astype(F32)).astype(BF)
        dh_ref[...] = dh
        df_ref[...] = df
        dir_ref[...] = (dm * k_ref[...].astype(F32)).astype(BF)
        de = col_inner(dh, h_scr[...]) + col_inner(df, f_scr[...])
        for u, w, g_ref, m_ref, a_out, d_out in ((uo, wo, go, mo, ao, do), (u_scr, w_scr, gt, mt, at, dt)):
            dg = col_inner(dh, u[...])
            a_out[...] = (dg * g_ref[...].astype(F32)).astype(BF)
            low = (dg * m_ref[...].astype(F32)).astype(BF)
            d_out[...] = low
            de = de + col_inner(low, w[...])
        de_ref[...] = de.astype(BF)

    ins = [dl, acc, cot, mixed, fac_h, fac_f, keep, g_own, g_oth, m_own, m_oth, u_own, wg_own, h_own, f_own]
    ins += [*packs_g, *packs_u, *packs_h, *packs_h]
    specs = [rows_of(d)] * 7 + [rows_of(half)] * 4
    specs += [whole((half, d)), whole((d, half)), whole((ch, d)), whole((ch, d))]
    specs += [piece_whole(rg, half, 0)] * 4 + [piece_whole(ru, d, 0)] * 4
    specs += [piece_whole(rh, d, 0)] * 4 + [piece_whole(rh, d, 1)] * 4
    return run(
        body, (n // ROWS,), scal, ins, specs,
        [sds((n, d))] * 4 + [sds((n, half))] * 4 + [sds((n, d))],
        [rows_of(d)] * 4 + [rows_of(half)] * 4 + [rows_of(d)],
        [pltpu.VMEM((half, d), BF), pltpu.VMEM((d, half), BF), pltpu.VMEM((2 * ch, d), BF), pltpu.VMEM((2 * ch, d), BF)],
        flops=2 * n * d * (4 * half + 4 * ch), name="mid_back",
    )


def k_attend_back(scal, p, da_own, da_oth, v_own, v_oth, vs_own, vs_oth, q, k, z_pre, gain):
    n, zw = q.shape
    half = da_own.shape[1]
    blocks = n // ROWS
    scale = zw ** (-0.5)

    def body(s, p_ref, ao, at, vo, vt, so, st, q_ref, k_ref, z_ref, g_ref, oo, ot, dz_ref, sum_ref, dvo, dvt, dks):
        for step, i in enumerate(reversed(range(blocks))):

            @pl.when(pl.program_id(0) == step)
            def _(i=i):
                seen = (i + 1) * ROWS
                lo = i * ROWS
                last = i == blocks - 1
                pb = p_ref[:, 0:seen]
                pr = pb.astype(F32)
                dp = col_inner(ao[...], vo[0:seen, :]) + col_inner(at[...], vt[0:seen, :])
                ds = (pr * (dp - jnp.sum(pr * dp, axis=-1, keepdims=True))).astype(BF)
                dq = matmul(ds, k_ref[0:seen, :]) * scale
                dk = row_inner(ds, q_ref[...]) * scale
                if not last:
                    dk = dk + dks[0:seen, :]
                for a_ref, acc, sl, o_ref in ((ao, dvo, so, oo), (at, dvt, st, ot)):
                    dv = row_inner(pb, a_ref[...])
                    if not last:
                        dv = dv + acc[0:seen, :]
                    if i:
                        acc[0:lo, :] = dv[0:lo]
                    o_ref[...] = (dv[lo:seen] * sl[...].astype(F32)).astype(BF)
                if i:
                    dks[0:lo, :] = dk[0:lo]
                dk = dk[lo:seen]
                act, slope = silu_pair(z_ref[...])
                dz_ref[...] = (slope * (dq * g_ref[0:1, :] + dk * g_ref[1:2, :])).astype(BF)
                for j, v in enumerate((dq * act, dk * act, dq, dk)):
                    part = jnp.sum(v, axis=0, keepdims=True)
                    sum_ref[j : j + 1, :] = part if last else sum_ref[j : j + 1, :] + part
                if last:
                    sum_ref[4:8, :] = jnp.zeros((4, zw), F32)

    def back_rows(cols):
        return pl.BlockSpec((ROWS, cols), lambda i, s: (blocks - 1 - i, 0))

    low = n - ROWS
    return run(
        body, (blocks,), scal, [p, da_own, da_oth, v_own, v_oth, vs_own, vs_oth, q, k, z_pre, gain],
        [back_rows(n), back_rows(half), back_rows(half), whole((n, half)), whole((n, half)), back_rows(half),
         back_rows(half), back_rows(zw), whole((n, zw)), back_rows(zw), whole((2, zw))],
        [sds((n, half)), sds((n, half)), sds((n, zw)), sds((8, zw), F32)],
        [back_rows(half), back_rows(half), back_rows(zw), pl.BlockSpec((8, zw), lambda i, s: (0, 0))],
        [pltpu.VMEM((low, half), F32), pltpu.VMEM((low, half), F32), pltpu.VMEM((low, zw), F32)],
        flops=n * n * 4 * half * 1.25, name="attend_back",
    )


def k_input_back(scal, dv_own, dv_oth, w_own, packs, d_sig, tokens, direct, first, count, before=None):
    n, d = tokens.shape
    rp = packs[0].shape[0]
    half = dv_own.shape[1]

    def body(s, vo, vt, wo, w0, w1, w2, w3, sg, x_ref, dir_ref, *refs):
        o_ref, w_scr = refs[-2:]

        @pl.when(pl.program_id(0) == 0)
        def _():
            place(w_scr, s, (w0, w1, w2, w3))

        dn = col_inner(vo[...], wo[...]) + col_inner(vt[...], w_scr[...]) + sg[...]
        x = x_ref[...].astype(F32)
        r = lax.rsqrt(jnp.mean(x * x, axis=-1, keepdims=True) + norm_eps)
        n1 = x * r
        o_ref[...] = dir_ref[...].astype(F32) + r * (dn - n1 * jnp.mean(dn * n1, axis=-1, keepdims=True))

    def at(cols):
        return pl.BlockSpec((ROWS, cols), lambda i, s: (first + i, 0))

    more = [before] if before is not None else []
    return run(
        body, (count,), scal, [dv_own, dv_oth, w_own, *packs, d_sig, tokens, direct, *more],
        [at(half), at(half), whole((d, half))] + [piece_whole(rp, half, 0)] * 4 + [at(d)] * 3
        + [pl.BlockSpec(memory_space=pltpu.HBM)] * len(more),
        [sds((n, d), F32)], [at(d)],
        [pltpu.VMEM((d, half), BF)],
        flops=4 * ROWS * count * d * half, name="input_back", aliases={11: 0} if more else {},
    )[0]


def k_weight_mid(scal, ema_low, left, right_own, right_oth, gate, part, got=None):
    n, d = ema_low.shape
    tn = d // 4
    rows = d // 2

    def body(s, *refs):
        if gate:
            e_ref, *refs = refs
        l_ref, ro, rt, eo, et, *refs = refs
        for i in range(3):

            @pl.when(pl.program_id(0) == i)
            def _(i=i):
                for k, (r, e) in enumerate(((ro, eo), (rt, et))):
                    lhs = e_ref if gate and i < 2 else l_ref
                    grad = split_rows(s, row_inner(lhs[...], r[...] if i < 2 else e[...]))
                    for j in range(2):
                        if got is None:
                            put_rows(s, refs[0], grad[j], (k, j))
                        elif gate:
                            put_rows(s, refs[1 + k], grad[j], (j,), (refs[0], (k, j)))
                        else:
                            put_rows(s, refs[2 - j], grad[j], (k,), (refs[0], (k, j)))

    at = pl.BlockSpec((n, tn), lambda i, s: (0, s[part] * 2 + jnp.minimum(i, 1)))
    e_own = pl.BlockSpec((n, tn), lambda i, s: (0, s[6] * 2 + s[part]), pipeline_mode=pl.Buffered(1))
    e_oth = pl.BlockSpec((n, tn), lambda i, s: (0, s[7] * 2 + s[part]), pipeline_mode=pl.Buffered(1))
    four = pl.BlockSpec((2, 2, rows, tn), lambda i, s: (0, 0, 0, i))
    two = pl.BlockSpec((2, rows, tn), lambda i, s: (0, 0, i))
    adds = [got] if got is not None else []
    lead = [ema_low] if gate else []
    return run(
        body, (3,), scal, [*lead, left, right_own, right_oth, ema_low, ema_low] + adds,
        [whole((n, d))] * (1 + len(lead)) + [at] * 2 + [e_own, e_oth] + [four] * len(adds),
        [sds((2, rows, 3 * tn))] * 2 if adds else [sds((2, 2, rows, 3 * tn))],
        [two] * 2 if adds else [four],
        flops=2 * n * d * 6 * tn, name="weight_mid",
    )


def k_weight_value(scal, normed, dv_own, dv_oth, ema_low, dz, part, got=None):
    n, d = normed.shape
    width = dv_own.shape[1] // 2
    zw = dz.shape[1]
    shape = (2, 2, d // 2, width + zw)

    def body(s, x_ref, vo, vt, e_ref, z_ref, *refs):
        def put(lanes, value, k, j):
            add = (refs[0].at[:, :, :, lanes], (k, j)) if got is not None else None
            put_rows(s, refs[-1].at[:, :, :, lanes], value, (k, j), add)

        for k, v in enumerate((vo, vt)):
            grad = split_rows(s, row_inner(x_ref[...], v[...]))
            for j in range(2):
                put(slice(0, width), grad[j], k, j)
        grad = split_rows(s, row_inner(e_ref[...], z_ref[...]))
        for j in range(2):
            for k in range(2):
                put(slice(width, width + zw), grad[j], k, j)

    at = pl.BlockSpec((n, width), lambda i, s: (0, s[part]))
    adds = [got] if got is not None else []
    return run(
        body, (1,), scal, [normed, dv_own, dv_oth, ema_low, dz] + adds,
        [whole((n, d)), at, at, whole((n, d)), whole((n, zw))] + [whole(shape)] * len(adds),
        [sds(shape)], [pl.BlockSpec(shape, lambda i, s: (0, 0, 0, 0))],
        flops=2 * n * d * (2 * width + zw), name="weight_value",
    )[0]


def swap(values, axis, bit, size):
    return lax.ppermute(values, axis, [(i, i ^ bit) for i in range(size)])


def pick(values, index, axis):
    return lax.dynamic_index_in_dim(values, index, axis, keepdims=False)


def one_sequence(
    tokens, alpha_logit, delta_logit, ema_beta, ema_eta, ema_omega, w_z, qk_gain, qk_bias,
    w_v, w_gamma, u_h, w_h, w_phi, w_up, w_down, cotangent,
):
    n, d = tokens.shape
    dp_size = lax.axis_size("dp")
    me = lax.axis_index("dp").astype(jnp.int32)
    t = lax.axis_index("tensor").astype(jnp.int32)
    core = me % 2
    x_pos = (me // 2) % 2
    z_pos = me // 4
    kx = core * 2 + x_pos
    kz = core * 2 + z_pos % 2
    scal = jnp.stack(
        [kx, kx ^ 1, kx ^ 2, kx ^ 3, core, 1 - core, t, 1 - t, kz, kz ^ 1, kz ^ 2, kz ^ 3, x_pos, z_pos, 2 * core, 2 * core + 1]
    )

    def held(values, *deps):
        return lax.optimization_barrier((values, deps))[0]

    def after(*deps):
        return held(scal, *deps)

    def over_core(v):
        return swap(v, "dp", 1, dp_size)

    def over_x(v):
        return swap(v, "dp", 2, dp_size)

    def over_z(v):
        return swap(v, "dp", 4, dp_size)

    def over_tensor(v):
        return swap(v, "tensor", 1, 2)

    def my_rows(w, k):
        rows = w.shape[0] // 4
        return lax.dynamic_slice_in_dim(w, k * rows, rows, 0)

    piece_v = my_rows(w_v, kx)
    pv = [over_tensor(piece_v)]
    own_params = k_pack_params(
        after(piece_v), [a.T for a in (alpha_logit, delta_logit, ema_beta, ema_eta)], ema_omega[None]
    )
    oth_params = over_tensor(own_params)
    piece_g, piece_u, piece_h, piece_up, piece_dn = k_pieces(
        after(own_params),
        [[(w_gamma, 8)], [(u_h, 0)], [(w_h, 8), (w_phi, 8)], [(w_up, 0)], [(w_down, 14), (w_down, 15)]],
    )
    normed, v_own, vs_own = k_value_own(after(piece_g), tokens, w_v)
    pg = [over_tensor(held(piece_g, v_own))]
    decay, coef, omega = k_ema_params(after(v_own), own_params, oth_params)
    blocks = n // 128
    ema_a = k_ema_forward(after(v_own), normed, decay, coef, omega, 0, blocks // 2)
    pv.append(over_x(held(pv[0], ema_a[0])))
    pu = [over_tensor(held(piece_u, ema_a[0]))]
    ema_low, e_slope, state = k_ema_forward(
        after(ema_a[0]), normed, decay, coef, omega, blocks // 2, blocks // 2, (ema_a[2], ema_a[0], ema_a[1])
    )
    pg.append(over_z(held(pg[0], ema_a[0])))
    ph = [over_tensor(held(piece_h, state))]
    z_pre, query, key = k_query_key(scal, ema_low, w_z, qk_gain, qk_bias)
    pv += [over_core(v) for v in held((pv[0], pv[1]), query)]
    pu.append(over_x(held(pu[0], query)))
    pup = [over_tensor(held(piece_up, query))]
    v_oth, vs_oth = k_act_other(after(query, pu[0], pg[1]), normed, pv, 0, 512)
    pg += [over_core(v) for v in held((pg[0], pg[1]), v_oth)]
    ph.append(over_z(held(ph[0], v_oth)))
    pdn = [over_tensor(held(piece_dn, v_oth))]
    gated_own, gated_oth, g_own, g_oth, m_own, m_oth, probs = k_attend(
        after(v_oth), query, key, v_own, v_oth, ema_low, w_gamma, pg
    )
    pu += [over_core(v) for v in held((pu[0], pu[1]), probs)]
    ph += [over_core(v) for v in held((ph[0], ph[1]), probs)]
    pup.append(over_x(held(pup[0], probs)))
    mixed, lowered, fac_h, fac_f, keep = k_gate(
        after(probs), gated_own, gated_oth, ema_low, tokens, u_h, w_h, w_phi, pu, ph
    )
    acc, dl, sent_o = k_ffn(after(mixed), lowered, cotangent, [w_up], [w_down], 1)
    pup += [over_core(v) for v in held((pup[0], pup[1]), acc)]
    got_o = over_core(sent_o)
    acc, dl, dno, dno_x, upo, upo_x = k_ffn(
        after(acc), lowered, cotangent, [w_up], [w_down], 0, (acc, dl), "own"
    )
    pdn.append(over_core(held(pdn[0], acc)))

    def total(*values):
        value = values[0].astype(F32)
        for v in values[1:]:
            value = value + v.astype(F32)
        return value

    def add(*values):
        return total(*values).astype(BF)

    def by_z(v):
        return v.reshape(2, 2, d // 8, v.shape[-1])

    def z_send(terms):
        return add(*[by_z(v)[:, 1] for v in terms])

    def z_keep(terms):
        return [by_z(v)[:, 0] for v in terms]

    def over_z2(v):
        return swap(v, "dp", 8, dp_size)

    def core_split(value):
        rows = value.reshape(2, d // 16, value.shape[-1])
        return pick(rows, 1 - core, 0).astype(BF), pick(rows, core, 0)

    def joined(kept, got):
        kept, got = kept.astype(F32), got.astype(F32)
        return jnp.where(
            core == 0, jnp.concatenate([kept, got], axis=1), jnp.concatenate([got, kept], axis=1)
        )

    dn_x1 = add(dno_x, got_o[0, 1])
    dn_got_x1 = over_x(dn_x1)
    acc, dl, sent_t = k_ffn(after(acc, dn_x1), lowered, cotangent, pup, pdn, 1, (acc, dl))
    got_t = over_core(sent_t)
    acc, dl, dnt, dnt_x, upt = k_ffn(after(acc), lowered, cotangent, pup, pdn, 0, (acc, dl), "other")
    dn_x2 = add(dnt_x, got_t[0, 1])
    up_y1 = add(upt, got_t[1])
    dn_got_x2 = over_x(dn_x2)
    up_got_y = over_tensor(up_y1)
    output, dh, df, direct, da_own, da_oth, dg_own, dg_oth, de_part = k_mid_back(
        after(acc, dn_x2, up_y1, dn_got_x1), dl, acc, cotangent, mixed, fac_h, fac_f, keep,
        g_own, g_oth, m_own, m_oth, u_h, w_gamma, w_h, w_phi, pg, pu, ph,
    )
    dn_y = {}

    def start_dn(place, dep):
        if opt["dn"] == place:
            dn_y[0] = add(dnt, got_t[0, 0], held(dn_got_x2, dep))
            dn_y[1] = over_tensor(dn_y[0])
            return (dn_y[0],)
        return ()

    ma_sent = k_weight_mid(after(dh, *start_dn(0, dh)), ema_low, dh, gated_own, gated_oth, False, 5)[0]
    ma_got = over_core(ma_sent)
    mb_sent = k_weight_mid(after(ma_sent, *start_dn(1, ma_sent)), ema_low, df, dg_own, dg_oth, True, 5)[0]
    mb_got = over_core(mb_sent)
    dv_own, dv_oth, dz, stats = k_attend_back(
        after(mb_sent, *start_dn(2, mb_sent)), probs, da_own, da_oth, v_own, v_oth, vs_own, vs_oth, query, key, z_pre, qk_gain
    )
    up_got_y = held(up_got_y, dv_own)
    up_x = add(upo_x, got_o[1, 1], up_got_y[1])
    up_got_x = over_x(up_x)
    ma_theirs, ma_mine = k_weight_mid(after(dv_own, up_x), ema_low, dh, gated_own, gated_oth, False, 4, ma_got)
    ma_got_x = over_x(ma_theirs)
    mb_own, mb_oth = k_weight_mid(after(ma_theirs), ema_low, df, dg_own, dg_oth, True, 4, mb_got)
    mb_got_y = over_tensor(mb_oth)
    val_sent = k_weight_value(after(mb_own), normed, dv_own, dv_oth, ema_low, dz, 5)
    val_got = over_core(val_sent)
    dn_got_y = dn_y[1]
    quarter = blocks // 4

    def ema_back(dep, first, count, before=None):
        return k_ema_backward(
            after(*dep), normed, de_part, dz, e_slope, w_z, decay, coef, omega, first, count, before
        )

    eb = ema_back((val_sent,), 0, quarter)
    up_got_x, dn_got_y = held((up_got_x, dn_got_y), eb[1])
    dn_terms = [dno, got_o[0, 0], dn_got_x1, dn_got_y]
    up_terms = [upo, got_o[1, 0], up_got_y[0], up_got_x]
    ffn_z = jnp.stack([z_send(dn_terms), z_send(up_terms)])
    dn_terms, up_terms = z_keep(dn_terms), z_keep(up_terms)
    ffn_got_z = over_z(ffn_z)
    val = k_weight_value(
        after(eb[1], ffn_z), normed, dv_own, dv_oth, ema_low, dz, 4, val_got
    )
    val = val.reshape(2, 2, 2, 2, d // 8, val.shape[-1])
    val_z1 = val[:, :, :, 1]
    val_kept = val[:, :, :, 0]
    val_got_z1 = over_z(val_z1)
    eb = ema_back((val_z1,), quarter, quarter, eb)
    done = {}

    def second(place, dep):
        forced = []
        if opt["m2"] == place:
            gx, gy = held((ma_got_x, mb_got_y), dep)
            ma_y, mb_x = add(ma_mine[1], gx[1]), add(mb_own[1], gy[1])
            done["m"] = (gx, gy, over_tensor(ma_y), over_x(mb_x))
            forced += [ma_y, mb_x]
        if opt.get("z2", opt["m2"]) == place:
            gz = held(ffn_got_z, dep)
            done["z"] = [*dn_terms, gz[0]], [*up_terms, gz[1]]
            ffn_z2 = jnp.stack([add(*[v[1] for v in ts]) for ts in done["z"]])
            done["z2"] = over_z2(ffn_z2)
            forced.append(ffn_z2)
        if opt["v2"] == place:
            gz = held(val_got_z1, dep)
            val_x = add(val_kept[:, 1], gz[:, 1])
            done["v"] = (gz, over_x(val_x))
            forced.append(val_x)
        if opt.get("z1m", 6) == place:
            gy, gx = held((done["m"][2], done["m"][3]), dep)
            a_terms = [ma_mine[0], done["m"][0][0], gy]
            b_terms = [mb_own[0], done["m"][1][0], gx]
            mid_z = jnp.stack([z_send(a_terms), z_send(b_terms)])
            done["mz"] = (z_keep(a_terms), z_keep(b_terms), over_z(mid_z))
            forced.append(mid_z)
        return forced

    f2 = second(2, eb[1])
    eb = ema_back((eb[1], *f2), 2 * quarter, quarter, eb)
    f3 = second(3, eb[1])
    eb = ema_back((eb[1], *f3), 3 * quarter, quarter, eb)
    d_sig, _, _, sum_a, sum_b, sum_w = eb
    f4 = second(4, sum_a)
    sums = jnp.concatenate([sum_a, sum_b, sum_w, stats], axis=0)
    others = over_z(sums)
    halves = n // ROWS // 2
    part = k_input_back(
        after(sum_a, sums, done["z2"], *f4), dv_own, dv_oth, w_v, pv, d_sig, tokens, direct, 0, halves
    )
    ffn_got_z2 = held(done["z2"], part)
    ffn_total = jnp.stack([total(*[v[0] for v in ts], ffn_got_z2[i]) for i, ts in enumerate(done["z"])])
    ffn_rows = ffn_total.reshape(2, 2, d // 16, -1)
    ffn_got = over_core(pick(ffn_rows, 1 - core, 1).astype(BF))
    ffn_kept = pick(ffn_rows, core, 1)
    f5 = second(5, part)
    sums = sums + held(others, part)
    others = over_z2(sums)
    input_grad = k_input_back(
        after(part, sums, *f5), dv_own, dv_oth, w_v, pv, d_sig, tokens, direct, halves, halves, part
    )
    gz, gx = held(done["v"], input_grad)
    val_y = add(val_kept[1, 0], gz[1, 0], gx[1])
    val_terms = [val_kept[0, 0], gz[0, 0], gx[0], over_tensor(val_y)]
    dn_terms, up_terms = done["z"]
    ma_terms, mb_terms, mid_got_z = done["mz"]

    def last(terms):
        return total(*[v[0] for v in terms])

    sums = sums + held(others, input_grad)
    sums = sums + over_core(sums)
    sums = sums + over_x(sums)
    mid_got_z = held(mid_got_z, sums)
    ma_terms, mb_terms = [*ma_terms, mid_got_z[0]], [*mb_terms, mid_got_z[1]]
    mid_z2 = jnp.stack([add(*[v[1] for v in ma_terms]), add(*[v[1] for v in mb_terms])])
    mid_got_z2 = over_z2(mid_z2)
    sums_got = over_tensor(held(sums, mid_z2))
    val_terms[-1] = held(val_terms[-1], sums_got)
    val_z2 = add(*[v[1] for v in val_terms])
    val_got_z2 = over_z2(val_z2)
    sums = held(sums + sums_got, val_z2)
    down_t, up = joined(ffn_kept[0], ffn_got[0]), joined(ffn_kept[1], ffn_got[1])
    gh = sum_a.shape[0]

    def own_half(v):
        return lax.dynamic_slice_in_dim(v, t * (d // 2), d // 2, 1).T

    tot_a = own_half(sums[:gh].reshape(H, d))
    tot_b = own_half(sums[gh : 2 * gh].reshape(H, d))
    omega_grad = lax.dynamic_slice_in_dim(sums[2 * gh : 2 * gh + d // 128].reshape(d), t * (d // 2), d // 2, 0)
    zsum = sums[2 * gh + d // 128 :]
    rate = jax.nn.sigmoid(alpha_logit)
    damp = jax.nn.sigmoid(delta_logit)
    feed = rate * ema_beta
    feed_grad = ema_eta * tot_a
    decay_grad = feed * ema_eta * tot_b
    alpha_grad = (feed_grad * ema_beta - decay_grad * damp) * rate * (1.0 - rate)
    delta_grad = -decay_grad * rate * damp * (1.0 - damp)
    params = (alpha_grad, delta_grad, feed_grad * rate, feed * tot_a, omega_grad)
    down_grad = down_t.T
    mid_got_z2, val_got_z2 = held((mid_got_z2, val_got_z2), params, down_grad, up)
    mid_total = jnp.stack([total(last(ma_terms), mid_got_z2[0]), total(last(mb_terms), mid_got_z2[1])])
    mid_rows = mid_total.reshape(2, 2, d // 16, -1)
    mid_got = over_core(pick(mid_rows, 1 - core, 1).astype(BF))
    mid_kept = pick(mid_rows, core, 1)
    val_total = last(val_terms) + val_got_z2.astype(F32)
    val_sent, val_rows = core_split(val_total)
    zw = dz.shape[1]
    val_got = over_core(val_sent)
    tn = d // 4
    uh_t, gamma = (joined(mid_kept[i][:, : 2 * tn], mid_got[i][:, : 2 * tn]) for i in range(2))
    wh_t, phi_t = (joined(mid_kept[i][:, 2 * tn :], mid_got[i][:, 2 * tn :]) for i in range(2))
    value = joined(val_rows[:, :-zw], val_got[:, :-zw])
    z_grad = val_rows[:, -zw:]
    return (
        output, input_grad, *params,
        z_grad, zsum[0:2], zsum[2:4], value, gamma, uh_t.T, wh_t.T, phi_t.T, up, down_grad,
    )


def solution(mesh):
    placed = (
        P(("dp", "tensor"), None),
        P("tensor", None),
        P("tensor", None),
        P("tensor", None),
        P("tensor", None),
        P("tensor"),
        P(),
        P(),
        P(),
        P(None, "tensor"),
        P(None, "tensor"),
        P("tensor", None),
        P("tensor", None),
        P("tensor", None),
        P(None, "tensor"),
        P("tensor", None),
        P(("dp", "tensor"), None),
    )

    def per_device(tokens, *rest):
        whole_sequence = tokens.shape[0] == LEN and dict(mesh.shape) == {"dp": 16, "tensor": 2}
        return (one_sequence if whole_sequence else shards)(tokens, *rest)

    return jax.shard_map(
        per_device,
        mesh=mesh,
        in_specs=placed,
        out_specs=(
            P(("dp", "tensor"), None),
            P(("dp", "tensor"), None),
            P("tensor", None),
            P("tensor", None),
            P("tensor", None),
            P("tensor", None),
            P("tensor"),
            P("dp", None),
            P(),
            P(),
            P("dp", "tensor"),
            P("dp", "tensor"),
            P("tensor", "dp"),
            P("tensor", "dp"),
            P("tensor", "dp"),
            P("dp", "tensor"),
            P("tensor", "dp"),
        ),
        check_vma=False,
    )
```
